32 devices in a mesh: dp: 8 (over y, x, core), fsdp: 4 (over z).
Axes of the slice: x: 2, y: 2, z: 4, core: 2. Of those that a mesh axis runs over, the one named last changes fastest.
Arguments:
- tokens: bfloat16 [8192, 1024], P(('dp', 'fsdp')), may hold values from -6 to 6
- lengths: int32 [8, 4], P('dp'), may hold values from 0 to 1024, as said below
- packing: int32 [8, 1024], P('dp'), may hold values from 0 to 1023, each once within a row
- w_query: bfloat16 [1024, 1024], P(('dp', 'fsdp')), may hold values from -0.1875 to 0.1875
- w_key: bfloat16 [1024, 1024], P(('dp', 'fsdp')), may hold values from -0.1875 to 0.1875
- w_value: bfloat16 [1024, 1024], P(('dp', 'fsdp')), may hold values from -0.1875 to 0.1875
- w_gate: bfloat16 [1024, 1024], P(('dp', 'fsdp')), may hold values from -0.1875 to 0.1875
- w_beta: bfloat16 [1024, 8], P(('dp', 'fsdp')), may hold values from -0.1875 to 0.1875
- conv_taps: bfloat16 [3, 4, 1024], P(None, None, ('dp', 'fsdp')), may hold values from -3 to 3
- w_out: bfloat16 [1024, 1024], P(('dp', 'fsdp')), may hold values from -0.3125 to 0.3125
- gain_mix: bfloat16 [1024], P(('dp', 'fsdp')), may hold values from 0.5 to 1.5
- gain_head: bfloat16 [128], P(('dp', 'fsdp')), may hold values from 0.5 to 1.5
- gain_ffn: bfloat16 [1024], P(('dp', 'fsdp')), may hold values from 0.5 to 1.5
- w_ffn_gate: bfloat16 [1024, 2816], P(('dp', 'fsdp')), may hold values from -0.1875 to 0.1875
- w_ffn_up: bfloat16 [1024, 2816], P(('dp', 'fsdp')), may hold values from -0.1875 to 0.1875
- w_ffn_down: bfloat16 [2816, 1024], P(('dp', 'fsdp')), may hold values from -0.1875 to 0.1875
- cotangent: bfloat16 [8192, 1024], P(('dp', 'fsdp')), may hold values from -6 to 6
Outputs:
- layer_out: bfloat16 [8192, 1024], P(('dp', 'fsdp'))
- grad_tokens: float32 [8192, 1024], P(('dp', 'fsdp'))
- grad_w_query: float32 [1024, 1024], P(('dp', 'fsdp'))
- grad_w_key: float32 [1024, 1024], P(('dp', 'fsdp'))
- grad_w_value: float32 [1024, 1024], P(('dp', 'fsdp'))
- grad_w_gate: float32 [1024, 1024], P(('dp', 'fsdp'))
- grad_w_beta: float32 [1024, 8], P(('dp', 'fsdp'))
- grad_conv_taps: float32 [3, 4, 1024], P(None, None, ('dp', 'fsdp'))
- grad_w_out: float32 [1024, 1024], P(('dp', 'fsdp'))
- grad_gain_mix: float32 [1024], P(('dp', 'fsdp'))
- grad_gain_head: float32 [128], P(('dp', 'fsdp'))
- grad_gain_ffn: float32 [1024], P(('dp', 'fsdp'))
- grad_w_ffn_gate: float32 [1024, 2816], P(('dp', 'fsdp'))
- grad_w_ffn_up: float32 [1024, 2816], P(('dp', 'fsdp'))
- grad_w_ffn_down: float32 [2816, 1024], P(('dp', 'fsdp'))
The draws below stay inside these ranges and needn't reach their ends.
Inputs may be any that keep to these rules, and one draw needn't show every extreme that they name: `lengths`: each row sums to 1024; its nonzero entries come first; in every draw some group holds a single sequence of 1024 tokens. `packing`: each row lists every arrival index of its group once.
All inputs are finite; a program needn't handle non-finite values.
Results may differ from the reference program's by a relative error of at most 0.014.
Values may be sent and summed in bfloat16 or wider, within the bound.
No kernel may reach another device: no remote copies, remote signals or barrier semaphores. Data moves between devices by JAX's collectives and lax.ppermute only.
A program may use at most 192 MiB of HBM per device.

```python
import jax
import jax.numpy as jnp
from jax import lax

D = 1024
H = 8
DH = 128
FF = 2816
BLOCK = 64
CONV = 4
SLOTS = 4
GROUP_TOK = 1024
TOKENS = 8192
N_DP = 8


def draw_lengths(key, part):
    groups = N_DP
    subkeys = jax.random.split(key, groups)
    forced = jax.random.randint(jax.random.fold_in(key, 7), (), 0, groups)

    def single(subkey, group_index):
        count = jax.random.randint(jax.random.fold_in(subkey, 1), (), 1, SLOTS + 1)
        count = jnp.where(group_index == forced, 1, count)
        cuts = jax.random.permutation(jax.random.fold_in(subkey, 2), GROUP_TOK - 1)[:SLOTS - 1] + 1
        live = jnp.arange(SLOTS - 1) < count - 1
        cuts = jnp.sort(jnp.where(live, cuts, GROUP_TOK)).astype(jnp.int32)
        bounds = jnp.concatenate([jnp.zeros((1,), jnp.int32), cuts, jnp.full((1,), GROUP_TOK, jnp.int32)])
        return (bounds[1:] - bounds[:-1]).astype(jnp.int32)
    return jax.vmap(single)(subkeys, jnp.arange(groups))


def level_of(stream_key, dims, pieces, low, largest):
    factor_of = 1.0
    for axis_at, shards_of in pieces:
        steps = jax.random.uniform(jax.random.fold_in(jax.random.fold_in(stream_key, 6), axis_at), (shards_of,), jnp.float32, low / len(pieces), largest / len(pieces))
        factor_of = factor_of * jnp.repeat(jnp.exp(steps), dims[axis_at] // shards_of).reshape((-1,) + (1,) * (len(dims) - 1 - axis_at))
    return factor_of


def gaussian(key, dims, scale, limit, cuts=(), held_as=jnp.bfloat16):
    values = scale * jax.random.normal(key, dims, jnp.float32)
    if cuts:
        values = values * level_of(key, dims, cuts, -0.22, 0.18)
    return jnp.clip(values, -limit, limit).astype(held_as)


def setup_inputs(seed: int = 0) -> dict:
    streams_of = jax.random.split(jax.random.key(seed), 18)
    tokens = gaussian(streams_of[0], (TOKENS, D), 1.0, 6.0, ((0, 32),))
    lengths = draw_lengths(jax.random.fold_in(streams_of[17], 71), 0)
    packing = jax.vmap(lambda own: jax.random.permutation(own, GROUP_TOK))(jax.random.split(streams_of[2], N_DP)).reshape((N_DP, GROUP_TOK)).astype(jnp.int32)
    w_query = gaussian(streams_of[3], (D, D), D ** -0.5, 0.1875, ((0, 32),))
    w_key = gaussian(streams_of[4], (D, D), D ** -0.5, 0.1875, ((0, 32),))
    w_value = gaussian(streams_of[5], (D, D), D ** -0.5, 0.1875, ((0, 32),))
    w_gate = gaussian(streams_of[6], (D, D), D ** -0.5, 0.1875, ((0, 32),))
    w_beta = gaussian(streams_of[7], (D, H), D ** -0.5, 0.1875, ((0, 32),))
    conv_taps = gaussian(streams_of[8], (3, CONV, D), CONV ** -0.5, 3.0, ((2, 32),))
    w_out = gaussian(streams_of[9], (D, D), (D // 3) ** -0.5, 0.3125, ((0, 32),))
    gain_mix = jnp.clip(1.0 + 0.1 * jax.random.normal(streams_of[10], (D,), jnp.float32), 0.5, 1.5).astype(jnp.bfloat16)
    gain_head = jnp.clip(1.0 + 0.1 * jax.random.normal(streams_of[11], (DH,), jnp.float32), 0.5, 1.5).astype(jnp.bfloat16)
    gain_ffn = jnp.clip(1.0 + 0.1 * jax.random.normal(streams_of[12], (D,), jnp.float32), 0.5, 1.5).astype(jnp.bfloat16)
    w_ffn_gate = gaussian(streams_of[13], (D, FF), D ** -0.5, 0.1875, ((0, 32),))
    w_ffn_up = gaussian(streams_of[14], (D, FF), D ** -0.5, 0.1875, ((0, 32),))
    w_ffn_down = gaussian(streams_of[15], (FF, D), (FF // 3) ** -0.5, 0.1875, ((0, 32),))
    cotangent = gaussian(streams_of[16], (TOKENS, D), 1.0, 6.0, ((0, 32),))
    return {"tokens": tokens, "lengths": lengths, "packing": packing, "w_query": w_query, "w_key": w_key, "w_value": w_value, "w_gate": w_gate, "w_beta": w_beta, "conv_taps": conv_taps, "w_out": w_out, "gain_mix": gain_mix, "gain_head": gain_head, "gain_ffn": gain_ffn, "w_ffn_gate": w_ffn_gate, "w_ffn_up": w_ffn_up, "w_ffn_down": w_ffn_down, "cotangent": cotangent}


@jax.custom_vjp
def low(v):
    return lax.optimization_barrier(v.astype(jnp.bfloat16)).astype(jnp.float32)

@jax.custom_vjp
def low_back(v):
    return v

def low_keep(v):
    return (low(v), None)

def low_pass(kept, grad):
    return (grad,)

def back_keep(v):
    return (v, None)

def back_low(kept, grad):
    return (low(grad),)
low.defvjp(low_keep, low_pass)
low_back.defvjp(back_keep, back_low)
norm_eps = 1e-05
unit_eps = 1e-06

def matmul(left, right):
    return jnp.dot(left.astype(jnp.float32), right.astype(jnp.float32), precision=lax.Precision.HIGHEST, preferred_element_type=jnp.float32)

def rms_scale(values, gain):
    return values * lax.rsqrt(lax.optimization_barrier(jnp.mean(values * values, axis=-1, keepdims=True)) + norm_eps) * gain

def gated_norm(mixed_rows, gate_proj, gain):
    count, width = mixed_rows.shape
    split = mixed_rows.reshape(count, width // gain.shape[0], gain.shape[0])
    normed = split * lax.rsqrt(lax.optimization_barrier(jnp.mean(split * split, axis=-1, keepdims=True)) + norm_eps) * gain
    return normed.reshape(count, width) * jax.nn.silu(gate_proj)

def swiglu(gate_proj, up_proj):
    return jax.nn.silu(gate_proj) * up_proj

def sequence_layout(lengths_row, total):
    ends = jnp.cumsum(lengths_row).astype(jnp.int32)
    index = jnp.arange(total, dtype=jnp.int32)
    before = index[:, None] >= ends[None, :]
    segment = lax.optimization_barrier(jnp.sum(before.astype(jnp.int32), axis=1)).astype(jnp.int32)
    start = lax.optimization_barrier(jnp.sum(jnp.where(before, lengths_row[None, :].astype(jnp.int32), 0), axis=1)).astype(jnp.int32)
    return (segment, index - start)

def short_conv(values, taps, position):
    width = taps.shape[0]
    total = values.shape[0]
    result = taps[width - 1] * values
    for offset in range(1, width):
        moved = jnp.pad(values, ((offset, 0), (0, 0)))[:total]
        result = result + jnp.where((position >= offset)[:, None], taps[width - 1 - offset] * moved, 0.0)
    return result

def block_step(state, query, keys, values, beta, segment, previous):
    high = lax.Precision.HIGHEST
    size = segment.shape[0]
    same = segment[:, None] == segment[None, :]
    places = jnp.arange(size)
    strict = (places[:, None] > places[None, :]) & same
    inclusive = (places[:, None] >= places[None, :]) & same
    carried = (segment == previous).astype(jnp.float32)
    keys_dot = jnp.einsum('hcd,hed->hce', keys, keys, precision=high)
    system = jnp.eye(size, dtype=jnp.float32) + jnp.where(strict, beta[:, :, None] * keys_dot, 0.0)
    right_side = jnp.concatenate([beta[..., None] * values, (beta * carried)[..., None] * keys], axis=-1)
    solved = jax.scipy.linalg.solve_triangular(system, right_side, lower=True, unit_diagonal=True)
    value_width = values.shape[-1]
    update = solved[..., :value_width] - jnp.einsum('hcd,hde->hce', solved[..., value_width:], state, precision=high)
    scores = jnp.where(inclusive, jnp.einsum('hcd,hed->hce', query, keys, precision=high), 0.0)
    output = carried[:, None] * jnp.einsum('hcd,hde->hce', query, state, precision=high)
    output = output + jnp.einsum('hce,hed->hcd', scores, update, precision=high)
    last_seq = (segment == segment[-1]).astype(jnp.float32)
    new_state = carried[-1] * state + jnp.einsum('hcd,hce->hde', keys * last_seq[:, None], update, precision=high)
    return (new_state, output)

def delta_blocks(query, keys, values, beta, segment):
    total, heads, width = query.shape
    count = total // BLOCK

    def blocks(array):
        return jnp.swapaxes(array.reshape(count, BLOCK, heads, -1), 1, 2)
    beta_blocks = jnp.swapaxes(beta.reshape(count, BLOCK, heads), 1, 2)
    seg_blocks = segment.reshape(count, BLOCK)
    previous = jnp.concatenate([jnp.full((1,), -1, jnp.int32), seg_blocks[:-1, -1].astype(jnp.int32)])
    state = jnp.zeros((heads, width, values.shape[-1]), jnp.float32)

    def advance(carry, block):
        return block_step(carry, block[0], block[1], block[2], block[3], block[4], block[5])
    _, outputs = lax.scan(jax.checkpoint(advance), state, (blocks(query), blocks(keys), blocks(values), beta_blocks, seg_blocks, previous))
    return jnp.swapaxes(outputs, 1, 2).reshape(total, heads, -1)

def head_mixer(query_raw, key_raw, value_raw, beta_raw, taps, packing_row, lengths_row):
    total, width = query_raw.shape
    heads = beta_raw.shape[1]
    segment, position = sequence_layout(lengths_row, total)

    def prepare(raw_rows, tap_rows):
        return jax.nn.silu(short_conv(raw_rows[packing_row], tap_rows, position)).reshape(total, heads, width // heads)
    query = prepare(query_raw, taps[0])
    query = query * lax.rsqrt(lax.optimization_barrier(jnp.sum(query * query, axis=-1, keepdims=True)) + unit_eps)
    keys = prepare(key_raw, taps[1])
    keys = keys * lax.rsqrt(lax.optimization_barrier(jnp.sum(keys * keys, axis=-1, keepdims=True)) + unit_eps)
    values = prepare(value_raw, taps[2])
    beta = jax.nn.sigmoid(beta_raw[packing_row])
    output = delta_blocks(query, keys, values, beta, segment).reshape(total, width)
    return jnp.zeros_like(output).at[packing_row].set(output)

def layer_group(params, group_rows, packing_row, lengths_row):
    w_query, w_key, w_value, w_gate, w_beta, conv_taps, w_out, gain_mix, gain_head, gain_ffn, w_ffn_gate, w_ffn_up, w_ffn_down = params
    hidden = low(rms_scale(group_rows, gain_mix))
    query_raw = low(low_back(matmul(hidden, w_query)))
    key_raw = low(low_back(matmul(hidden, w_key)))
    value_raw = low(low_back(matmul(hidden, w_value)))
    beta_raw = low(low_back(matmul(hidden, w_beta)))
    gate_proj = low_back(matmul(hidden, w_gate))
    mixed = head_mixer(query_raw, key_raw, value_raw, beta_raw, conv_taps, packing_row, lengths_row)
    mixed = low(low_back(mixed))
    normed = low(gated_norm(mixed, gate_proj, gain_head))
    middle = group_rows + low_back(matmul(normed, w_out))
    ffn_in = low(rms_scale(middle, gain_ffn))
    gate_ffn = low_back(matmul(ffn_in, w_ffn_gate))
    up_ffn = low_back(matmul(ffn_in, w_ffn_up))
    active = low(swiglu(gate_ffn, up_ffn))
    return middle + low_back(matmul(active, w_ffn_down))

def forward(all_rows, params, packing, lengths):
    groups = packing.shape[0]
    grouped = all_rows.reshape(groups, -1, all_rows.shape[1])

    def visit(carry, item):
        return (carry, jax.checkpoint(layer_group)(params, item[0], item[1], item[2]))
    _, outputs = lax.scan(visit, None, (grouped, packing, lengths))
    return outputs.reshape(all_rows.shape)

def reference(tokens, lengths, packing, w_query, w_key, w_value, w_gate, w_beta, conv_taps, w_out, gain_mix, gain_head, gain_ffn, w_ffn_gate, w_ffn_up, w_ffn_down, cotangent):
    params = (w_query.astype(jnp.float32), w_key.astype(jnp.float32), w_value.astype(jnp.float32), w_gate.astype(jnp.float32), w_beta.astype(jnp.float32), conv_taps.astype(jnp.float32), w_out.astype(jnp.float32), gain_mix.astype(jnp.float32), gain_head.astype(jnp.float32), gain_ffn.astype(jnp.float32), w_ffn_gate.astype(jnp.float32), w_ffn_up.astype(jnp.float32), w_ffn_down.astype(jnp.float32))
    inputs_f = tokens.astype(jnp.float32)

    def whole(rows_in, weights_in):
        return forward(rows_in, weights_in, packing, lengths)
    output, pullback = jax.vjp(whole, inputs_f, params)
    grad_tokens, grads = pullback(cotangent.astype(jnp.float32))
    return (output.astype(jnp.bfloat16), grad_tokens, grads[0], grads[1], grads[2], grads[3], grads[4], grads[5], grads[6], grads[7], grads[8], grads[9], grads[10], grads[11], grads[12])
```

```python
import functools

import jax
import jax.numpy as jnp
from jax import lax
from jax.experimental import pallas as pl
from jax.experimental.pallas import tpu as pltpu
from jax.sharding import PartitionSpec as P

CHUNK = 128
HALO = 8
norm_eps = 1e-05
unit_eps = 1e-06
NARROW = jnp.bfloat16
WIDE = jnp.float32


def halves(value):
    top = value.astype(NARROW)
    return top, (value - top.astype(WIDE)).astype(NARROW)


def product(left, right, left_dim=1, right_dim=0):
    dims = (((left_dim,), (right_dim,)), ((), ()))

    def one(a, b):
        return lax.dot_general(a, b, dims, preferred_element_type=WIDE)

    if PASSES == 1:
        return one(left[0], right[0])
    return one(left[0], right[0]) + (one(left[0], right[1]) + one(left[1], right[0]))


PASSES = 3


def turned(value):
    return halves(value.T)


def chunk_masks(seg_col, seg_row, before, after):
    size = seg_col.shape[0]
    down = lax.broadcasted_iota(jnp.int32, (size, size), 0)
    across = lax.broadcasted_iota(jnp.int32, (size, size), 1)
    same = seg_col == seg_row
    strict = same & (down > across)
    inclusive = same & (down >= across)
    carried = jnp.where(seg_col == before, 1.0, 0.0).astype(WIDE)
    last = jnp.where(seg_col == after, 1.0, 0.0).astype(WIDE)
    return strict, inclusive, carried, last


def unit_lower_inverse(system):
    size = system.shape[0]
    down = lax.broadcasted_iota(jnp.int32, (size, size), 0)
    across = lax.broadcasted_iota(jnp.int32, (size, size), 1)
    gap = down ^ across
    result = jnp.where(down == across, 1.0, 0.0) - jnp.where((gap == 1) & (down > across), system, 0.0)
    step = 2
    while step < size:
        part = halves(jnp.where((gap >= step) & (gap < 2 * step) & (down > across), system, 0.0))
        done = halves(result)
        result = result - product(done, halves(product(part, done)))
        step *= 2
    return result


def conv_rows(pad_ref, taps, pos, start, column, width):
    window = pad_ref[pl.ds(start, CHUNK + HALO), pl.ds(column, width)]
    count = taps.shape[0]
    result = taps[count - 1 : count] * window[HALO : HALO + CHUNK]
    moved = []
    for offset in range(1, count):
        rows = jnp.where(pos >= offset, window[HALO - offset : HALO - offset + CHUNK], 0.0)
        moved.append(rows)
        result = result + taps[count - 1 - offset : count - offset] * rows
    return result, window[HALO : HALO + CHUNK], moved


def fill_padded(raw_ref, pad_ref, width):
    pad_ref[0:HALO, :] = jnp.zeros((HALO, width), WIDE)
    total = raw_ref.shape[0]

    def copy(index, _):
        start = pl.multiple_of(index * CHUNK, CHUNK)
        pad_ref[pl.ds(start + HALO, CHUNK), :] = raw_ref[pl.ds(start, CHUNK), 0:width].astype(WIDE)
        return 0

    lax.fori_loop(0, total // CHUNK, copy, 0)


def forward_kernel(heads, width, raw_ref, taps_ref, segcol_ref, poscol_ref, segrow_ref, edges_ref,
                   out_ref, q_ref, k_ref, inv_ref, score_ref, dots_ref, upd_ref, state_ref, move_ref,
                   pad_ref, v_ref, base_ref, w_ref):
    total = raw_ref.shape[0]
    count = total // CHUNK
    span = heads * width
    fill_padded(raw_ref, pad_ref, 3 * span)

    def first(index, _):
        start = pl.multiple_of(index * CHUNK, CHUNK)
        rows = pl.ds(start, CHUNK)
        pos = poscol_ref[rows, :]
        before, after = edges_ref[index, 0], edges_ref[index, 1]
        strict, inclusive, carried, last = chunk_masks(
            segcol_ref[rows, :], segrow_ref[pl.ds(index, 1), :], before, after)
        keep = jnp.where(before == after, 1.0, 0.0).astype(WIDE)
        for head in range(heads):
            cols = pl.ds(head * width, width)
            parts = []
            for which in range(3):
                column = which * span + head * width
                value = conv_rows(pad_ref, taps_ref[which, :, head * width:(head + 1) * width], pos,
                                  start, column, width)[0]
                parts.append(value * jax.nn.sigmoid(value))
            query, key, value = parts
            query = query * lax.rsqrt(jnp.sum(query * query, axis=-1, keepdims=True) + unit_eps)
            key = key * lax.rsqrt(jnp.sum(key * key, axis=-1, keepdims=True) + unit_eps)
            q_ref[rows, cols] = query
            k_ref[rows, cols] = key
            beta = jax.nn.sigmoid(raw_ref[rows, 3 * span + head:3 * span + head + 1].astype(WIDE))
            key_h, query_h = halves(key), halves(query)
            dots = product(key_h, key_h, 1, 1)
            score = jnp.where(inclusive, product(query_h, key_h, 1, 1), 0.0)
            inverse = unit_lower_inverse(jnp.where(strict, beta * dots, 0.0))
            inv_h = halves(inverse)
            base = product(inv_h, halves(beta * value))
            carry = product(inv_h, halves((beta * carried) * key))
            tail = turned(last * key)
            eye = jnp.where(lax.broadcasted_iota(jnp.int32, (width, width), 0)
                            == lax.broadcasted_iota(jnp.int32, (width, width), 1), keep, 0.0)
            at = index * heads + head
            dots_ref[at] = dots
            score_ref[at] = score
            inv_ref[at] = inverse
            base_ref[rows, cols] = base
            w_ref[rows, cols] = carry
            move_ref[at] = eye - product(tail, halves(carry))
            state_ref[at] = product(tail, halves(base))
        return 0

    lax.fori_loop(0, count, first, 0)

    def second(index, states):
        result = []
        for head in range(heads):
            at = index * heads + head
            added = state_ref[at]
            state_ref[at] = states[head]
            result.append(product(halves(move_ref[at]), halves(states[head])) + added)
        return tuple(result)

    lax.fori_loop(0, count, second, tuple(jnp.zeros((width, width), WIDE) for _ in range(heads)))

    def third(index, _):
        rows = pl.ds(pl.multiple_of(index * CHUNK, CHUNK), CHUNK)
        carried = jnp.where(segcol_ref[rows, :] == edges_ref[index, 0], 1.0, 0.0).astype(WIDE)
        for head in range(heads):
            cols = pl.ds(head * width, width)
            at = index * heads + head
            state = halves(state_ref[at])
            update = base_ref[rows, cols] - product(halves(w_ref[rows, cols]), state)
            upd_ref[rows, cols] = update
            out = carried * product(halves(q_ref[rows, cols]), state)
            out = out + product(halves(score_ref[at]), halves(update))
            out_ref[rows, cols] = out.astype(out_ref.dtype)
        return 0

    lax.fori_loop(0, count, third, 0)


def backward_kernel(heads, width, raw_ref, taps_ref, segcol_ref, poscol_ref, segrow_ref, edges_ref,
                    q_ref, k_ref, inv_ref, score_ref, dots_ref, upd_ref, state_ref, move_ref, dout_ref,
                    draw_ref, dtaps_ref,
                    pad_ref, grad_ref, pdo_ref, dconv_ref):
    total = raw_ref.shape[0]
    count = total // CHUNK
    span = heads * width
    fill_padded(raw_ref, pad_ref, 3 * span)

    def beta_of(rows, head):
        return jax.nn.sigmoid(raw_ref[rows, 3 * span + head:3 * span + head + 1].astype(WIDE))

    def first(index, _):
        rows = pl.ds(pl.multiple_of(index * CHUNK, CHUNK), CHUNK)
        carried = jnp.where(segcol_ref[rows, :] == edges_ref[index, 0], 1.0, 0.0).astype(WIDE)
        for head in range(heads):
            cols = pl.ds(head * width, width)
            at = index * heads + head
            dout = (dout_ref[rows, cols],)
            dout = (dout[0], jnp.zeros_like(dout[0]))
            score_t = turned(score_ref[at])
            back = product_exact(score_t, dout[0])
            pdo_ref[rows, cols] = back
            inv_t = turned(inv_ref[at])
            back = product(inv_t, halves(back))
            query_t = turned(carried * q_ref[rows, cols])
            key_t = turned((beta_of(rows, head) * carried) * k_ref[rows, cols])
            grad_ref[at] = product_exact(query_t, dout[0]) - product(key_t, halves(back))
        return 0

    lax.fori_loop(0, count, first, 0)

    def second(step, grads):
        index = count - 1 - step
        result = []
        for head in range(heads):
            at = index * heads + head
            added = grad_ref[at]
            grad_ref[at] = grads[head]
            result.append(product(turned(move_ref[at]), halves(grads[head])) + added)
        return tuple(result)

    lax.fori_loop(0, count, second, tuple(jnp.zeros((width, width), WIDE) for _ in range(heads)))
    dconv_ref[total:total + HALO, :] = jnp.zeros((HALO, 3 * span), WIDE)

    def third(index, tap_sums):
        start = pl.multiple_of(index * CHUNK, CHUNK)
        rows = pl.ds(start, CHUNK)
        pos = poscol_ref[rows, :]
        strict, inclusive, carried, last = chunk_masks(
            segcol_ref[rows, :], segrow_ref[pl.ds(index, 1), :], edges_ref[index, 0], edges_ref[index, 1])
        new_sums = []
        dbetas = []
        for head in range(heads):
            cols = pl.ds(head * width, width)
            at = index * heads + head
            beta = beta_of(rows, head)
            query, key, update = q_ref[rows, cols], k_ref[rows, cols], upd_ref[rows, cols]
            query_h, key_h, update_h = halves(query), halves(key), halves(update)
            dout = dout_ref[rows, cols]
            state, grad = halves(state_ref[at]), halves(grad_ref[at])
            convs = []
            for which in range(3):
                column = which * span + head * width
                convs.append(conv_rows(pad_ref, taps_ref[which, :, head * width:(head + 1) * width], pos,
                                       start, column, width))
            gates = [jax.nn.sigmoid(c[0]) for c in convs]
            value = convs[2][0] * gates[2]
            dupdate = pdo_ref[rows, cols] + last * product(key_h, grad)
            dright = product(turned(inv_ref[at]), halves(dupdate))
            dright_h = halves(dright)
            dscore = jnp.where(inclusive, product_exact(update_h, dout, 1, 1, flip=True), 0.0)
            dsystem = jnp.where(strict, product(dright_h, update_h, 1, 1), 0.0)
            dscore_h = halves(dscore)
            dquery = carried * product_exact(state, dout, 1, 1, flip=True) + product(dscore_h, key_h)
            weighted = beta * dsystem
            scaled = beta * carried
            dkey = product(turned(dscore), query_h) + last * product(update_h, grad, 1, 1)
            dkey = dkey - product(halves(weighted + weighted.T), key_h)
            dkey = dkey - scaled * product(dright_h, state, 1, 1)
            dvalue = beta * dright
            seen = carried * product(key_h, state)
            dbeta = jnp.sum(dright * (value - seen), axis=-1, keepdims=True) - jnp.sum(
                dsystem * dots_ref[at], axis=-1, keepdims=True)
            dbetas.append(dbeta * beta * (1.0 - beta))
            sides = []
            for grads, unit, conv, gate in ((dquery, query, convs[0][0], gates[0]), (dkey, key, convs[1][0], gates[1])):
                plain = conv * gate
                inv_norm = lax.rsqrt(jnp.sum(plain * plain, axis=-1, keepdims=True) + unit_eps)
                sides.append(inv_norm * (grads - unit * jnp.sum(unit * grads, axis=-1, keepdims=True)))
            sides.append(dvalue)
            for which in range(3):
                conv, plain, moved = convs[which]
                gate = gates[which]
                dconv = sides[which] * gate * (1.0 + conv * (1.0 - gate))
                column = which * span + head * width
                dconv_ref[rows, pl.ds(column, width)] = dconv
                sums = [jnp.sum(dconv * plain, axis=0, keepdims=True)]
                for shifted in moved:
                    sums.append(jnp.sum(dconv * shifted, axis=0, keepdims=True))
                new_sums.append(jnp.concatenate(sums[::-1], axis=0))
        lane = lax.broadcasted_iota(jnp.int32, (CHUNK, draw_ref.shape[1] - 3 * span), 1)
        packed = jnp.zeros(lane.shape, WIDE)
        for head in range(heads):
            packed = jnp.where(lane == head, dbetas[head], packed)
        draw_ref[rows, pl.ds(3 * span, lane.shape[1])] = packed.astype(draw_ref.dtype)
        return tuple(old + new for old, new in zip(tap_sums, new_sums))

    zero = tuple(jnp.zeros((taps_ref.shape[1], width), WIDE) for _ in range(3 * heads))
    sums = lax.fori_loop(0, count, third, zero)
    for head in range(heads):
        for which in range(3):
            dtaps_ref[which, :, head * width:(head + 1) * width] = sums[head * 3 + which]
    taps_count = taps_ref.shape[1]

    def fourth(index, _):
        start = pl.multiple_of(index * CHUNK, CHUNK)
        pos_window = poscol_ref[pl.ds(start, CHUNK + HALO), :]
        for which in range(3):
            columns = pl.ds(which * span, span)
            window = dconv_ref[pl.ds(start, CHUNK + HALO), columns]
            result = taps_ref[which, taps_count - 1:taps_count, :] * window[0:CHUNK]
            for offset in range(1, taps_count):
                part = jnp.where(pos_window >= offset, window, 0.0)[offset:offset + CHUNK]
                result = result + taps_ref[which, taps_count - 1 - offset:taps_count - offset, :] * part
            draw_ref[pl.ds(start, CHUNK), columns] = result.astype(draw_ref.dtype)
        return 0

    lax.fori_loop(0, count, fourth, 0)


def product_exact(left, exact, left_dim=1, right_dim=0, flip=False):
    def one(a):
        if flip:
            return lax.dot_general(exact, a, (((right_dim,), (left_dim,)), ((), ())), preferred_element_type=WIDE)
        return lax.dot_general(a, exact, (((left_dim,), (right_dim,)), ((), ())), preferred_element_type=WIDE)

    if PASSES == 1:
        return one(left[0])
    return one(left[0]) + one(left[1])


def cost(flops, size):
    return pl.CostEstimate(flops=flops, bytes_accessed=size, transcendentals=0)


def delta_forward(raw, taps, segcol, poscol, segrow, edges, heads, width):
    total, lanes = raw.shape
    count = total // CHUNK
    span = heads * width
    vm = pl.BlockSpec(memory_space=pltpu.VMEM)
    sm = pl.BlockSpec(memory_space=pltpu.SMEM)
    rows = jax.ShapeDtypeStruct((total, span), WIDE)
    square = jax.ShapeDtypeStruct((count * heads, CHUNK, CHUNK), WIDE)
    state = jax.ShapeDtypeStruct((count * heads, width, width), WIDE)
    return pl.pallas_call(
        lambda *refs: forward_kernel(heads, width, *refs),
        out_shape=(jax.ShapeDtypeStruct((total, span), NARROW), rows, rows, square, square, square, rows, state, state),
        in_specs=[vm, vm, vm, vm, vm, sm],
        out_specs=(vm,) * 9,
        scratch_shapes=[
            pltpu.VMEM((total + HALO, 3 * span), WIDE),
            pltpu.VMEM((8, 128), WIDE),
            pltpu.VMEM((total, span), WIDE),
            pltpu.VMEM((total, span), WIDE),
        ],
        compiler_params=pltpu.CompilerParams(vmem_limit_bytes=48 << 20),
        cost_estimate=cost(40_000_000_000, 4 << 20),
        name="delta_forward",
    )(raw, taps, segcol, poscol, segrow, edges)


def delta_backward(raw, taps, segcol, poscol, segrow, edges, kept, dout, heads, width):
    total, lanes = raw.shape
    count = total // CHUNK
    span = heads * width
    vm = pl.BlockSpec(memory_space=pltpu.VMEM)
    sm = pl.BlockSpec(memory_space=pltpu.SMEM)
    poscol = jnp.pad(poscol, ((0, HALO), (0, 0)))
    return pl.pallas_call(
        lambda *refs: backward_kernel(heads, width, *refs),
        out_shape=(jax.ShapeDtypeStruct((total, lanes), NARROW), jax.ShapeDtypeStruct(taps.shape, WIDE)),
        in_specs=[vm, vm, vm, vm, vm, sm] + [vm] * 9,
        out_specs=(vm, vm),
        scratch_shapes=[
            pltpu.VMEM((total + HALO, 3 * span), WIDE),
            pltpu.VMEM((count * heads, width, width), WIDE),
            pltpu.VMEM((total, span), WIDE),
            pltpu.VMEM((total + HALO, 3 * span), WIDE),
        ],
        compiler_params=pltpu.CompilerParams(vmem_limit_bytes=48 << 20),
        cost_estimate=cost(60_000_000_000, 4 << 20),
        name="delta_backward",
    )(raw, taps, segcol, poscol, segrow, edges, *kept, dout)


def rms_scale(values, gain):
    return values * lax.rsqrt(jnp.mean(values * values, axis=-1, keepdims=True) + norm_eps) * gain


def gated_norm(mixed_rows, gate_proj, gain):
    count, width = mixed_rows.shape
    split = mixed_rows.reshape(count, width // gain.shape[0], gain.shape[0])
    normed = split * lax.rsqrt(jnp.mean(split * split, axis=-1, keepdims=True) + norm_eps) * gain
    return normed.reshape(count, width) * jax.nn.silu(gate_proj)


def swiglu(gate_proj, up_proj):
    return jax.nn.silu(gate_proj) * up_proj


def sequence_layout(lengths_row, total):
    ends = jnp.cumsum(lengths_row)
    index = jnp.arange(total, dtype=jnp.int32)
    before = index[:, None] >= ends[None, :]
    segment = jnp.sum(before.astype(jnp.int32), axis=1)
    start = jnp.sum(jnp.where(before, lengths_row[None, :], 0), axis=1)
    return (segment, index - start)


def project(left, right):
    return jnp.dot(left, right, preferred_element_type=WIDE)


def project_back(left, right):
    return lax.dot_general(left, right, (((1,), (1,)), ((), ())), preferred_element_type=WIDE)


def weight_grad(left, right):
    return lax.dot_general(left, right, (((0,), (0,)), ((), ())), preferred_element_type=WIDE)


def flip(value, bit, n_dp):
    return lax.ppermute(value, "dp", [(i, i ^ bit) for i in range(n_dp)])


def shift(value, by, n_fs):
    return lax.ppermute(value, "fsdp", [(i, (i + by) % n_fs) for i in range(n_fs)])


def gather_line(shard, z, n_fs):
    rows = shard.shape[0]
    whole = jnp.zeros((n_fs * rows,) + shard.shape[1:], shard.dtype)
    whole = lax.dynamic_update_slice_in_dim(whole, shard, z * rows, 0)
    for by in range(1, n_fs):
        place = lax.rem(z + n_fs - by, n_fs) * rows
        whole = lax.dynamic_update_slice_in_dim(whole, shift(shard, by, n_fs), place, 0)
    return whole


def gather_cube(piece, order, n_dp):
    pieces = {0: piece}
    for bit in order:
        for key in list(pieces):
            pieces[key ^ bit] = flip(pieces[key], bit, n_dp)
    return pieces


def in_order(pieces, me, columns=slice(None)):
    rows = pieces[0].shape[0]
    whole = None
    for key, piece in pieces.items():
        part = piece[:, columns]
        if whole is None:
            whole = jnp.zeros((len(pieces) * rows, part.shape[1]), part.dtype)
        whole = lax.dynamic_update_slice_in_dim(whole, part, (me ^ key) * rows, 0)
    return whole


def exchange_rows(value, z, n_fs):
    rows = value.shape[0] // n_fs
    total = lax.dynamic_slice_in_dim(value, z * rows, rows, 0)
    for by in range(1, n_fs):
        block = lax.dynamic_slice_in_dim(value, lax.rem(z + by, n_fs) * rows, rows, 0)
        total = total + shift(block.astype(NARROW), by, n_fs).astype(WIDE)
    return total


def scatter_cube(left, right, order, me, n_dp):
    keys = sorted(range(n_dp), key=lambda key: tuple((key & bit) != 0 for bit in order))
    arrived = []
    keep = n_dp
    rows = left.shape[2]

    def term(lo, hi):
        blocks = [lax.dynamic_index_in_dim(left, me ^ key, 0, keepdims=False) for key in keys[lo:hi]]
        stacked = jnp.concatenate(blocks, axis=1) if len(blocks) > 1 else blocks[0]
        value = weight_grad(stacked, right)
        for earlier in arrived:
            value = value + earlier[lo * rows : hi * rows].astype(WIDE)
        return value

    for bit in order:
        keep //= 2
        arrived.append(flip(term(keep, 2 * keep).astype(NARROW), bit, n_dp))
    return term(0, 1)


def column_blocks(value, count):
    tokens = value.shape[0]
    return jnp.swapaxes(value.reshape(tokens, count, -1), 0, 1)


def per_device(
    n_dp,
    n_fs,
    tokens,
    lengths,
    packing,
    w_query,
    w_key,
    w_value,
    w_gate,
    w_beta,
    conv_taps,
    w_out,
    gain_mix,
    gain_head,
    gain_ffn,
    w_ffn_gate,
    w_ffn_up,
    w_ffn_down,
    cotangent,
):
    me = lax.axis_index("dp")
    z = lax.axis_index("fsdp")
    bits = [1 << k for k in range(n_dp.bit_length() - 1)]
    first_order = bits[:1] + bits[1:]
    second_order = bits[:1] + bits[1:][::-1]
    packing_row = packing[0]
    lengths_row = lengths[0]
    own_rows, features = tokens.shape
    total = own_rows * n_fs
    rows = w_query.shape[0]
    heads_all = w_beta.shape[1]
    heads = heads_all // n_fs
    span = features // n_fs
    width = span // heads
    hidden_ffn = w_ffn_gate.shape[1]
    head_rows = gain_head.shape[0]
    n_taps = conv_taps.shape[1]

    def by_owner(matrix):
        return jnp.swapaxes(matrix.reshape(rows, n_fs, -1), 0, 1)

    small = jnp.concatenate(
        [
            gain_mix[:, None],
            gain_ffn[:, None],
            conv_taps.reshape(3 * n_taps, rows).T,
            jnp.pad(gain_head, (0, rows - head_rows))[:, None],
        ],
        axis=1,
    )
    n_small = small.shape[1]
    side = jnp.concatenate(
        [by_owner(w_beta), jnp.broadcast_to(small[None], (n_fs, rows, n_small))], axis=2
    )
    side = jnp.pad(side, ((0, 0), (0, 0), (0, 128 - heads - n_small)))
    packet = jnp.concatenate([by_owner(w_query), by_owner(w_key), by_owner(w_value), side], axis=2)
    packet = lax.all_to_all(packet, "fsdp", split_axis=0, concat_axis=0, tiled=True)
    packet = packet.reshape(n_fs * rows, 3 * span + 128)
    w_in = in_order(gather_cube(packet, first_order[::-1], n_dp), me)
    side_rows = w_in[:, 3 * span :].astype(WIDE).T
    full_gmix = side_rows[heads]
    full_gffn = side_rows[heads + 1]
    local_taps = lax.dynamic_slice_in_dim(
        side_rows[heads + 2 : heads + 2 + 3 * n_taps], z * span, span, 1
    ).reshape(3, n_taps, span)
    full_ghead = side_rows[heads + 2 + 3 * n_taps].reshape(-1, rows)[:, :head_rows].reshape(-1)

    tokens_near = jnp.concatenate([tokens] + [shift(tokens, by, n_fs) for by in range(1, n_fs)], axis=0)
    near_index = lax.rem(z + n_fs - packing_row // own_rows, n_fs) * own_rows + lax.rem(packing_row, own_rows)
    places = jnp.arange(total, dtype=jnp.int32)
    pick_near = (near_index[:, None] == places[None, :]).astype(NARROW)
    pick = (packing_row[:, None] == places[None, :]).astype(NARROW)
    packed = project(pick_near, tokens_near)
    packed_unit = packed * lax.rsqrt(jnp.mean(packed * packed, axis=-1, keepdims=True) + norm_eps)
    hidden_p = (packed_unit * full_gmix).astype(NARROW)
    raw = project(hidden_p, w_in).astype(NARROW)

    segment, position = sequence_layout(lengths_row, total)
    seg_rows = segment.reshape(-1, CHUNK)
    ends = seg_rows[:, -1]
    edges = jnp.stack([jnp.concatenate([jnp.full((1,), -1, jnp.int32), ends[:-1]]), ends], axis=1)
    layout = (segment[:, None], position[:, None], seg_rows, edges)
    forward = delta_forward(raw, local_taps, *layout, heads, width)
    mixed_packed, kept = forward[0], forward[1:]

    pair = gather_cube(
        gather_line(jnp.concatenate([w_gate, w_out], axis=1), z, n_fs), second_order[::-1], n_dp
    )
    full_gate = in_order(pair, me, slice(0, features))
    full_out = in_order(pair, me, slice(features, None))
    full_both = in_order(
        gather_cube(
            gather_line(jnp.concatenate([w_ffn_gate, w_ffn_up], axis=1), z, n_fs),
            first_order[::-1],
            n_dp,
        ),
        me,
    )
    full_down = in_order(gather_cube(gather_line(w_ffn_down, z, n_fs), second_order[::-1], n_dp), me)

    inputs_f = tokens.astype(WIDE)
    hidden, norm_mix_back = jax.vjp(rms_scale, inputs_f, full_gmix)
    hidden_b = hidden.astype(NARROW)
    gate_proj = project(hidden_b, full_gate)
    mixed_arrived = weight_grad(pick, mixed_packed).astype(NARROW)
    mixed = lax.all_to_all(mixed_arrived, "fsdp", split_axis=0, concat_axis=1, tiled=True)
    normed, gated_back = jax.vjp(gated_norm, mixed.astype(WIDE), gate_proj, full_ghead)
    normed_b = normed.astype(NARROW)
    middle = inputs_f + project(normed_b, full_out)
    ffn_in, norm_ffn_back = jax.vjp(rms_scale, middle, full_gffn)
    ffn_in_b = ffn_in.astype(NARROW)
    both = project(ffn_in_b, full_both)
    active, active_back = jax.vjp(swiglu, both[:, :hidden_ffn], both[:, hidden_ffn:])
    active_b = active.astype(NARROW)
    layer_out = (middle + project(active_b, full_down)).astype(NARROW)

    active_blocks = jnp.swapaxes(active_b.T.reshape(n_dp, hidden_ffn // n_dp, own_rows), 1, 2)
    sum_down = scatter_cube(active_blocks, cotangent, second_order, me, n_dp)
    grad_fdown = exchange_rows(sum_down, z, n_fs)
    d_active = project_back(cotangent, full_down)
    d_fgate, d_fup = active_back(d_active)
    d_both = jnp.concatenate([d_fgate.astype(NARROW), d_fup.astype(NARROW)], axis=1)
    d_ffn_in = project_back(d_both, full_both)
    d_middle_norm, d_gffn = norm_ffn_back(d_ffn_in)
    d_middle = cotangent.astype(WIDE) + d_middle_norm
    d_branch = d_middle.astype(NARROW)
    d_normed = project_back(d_branch, full_out)
    d_mixed, d_gate_proj, d_ghead = gated_back(d_normed)
    d_gate_b = d_gate_proj.astype(NARROW)
    d_mixed_arrived = lax.all_to_all(
        d_mixed.astype(NARROW), "fsdp", split_axis=1, concat_axis=0, tiled=True
    )
    d_mixed_packed = project(pick, d_mixed_arrived).astype(NARROW)
    sum_both = scatter_cube(column_blocks(ffn_in_b, n_dp), d_both, first_order, me, n_dp)
    grad_both = exchange_rows(sum_both, z, n_fs)
    sum_out = scatter_cube(column_blocks(normed_b, n_dp), d_branch, second_order, me, n_dp)
    grad_wout = exchange_rows(sum_out, z, n_fs)
    sum_gate = scatter_cube(column_blocks(hidden_b, n_dp), d_gate_b, second_order, me, n_dp)
    grad_wgate = exchange_rows(sum_gate, z, n_fs)

    d_raw, d_taps = delta_backward(raw, local_taps, *layout, kept, d_mixed_packed, heads, width)
    d_hidden_packed = project_back(d_raw, w_in)
    d_hidden_group = weight_grad(pick, d_hidden_packed.astype(NARROW))
    d_hidden_gate = project_back(d_gate_b, full_gate)
    d_hidden = exchange_rows(d_hidden_group, z, n_fs) + d_hidden_gate
    d_inputs_norm, _ = norm_mix_back(d_hidden)
    grad_tokens = d_middle + d_inputs_norm
    own_unit = inputs_f * lax.rsqrt(jnp.mean(inputs_f * inputs_f, axis=-1, keepdims=True) + norm_eps)
    d_gmix = jnp.sum(d_hidden_packed * packed_unit, axis=0) + jnp.sum(d_hidden_gate * own_unit, axis=0)

    grad_in = weight_grad(hidden_p, d_raw)
    taps_rows = lax.dynamic_update_slice_in_dim(
        jnp.zeros((3 * n_taps, features), WIDE), d_taps.reshape(3 * n_taps, span), z * span, 1
    )
    ghead_row = jnp.pad(d_ghead.reshape(-1, head_rows), ((0, 0), (0, rows - head_rows))).reshape(1, features)
    small_rows = jnp.concatenate([d_gmix[None], d_gffn[None], taps_rows, ghead_row], axis=0)
    small_grads = jnp.pad(small_rows.T, ((0, 0), (heads, 128 - heads - n_small)))
    grad_in = jnp.concatenate([grad_in[:, : 3 * span], grad_in[:, 3 * span :] + small_grads], axis=1)
    part = grad_in.reshape(n_dp, n_fs * rows, 3 * span + 128)
    keys = sorted(range(n_dp), key=lambda key: tuple((key & bit) != 0 for bit in first_order))
    part = jnp.stack([lax.dynamic_index_in_dim(part, me ^ key, 0, keepdims=False) for key in keys])
    for bit in first_order:
        keep = part.shape[0] // 2
        part = part[:keep] + flip(part[keep:].astype(NARROW), bit, n_dp).astype(WIDE)
    part = part.reshape(n_fs, rows, 3 * span + 128)
    part = lax.all_to_all(part, "fsdp", split_axis=0, concat_axis=0, tiled=True)

    def columns_of(which):
        return jnp.swapaxes(part[:, :, which * span : (which + 1) * span], 0, 1).reshape(rows, features)

    grad_beta = jnp.swapaxes(part[:, :, 3 * span : 3 * span + heads], 0, 1).reshape(rows, heads_all)
    small_sum = jnp.sum(part[:, :, 3 * span + heads : 3 * span + heads + n_small], axis=0)
    grad_taps = small_sum[:, 2 : 2 + 3 * n_taps].T.reshape(3, n_taps, rows)
    return (
        layer_out,
        grad_tokens,
        columns_of(0),
        columns_of(1),
        columns_of(2),
        grad_wgate,
        grad_beta,
        grad_taps,
        grad_wout,
        small_sum[:, 0],
        small_sum[:head_rows, 2 + 3 * n_taps],
        small_sum[:, 1],
        grad_both[:, :hidden_ffn],
        grad_both[:, hidden_ffn:],
        grad_fdown,
    )


def solution(mesh):
    both = ("dp", "fsdp")
    rows = P(both, None)
    group = P("dp", None)
    taps = P(None, None, both)
    line = P(both)
    in_specs = (rows, group, group) + (rows,) * 5 + (taps, rows, line, line, line) + (rows,) * 4
    out_specs = (rows,) * 7 + (taps, rows, line, line, line) + (rows,) * 3
    return jax.shard_map(
        functools.partial(per_device, mesh.shape["dp"], mesh.shape["fsdp"]),
        mesh=mesh,
        in_specs=in_specs,
        out_specs=out_specs,
        check_vma=False,
    )
```

```python
import functools

import jax
import jax.numpy as jnp
from jax import lax
from jax.experimental import pallas as pl
from jax.experimental.pallas import tpu as pltpu
from jax.sharding import PartitionSpec as P

CHUNK = 128
TP = 4
PER_STEP = 4
BACK_STEP = 2
ENTER = 256
HALO = 8
norm_eps = 1e-05
unit_eps = 1e-06
NARROW = jnp.bfloat16
WIDE = jnp.float32


def halves(value):
    top = value.astype(NARROW)
    return top, (value - top.astype(WIDE)).astype(NARROW)


def product(left, right, left_dim=1, right_dim=0):
    dims = (((left_dim,), (right_dim,)), ((), ()))

    def one(a, b):
        return lax.dot_general(a, b, dims, preferred_element_type=WIDE)

    if PASSES == 1:
        return one(left[0], right[0])
    return one(left[0], right[0]) + (one(left[0], right[1]) + one(left[1], right[0]))


PASSES = 3


def turned(value):
    return halves(value.T)


def chunk_masks(seg_col, seg_row, before, after):
    size = seg_col.shape[0]
    down = lax.broadcasted_iota(jnp.int32, (size, size), 0)
    across = lax.broadcasted_iota(jnp.int32, (size, size), 1)
    same = seg_col == seg_row
    strict = same & (down > across)
    inclusive = same & (down >= across)
    carried = jnp.where(seg_col == before, 1.0, 0.0).astype(WIDE)
    last = jnp.where(seg_col == after, 1.0, 0.0).astype(WIDE)
    return strict, inclusive, carried, last


def unit_lower_inverses(systems):
    size = systems[0].shape[0]
    down = lax.broadcasted_iota(jnp.int32, (size, size), 0)
    across = lax.broadcasted_iota(jnp.int32, (size, size), 1)
    gap = jnp.where(down > across, down ^ across, 0)
    eye = jnp.where(down == across, 1.0, 0.0)
    results = [eye - jnp.where(gap == 1, system, 0.0) for system in systems]
    step = 2
    while step < size:
        picked = (gap >= step) & (gap < 2 * step)
        parts = [halves(jnp.where(picked, system, 0.0)) for system in systems]
        done = [halves(result) for result in results]
        inner = [halves(product(part, own)) for part, own in zip(parts, done)]
        results = [result - product(own, side) for result, own, side in zip(results, done, inner)]
        step *= 2
    return results


def conv_rows(pad_ref, taps, pos, start, column, width):
    window = pad_ref[pl.ds(start, CHUNK + HALO), pl.ds(column, width)]
    count = taps.shape[0]
    result = taps[count - 1 : count] * window[HALO : HALO + CHUNK]
    moved = []
    for offset in range(1, count):
        rows = jnp.where(pos >= offset, window[HALO - offset : HALO - offset + CHUNK], 0.0)
        moved.append(rows)
        result = result + taps[count - 1 - offset : count - offset] * rows
    return result, window[HALO : HALO + CHUNK], moved


def fill_padded(raw_ref, pad_ref, width):
    pad_ref[0:HALO, :] = jnp.zeros((HALO, width), WIDE)
    total = raw_ref.shape[0]

    def copy(index, _):
        start = pl.multiple_of(index * CHUNK, CHUNK)
        pad_ref[pl.ds(start + HALO, CHUNK), :] = raw_ref[pl.ds(start, CHUNK), 0:width].astype(NARROW).astype(WIDE)
        return 0

    lax.fori_loop(0, total // CHUNK, copy, 0)


def one_hot(first, second, offset):
    return jnp.where(first - offset == second, 1.0, 0.0).astype(NARROW)


def plain_dot(left, right, left_dim=1, right_dim=0):
    return lax.dot_general(left, right, (((left_dim,), (right_dim,)), ((), ())), preferred_element_type=WIDE)


def pack_rows(near_col, pieces):
    size = pieces[0].shape[0]
    lane = lax.broadcasted_iota(jnp.int32, (near_col.shape[0], size), 1)
    total = plain_dot(one_hot(near_col, lane, 0), pieces[0][...])
    for k in range(1, len(pieces)):
        total = total + plain_dot(one_hot(near_col, lane, k * size), pieces[k][...])
    return total


def unpack_rows(far_row, packed, k, size):
    down = lax.broadcasted_iota(jnp.int32, (size, far_row.shape[1]), 0)
    return plain_dot(one_hot(far_row, down, k * size), packed).astype(NARROW)


def beta_of(raw_ref, rows, lane):
    return jax.nn.sigmoid(raw_ref[rows, lane:lane + 1].astype(NARROW).astype(WIDE))


def forward_kernel(heads, width, n_fs, *refs):
    pieces, refs = refs[:n_fs], refs[n_fs:]
    (win_ref, gmix_ref, near_ref, far_ref, taps_ref, gain_ref, segcol_ref, poscol_ref, segrow_ref, edges_ref,
     *refs) = refs
    blocks, refs = refs[:n_fs], refs[n_fs:]
    (hidden_ref, packed_ref, raw_ref, out_ref, q_ref, k_ref, inv_ref, score_ref, dots_ref, upd_ref, state_ref,
     move_ref, pad_ref, base_ref, w_ref, normed_ref) = refs
    total = raw_ref.shape[0]
    count = total // CHUNK
    span = heads * width

    def enter(index, _):
        rows = pl.ds(pl.multiple_of(index * ENTER, ENTER), ENTER)
        packed = pack_rows(near_ref[rows, :], pieces)
        packed_ref[rows, :] = packed.astype(NARROW)
        scale = lax.rsqrt(jnp.mean(packed * packed, axis=-1, keepdims=True) + norm_eps)
        hidden = (packed * scale * gmix_ref[...]).astype(NARROW)
        hidden_ref[rows, :] = hidden
        raw_ref[rows, :] = plain_dot(hidden, win_ref[...])
        return 0

    lax.fori_loop(0, total // ENTER, enter, 0)
    fill_padded(raw_ref, pad_ref, 3 * span)

    def first(group, _):
        work = []
        for sub in range(PER_STEP):
            index = group * PER_STEP + sub
            start = pl.multiple_of(index * CHUNK, CHUNK)
            rows = pl.ds(start, CHUNK)
            pos = poscol_ref[rows, :]
            before, after = edges_ref[index, 0], edges_ref[index, 1]
            strict, inclusive, carried, last = chunk_masks(
                segcol_ref[rows, :], segrow_ref[pl.ds(index, 1), :], before, after)
            keep = jnp.where(before == after, 1.0, 0.0).astype(WIDE)
            for head in range(heads):
                cols = pl.ds(head * width, width)
                parts = []
                for which in range(3):
                    column = which * span + head * width
                    value = conv_rows(pad_ref, taps_ref[which, :, head * width:(head + 1) * width], pos,
                                      start, column, width)[0]
                    parts.append(value * jax.nn.sigmoid(value))
                query, key, value = parts
                query = query * lax.rsqrt(jnp.sum(query * query, axis=-1, keepdims=True) + unit_eps)
                key = key * lax.rsqrt(jnp.sum(key * key, axis=-1, keepdims=True) + unit_eps)
                q_ref[rows, cols] = query
                k_ref[rows, cols] = key
                beta = beta_of(raw_ref, rows, 4 * span + head)
                key_h, query_h = halves(key), halves(query)
                dots = product(key_h, key_h, 1, 1)
                score = jnp.where(inclusive, product(query_h, key_h, 1, 1), 0.0)
                at = index * heads + head
                dots_ref[at] = dots
                score_ref[at] = score
                work.append((at, rows, cols, keep, jnp.where(strict, beta * dots, 0.0),
                             beta * value, (beta * carried) * key, last * key))
        inverses = unit_lower_inverses([item[4] for item in work])
        for inverse, (at, rows, cols, keep, _, right, carry_in, tail_in) in zip(inverses, work):
            inv_h = halves(inverse)
            base = product(inv_h, halves(right))
            carry = product(inv_h, halves(carry_in))
            tail = turned(tail_in)
            eye = jnp.where(lax.broadcasted_iota(jnp.int32, (width, width), 0)
                            == lax.broadcasted_iota(jnp.int32, (width, width), 1), keep, 0.0)
            inv_ref[at] = inverse
            base_ref[rows, cols] = base
            w_ref[rows, cols] = carry
            move_ref[at] = eye - product(tail, halves(carry))
            state_ref[at] = product(tail, halves(base))
        return 0

    lax.fori_loop(0, count // PER_STEP, first, 0)

    def second(index, states):
        result = []
        for head in range(heads):
            at = index * heads + head
            added = state_ref[at]
            state_ref[at] = states[head]
            result.append(product(halves(move_ref[at]), halves(states[head])) + added)
        return tuple(result)

    lax.fori_loop(0, count, second, tuple(jnp.zeros((width, width), WIDE) for _ in range(heads)))

    def third(index, _):
        rows = pl.ds(pl.multiple_of(index * CHUNK, CHUNK), CHUNK)
        carried = jnp.where(segcol_ref[rows, :] == edges_ref[index, 0], 1.0, 0.0).astype(WIDE)
        for head in range(heads):
            cols = pl.ds(head * width, width)
            at = index * heads + head
            state = halves(state_ref[at])
            update = base_ref[rows, cols] - product(halves(w_ref[rows, cols]), state)
            upd_ref[rows, cols] = update
            out = carried * product(halves(q_ref[rows, cols]), state)
            out = out + product(halves(score_ref[at]), halves(update))
            mixed = out.astype(NARROW)
            out_ref[rows, cols] = mixed
            mixed = mixed.astype(WIDE)
            scale = lax.rsqrt(jnp.mean(mixed * mixed, axis=-1, keepdims=True) + norm_eps)
            gate = raw_ref[rows, pl.ds(3 * span + head * width, width)]
            normed = mixed * scale * gain_ref[...] * (gate * jax.nn.sigmoid(gate))
            normed_ref[rows, cols] = normed.astype(NARROW)
        return 0

    lax.fori_loop(0, count, third, 0)
    for k, block in enumerate(blocks):
        block[...] = unpack_rows(far_ref[...], normed_ref[...], k, total // n_fs)


def backward_kernel(heads, width, n_fs, *refs):
    pieces, refs = refs[:n_fs], refs[n_fs:]
    (win_ref, near_ref, far_ref, taps_ref, gain_ref, segcol_ref, poscol_ref, segrow_ref, edges_ref,
     packed_ref, raw_ref, mixed_ref, q_ref, k_ref, inv_ref, score_ref, dots_ref, upd_ref, state_ref, move_ref,
     *refs) = refs
    blocks, refs = refs[:n_fs], refs[n_fs:]
    (draw_ref, dtaps_ref, dgain_ref, dgmix_ref,
     pad_ref, grad_ref, pdo_ref, dconv_ref, dout_ref, dnormed_ref, dhid_ref) = refs
    total = raw_ref.shape[0]

    def enter(index, _):
        rows = pl.ds(pl.multiple_of(index * ENTER, ENTER), ENTER)
        dnormed_ref[rows, :] = pack_rows(near_ref[rows, :], pieces).astype(NARROW)
        return 0

    lax.fori_loop(0, total // ENTER, enter, 0)
    count = total // CHUNK
    span = heads * width
    fill_padded(raw_ref, pad_ref, 3 * span)

    def first(group, dgain):
        for sub in range(BACK_STEP):
            index = group * BACK_STEP + sub
            rows = pl.ds(pl.multiple_of(index * CHUNK, CHUNK), CHUNK)
            carried = jnp.where(segcol_ref[rows, :] == edges_ref[index, 0], 1.0, 0.0).astype(WIDE)
            for head in range(heads):
                cols = pl.ds(head * width, width)
                at = index * heads + head
                mixed = mixed_ref[rows, cols].astype(WIDE)
                scale = lax.rsqrt(jnp.mean(mixed * mixed, axis=-1, keepdims=True) + norm_eps)
                gate_cols = pl.ds(3 * span + head * width, width)
                gate = raw_ref[rows, gate_cols]
                sig = jax.nn.sigmoid(gate)
                given = dnormed_ref[rows, cols].astype(WIDE)
                unit = mixed * scale
                dgate = given * unit * gain_ref[...] * (sig * (1.0 + gate * (1.0 - sig)))
                draw_ref[rows, gate_cols] = dgate.astype(NARROW)
                given = given * (gate * sig)
                dgain = dgain + jnp.sum(given * unit, axis=0, keepdims=True)
                given = given * gain_ref[...]
                dout = scale * (given - unit * jnp.mean(unit * given, axis=-1, keepdims=True))
                dout = dout.astype(NARROW)
                dout_ref[rows, cols] = dout
                score_t = turned(score_ref[at])
                back = product_exact(score_t, dout)
                pdo_ref[rows, cols] = back
                inv_t = turned(inv_ref[at])
                back = product(inv_t, halves(back))
                query_t = turned(carried * q_ref[rows, cols])
                key_t = turned((beta_of(raw_ref, rows, 4 * span + head) * carried) * k_ref[rows, cols])
                grad_ref[at] = product_exact(query_t, dout) - product(key_t, halves(back))
        return dgain

    dgain_ref[...] = lax.fori_loop(0, count // BACK_STEP, first, jnp.zeros((1, width), WIDE))

    def second(step, grads):
        index = count - 1 - step
        result = []
        for head in range(heads):
            at = index * heads + head
            added = grad_ref[at]
            grad_ref[at] = grads[head]
            result.append(product(turned(move_ref[at]), halves(grads[head])) + added)
        return tuple(result)

    lax.fori_loop(0, count, second, tuple(jnp.zeros((width, width), WIDE) for _ in range(heads)))
    dconv_ref[total:total + HALO, :] = jnp.zeros((HALO, 3 * span), WIDE)

    def third(group, tap_sums):
        for sub in range(BACK_STEP):
            index = group * BACK_STEP + sub
            start = pl.multiple_of(index * CHUNK, CHUNK)
            rows = pl.ds(start, CHUNK)
            pos = poscol_ref[rows, :]
            strict, inclusive, carried, last = chunk_masks(
                segcol_ref[rows, :], segrow_ref[pl.ds(index, 1), :], edges_ref[index, 0], edges_ref[index, 1])
            new_sums = []
            dbetas = []
            for head in range(heads):
                cols = pl.ds(head * width, width)
                at = index * heads + head
                beta = beta_of(raw_ref, rows, 4 * span + head)
                query, key, update = q_ref[rows, cols], k_ref[rows, cols], upd_ref[rows, cols]
                query_h, key_h, update_h = halves(query), halves(key), halves(update)
                dout = dout_ref[rows, cols]
                state, grad = halves(state_ref[at]), halves(grad_ref[at])
                convs = []
                for which in range(3):
                    column = which * span + head * width
                    convs.append(conv_rows(pad_ref, taps_ref[which, :, head * width:(head + 1) * width], pos,
                                           start, column, width))
                gates = [jax.nn.sigmoid(c[0]) for c in convs]
                value = convs[2][0] * gates[2]
                dupdate = pdo_ref[rows, cols] + last * product(key_h, grad)
                dright = product(turned(inv_ref[at]), halves(dupdate))
                dright_h = halves(dright)
                dscore = jnp.where(inclusive, product_exact(update_h, dout, 1, 1, flip=True), 0.0)
                dsystem = jnp.where(strict, product(dright_h, update_h, 1, 1), 0.0)
                dscore_h = halves(dscore)
                dquery = carried * product_exact(state, dout, 1, 1, flip=True) + product(dscore_h, key_h)
                weighted = beta * dsystem
                scaled = beta * carried
                dkey = product(turned(dscore), query_h) + last * product(update_h, grad, 1, 1)
                dkey = dkey - product(halves(weighted + weighted.T), key_h)
                dkey = dkey - scaled * product(dright_h, state, 1, 1)
                dvalue = beta * dright
                seen = carried * product(key_h, state)
                dbeta = jnp.sum(dright * (value - seen), axis=-1, keepdims=True) - jnp.sum(
                    dsystem * dots_ref[at], axis=-1, keepdims=True)
                dbetas.append(dbeta * beta * (1.0 - beta))
                sides = []
                for grads, unit, conv, gate in ((dquery, query, convs[0][0], gates[0]), (dkey, key, convs[1][0], gates[1])):
                    plain = conv * gate
                    inv_norm = lax.rsqrt(jnp.sum(plain * plain, axis=-1, keepdims=True) + unit_eps)
                    sides.append(inv_norm * (grads - unit * jnp.sum(unit * grads, axis=-1, keepdims=True)))
                sides.append(dvalue)
                for which in range(3):
                    conv, plain, moved = convs[which]
                    gate = gates[which]
                    dconv = sides[which] * gate * (1.0 + conv * (1.0 - gate))
                    column = which * span + head * width
                    dconv_ref[rows, pl.ds(column, width)] = dconv
                    sums = [jnp.sum(dconv * plain, axis=0, keepdims=True)]
                    for shifted in moved:
                        sums.append(jnp.sum(dconv * shifted, axis=0, keepdims=True))
                    new_sums.append(jnp.concatenate(sums[::-1], axis=0))
            lane = lax.broadcasted_iota(jnp.int32, (CHUNK, draw_ref.shape[1] - 4 * span), 1)
            packed = jnp.zeros(lane.shape, WIDE)
            for head in range(heads):
                packed = jnp.where(lane == head, dbetas[head], packed)
            draw_ref[rows, pl.ds(4 * span, lane.shape[1])] = packed.astype(draw_ref.dtype)
            tap_sums = tuple(old + new for old, new in zip(tap_sums, new_sums))
        return tap_sums

    zero = tuple(jnp.zeros((taps_ref.shape[1], width), WIDE) for _ in range(3 * heads))
    sums = lax.fori_loop(0, count // BACK_STEP, third, zero)
    for head in range(heads):
        for which in range(3):
            dtaps_ref[which, :, head * width:(head + 1) * width] = sums[head * 3 + which]
    taps_count = taps_ref.shape[1]

    def fourth(index, _):
        start = pl.multiple_of(index * CHUNK, CHUNK)
        pos_window = poscol_ref[pl.ds(start, CHUNK + HALO), :]
        for which in range(3):
            columns = pl.ds(which * span, span)
            window = dconv_ref[pl.ds(start, CHUNK + HALO), columns]
            result = taps_ref[which, taps_count - 1:taps_count, :] * window[0:CHUNK]
            for offset in range(1, taps_count):
                part = jnp.where(pos_window >= offset, window, 0.0)[offset:offset + CHUNK]
                result = result + taps_ref[which, taps_count - 1 - offset:taps_count - offset, :] * part
            draw_ref[pl.ds(start, CHUNK), columns] = result.astype(draw_ref.dtype)
        return 0

    lax.fori_loop(0, count, fourth, 0)

    def leave(index, sums):
        rows = pl.ds(pl.multiple_of(index * ENTER, ENTER), ENTER)
        dhidden = plain_dot(draw_ref[rows, :], win_ref[...], 1, 1)
        dhid_ref[rows, :] = dhidden.astype(NARROW)
        packed = packed_ref[rows, :].astype(WIDE)
        scale = lax.rsqrt(jnp.mean(packed * packed, axis=-1, keepdims=True) + norm_eps)
        return sums + jnp.sum(dhidden * (packed * scale), axis=0, keepdims=True)

    dgmix_ref[...] = lax.fori_loop(0, total // ENTER, leave, jnp.zeros(dgmix_ref.shape, WIDE))
    for k, block in enumerate(blocks):
        block[...] = unpack_rows(far_ref[...], dhid_ref[...], k, total // n_fs)


def weigh_kernel(heads, width, shard_rows, z_ref, hidden_ref, draw_ref, dtaps_ref, dgain_ref, dgmix_ref, dgffn_ref,
                 out_ref, gradin_ref, small_ref):
    total = hidden_ref.shape[0]
    span = heads * width
    taps_count = dtaps_ref.shape[1]

    def weigh(index, _):
        rows = pl.ds(pl.multiple_of(index * ENTER, ENTER), ENTER)
        gradin_ref[...] += plain_dot(hidden_ref[rows, :], draw_ref[rows, :], 0, 0)
        return 0

    gradin_ref[...] = jnp.zeros(gradin_ref.shape, WIDE)
    lax.fori_loop(0, total // ENTER, weigh, 0)
    features = small_ref.shape[1]
    small_ref[...] = jnp.zeros(small_ref.shape, WIDE)
    small_ref[heads:heads + 1, :] = dgmix_ref[...]
    small_ref[heads + 1:heads + 2, :] = dgffn_ref[...]
    own = pl.ds(pl.multiple_of(z_ref[0] * span, span), span)
    for which in range(3):
        first_row = heads + 2 + which * taps_count
        small_ref[first_row:first_row + taps_count, own] = dtaps_ref[which]
    unit, each = shard_rows
    value = lax.broadcasted_iota(jnp.int32, (width, features), 0)
    lane = lax.broadcasted_iota(jnp.int32, (width, features), 1)
    chosen = (lane // unit == value // each) & (lane % unit == value % each)
    chosen = jnp.where(chosen, 1.0, 0.0).astype(NARROW)
    last_row = heads + 2 + 3 * taps_count
    small_ref[last_row:last_row + 1, :] = product_exact(halves(jnp.broadcast_to(dgain_ref[...], (8, width))), chosen)[0:1]
    side = pl.ds(4 * span, small_ref.shape[0])
    gradin_ref[:, side] += small_ref[...].T
    out_ref[...] = gradin_ref[...].astype(NARROW)


def product_exact(left, exact, left_dim=1, right_dim=0, flip=False):
    def one(a):
        if flip:
            return lax.dot_general(exact, a, (((right_dim,), (left_dim,)), ((), ())), preferred_element_type=WIDE)
        return lax.dot_general(a, exact, (((left_dim,), (right_dim,)), ((), ())), preferred_element_type=WIDE)

    if PASSES == 1:
        return one(left[0])
    return one(left[0]) + one(left[1])


def cost(flops, size):
    return pl.CostEstimate(flops=flops, bytes_accessed=size, transcendentals=0)


def specs(count):
    return [pl.BlockSpec(memory_space=pltpu.VMEM)] * count


def in_scalars():
    return pl.BlockSpec(memory_space=pltpu.SMEM)


def delta_forward(pieces, w_in, gmix, near, far, taps, gain, segcol, poscol, segrow, edges, heads, width):
    n_fs = len(pieces)
    total = near.shape[0]
    features, lanes = w_in.shape
    count = total // CHUNK
    span = heads * width
    thin = jax.ShapeDtypeStruct((total, span), NARROW)
    rows = jax.ShapeDtypeStruct((total, span), WIDE)
    full = jax.ShapeDtypeStruct((total, features), NARROW)
    square = jax.ShapeDtypeStruct((count * heads, CHUNK, CHUNK), WIDE)
    state = jax.ShapeDtypeStruct((count * heads, width, width), WIDE)
    block = jax.ShapeDtypeStruct((total // n_fs, span), NARROW)
    raw = jax.ShapeDtypeStruct((total, lanes), WIDE)
    result = pl.pallas_call(
        functools.partial(forward_kernel, heads, width, n_fs),
        out_shape=(block,) * n_fs
        + (full, full, raw, thin, rows, rows, square, square, square, rows, state, state),
        in_specs=specs(n_fs + 9) + [in_scalars()],
        out_specs=tuple(specs(n_fs + 12)),
        scratch_shapes=[
            pltpu.VMEM((total + HALO, 3 * span), WIDE),
            pltpu.VMEM((total, span), WIDE),
            pltpu.VMEM((total, span), WIDE),
            pltpu.VMEM((total, span), NARROW),
        ],
        compiler_params=pltpu.CompilerParams(vmem_limit_bytes=52 << 20),
        cost_estimate=cost(30_000_000_000, 16 << 20),
        name="delta_forward",
    )(*pieces, w_in, gmix, near, far, taps, gain, segcol, poscol, segrow, edges)
    return result[:n_fs], result[n_fs], result[n_fs + 1 :]


def delta_backward(pieces, w_in, near, far, taps, gain, segcol, poscol, segrow, edges, kept, heads, width):
    n_fs = len(pieces)
    total = near.shape[0]
    features, lanes = w_in.shape
    count = total // CHUNK
    span = heads * width
    poscol = jnp.pad(poscol, ((0, HALO), (0, 0)))
    block = jax.ShapeDtypeStruct((total // n_fs, features), NARROW)
    result = pl.pallas_call(
        functools.partial(backward_kernel, heads, width, n_fs),
        out_shape=(block,) * n_fs
        + (
            jax.ShapeDtypeStruct((total, lanes), NARROW),
            jax.ShapeDtypeStruct(taps.shape, WIDE),
            jax.ShapeDtypeStruct(gain.shape, WIDE),
            jax.ShapeDtypeStruct((1, features), WIDE),
        ),
        in_specs=specs(n_fs + 8) + [in_scalars()] + specs(11),
        out_specs=tuple(specs(n_fs + 4)),
        scratch_shapes=[
            pltpu.VMEM((total + HALO, 3 * span), WIDE),
            pltpu.VMEM((count * heads, width, width), WIDE),
            pltpu.VMEM((total, span), WIDE),
            pltpu.VMEM((total + HALO, 3 * span), WIDE),
            pltpu.VMEM((total, span), NARROW),
            pltpu.VMEM((total, span), NARROW),
            pltpu.VMEM((total, features), NARROW),
        ],
        compiler_params=pltpu.CompilerParams(vmem_limit_bytes=52 << 20),
        cost_estimate=cost(40_000_000_000, 16 << 20),
        name="delta_backward",
    )(*pieces, w_in, near, far, taps, gain, segcol, poscol, segrow, edges, *kept)
    return (result[:n_fs],) + tuple(result[n_fs:])


def weigh_inputs(z, hidden, d_raw, dtaps, dgain, dgmix, dgffn, heads, width, shard_rows):
    features, lanes = hidden.shape[1], d_raw.shape[1]
    return pl.pallas_call(
        functools.partial(weigh_kernel, heads, width, shard_rows),
        out_shape=jax.ShapeDtypeStruct((features, lanes), NARROW),
        in_specs=[in_scalars()] + specs(6),
        out_specs=specs(1)[0],
        scratch_shapes=[pltpu.VMEM((features, lanes), WIDE), pltpu.VMEM((128, features), WIDE)],
        compiler_params=pltpu.CompilerParams(vmem_limit_bytes=40 << 20),
        cost_estimate=cost(60_000_000_000, 8 << 20),
        name="weigh_inputs",
    )(z, hidden, d_raw, dtaps, dgain, dgmix, dgffn)


def mix_out_kernel(n_fs, z_ref, *refs):
    pieces, refs = refs[:n_fs], refs[n_fs:]
    wout_ref, tokens_ref, gain_ref, middle_ref, ffn_ref, normed_ref = refs
    span = pieces[0].shape[1]
    middle = tokens_ref[...].astype(WIDE)
    for k, piece in enumerate(pieces):
        place = pl.ds(pl.multiple_of(lax.rem(z_ref[0] + n_fs - k, n_fs) * span, span), span)
        normed_ref[:, place] = piece[...]
        middle = middle + plain_dot(piece[...], wout_ref[place, :])
    middle_ref[...] = middle
    scale = lax.rsqrt(jnp.mean(middle * middle, axis=-1, keepdims=True) + norm_eps)
    ffn_ref[...] = (middle * scale * gain_ref[...]).astype(NARROW)


def mix_out(z, pieces, w_out, tokens, gain):
    n_fs = len(pieces)
    shape = tokens.shape
    return pl.pallas_call(
        functools.partial(mix_out_kernel, n_fs),
        out_shape=(
            jax.ShapeDtypeStruct(shape, WIDE),
            jax.ShapeDtypeStruct(shape, NARROW),
            jax.ShapeDtypeStruct(shape, NARROW),
        ),
        in_specs=[in_scalars()] + specs(n_fs + 3),
        out_specs=tuple(specs(3)),
        compiler_params=pltpu.CompilerParams(vmem_limit_bytes=40 << 20),
        cost_estimate=cost(2_000_000_000, 6 << 20),
        name="mix_out",
    )(z, *pieces, w_out, tokens, gain)


def mix_back_kernel(n_fs, z_ref, dffn_ref, middle_ref, gain_ref, cot_ref, wout_ref, *refs):
    blocks, (dmiddle_ref, dbranch_ref, dgain_ref) = refs[:n_fs], refs[n_fs:]
    middle, given = middle_ref[...], dffn_ref[...]
    scale = lax.rsqrt(jnp.mean(middle * middle, axis=-1, keepdims=True) + norm_eps)
    unit = middle * scale
    dgain_ref[...] = jnp.sum(given * unit, axis=0, keepdims=True)
    given = given * gain_ref[...]
    dmiddle = cot_ref[...].astype(WIDE) + scale * (given - unit * jnp.mean(unit * given, axis=-1, keepdims=True))
    dmiddle_ref[...] = dmiddle
    dbranch = dmiddle.astype(NARROW)
    dbranch_ref[...] = dbranch
    span = blocks[0].shape[1]
    for k, block in enumerate(blocks):
        place = pl.ds(pl.multiple_of(lax.rem(z_ref[0] + k, n_fs) * span, span), span)
        block[...] = plain_dot(dbranch, wout_ref[place, :], 1, 1).astype(NARROW)


def mix_back(z, dffn, middle, gain, cotangent, w_out, n_fs):
    count, features = middle.shape
    block = jax.ShapeDtypeStruct((count, features // n_fs), NARROW)
    result = pl.pallas_call(
        functools.partial(mix_back_kernel, n_fs),
        out_shape=(block,) * n_fs
        + (
            jax.ShapeDtypeStruct(middle.shape, WIDE),
            jax.ShapeDtypeStruct(middle.shape, NARROW),
            jax.ShapeDtypeStruct(gain.shape, WIDE),
        ),
        in_specs=[in_scalars()] + specs(5),
        out_specs=tuple(specs(n_fs + 3)),
        compiler_params=pltpu.CompilerParams(vmem_limit_bytes=40 << 20),
        cost_estimate=cost(2_000_000_000, 6 << 20),
        name="mix_back",
    )(z, dffn, middle, gain, cotangent, w_out)
    return (result[:n_fs],) + tuple(result[n_fs:])


def rms_scale(values, gain):
    return values * lax.rsqrt(jnp.mean(values * values, axis=-1, keepdims=True) + norm_eps) * gain


def swiglu(gate_proj, up_proj):
    return jax.nn.silu(gate_proj) * up_proj


def sequence_layout(lengths_row, total):
    ends = jnp.cumsum(lengths_row)
    index = jnp.arange(total, dtype=jnp.int32)
    before = index[:, None] >= ends[None, :]
    segment = jnp.sum(before.astype(jnp.int32), axis=1)
    start = jnp.sum(jnp.where(before, lengths_row[None, :], 0), axis=1)
    return (segment, index - start)


def project(left, right):
    return jnp.dot(left, right, preferred_element_type=WIDE)


def project_back(left, right):
    return lax.dot_general(left, right, (((1,), (1,)), ((), ())), preferred_element_type=WIDE)


def weight_grad(left, right):
    return lax.dot_general(left, right, (((0,), (0,)), ((), ())), preferred_element_type=WIDE)


def flip(value, bit, n_dp):
    return lax.ppermute(value, "dp", [(i, i ^ bit) for i in range(n_dp)])


def shift(value, by, n_fs):
    return lax.ppermute(value, "fsdp", [(i, (i + by) % n_fs) for i in range(n_fs)])


def line_pieces(shard, n_fs):
    return [shard] + [shift(shard, by, n_fs) for by in range(1, n_fs)]


def line_order(pieces, z):
    n_fs = len(pieces)
    shape = pieces[0].shape
    whole = jnp.zeros((shape[0], n_fs) + shape[1:], pieces[0].dtype)
    for by, piece in enumerate(pieces):
        whole = lax.dynamic_update_slice_in_dim(whole, piece[:, None], lax.rem(z + n_fs - by, n_fs), 1)
    return whole


def gather_cube(piece, order, n_dp):
    pieces = {0: piece}
    for bit in order:
        for key in list(pieces):
            pieces[key ^ bit] = flip(pieces[key], bit, n_dp)
    return pieces


def in_order(pieces, me):
    rows = pieces[0].shape[0]
    whole = jnp.zeros((len(pieces) * rows,) + pieces[0].shape[1:], pieces[0].dtype)
    unit = max(pieces).bit_length()
    step = (1 << unit) // len(pieces)
    for key, piece in pieces.items():
        whole = lax.dynamic_update_slice_in_dim(whole, piece, lax.bitwise_xor(me, key // step) * rows, 0)
    return whole


def per_device(
    n_dp,
    n_fs,
    tokens,
    lengths,
    packing,
    w_query,
    w_key,
    w_value,
    w_gate,
    w_beta,
    conv_taps,
    w_out,
    gain_mix,
    gain_head,
    gain_ffn,
    w_ffn_gate,
    w_ffn_up,
    w_ffn_down,
    cotangent,
):
    me = lax.axis_index("dp")
    z = lax.axis_index("fsdp")
    bits = [1 << k for k in range(n_dp.bit_length() - 1)]
    first_order = bits[:1] + bits[1:]
    second_order = bits[:1] + bits[1:][::-1]
    packing_row = packing[0]
    lengths_row = lengths[0]
    own_rows, features = tokens.shape
    total = own_rows * n_fs
    rows = w_query.shape[0]
    heads_all = w_beta.shape[1]
    heads = heads_all // n_fs
    span = features // n_fs
    width = span // heads
    hidden_ffn = w_ffn_gate.shape[1]
    head_rows = gain_head.shape[0]
    n_taps = conv_taps.shape[1]

    def by_owner(matrix):
        return jnp.swapaxes(matrix.reshape(rows, n_fs, -1), 0, 1)

    small = jnp.concatenate(
        [
            gain_mix[:, None],
            gain_ffn[:, None],
            conv_taps.reshape(3 * n_taps, rows).T,
            jnp.pad(gain_head, (0, rows - head_rows))[:, None],
        ],
        axis=1,
    )
    n_small = small.shape[1]
    side = jnp.concatenate(
        [by_owner(w_beta), jnp.broadcast_to(small[None], (n_fs, rows, n_small))], axis=2
    )
    side = jnp.pad(side, ((0, 0), (0, 0), (0, 128 - heads - n_small)))
    packet = jnp.concatenate(
        [by_owner(w_query), by_owner(w_key), by_owner(w_value), by_owner(w_gate), side], axis=2
    )
    member = lax.rem(me, TP)
    block = me // TP
    n_rest = n_dp // TP
    ff_block = hidden_ffn // n_dp
    ff_own = n_rest * ff_block
    ff_pad = -(-ff_own // 128) * 128
    tp_bits = [bit for bit in bits if bit < TP]
    rest_bits = [bit for bit in bits if bit >= TP]

    def by_member(matrix):
        split = matrix.reshape(rows, n_rest, TP, ff_block)
        split = jnp.transpose(split, (2, 0, 1, 3)).reshape(TP, rows, ff_own)
        return jnp.pad(split, ((0, 0), (0, 0), (0, ff_pad - ff_own)))

    def hand_out(blocks):
        pieces = [lax.dynamic_index_in_dim(blocks, z, 0)]
        for by in range(1, n_fs):
            pieces.append(shift(lax.dynamic_index_in_dim(blocks, lax.rem(z + by, n_fs), 0), by, n_fs))
        return pieces

    packet = line_order(hand_out(packet), z).reshape(n_fs * rows, 4 * span + 128)
    w_in = lax.all_gather(packet, "dp", axis=0, tiled=True)
    full_out = lax.all_gather(w_out, ("dp", "fsdp"), axis=0, tiled=True)
    side_rows = w_in[:, 4 * span :].astype(WIDE).T
    full_gmix = side_rows[heads]
    full_gffn = side_rows[heads + 1]
    local_taps = lax.dynamic_slice_in_dim(
        side_rows[heads + 2 : heads + 2 + 3 * n_taps], z * span, span, 1
    ).reshape(3, n_taps, span)
    full_ghead = side_rows[heads + 2 + 3 * n_taps].reshape(-1, rows)[:, :head_rows].reshape(-1)

    owner, place = packing_row // own_rows, lax.rem(packing_row, own_rows)
    near = (lax.rem(z + n_fs - owner, n_fs) * own_rows + place)[:, None]
    far = (lax.rem(owner + n_fs - z, n_fs) * own_rows + place)[None]
    segment, position = sequence_layout(lengths_row, total)
    seg_rows = segment.reshape(-1, CHUNK)
    ends = seg_rows[:, -1]
    edges = jnp.stack([jnp.concatenate([jnp.full((1,), -1, jnp.int32), ends[:-1]]), ends], axis=1)
    layout = (near, far, local_taps, full_ghead[None], segment[:, None], position[:, None], seg_rows, edges)
    token_pieces = [tokens] + [shift(tokens, by, n_fs) for by in range(1, n_fs)]
    own_gate, own_up, own_cotangent, _ = lax.optimization_barrier(
        (w_ffn_gate, w_ffn_up, cotangent, token_pieces[1])
    )
    both_sends = jnp.concatenate([by_member(own_gate), by_member(own_up)], axis=2)
    blocks, hidden_p, kept = delta_forward(token_pieces, w_in, full_gmix[None], *layout, heads, width)

    both_pieces = {
        key: flip(lax.dynamic_index_in_dim(both_sends, member ^ key, 0, keepdims=False), key, n_dp)
        if key
        else lax.dynamic_index_in_dim(both_sends, member, 0, keepdims=False)
        for key in range(TP)
    }
    both_rows, _ = lax.optimization_barrier((in_order(both_pieces, member), token_pieces))
    both_line = line_pieces(both_rows.reshape(TP, rows, 2 * ff_pad), n_fs)
    both_line, blocks = lax.optimization_barrier((both_line, blocks))
    both_rows = line_order(both_line, z).reshape(-1, 2 * ff_pad)
    w_both = in_order(gather_cube(both_rows, rest_bits, n_dp), block)
    tp_order = sorted(range(TP), key=lambda key: tuple((key & bit) != 0 for bit in tp_bits))

    def spread(value):
        pieces = gather_cube(value, tp_bits[::-1], n_dp)
        return jnp.concatenate([pieces[key] for key in tp_order], axis=0)

    cotangent_near = spread(own_cotangent)

    def collect(left, right, dims):
        arrived = []
        keep = TP

        def term(lo, hi):
            value = lax.dot_general(
                left[lo * own_rows : hi * own_rows], right, (dims, ((), ())), preferred_element_type=WIDE
            )
            for earlier in arrived:
                value = value + earlier[lo * own_rows : hi * own_rows].astype(WIDE)
            return value

        for bit in tp_bits:
            keep //= 2
            arrived.append(flip(term(keep, 2 * keep).astype(NARROW), bit, n_dp))
        return term(0, 1)

    def halve(value, index, some_bits):
        unit = some_bits[0] if some_bits else 1
        for bit in some_bits[::-1]:
            half = value.shape[0] // 2
            mine = (index // (bit // unit)) % 2
            sent = lax.dynamic_slice_in_dim(value, (1 - mine) * half, half, 0)
            value = lax.dynamic_slice_in_dim(value, mine * half, half, 0)
            value = value.astype(WIDE) + flip(sent.astype(NARROW), bit, n_dp).astype(WIDE)
        return value

    def sum_up(pieces, whole):
        total = lax.dynamic_index_in_dim(whole, z, 0, keepdims=False).astype(WIDE)
        for piece in pieces[1:]:
            total = total + piece[0].astype(WIDE)
        return total

    def pass_on(parts):
        return [parts[0]] + [shift(part, by, n_fs) for by, part in enumerate(parts) if by]

    z_ref = z.reshape(1)
    mixed_pieces = pass_on(blocks)
    own_down, _ = lax.optimization_barrier((w_ffn_down, mixed_pieces))
    down_line = line_pieces(own_down[None], n_fs)
    middle, ffn_in, normed_b = mix_out(z_ref, mixed_pieces, full_out, tokens, full_gffn[None])
    down_rows = line_order(down_line, z).reshape(-1, features)
    w_down = in_order(gather_cube(down_rows, rest_bits, n_dp), block)
    w_down = jnp.pad(w_down, ((0, ff_pad - ff_own), (0, 0)))
    ffn_near = spread(ffn_in)
    both = project(ffn_near, w_both)
    active, active_back = jax.vjp(swiglu, both[:, :ff_pad], both[:, ff_pad:])
    active_b = active.astype(NARROW)
    down_terms = weight_grad(active_b, cotangent_near)[:ff_own].reshape(n_rest, -1, features)
    down_sum = halve(down_terms, block, rest_bits).reshape(n_fs, -1, features)
    d_active = project_back(cotangent_near, w_down)
    d_fgate, d_fup = active_back(d_active)
    d_both = jnp.concatenate([d_fgate.astype(NARROW), d_fup.astype(NARROW)], axis=1)
    both_terms = weight_grad(ffn_near, d_both).astype(NARROW)
    both_sum = lax.psum_scatter(
        both_terms.reshape(n_dp, n_fs * rows, 2 * ff_pad), "fsdp", scatter_dimension=1, tiled=True
    )
    d_ffn_in = collect(d_both, w_both, ((1,), (1,)))
    d_ffn_in, both_terms = lax.optimization_barrier((d_ffn_in, both_terms))

    d_blocks, d_middle, d_branch, d_gffn = mix_back(
        z_ref, d_ffn_in, middle, full_gffn[None], cotangent, full_out, n_fs
    )
    d_blocks, down_sum = lax.optimization_barrier((d_blocks, down_sum))
    d_pieces = pass_on(d_blocks)
    grad_fdown = sum_up(hand_out(down_sum.astype(NARROW)), down_sum)
    sum_out = lax.psum_scatter(
        weight_grad(normed_b, d_branch).astype(NARROW), "dp", scatter_dimension=0, tiled=True
    )
    layer_out = (middle + collect(active_b, w_down, ((1,), (0,)))).astype(NARROW)
    d_blocks, d_raw, d_taps, d_ghead, d_gmix = delta_backward(d_pieces, w_in, *layout, kept, heads, width)
    d_blocks = pass_on(d_blocks)
    grad_in = weigh_inputs(
        z_ref, hidden_p, d_raw, d_taps, d_ghead, d_gmix, d_gffn, heads, width, (rows, head_rows)
    )
    grad_in, both_sum, layer_out, grad_fdown = lax.optimization_barrier((grad_in, both_sum, layer_out, grad_fdown))
    part = lax.psum_scatter(grad_in, "dp", scatter_dimension=0, tiled=True)
    d_blocks, both_sum = lax.optimization_barrier((d_blocks, both_sum))
    both_sum = halve(both_sum, block, rest_bits)
    both_pieces = {
        key: flip(lax.dynamic_index_in_dim(both_sum, member ^ key, 0, keepdims=False), key, n_dp)
        if key
        else lax.dynamic_index_in_dim(both_sum, member, 0, keepdims=False)
        for key in range(TP)
    }
    both_mine = in_order({key: piece[None] for key, piece in both_pieces.items()}, member)
    d_hidden = d_blocks[0].astype(WIDE)
    for block_of in d_blocks[1:]:
        d_hidden = d_hidden + block_of.astype(WIDE)

    def units_of(which):
        part = both_mine[:, :, which * ff_pad : which * ff_pad + ff_own].reshape(TP, rows, n_rest, ff_block)
        return jnp.transpose(part, (1, 2, 0, 3)).reshape(rows, hidden_ffn)

    _, norm_mix_back = jax.vjp(rms_scale, tokens.astype(WIDE), full_gmix)
    d_inputs_norm, _ = norm_mix_back(d_hidden)
    grad_tokens = d_middle + d_inputs_norm

    lanes = part.shape[1]
    joint = jnp.concatenate([part, sum_out], axis=1).reshape(n_fs, rows, -1)
    arrived = [piece[0] for piece in hand_out(joint)]
    part = line_order([piece[None, :, :lanes] for piece in arrived], z)[0].astype(WIDE)
    grad_wout = jnp.zeros((rows, features), WIDE)
    for piece in arrived:
        grad_wout = grad_wout + piece[:, lanes:].astype(WIDE)

    def columns_of(which):
        return jnp.swapaxes(part[:, :, which * span : (which + 1) * span], 0, 1).reshape(rows, features)

    grad_beta = jnp.swapaxes(part[:, :, 4 * span : 4 * span + heads], 0, 1).reshape(rows, heads_all)
    small_sum = jnp.sum(part[:, :, 4 * span + heads : 4 * span + heads + n_small], axis=0)
    grad_taps = small_sum[:, 2 : 2 + 3 * n_taps].T.reshape(3, n_taps, rows)
    return (
        layer_out,
        grad_tokens,
        columns_of(0),
        columns_of(1),
        columns_of(2),
        columns_of(3),
        grad_beta,
        grad_taps,
        grad_wout,
        small_sum[:, 0],
        small_sum[:head_rows, 2 + 3 * n_taps],
        small_sum[:, 1],
        units_of(0),
        units_of(1),
        grad_fdown,
    )


def solution(mesh):
    both = ("dp", "fsdp")
    rows = P(both, None)
    group = P("dp", None)
    taps = P(None, None, both)
    line = P(both)
    in_specs = (rows, group, group) + (rows,) * 5 + (taps, rows, line, line, line) + (rows,) * 4
    out_specs = (rows,) * 7 + (taps, rows, line, line, line) + (rows,) * 3
    return jax.shard_map(
        functools.partial(per_device, mesh.shape["dp"], mesh.shape["fsdp"]),
        mesh=mesh,
        in_specs=in_specs,
        out_specs=out_specs,
        check_vma=False,
    )
```

```python
import functools

import jax
import jax.numpy as jnp
from jax import lax
from jax.experimental import pallas as pl
from jax.experimental.pallas import tpu as pltpu
from jax.sharding import PartitionSpec as P

CHUNK = 128
TP = 4
PER_STEP = 4
BACK_STEP = 2
ENTER = 256
HALO = 8
norm_eps = 1e-05
unit_eps = 1e-06
NARROW = jnp.bfloat16
WIDE = jnp.float32


def halves(value):
    top = value.astype(NARROW)
    return top, (value - top.astype(WIDE)).astype(NARROW)


def product(left, right, left_dim=1, right_dim=0):
    dims = (((left_dim,), (right_dim,)), ((), ()))

    def one(a, b):
        return lax.dot_general(a, b, dims, preferred_element_type=WIDE)

    if PASSES == 1:
        return one(left[0], right[0])
    return one(left[0], right[0]) + (one(left[0], right[1]) + one(left[1], right[0]))


PASSES = 3


def turned(value):
    return halves(value.T)


def chunk_masks(seg_col, seg_row, before, after):
    size = seg_col.shape[0]
    down = lax.broadcasted_iota(jnp.int32, (size, size), 0)
    across = lax.broadcasted_iota(jnp.int32, (size, size), 1)
    same = seg_col == seg_row
    strict = same & (down > across)
    inclusive = same & (down >= across)
    carried = jnp.where(seg_col == before, 1.0, 0.0).astype(WIDE)
    last = jnp.where(seg_col == after, 1.0, 0.0).astype(WIDE)
    return strict, inclusive, carried, last


def unit_lower_inverses(systems):
    size = systems[0].shape[0]
    down = lax.broadcasted_iota(jnp.int32, (size, size), 0)
    across = lax.broadcasted_iota(jnp.int32, (size, size), 1)
    gap = jnp.where(down > across, down ^ across, 0)
    eye = jnp.where(down == across, 1.0, 0.0)
    results = [eye - jnp.where(gap == 1, system, 0.0) for system in systems]
    step = 2
    while step < size:
        picked = (gap >= step) & (gap < 2 * step)
        parts = [halves(jnp.where(picked, system, 0.0)) for system in systems]
        done = [halves(result) for result in results]
        inner = [halves(product(part, own)) for part, own in zip(parts, done)]
        results = [result - product(own, side) for result, own, side in zip(results, done, inner)]
        step *= 2
    return results


def conv_rows(pad_ref, taps, pos, start, column, width):
    window = pad_ref[pl.ds(start, CHUNK + HALO), pl.ds(column, width)]
    count = taps.shape[0]
    result = taps[count - 1 : count] * window[HALO : HALO + CHUNK]
    moved = []
    for offset in range(1, count):
        rows = jnp.where(pos >= offset, window[HALO - offset : HALO - offset + CHUNK], 0.0)
        moved.append(rows)
        result = result + taps[count - 1 - offset : count - offset] * rows
    return result, window[HALO : HALO + CHUNK], moved


def fill_padded(raw_ref, pad_ref, width):
    pad_ref[0:HALO, :] = jnp.zeros((HALO, width), WIDE)
    total = raw_ref.shape[0]

    def copy(index, _):
        start = pl.multiple_of(index * CHUNK, CHUNK)
        pad_ref[pl.ds(start + HALO, CHUNK), :] = raw_ref[pl.ds(start, CHUNK), 0:width].astype(NARROW).astype(WIDE)
        return 0

    lax.fori_loop(0, total // CHUNK, copy, 0)


def one_hot(first, second, offset):
    return jnp.where(first - offset == second, 1.0, 0.0).astype(NARROW)


def plain_dot(left, right, left_dim=1, right_dim=0):
    return lax.dot_general(left, right, (((left_dim,), (right_dim,)), ((), ())), preferred_element_type=WIDE)


def pack_rows(near_col, pieces):
    size = pieces[0].shape[0]
    lane = lax.broadcasted_iota(jnp.int32, (near_col.shape[0], size), 1)
    total = plain_dot(one_hot(near_col, lane, 0), pieces[0][...])
    for k in range(1, len(pieces)):
        total = total + plain_dot(one_hot(near_col, lane, k * size), pieces[k][...])
    return total


def unpack_rows(far_row, packed, k, size):
    down = lax.broadcasted_iota(jnp.int32, (size, far_row.shape[1]), 0)
    return plain_dot(one_hot(far_row, down, k * size), packed).astype(NARROW)


def beta_of(raw_ref, rows, lane):
    return jax.nn.sigmoid(raw_ref[rows, lane:lane + 1].astype(NARROW).astype(WIDE))


def shard_places(size, features, shard_rows, turned_round):
    unit, each = shard_rows
    shape = (features, size) if turned_round else (size, features)
    value = lax.broadcasted_iota(jnp.int32, shape, 1 if turned_round else 0)
    lane = lax.broadcasted_iota(jnp.int32, shape, 0 if turned_round else 1)
    chosen = (lane // unit == value // each) & (lane % unit == value % each)
    return jnp.where(chosen, 1.0, 0.0).astype(NARROW)


def forward_kernel(heads, width, n_fs, shard_rows, *refs):
    pieces, refs = refs[:n_fs], refs[n_fs:]
    (win_ref, near_ref, far_ref, segcol_ref, poscol_ref, segrow_ref, edges_ref, z_ref, *refs) = refs
    blocks, refs = refs[:n_fs], refs[n_fs:]
    (side_ref, taps_ref, gain_ref, hidden_ref, raw_ref, out_ref, q_ref, k_ref, inv_ref, score_ref, dots_ref, upd_ref, state_ref,
     move_ref, pad_ref, base_ref, w_ref, normed_ref) = refs
    total = raw_ref.shape[0]
    count = total // CHUNK
    span = heads * width
    side_ref[...] = win_ref[:, 4 * span:].astype(WIDE).T
    taps_count = taps_ref.shape[1]
    own = pl.ds(pl.multiple_of(z_ref[0] * span, span), span)
    for which in range(3):
        first_row = heads + 2 + which * taps_count
        taps_ref[which] = side_ref[first_row:first_row + taps_count, own]
    last_row = heads + 2 + 3 * taps_count
    entries = jnp.broadcast_to(side_ref[last_row:last_row + 1, :], (8, side_ref.shape[1])).astype(NARROW)
    gain_ref[...] = plain_dot(entries, shard_places(width, side_ref.shape[1], shard_rows, True))[0:1]

    def enter(index, _):
        rows = pl.ds(pl.multiple_of(index * ENTER, ENTER), ENTER)
        packed = pack_rows(near_ref[rows, :], pieces)
        scale = lax.rsqrt(jnp.mean(packed * packed, axis=-1, keepdims=True) + norm_eps)
        hidden = (packed * scale * side_ref[heads:heads + 1, :]).astype(NARROW)
        hidden_ref[rows, :] = hidden
        raw_ref[rows, :] = plain_dot(hidden, win_ref[...])
        return 0

    lax.fori_loop(0, total // ENTER, enter, 0)
    fill_padded(raw_ref, pad_ref, 3 * span)

    def first(group, _):
        work = []
        for sub in range(PER_STEP):
            index = group * PER_STEP + sub
            start = pl.multiple_of(index * CHUNK, CHUNK)
            rows = pl.ds(start, CHUNK)
            pos = poscol_ref[rows, :]
            before, after = edges_ref[index, 0], edges_ref[index, 1]
            strict, inclusive, carried, last = chunk_masks(
                segcol_ref[rows, :], segrow_ref[pl.ds(index, 1), :], before, after)
            keep = jnp.where(before == after, 1.0, 0.0).astype(WIDE)
            for head in range(heads):
                cols = pl.ds(head * width, width)
                parts = []
                for which in range(3):
                    column = which * span + head * width
                    value = conv_rows(pad_ref, taps_ref[which, :, head * width:(head + 1) * width], pos,
                                      start, column, width)[0]
                    parts.append(value * jax.nn.sigmoid(value))
                query, key, value = parts
                query = query * lax.rsqrt(jnp.sum(query * query, axis=-1, keepdims=True) + unit_eps)
                key = key * lax.rsqrt(jnp.sum(key * key, axis=-1, keepdims=True) + unit_eps)
                q_ref[rows, cols] = query
                k_ref[rows, cols] = key
                beta = beta_of(raw_ref, rows, 4 * span + head)
                key_h, query_h = halves(key), halves(query)
                dots = product(key_h, key_h, 1, 1)
                score = jnp.where(inclusive, product(query_h, key_h, 1, 1), 0.0)
                at = index * heads + head
                dots_ref[at] = dots
                score_ref[at] = score
                work.append((at, rows, cols, keep, jnp.where(strict, beta * dots, 0.0),
                             beta * value, (beta * carried) * key, last * key))
        inverses = unit_lower_inverses([item[4] for item in work])
        for inverse, (at, rows, cols, keep, _, right, carry_in, tail_in) in zip(inverses, work):
            inv_h = halves(inverse)
            base = product(inv_h, halves(right))
            carry = product(inv_h, halves(carry_in))
            tail = turned(tail_in)
            eye = jnp.where(lax.broadcasted_iota(jnp.int32, (width, width), 0)
                            == lax.broadcasted_iota(jnp.int32, (width, width), 1), keep, 0.0)
            inv_ref[at] = inverse
            base_ref[rows, cols] = base
            w_ref[rows, cols] = carry
            move_ref[at] = eye - product(tail, halves(carry))
            state_ref[at] = product(tail, halves(base))
        return 0

    lax.fori_loop(0, count // PER_STEP, first, 0)

    def second(index, states):
        result = []
        for head in range(heads):
            at = index * heads + head
            added = state_ref[at]
            state_ref[at] = states[head]
            result.append(product(halves(move_ref[at]), halves(states[head])) + added)
        return tuple(result)

    lax.fori_loop(0, count, second, tuple(jnp.zeros((width, width), WIDE) for _ in range(heads)))

    def third(index, _):
        rows = pl.ds(pl.multiple_of(index * CHUNK, CHUNK), CHUNK)
        carried = jnp.where(segcol_ref[rows, :] == edges_ref[index, 0], 1.0, 0.0).astype(WIDE)
        for head in range(heads):
            cols = pl.ds(head * width, width)
            at = index * heads + head
            state = halves(state_ref[at])
            update = base_ref[rows, cols] - product(halves(w_ref[rows, cols]), state)
            upd_ref[rows, cols] = update
            out = carried * product(halves(q_ref[rows, cols]), state)
            out = out + product(halves(score_ref[at]), halves(update))
            mixed = out.astype(NARROW)
            out_ref[rows, cols] = mixed
            mixed = mixed.astype(WIDE)
            scale = lax.rsqrt(jnp.mean(mixed * mixed, axis=-1, keepdims=True) + norm_eps)
            gate = raw_ref[rows, pl.ds(3 * span + head * width, width)]
            normed = mixed * scale * gain_ref[...] * (gate * jax.nn.sigmoid(gate))
            normed_ref[rows, cols] = normed.astype(NARROW)
        return 0

    lax.fori_loop(0, count, third, 0)
    for k, block in enumerate(blocks):
        block[...] = unpack_rows(far_ref[...], normed_ref[...], k, total // n_fs)


def backward_kernel(heads, width, n_fs, shard_rows, *refs):
    pieces, refs = refs[:n_fs], refs[n_fs:]
    (win_ref, near_ref, segcol_ref, poscol_ref, segrow_ref, edges_ref, z_ref, dgffn_ref,
     taps_ref, gain_ref, hidden_ref, raw_ref, mixed_ref, q_ref, k_ref, inv_ref, score_ref, dots_ref, upd_ref, state_ref,
     move_ref, draw_ref, gradin_ref,
     dtaps_ref, sum_ref, small_ref, pad_ref, grad_ref, pdo_ref, dconv_ref, dout_ref, dnormed_ref) = refs
    total = raw_ref.shape[0]

    def enter(index, _):
        rows = pl.ds(pl.multiple_of(index * ENTER, ENTER), ENTER)
        dnormed_ref[rows, :] = pack_rows(near_ref[rows, :], pieces).astype(NARROW)
        return 0

    lax.fori_loop(0, total // ENTER, enter, 0)
    count = total // CHUNK
    span = heads * width
    fill_padded(raw_ref, pad_ref, 3 * span)

    def first(group, dgain):
        for sub in range(BACK_STEP):
            index = group * BACK_STEP + sub
            rows = pl.ds(pl.multiple_of(index * CHUNK, CHUNK), CHUNK)
            carried = jnp.where(segcol_ref[rows, :] == edges_ref[index, 0], 1.0, 0.0).astype(WIDE)
            for head in range(heads):
                cols = pl.ds(head * width, width)
                at = index * heads + head
                mixed = mixed_ref[rows, cols].astype(WIDE)
                scale = lax.rsqrt(jnp.mean(mixed * mixed, axis=-1, keepdims=True) + norm_eps)
                gate_cols = pl.ds(3 * span + head * width, width)
                gate = raw_ref[rows, gate_cols]
                sig = jax.nn.sigmoid(gate)
                given = dnormed_ref[rows, cols].astype(WIDE)
                unit = mixed * scale
                dgate = given * unit * gain_ref[...] * (sig * (1.0 + gate * (1.0 - sig)))
                draw_ref[rows, gate_cols] = dgate.astype(NARROW)
                given = given * (gate * sig)
                dgain = dgain + jnp.sum(given * unit, axis=0, keepdims=True)
                given = given * gain_ref[...]
                dout = scale * (given - unit * jnp.mean(unit * given, axis=-1, keepdims=True))
                dout = dout.astype(NARROW)
                dout_ref[rows, cols] = dout
                score_t = turned(score_ref[at])
                back = product_exact(score_t, dout)
                pdo_ref[rows, cols] = back
                inv_t = turned(inv_ref[at])
                back = product(inv_t, halves(back))
                query_t = turned(carried * q_ref[rows, cols])
                key_t = turned((beta_of(raw_ref, rows, 4 * span + head) * carried) * k_ref[rows, cols])
                grad_ref[at] = product_exact(query_t, dout) - product(key_t, halves(back))
        return dgain

    dgain = lax.fori_loop(0, count // BACK_STEP, first, jnp.zeros((1, width), WIDE))

    def second(step, grads):
        index = count - 1 - step
        result = []
        for head in range(heads):
            at = index * heads + head
            added = grad_ref[at]
            grad_ref[at] = grads[head]
            result.append(product(turned(move_ref[at]), halves(grads[head])) + added)
        return tuple(result)

    lax.fori_loop(0, count, second, tuple(jnp.zeros((width, width), WIDE) for _ in range(heads)))
    dconv_ref[total:total + HALO, :] = jnp.zeros((HALO, 3 * span), WIDE)

    def third(group, tap_sums):
        for sub in range(BACK_STEP):
            index = group * BACK_STEP + sub
            start = pl.multiple_of(index * CHUNK, CHUNK)
            rows = pl.ds(start, CHUNK)
            pos = poscol_ref[rows, :]
            strict, inclusive, carried, last = chunk_masks(
                segcol_ref[rows, :], segrow_ref[pl.ds(index, 1), :], edges_ref[index, 0], edges_ref[index, 1])
            new_sums = []
            dbetas = []
            for head in range(heads):
                cols = pl.ds(head * width, width)
                at = index * heads + head
                beta = beta_of(raw_ref, rows, 4 * span + head)
                query, key, update = q_ref[rows, cols], k_ref[rows, cols], upd_ref[rows, cols]
                query_h, key_h, update_h = halves(query), halves(key), halves(update)
                dout = dout_ref[rows, cols]
                state, grad = halves(state_ref[at]), halves(grad_ref[at])
                convs = []
                for which in range(3):
                    column = which * span + head * width
                    convs.append(conv_rows(pad_ref, taps_ref[which, :, head * width:(head + 1) * width], pos,
                                           start, column, width))
                gates = [jax.nn.sigmoid(c[0]) for c in convs]
                value = convs[2][0] * gates[2]
                dupdate = pdo_ref[rows, cols] + last * product(key_h, grad)
                dright = product(turned(inv_ref[at]), halves(dupdate))
                dright_h = halves(dright)
                dscore = jnp.where(inclusive, product_exact(update_h, dout, 1, 1, flip=True), 0.0)
                dsystem = jnp.where(strict, product(dright_h, update_h, 1, 1), 0.0)
                dscore_h = halves(dscore)
                dquery = carried * product_exact(state, dout, 1, 1, flip=True) + product(dscore_h, key_h)
                weighted = beta * dsystem
                scaled = beta * carried
                dkey = product(turned(dscore), query_h) + last * product(update_h, grad, 1, 1)
                dkey = dkey - product(halves(weighted + weighted.T), key_h)
                dkey = dkey - scaled * product(dright_h, state, 1, 1)
                dvalue = beta * dright
                seen = carried * product(key_h, state)
                dbeta = jnp.sum(dright * (value - seen), axis=-1, keepdims=True) - jnp.sum(
                    dsystem * dots_ref[at], axis=-1, keepdims=True)
                dbetas.append(dbeta * beta * (1.0 - beta))
                sides = []
                for grads, unit, conv, gate in ((dquery, query, convs[0][0], gates[0]), (dkey, key, convs[1][0], gates[1])):
                    plain = conv * gate
                    inv_norm = lax.rsqrt(jnp.sum(plain * plain, axis=-1, keepdims=True) + unit_eps)
                    sides.append(inv_norm * (grads - unit * jnp.sum(unit * grads, axis=-1, keepdims=True)))
                sides.append(dvalue)
                for which in range(3):
                    conv, plain, moved = convs[which]
                    gate = gates[which]
                    dconv = sides[which] * gate * (1.0 + conv * (1.0 - gate))
                    column = which * span + head * width
                    dconv_ref[rows, pl.ds(column, width)] = dconv
                    sums = [jnp.sum(dconv * plain, axis=0, keepdims=True)]
                    for shifted in moved:
                        sums.append(jnp.sum(dconv * shifted, axis=0, keepdims=True))
                    new_sums.append(jnp.concatenate(sums[::-1], axis=0))
            lane = lax.broadcasted_iota(jnp.int32, (CHUNK, draw_ref.shape[1] - 4 * span), 1)
            packed = jnp.zeros(lane.shape, WIDE)
            for head in range(heads):
                packed = jnp.where(lane == head, dbetas[head], packed)
            draw_ref[rows, pl.ds(4 * span, lane.shape[1])] = packed.astype(draw_ref.dtype)
            tap_sums = tuple(old + new for old, new in zip(tap_sums, new_sums))
        return tap_sums

    zero = tuple(jnp.zeros((taps_ref.shape[1], width), WIDE) for _ in range(3 * heads))
    sums = lax.fori_loop(0, count // BACK_STEP, third, zero)
    for head in range(heads):
        for which in range(3):
            dtaps_ref[which, :, head * width:(head + 1) * width] = sums[head * 3 + which]
    taps_count = taps_ref.shape[1]

    def fourth(index, _):
        start = pl.multiple_of(index * CHUNK, CHUNK)
        pos_window = poscol_ref[pl.ds(start, CHUNK + HALO), :]
        for which in range(3):
            columns = pl.ds(which * span, span)
            window = dconv_ref[pl.ds(start, CHUNK + HALO), columns]
            result = taps_ref[which, taps_count - 1:taps_count, :] * window[0:CHUNK]
            for offset in range(1, taps_count):
                part = jnp.where(pos_window >= offset, window, 0.0)[offset:offset + CHUNK]
                result = result + taps_ref[which, taps_count - 1 - offset:taps_count - offset, :] * part
            draw_ref[pl.ds(start, CHUNK), columns] = result.astype(draw_ref.dtype)
        return 0

    lax.fori_loop(0, count, fourth, 0)

    def weigh(index, _):
        rows = pl.ds(pl.multiple_of(index * ENTER, ENTER), ENTER)
        sum_ref[...] += plain_dot(hidden_ref[rows, :], draw_ref[rows, :], 0, 0)
        return 0

    sum_ref[...] = jnp.zeros(sum_ref.shape, WIDE)
    lax.fori_loop(0, total // ENTER, weigh, 0)
    features = small_ref.shape[1]
    small_ref[...] = jnp.zeros(small_ref.shape, WIDE)
    small_ref[heads + 1:heads + 2, :] = dgffn_ref[...]
    own = pl.ds(pl.multiple_of(z_ref[0] * span, span), span)
    for which in range(3):
        first_row = heads + 2 + which * taps_count
        small_ref[first_row:first_row + taps_count, own] = dtaps_ref[which]
    last_row = heads + 2 + 3 * taps_count
    small_ref[last_row:last_row + 1, :] = product_exact(
        halves(jnp.broadcast_to(dgain, (8, width))), shard_places(width, features, shard_rows, False))[0:1]
    gain = win_ref[:, 4 * span + heads:4 * span + heads + 1].astype(WIDE)
    across = jnp.sum(sum_ref[...] * win_ref[...].astype(WIDE), axis=-1, keepdims=True) / gain
    beside = small_ref[...].T
    lane = lax.broadcasted_iota(jnp.int32, beside.shape, 1)
    gradin_ref[:, 0:4 * span] = sum_ref[:, 0:4 * span].astype(NARROW)
    beside = sum_ref[:, 4 * span:] + beside + jnp.where(lane == heads, across, 0.0)
    gradin_ref[:, 4 * span:] = beside.astype(NARROW)


def leave_kernel(n_fs, win_ref, far_ref, draw_ref, *refs):
    blocks, (dhid_ref,) = refs[:n_fs], refs[n_fs:]
    total = draw_ref.shape[0]

    def leave(index, _):
        rows = pl.ds(pl.multiple_of(index * ENTER, ENTER), ENTER)
        dhid_ref[rows, :] = plain_dot(draw_ref[rows, :], win_ref[...], 1, 1).astype(NARROW)
        return 0

    lax.fori_loop(0, total // ENTER, leave, 0)
    for k, block in enumerate(blocks):
        block[...] = unpack_rows(far_ref[...], dhid_ref[...], k, total // n_fs)


def product_exact(left, exact, left_dim=1, right_dim=0, flip=False):
    def one(a):
        if flip:
            return lax.dot_general(exact, a, (((right_dim,), (left_dim,)), ((), ())), preferred_element_type=WIDE)
        return lax.dot_general(a, exact, (((left_dim,), (right_dim,)), ((), ())), preferred_element_type=WIDE)

    if PASSES == 1:
        return one(left[0])
    return one(left[0]) + one(left[1])


def cost(flops, size):
    return pl.CostEstimate(flops=flops, bytes_accessed=size, transcendentals=0)


def specs(count):
    return [pl.BlockSpec(memory_space=pltpu.VMEM)] * count


def in_scalars():
    return pl.BlockSpec(memory_space=pltpu.SMEM)


def delta_forward(pieces, w_in, near, far, segcol, poscol, segrow, edges, z, heads, width, n_taps, shard_rows):
    n_fs = len(pieces)
    total = near.shape[0]
    features, lanes = w_in.shape
    count = total // CHUNK
    span = heads * width
    thin = jax.ShapeDtypeStruct((total, span), NARROW)
    rows = jax.ShapeDtypeStruct((total, span), WIDE)
    full = jax.ShapeDtypeStruct((total, features), NARROW)
    square = jax.ShapeDtypeStruct((count * heads, CHUNK, CHUNK), WIDE)
    state = jax.ShapeDtypeStruct((count * heads, width, width), WIDE)
    block = jax.ShapeDtypeStruct((total // n_fs, span), NARROW)
    raw = jax.ShapeDtypeStruct((total, lanes), WIDE)
    side = jax.ShapeDtypeStruct((lanes - 4 * span, features), WIDE)
    taps = jax.ShapeDtypeStruct((3, n_taps, span), WIDE)
    gain = jax.ShapeDtypeStruct((1, width), WIDE)
    result = pl.pallas_call(
        functools.partial(forward_kernel, heads, width, n_fs, shard_rows),
        out_shape=(block,) * n_fs
        + (side, taps, gain, full, raw, thin, rows, rows, square, square, square, rows, state, state),
        in_specs=specs(n_fs + 6) + [in_scalars()] * 2,
        out_specs=tuple(specs(n_fs + 14)),
        scratch_shapes=[
            pltpu.VMEM((total + HALO, 3 * span), WIDE),
            pltpu.VMEM((total, span), WIDE),
            pltpu.VMEM((total, span), WIDE),
            pltpu.VMEM((total, span), NARROW),
        ],
        compiler_params=pltpu.CompilerParams(vmem_limit_bytes=52 << 20),
        cost_estimate=cost(30_000_000_000, 16 << 20),
        name="delta_forward",
    )(*pieces, w_in, near, far, segcol, poscol, segrow, edges, z)
    return result[:n_fs], result[n_fs], result[n_fs + 1 :]


def delta_backward(pieces, w_in, near, segcol, poscol, segrow, edges, z, dgffn, kept, heads, width, shard_rows):
    n_fs = len(pieces)
    total = near.shape[0]
    features, lanes = w_in.shape
    count = total // CHUNK
    span = heads * width
    return pl.pallas_call(
        functools.partial(backward_kernel, heads, width, n_fs, shard_rows),
        out_shape=(
            jax.ShapeDtypeStruct((total, lanes), NARROW),
            jax.ShapeDtypeStruct((features, lanes), NARROW),
        ),
        in_specs=specs(n_fs + 5) + [in_scalars()] * 2 + specs(14),
        out_specs=tuple(specs(2)),
        scratch_shapes=[
            pltpu.VMEM(kept[0].shape, WIDE),
            pltpu.VMEM((features, lanes), WIDE),
            pltpu.VMEM((lanes - 4 * span, features), WIDE),
            pltpu.VMEM((total + HALO, 3 * span), WIDE),
            pltpu.VMEM((count * heads, width, width), WIDE),
            pltpu.VMEM((total, span), WIDE),
            pltpu.VMEM((total + HALO, 3 * span), WIDE),
            pltpu.VMEM((total, span), NARROW),
            pltpu.VMEM((total, span), NARROW),
        ],
        compiler_params=pltpu.CompilerParams(vmem_limit_bytes=52 << 20),
        cost_estimate=cost(40_000_000_000, 16 << 20),
        name="delta_backward",
    )(*pieces, w_in, near, segcol, poscol, segrow, edges, z, dgffn, *kept)


def leave_packed(w_in, far, d_raw, n_fs):
    total = d_raw.shape[0]
    features = w_in.shape[0]
    block = jax.ShapeDtypeStruct((total // n_fs, features), NARROW)
    return pl.pallas_call(
        functools.partial(leave_kernel, n_fs),
        out_shape=(block,) * n_fs,
        in_specs=specs(3),
        out_specs=tuple(specs(n_fs)),
        scratch_shapes=[pltpu.VMEM((total, features), NARROW)],
        compiler_params=pltpu.CompilerParams(vmem_limit_bytes=40 << 20),
        cost_estimate=cost(1_000_000, 1 << 10),
        name="leave_packed",
    )(w_in, far, d_raw)


def mix_out_kernel(n_fs, row, z_ref, *refs):
    pieces, refs = refs[:n_fs], refs[n_fs:]
    wout_ref, tokens_ref, gain_ref, middle_ref, ffn_ref, normed_ref = refs
    span = pieces[0].shape[1]
    middle = tokens_ref[...].astype(WIDE)
    for k, piece in enumerate(pieces):
        place = pl.ds(pl.multiple_of(lax.rem(z_ref[0] + n_fs - k, n_fs) * span, span), span)
        normed_ref[:, place] = piece[...]
        middle = middle + plain_dot(piece[...], wout_ref[place, :])
    middle_ref[...] = middle
    scale = lax.rsqrt(jnp.mean(middle * middle, axis=-1, keepdims=True) + norm_eps)
    ffn_ref[...] = (middle * scale * gain_ref[row:row + 1, :]).astype(NARROW)


def mix_out(z, pieces, w_out, tokens, side, row):
    n_fs = len(pieces)
    shape = tokens.shape
    return pl.pallas_call(
        functools.partial(mix_out_kernel, n_fs, row),
        out_shape=(
            jax.ShapeDtypeStruct(shape, WIDE),
            jax.ShapeDtypeStruct(shape, NARROW),
            jax.ShapeDtypeStruct(shape, NARROW),
        ),
        in_specs=[in_scalars()] + specs(n_fs + 3),
        out_specs=tuple(specs(3)),
        compiler_params=pltpu.CompilerParams(vmem_limit_bytes=40 << 20),
        cost_estimate=cost(2_000_000_000, 6 << 20),
        name="mix_out",
    )(z, *pieces, w_out, tokens, side)


def ffn_kernel(keys, unit, block_ref, *refs):
    count = TP
    rows_in, refs = refs[:count], refs[count:]
    cots, refs = refs[:count], refs[count:]
    weights, refs = refs[:len(keys)], refs[len(keys):]
    (wdown_ref, active_ref, dboth_ref, sent_ref, later_ref, own_ref, part_ref, *ordered) = refs
    own_rows = rows_in[0].shape[0]
    if ordered:
        for near, far in zip(weights, ordered):
            n_fs, size = near.shape[:2]
            for by in range(n_fs):
                line = lax.rem(block_ref[1] + n_fs - by, n_fs)
                for at in range(size // unit):
                    place = pl.ds(pl.multiple_of((at * n_fs + line) * unit, unit), unit)
                    far[place, :] = near[by, at * unit:(at + 1) * unit, :]
        weights = ordered
    depth = weights[0].shape[0]
    units = wdown_ref.shape[0]
    spots = [pl.ds(pl.multiple_of((block_ref[0] ^ key) * depth, depth), depth) for key in keys]
    half = count // 2 * own_rows
    for at in range(count - 1, -1, -1):
        rows = slice(at * own_rows, (at + 1) * own_rows)
        both = plain_dot(rows_in[at][:, spots[0]], weights[0][...])
        for spot, weight in zip(spots[1:], weights[1:]):
            both = both + plain_dot(rows_in[at][:, spot], weight[...])
        gate, up = both[:, :units], both[:, units:]
        sig = jax.nn.sigmoid(gate)
        silu = gate * sig
        active_ref[rows, :] = (silu * up).astype(NARROW)
        dactive = plain_dot(cots[at][...], wdown_ref[...], 1, 1)
        dboth_ref[rows, :units] = (dactive * up * (sig * (1.0 + gate * (1.0 - sig)))).astype(NARROW)
        dboth_ref[rows, units:] = (dactive * silu).astype(NARROW)
        dboth = dboth_ref[rows, :]
        for spot, weight in zip(spots, weights):
            part_ref[:, spot] = plain_dot(dboth, weight[...], 1, 1)
        if at >= count // 2:
            place = at * own_rows - half
            sent_ref[place:place + own_rows, :] = part_ref[...].astype(NARROW)
        elif at:
            later_ref[(at - 1) * own_rows:at * own_rows, :] = part_ref[...]
        else:
            own_ref[...] = part_ref[...]


def ffn_units(block, rows_in, cots, weights, keys, w_down, unit):
    own_rows, features = rows_in[0].shape
    units = w_down.shape[0]
    total = TP * own_rows
    return pl.pallas_call(
        functools.partial(ffn_kernel, keys, unit),
        out_shape=(
            jax.ShapeDtypeStruct((total, units), NARROW),
            jax.ShapeDtypeStruct((total, 2 * units), NARROW),
            jax.ShapeDtypeStruct((total // 2, features), NARROW),
            jax.ShapeDtypeStruct((total // 2 - own_rows, features), WIDE),
            jax.ShapeDtypeStruct((own_rows, features), WIDE),
        ),
        in_specs=[in_scalars()] + specs(2 * TP + len(weights) + 1),
        out_specs=tuple(specs(5)),
        scratch_shapes=[pltpu.VMEM((own_rows, features), WIDE)]
        + [pltpu.VMEM((features // len(keys), 2 * units), NARROW) for w in weights if w.ndim == 3],
        compiler_params=pltpu.CompilerParams(vmem_limit_bytes=52 << 20),
        cost_estimate=cost(8_000_000_000, 16 << 20),
        name="ffn_units",
    )(block, *rows_in, *cots, *weights, w_down)


def mix_back_kernel(n_fs, row, z_ref, own_ref, core_ref, side_ref, middle_ref, gain_ref, cot_ref, wout_ref, *refs):
    blocks, (dmiddle_ref, dbranch_ref, dgain_ref) = refs[:n_fs], refs[n_fs:]
    middle = middle_ref[...]
    given = own_ref[...] + core_ref[0:own_ref.shape[0], :].astype(WIDE) + side_ref[...].astype(WIDE)
    scale = lax.rsqrt(jnp.mean(middle * middle, axis=-1, keepdims=True) + norm_eps)
    unit = middle * scale
    dgain_ref[...] = jnp.sum(given * unit, axis=0, keepdims=True)
    given = given * gain_ref[row:row + 1, :]
    dmiddle = cot_ref[...].astype(WIDE) + scale * (given - unit * jnp.mean(unit * given, axis=-1, keepdims=True))
    dmiddle_ref[...] = dmiddle
    dbranch = dmiddle.astype(NARROW)
    dbranch_ref[...] = dbranch
    span = blocks[0].shape[1]
    for k, block in enumerate(blocks):
        place = pl.ds(pl.multiple_of(lax.rem(z_ref[0] + k, n_fs) * span, span), span)
        block[...] = plain_dot(dbranch, wout_ref[place, :], 1, 1).astype(NARROW)


def mix_back(z, parts, middle, side, row, cotangent, w_out, n_fs):
    count, features = middle.shape
    block = jax.ShapeDtypeStruct((count, features // n_fs), NARROW)
    result = pl.pallas_call(
        functools.partial(mix_back_kernel, n_fs, row),
        out_shape=(block,) * n_fs
        + (
            jax.ShapeDtypeStruct(middle.shape, WIDE),
            jax.ShapeDtypeStruct(middle.shape, NARROW),
            jax.ShapeDtypeStruct((1, features), WIDE),
        ),
        in_specs=[in_scalars()] + specs(7),
        out_specs=tuple(specs(n_fs + 3)),
        compiler_params=pltpu.CompilerParams(vmem_limit_bytes=40 << 20),
        cost_estimate=cost(2_000_000_000, 6 << 20),
        name="mix_back",
    )(z, *parts, middle, side, cotangent, w_out)
    return (result[:n_fs],) + tuple(result[n_fs:])


def rms_scale(values, gain):
    return values * lax.rsqrt(jnp.mean(values * values, axis=-1, keepdims=True) + norm_eps) * gain


def swiglu(gate_proj, up_proj):
    return jax.nn.silu(gate_proj) * up_proj


def sequence_layout(lengths_row, total):
    ends = jnp.cumsum(lengths_row)
    index = jnp.arange(total, dtype=jnp.int32)
    before = index[:, None] >= ends[None, :]
    segment = jnp.sum(before.astype(jnp.int32), axis=1)
    start = jnp.sum(jnp.where(before, lengths_row[None, :], 0), axis=1)
    return (segment, index - start)


def project(left, right):
    return jnp.dot(left, right, preferred_element_type=WIDE)


def project_back(left, right):
    return lax.dot_general(left, right, (((1,), (1,)), ((), ())), preferred_element_type=WIDE)


def weight_grad(left, right):
    return lax.dot_general(left, right, (((0,), (0,)), ((), ())), preferred_element_type=WIDE)


def flip(value, bit, n_dp):
    return lax.ppermute(value, "dp", [(i, i ^ bit) for i in range(n_dp)])


def shift(value, by, n_fs):
    return lax.ppermute(value, "fsdp", [(i, (i + by) % n_fs) for i in range(n_fs)])


def line_pieces(shard, n_fs):
    return [shard] + [shift(shard, by, n_fs) for by in range(1, n_fs)]


def line_order(pieces, z):
    n_fs = len(pieces)
    shape = pieces[0].shape
    whole = jnp.zeros((shape[0], n_fs) + shape[1:], pieces[0].dtype)
    for by, piece in enumerate(pieces):
        whole = lax.dynamic_update_slice_in_dim(whole, piece[:, None], lax.rem(z + n_fs - by, n_fs), 1)
    return whole


def gather_cube(piece, order, n_dp):
    pieces = {0: piece}
    for bit in order:
        for key in list(pieces):
            pieces[key ^ bit] = flip(pieces[key], bit, n_dp)
    return pieces


def in_order(pieces, me):
    rows = pieces[0].shape[0]
    whole = jnp.zeros((len(pieces) * rows,) + pieces[0].shape[1:], pieces[0].dtype)
    unit = max(pieces).bit_length()
    step = (1 << unit) // len(pieces)
    for key, piece in pieces.items():
        whole = lax.dynamic_update_slice_in_dim(whole, piece, lax.bitwise_xor(me, key // step) * rows, 0)
    return whole


def per_device(
    n_dp,
    n_fs,
    tokens,
    lengths,
    packing,
    w_query,
    w_key,
    w_value,
    w_gate,
    w_beta,
    conv_taps,
    w_out,
    gain_mix,
    gain_head,
    gain_ffn,
    w_ffn_gate,
    w_ffn_up,
    w_ffn_down,
    cotangent,
):
    me = lax.axis_index("dp")
    z = lax.axis_index("fsdp")
    bits = [1 << k for k in range(n_dp.bit_length() - 1)]
    first_order = bits[:1] + bits[1:]
    second_order = bits[:1] + bits[1:][::-1]
    packing_row = packing[0]
    lengths_row = lengths[0]
    own_rows, features = tokens.shape
    total = own_rows * n_fs
    rows = w_query.shape[0]
    heads_all = w_beta.shape[1]
    heads = heads_all // n_fs
    span = features // n_fs
    width = span // heads
    hidden_ffn = w_ffn_gate.shape[1]
    head_rows = gain_head.shape[0]
    n_taps = conv_taps.shape[1]

    def by_owner(matrix):
        return jnp.swapaxes(matrix.reshape(rows, n_fs, -1), 0, 1)

    small = jnp.concatenate(
        [
            gain_mix[:, None],
            gain_ffn[:, None],
            conv_taps.reshape(3 * n_taps, rows).T,
            jnp.pad(gain_head, (0, rows - head_rows))[:, None],
        ],
        axis=1,
    )
    n_small = small.shape[1]
    side = jnp.concatenate(
        [by_owner(w_beta), jnp.broadcast_to(small[None], (n_fs, rows, n_small))], axis=2
    )
    side = jnp.pad(side, ((0, 0), (0, 0), (0, 128 - heads - n_small)))
    packet = jnp.concatenate(
        [by_owner(w_query), by_owner(w_key), by_owner(w_value), by_owner(w_gate), side], axis=2
    )
    member = lax.rem(me, TP)
    block = me // TP
    n_rest = n_dp // TP
    ff_block = hidden_ffn // n_dp
    ff_own = n_rest * ff_block
    ff_pad = -(-ff_own // 128) * 128
    tp_bits = [bit for bit in bits if bit < TP]
    rest_bits = [bit for bit in bits if bit >= TP]

    def by_member(matrix):
        split = matrix.reshape(rows, n_rest, TP, ff_block)
        split = jnp.transpose(split, (2, 0, 1, 3)).reshape(TP, rows, ff_own)
        return jnp.pad(split, ((0, 0), (0, 0), (0, ff_pad - ff_own)))

    def hand_out(blocks):
        pieces = [lax.dynamic_index_in_dim(blocks, z, 0)]
        for by in range(1, n_fs):
            pieces.append(shift(lax.dynamic_index_in_dim(blocks, lax.rem(z + by, n_fs), 0), by, n_fs))
        return pieces

    lanes = 4 * span + 128
    packet = jnp.concatenate([packet, jnp.broadcast_to(w_out[None], (n_fs,) + w_out.shape)], axis=2)
    packet = hand_out(packet)
    token_pieces = [tokens] + [shift(tokens, by, n_fs) for by in range(1, n_fs)]
    packet, token_pieces[1] = lax.optimization_barrier((packet, token_pieces[1]))
    packet_in = line_order([piece[:, :, :lanes] for piece in packet], z).reshape(n_fs * rows, lanes)
    packet_out = line_order([piece[:, :, lanes:] for piece in packet], z).reshape(n_fs * rows, features)
    w_in = lax.all_gather(packet_in, "dp", axis=0, tiled=True)
    full_out = lax.all_gather(packet_out, "dp", axis=0, tiled=True)

    owner, place = packing_row // own_rows, lax.rem(packing_row, own_rows)
    near = (lax.rem(z + n_fs - owner, n_fs) * own_rows + place)[:, None]
    far = (lax.rem(owner + n_fs - z, n_fs) * own_rows + place)[None]
    segment, position = sequence_layout(lengths_row, total)
    seg_rows = segment.reshape(-1, CHUNK)
    ends = seg_rows[:, -1]
    edges = jnp.stack([jnp.concatenate([jnp.full((1,), -1, jnp.int32), ends[:-1]]), ends], axis=1)
    z_ref = z.reshape(1)
    layout = (segment[:, None], jnp.pad(position, (0, HALO))[:, None], seg_rows, edges, z_ref)
    shard_rows = (rows, head_rows)
    own_gate, own_up, _ = lax.optimization_barrier((w_ffn_gate, w_ffn_up, token_pieces[1]))
    both_sends = jnp.concatenate([by_member(own_gate), by_member(own_up)], axis=2)
    blocks, side, kept = delta_forward(
        token_pieces, w_in, near, far, *layout, heads, width, n_taps, shard_rows
    )
    gain_row = heads + 1

    both_pieces = {
        key: flip(lax.dynamic_index_in_dim(both_sends, member ^ key, 0, keepdims=False), key, n_dp)
        if key
        else lax.dynamic_index_in_dim(both_sends, member, 0, keepdims=False)
        for key in range(TP)
    }
    own_down, _ = lax.optimization_barrier((w_ffn_down, token_pieces[1]))
    down_rows = in_order(gather_cube(own_down, rest_bits, n_dp), block).reshape(n_rest, -1, features)
    both_rows = in_order(both_pieces, member).reshape(TP, rows, 2 * ff_pad)
    own_cotangent, both_rows, down_rows = lax.optimization_barrier((cotangent, both_rows, down_rows))
    both_rows, down_rows, _ = lax.optimization_barrier((both_rows, down_rows, token_pieces))
    both_line = line_pieces(both_rows, n_fs)
    both_line, blocks, down_rows = lax.optimization_barrier((both_line, blocks, down_rows))
    if rows % 16 == 0:
        both_rows = jnp.stack([piece.reshape(TP * rows, 2 * ff_pad) for piece in both_line])
    else:
        both_rows = line_order(both_line, z).reshape(-1, 2 * ff_pad)
    both_pieces = gather_cube(both_rows, rest_bits, n_dp)
    unit = 1 << (TP.bit_length() - 1)
    rest_keys = [key // unit for key in both_pieces]
    tp_order = sorted(range(TP), key=lambda key: tuple((key & bit) != 0 for bit in tp_bits))

    cot_pieces = gather_cube(own_cotangent, tp_bits[::-1], n_dp)
    cot_pieces, blocks = lax.optimization_barrier((cot_pieces, blocks))

    def collect(left, right, dims):
        arrived = []
        keep = TP

        def term(lo, hi):
            value = lax.dot_general(
                left[lo * own_rows : hi * own_rows], right, (dims, ((), ())), preferred_element_type=WIDE
            )
            for earlier in arrived:
                value = value + earlier[lo * own_rows : hi * own_rows].astype(WIDE)
            return value

        for bit in tp_bits:
            keep //= 2
            sent = yield term(keep, 2 * keep).astype(NARROW)
            arrived.append(flip(sent, bit, n_dp))
        yield term(0, 1)

    def halve(value, index, some_bits):
        unit = some_bits[0] if some_bits else 1
        for bit in some_bits[::-1]:
            half = value.shape[0] // 2
            mine = (index // (bit // unit)) % 2
            sent = lax.dynamic_slice_in_dim(value, (1 - mine) * half, half, 0)
            value = lax.dynamic_slice_in_dim(value, mine * half, half, 0)
            value = value.astype(WIDE) + flip(sent.astype(NARROW), bit, n_dp).astype(WIDE)
        return value

    def sum_up(pieces, whole):
        total = lax.dynamic_index_in_dim(whole, z, 0, keepdims=False).astype(WIDE)
        for piece in pieces[1:]:
            total = total + piece[0].astype(WIDE)
        return total

    def pass_on(parts):
        return [parts[0]] + [shift(part, by, n_fs) for by, part in enumerate(parts) if by]

    mixed_pieces = pass_on(blocks)
    down_line = line_pieces(down_rows, n_fs)
    middle, ffn_in, normed_b = mix_out(z_ref, mixed_pieces, full_out, tokens, side, gain_row)
    w_down = line_order(down_line, z).reshape(ff_own, features)
    w_down = jnp.pad(w_down, ((0, ff_pad - ff_own), (0, 0)))
    ffn_pieces = gather_cube(ffn_in, tp_bits[::-1], n_dp)
    active_b, d_both, first, second, d_own = ffn_units(
        jnp.stack([block, z]),
        [ffn_pieces[key] for key in tp_order],
        [cot_pieces[key] for key in tp_order],
        list(both_pieces.values()),
        rest_keys,
        w_down,
        rows,
    )
    ffn_near = jnp.concatenate([ffn_pieces[key] for key in tp_order], axis=0)

    def both_part(lo, size):
        part = weight_grad(lax.dynamic_slice_in_dim(ffn_near, lo, size, 1), d_both)
        return part.reshape(-1, n_fs * rows, 2 * ff_pad)

    split = features // 2 if rest_bits else features
    top = block // max(n_rest // 2, 1)
    if rest_bits:
        both_sent = both_part((1 - top) * split, split).astype(NARROW)
    else:
        both_sent = None
    from_core = flip(first, tp_bits[0], n_dp)
    second = second + from_core[own_rows:].astype(WIDE)
    second, both_sent, active_late = lax.optimization_barrier((second.astype(NARROW), both_sent, active_b))
    from_side = flip(second, tp_bits[1], n_dp)
    cotangent_near = jnp.concatenate([cot_pieces[key] for key in tp_order], axis=0)
    down_terms = weight_grad(active_late, cotangent_near)[:ff_own].reshape(n_rest, n_fs, -1, features)
    down_each = down_terms.shape[2]
    down_terms = jnp.pad(down_terms, ((0, 0), (0, 0), (0, -down_each % 32), (0, 0)))
    both_sum = both_part(top * split if rest_bits else 0, split)
    out_terms = collect(active_late, w_down, ((1,), (0,)))
    out_first = next(out_terms)
    down_terms = down_terms.astype(NARROW)
    down_sum = lax.psum_scatter(
        down_terms.reshape(n_rest, -1, features), "fsdp", scatter_dimension=1, tiled=True
    )
    from_side, down_terms, both_sum, out_first = lax.optimization_barrier(
        (from_side, down_terms, both_sum, out_first)
    )
    if rest_bits:
        both_sum = both_sum + flip(both_sent, rest_bits[-1], n_dp).astype(WIDE)
        both_sum = halve(both_sum, block, rest_bits[:-1])

    d_blocks, d_middle, d_branch, d_gffn = mix_back(
        z_ref, (d_own, from_core, from_side), middle, side, gain_row, cotangent, full_out, n_fs
    )
    d_pieces = pass_on(d_blocks)
    out_grad = weight_grad(normed_b, d_branch).astype(NARROW)
    sum_out = lax.psum_scatter(out_grad, "dp", scatter_dimension=0, tiled=True)
    both_sum = jnp.swapaxes(both_sum.reshape(TP, n_fs, rows, 2 * ff_pad), 0, 1)
    layer_out = (middle + out_terms.send(out_terms.send(out_first))).astype(NARROW)
    both_sum, layer_out, d_pieces, out_grad = lax.optimization_barrier((both_sum, layer_out, d_pieces, out_grad))
    both_line = hand_out(both_sum.astype(NARROW))

    d_raw, grad_in = delta_backward(
        d_pieces, w_in, near, *layout, d_gffn, kept, heads, width, shard_rows
    )
    grad_in, both_line, down_sum, sum_out = lax.optimization_barrier((grad_in, both_line, down_sum, sum_out))
    part = lax.psum_scatter(grad_in, "dp", scatter_dimension=0, tiled=True)
    d_blocks = leave_packed(w_in, far, d_raw, n_fs)
    d_blocks = pass_on(d_blocks)
    both_line, d_blocks[1] = lax.optimization_barrier((both_line, d_blocks[1]))
    both_sum = sum_up(both_line, both_sum)
    grad_fdown = halve(down_sum[:, :down_each], block, rest_bits)[0].astype(WIDE)
    both_pieces = {
        key: flip(lax.dynamic_index_in_dim(both_sum, member ^ key, 0, keepdims=False), key, n_dp)
        if key
        else lax.dynamic_index_in_dim(both_sum, member, 0, keepdims=False)
        for key in range(TP)
    }
    both_mine = in_order({key: piece[None] for key, piece in both_pieces.items()}, member)
    def units_of(which):
        part = both_mine[:, :, which * ff_pad : which * ff_pad + ff_own].reshape(TP, rows, n_rest, ff_block)
        return jnp.transpose(part, (1, 2, 0, 3)).reshape(rows, hidden_ffn)

    lanes = part.shape[1]
    joint = jnp.concatenate([part, sum_out], axis=1).reshape(n_fs, rows, -1)
    arrived = [piece[0] for piece in hand_out(joint)]
    d_blocks, arrived[1] = lax.optimization_barrier((d_blocks, arrived[1]))
    d_hidden = d_blocks[0].astype(WIDE)
    for block_of in d_blocks[1:]:
        d_hidden = d_hidden + block_of.astype(WIDE)

    d_hidden = d_blocks[0].astype(WIDE)
    for block_of in d_blocks[1:]:
        d_hidden = d_hidden + block_of.astype(WIDE)
    _, norm_mix_back = jax.vjp(rms_scale, tokens.astype(WIDE), side[heads])
    d_inputs_norm, _ = norm_mix_back(d_hidden)
    grad_tokens = d_middle + d_inputs_norm

    part = line_order([piece[None, :, :lanes] for piece in arrived], z)[0].astype(WIDE)
    grad_wout = jnp.zeros((rows, features), WIDE)
    for piece in arrived:
        grad_wout = grad_wout + piece[:, lanes:].astype(WIDE)

    def columns_of(which):
        return jnp.swapaxes(part[:, :, which * span : (which + 1) * span], 0, 1).reshape(rows, features)

    grad_beta = jnp.swapaxes(part[:, :, 4 * span : 4 * span + heads], 0, 1).reshape(rows, heads_all)
    small_sum = jnp.sum(part[:, :, 4 * span + heads : 4 * span + heads + n_small], axis=0)
    grad_taps = small_sum[:, 2 : 2 + 3 * n_taps].T.reshape(3, n_taps, rows)
    return (
        layer_out,
        grad_tokens,
        columns_of(0),
        columns_of(1),
        columns_of(2),
        columns_of(3),
        grad_beta,
        grad_taps,
        grad_wout,
        small_sum[:, 0],
        small_sum[:head_rows, 2 + 3 * n_taps],
        small_sum[:, 1],
        units_of(0),
        units_of(1),
        grad_fdown,
    )


def solution(mesh):
    both = ("dp", "fsdp")
    rows = P(both, None)
    group = P("dp", None)
    taps = P(None, None, both)
    line = P(both)
    in_specs = (rows, group, group) + (rows,) * 5 + (taps, rows, line, line, line) + (rows,) * 4
    out_specs = (rows,) * 7 + (taps, rows, line, line, line) + (rows,) * 3
    return jax.shard_map(
        functools.partial(per_device, mesh.shape["dp"], mesh.shape["fsdp"]),
        mesh=mesh,
        in_specs=in_specs,
        out_specs=out_specs,
        check_vma=False,
    )
```

```python
import functools

import jax
import jax.numpy as jnp
from jax import lax
from jax.experimental import pallas as pl
from jax.experimental.pallas import tpu as pltpu
from jax.sharding import PartitionSpec as P

CHUNK = 128
TP = 4
PER_STEP = 4
BACK_STEP = 2
ENTER = 256
HALO = 8
norm_eps = 1e-05
unit_eps = 1e-06
NARROW = jnp.bfloat16
WIDE = jnp.float32


def halves(value):
    top = value.astype(NARROW)
    return top, (value - top.astype(WIDE)).astype(NARROW)


def product(left, right, left_dim=1, right_dim=0):
    dims = (((left_dim,), (right_dim,)), ((), ()))

    def one(a, b):
        return lax.dot_general(a, b, dims, preferred_element_type=WIDE)

    if PASSES == 1:
        return one(left[0], right[0])
    return one(left[0], right[0]) + (one(left[0], right[1]) + one(left[1], right[0]))


PASSES = 3


def turned(value):
    return halves(value.T)


def chunk_masks(seg_col, seg_row, before, after):
    size = seg_col.shape[0]
    down = lax.broadcasted_iota(jnp.int32, (size, size), 0)
    across = lax.broadcasted_iota(jnp.int32, (size, size), 1)
    same = seg_col == seg_row
    strict = same & (down > across)
    inclusive = same & (down >= across)
    carried = jnp.where(seg_col == before, 1.0, 0.0).astype(WIDE)
    last = jnp.where(seg_col == after, 1.0, 0.0).astype(WIDE)
    return strict, inclusive, carried, last


def unit_lower_inverses(systems):
    size = systems[0].shape[0]
    down = lax.broadcasted_iota(jnp.int32, (size, size), 0)
    across = lax.broadcasted_iota(jnp.int32, (size, size), 1)
    gap = jnp.where(down > across, down ^ across, 0)
    eye = jnp.where(down == across, 1.0, 0.0)
    results = [eye - jnp.where(gap == 1, system, 0.0) for system in systems]
    step = 2
    while step < size:
        picked = (gap >= step) & (gap < 2 * step)
        parts = [jnp.where(picked, system, 0.0).astype(NARROW) for system in systems]
        done = [result.astype(NARROW) for result in results]
        inner = [plain_dot(part, own).astype(NARROW) for part, own in zip(parts, done)]
        results = [result - plain_dot(own, side) for result, own, side in zip(results, done, inner)]
        step *= 2
    left = [eye - result - product(halves(system), halves(result)) for system, result in zip(systems, results)]
    results = [
        result + plain_dot(result.astype(NARROW), rest.astype(NARROW)) for result, rest in zip(results, left)
    ]
    return results


def conv_rows(pad_ref, taps, pos, start, column, width):
    window = pad_ref[pl.ds(start, CHUNK + HALO), pl.ds(column, width)]
    count = taps.shape[0]
    result = taps[count - 1 : count] * window[HALO : HALO + CHUNK]
    moved = []
    for offset in range(1, count):
        rows = jnp.where(pos >= offset, window[HALO - offset : HALO - offset + CHUNK], 0.0)
        moved.append(rows)
        result = result + taps[count - 1 - offset : count - offset] * rows
    return result, window[HALO : HALO + CHUNK], moved


def fill_padded(raw_ref, pad_ref, width):
    pad_ref[0:HALO, :] = jnp.zeros((HALO, width), WIDE)
    total = raw_ref.shape[0]

    def copy(index, _):
        start = pl.multiple_of(index * CHUNK, CHUNK)
        pad_ref[pl.ds(start + HALO, CHUNK), :] = raw_ref[pl.ds(start, CHUNK), 0:width].astype(NARROW).astype(WIDE)
        return 0

    lax.fori_loop(0, total // CHUNK, copy, 0)


def one_hot(first, second, offset):
    return jnp.where(first - offset == second, 1.0, 0.0).astype(NARROW)


def plain_dot(left, right, left_dim=1, right_dim=0):
    return lax.dot_general(left, right, (((left_dim,), (right_dim,)), ((), ())), preferred_element_type=WIDE)


def pack_rows(near_col, pieces):
    size = pieces[0].shape[0]
    lane = lax.broadcasted_iota(jnp.int32, (near_col.shape[0], size), 1)
    total = plain_dot(one_hot(near_col, lane, 0), pieces[0][...])
    for k in range(1, len(pieces)):
        total = total + plain_dot(one_hot(near_col, lane, k * size), pieces[k][...])
    return total


def unpack_rows(far_row, packed, k, size):
    down = lax.broadcasted_iota(jnp.int32, (size, far_row.shape[1]), 0)
    return plain_dot(one_hot(far_row, down, k * size), packed).astype(NARROW)


def beta_of(raw_ref, rows, lane):
    return jax.nn.sigmoid(raw_ref[rows, lane:lane + 1].astype(NARROW).astype(WIDE))


def shard_places(size, features, shard_rows, turned_round):
    unit, each = shard_rows
    shape = (features, size) if turned_round else (size, features)
    value = lax.broadcasted_iota(jnp.int32, shape, 1 if turned_round else 0)
    lane = lax.broadcasted_iota(jnp.int32, shape, 0 if turned_round else 1)
    chosen = (lane // unit == value // each) & (lane % unit == value % each)
    return jnp.where(chosen, 1.0, 0.0).astype(NARROW)


def forward_kernel(heads, width, n_fs, shard_rows, *refs):
    pieces, refs = refs[:n_fs], refs[n_fs:]
    (win_ref, near_ref, far_ref, segcol_ref, poscol_ref, segrow_ref, edges_ref, z_ref, *refs) = refs
    blocks, refs = refs[:n_fs], refs[n_fs:]
    (side_ref, taps_ref, gain_ref, hidden_ref, raw_ref, out_ref, q_ref, k_ref, inv_ref, score_ref, dots_ref, upd_ref, state_ref,
     move_ref, pad_ref, base_ref, w_ref, normed_ref) = refs
    total = raw_ref.shape[0]
    count = total // CHUNK
    span = heads * width
    side_ref[...] = win_ref[:, 4 * span:].astype(WIDE).T
    taps_count = taps_ref.shape[1]
    own = pl.ds(pl.multiple_of(z_ref[0] * span, span), span)
    for which in range(3):
        first_row = heads + 2 + which * taps_count
        taps_ref[which] = side_ref[first_row:first_row + taps_count, own]
    last_row = heads + 2 + 3 * taps_count
    entries = jnp.broadcast_to(side_ref[last_row:last_row + 1, :], (8, side_ref.shape[1])).astype(NARROW)
    gain_ref[...] = plain_dot(entries, shard_places(width, side_ref.shape[1], shard_rows, True))[0:1]

    def enter(index, _):
        rows = pl.ds(pl.multiple_of(index * ENTER, ENTER), ENTER)
        packed = pack_rows(near_ref[rows, :], pieces)
        scale = lax.rsqrt(jnp.mean(packed * packed, axis=-1, keepdims=True) + norm_eps)
        hidden = (packed * scale * side_ref[heads:heads + 1, :]).astype(NARROW)
        hidden_ref[rows, :] = hidden
        raw_ref[rows, :] = plain_dot(hidden, win_ref[...])
        return 0

    lax.fori_loop(0, total // ENTER, enter, 0)
    fill_padded(raw_ref, pad_ref, 3 * span)

    def first(group, _):
        work = []
        for sub in range(PER_STEP):
            index = group * PER_STEP + sub
            start = pl.multiple_of(index * CHUNK, CHUNK)
            rows = pl.ds(start, CHUNK)
            pos = poscol_ref[rows, :]
            before, after = edges_ref[index, 0], edges_ref[index, 1]
            strict, inclusive, carried, last = chunk_masks(
                segcol_ref[rows, :], segrow_ref[pl.ds(index, 1), :], before, after)
            keep = jnp.where(before == after, 1.0, 0.0).astype(WIDE)
            for head in range(heads):
                cols = pl.ds(head * width, width)
                parts = []
                for which in range(3):
                    column = which * span + head * width
                    value = conv_rows(pad_ref, taps_ref[which, :, head * width:(head + 1) * width], pos,
                                      start, column, width)[0]
                    parts.append(value * jax.nn.sigmoid(value))
                query, key, value = parts
                query = query * lax.rsqrt(jnp.sum(query * query, axis=-1, keepdims=True) + unit_eps)
                key = key * lax.rsqrt(jnp.sum(key * key, axis=-1, keepdims=True) + unit_eps)
                q_ref[rows, cols] = query
                k_ref[rows, cols] = key
                beta = beta_of(raw_ref, rows, 4 * span + head)
                key_h, query_h = halves(key), halves(query)
                dots = product(key_h, key_h, 1, 1)
                score = jnp.where(inclusive, product(query_h, key_h, 1, 1), 0.0)
                at = index * heads + head
                dots_ref[at] = dots
                score_ref[at] = score
                work.append((at, rows, cols, keep, jnp.where(strict, beta * dots, 0.0),
                             beta * value, (beta * carried) * key, last * key))
        inverses = unit_lower_inverses([item[4] for item in work])
        for inverse, (at, rows, cols, keep, _, right, carry_in, tail_in) in zip(inverses, work):
            inv_h = halves(inverse)
            base = product(inv_h, halves(right))
            carry = product(inv_h, halves(carry_in))
            tail = turned(tail_in)
            eye = jnp.where(lax.broadcasted_iota(jnp.int32, (width, width), 0)
                            == lax.broadcasted_iota(jnp.int32, (width, width), 1), keep, 0.0)
            inv_ref[at] = inverse
            base_ref[rows, cols] = base
            w_ref[rows, cols] = carry
            move_ref[at] = eye - product(tail, halves(carry))
            state_ref[at] = product(tail, halves(base))
        return 0

    lax.fori_loop(0, count // PER_STEP, first, 0)

    def second(index, states):
        result = []
        for head in range(heads):
            at = index * heads + head
            added = state_ref[at]
            state_ref[at] = states[head]
            result.append(product(halves(move_ref[at]), halves(states[head])) + added)
        return tuple(result)

    lax.fori_loop(0, count, second, tuple(jnp.zeros((width, width), WIDE) for _ in range(heads)))

    def third(index, _):
        rows = pl.ds(pl.multiple_of(index * CHUNK, CHUNK), CHUNK)
        carried = jnp.where(segcol_ref[rows, :] == edges_ref[index, 0], 1.0, 0.0).astype(WIDE)
        for head in range(heads):
            cols = pl.ds(head * width, width)
            at = index * heads + head
            state = halves(state_ref[at])
            update = base_ref[rows, cols] - product(halves(w_ref[rows, cols]), state)
            upd_ref[rows, cols] = update
            out = carried * product(halves(q_ref[rows, cols]), state)
            out = out + product(halves(score_ref[at]), halves(update))
            mixed = out.astype(NARROW)
            out_ref[rows, cols] = mixed
            mixed = mixed.astype(WIDE)
            scale = lax.rsqrt(jnp.mean(mixed * mixed, axis=-1, keepdims=True) + norm_eps)
            gate = raw_ref[rows, pl.ds(3 * span + head * width, width)]
            normed = mixed * scale * gain_ref[...] * (gate * jax.nn.sigmoid(gate))
            normed_ref[rows, cols] = normed.astype(NARROW)
        return 0

    lax.fori_loop(0, count, third, 0)
    for k, block in enumerate(blocks):
        block[...] = unpack_rows(far_ref[...], normed_ref[...], k, total // n_fs)


def backward_kernel(heads, width, n_fs, shard_rows, *refs):
    pieces, refs = refs[:n_fs], refs[n_fs:]
    (win_ref, near_ref, far_ref, segcol_ref, poscol_ref, segrow_ref, edges_ref, z_ref, dgffn_ref,
     taps_ref, gain_ref, hidden_ref, raw_ref, mixed_ref, q_ref, k_ref, inv_ref, score_ref, dots_ref, upd_ref, state_ref,
     move_ref, gradin_ref, *refs) = refs
    blocks, refs = refs[:n_fs], refs[n_fs:]
    (draw_ref, dhid_ref, dtaps_ref, sum_ref, small_ref, pad_ref, grad_ref, pdo_ref, dconv_ref, dout_ref, dnormed_ref) = refs
    total = raw_ref.shape[0]

    def enter(index, _):
        rows = pl.ds(pl.multiple_of(index * ENTER, ENTER), ENTER)
        dnormed_ref[rows, :] = pack_rows(near_ref[rows, :], pieces).astype(NARROW)
        return 0

    lax.fori_loop(0, total // ENTER, enter, 0)
    count = total // CHUNK
    span = heads * width
    fill_padded(raw_ref, pad_ref, 3 * span)

    def first(group, dgain):
        for sub in range(BACK_STEP):
            index = group * BACK_STEP + sub
            rows = pl.ds(pl.multiple_of(index * CHUNK, CHUNK), CHUNK)
            carried = jnp.where(segcol_ref[rows, :] == edges_ref[index, 0], 1.0, 0.0).astype(WIDE)
            for head in range(heads):
                cols = pl.ds(head * width, width)
                at = index * heads + head
                mixed = mixed_ref[rows, cols].astype(WIDE)
                scale = lax.rsqrt(jnp.mean(mixed * mixed, axis=-1, keepdims=True) + norm_eps)
                gate_cols = pl.ds(3 * span + head * width, width)
                gate = raw_ref[rows, gate_cols]
                sig = jax.nn.sigmoid(gate)
                given = dnormed_ref[rows, cols].astype(WIDE)
                unit = mixed * scale
                dgate = given * unit * gain_ref[...] * (sig * (1.0 + gate * (1.0 - sig)))
                draw_ref[rows, gate_cols] = dgate.astype(NARROW)
                given = given * (gate * sig)
                dgain = dgain + jnp.sum(given * unit, axis=0, keepdims=True)
                given = given * gain_ref[...]
                dout = scale * (given - unit * jnp.mean(unit * given, axis=-1, keepdims=True))
                dout = dout.astype(NARROW)
                dout_ref[rows, cols] = dout
                score_t = turned(score_ref[at])
                back = product_exact(score_t, dout)
                pdo_ref[rows, cols] = back
                inv_t = turned(inv_ref[at])
                back = product(inv_t, halves(back))
                query_t = turned(carried * q_ref[rows, cols])
                key_t = turned((beta_of(raw_ref, rows, 4 * span + head) * carried) * k_ref[rows, cols])
                grad_ref[at] = product_exact(query_t, dout) - product(key_t, halves(back))
        return dgain

    dgain = lax.fori_loop(0, count // BACK_STEP, first, jnp.zeros((1, width), WIDE))

    def second(step, grads):
        index = count - 1 - step
        result = []
        for head in range(heads):
            at = index * heads + head
            added = grad_ref[at]
            grad_ref[at] = grads[head]
            result.append(product(turned(move_ref[at]), halves(grads[head])) + added)
        return tuple(result)

    lax.fori_loop(0, count, second, tuple(jnp.zeros((width, width), WIDE) for _ in range(heads)))
    dconv_ref[total:total + HALO, :] = jnp.zeros((HALO, 3 * span), WIDE)

    def third(group, tap_sums):
        for sub in range(BACK_STEP):
            index = group * BACK_STEP + sub
            start = pl.multiple_of(index * CHUNK, CHUNK)
            rows = pl.ds(start, CHUNK)
            pos = poscol_ref[rows, :]
            strict, inclusive, carried, last = chunk_masks(
                segcol_ref[rows, :], segrow_ref[pl.ds(index, 1), :], edges_ref[index, 0], edges_ref[index, 1])
            new_sums = []
            dbetas = []
            for head in range(heads):
                cols = pl.ds(head * width, width)
                at = index * heads + head
                beta = beta_of(raw_ref, rows, 4 * span + head)
                query, key, update = q_ref[rows, cols], k_ref[rows, cols], upd_ref[rows, cols]
                query_h, key_h, update_h = halves(query), halves(key), halves(update)
                dout = dout_ref[rows, cols]
                state, grad = halves(state_ref[at]), halves(grad_ref[at])
                convs = []
                for which in range(3):
                    column = which * span + head * width
                    convs.append(conv_rows(pad_ref, taps_ref[which, :, head * width:(head + 1) * width], pos,
                                           start, column, width))
                gates = [jax.nn.sigmoid(c[0]) for c in convs]
                value = convs[2][0] * gates[2]
                dupdate = pdo_ref[rows, cols] + last * product(key_h, grad)
                dright = product(turned(inv_ref[at]), halves(dupdate))
                dright_h = halves(dright)
                dscore = jnp.where(inclusive, product_exact(update_h, dout, 1, 1, flip=True), 0.0)
                dsystem = jnp.where(strict, product(dright_h, update_h, 1, 1), 0.0)
                dscore_h = halves(dscore)
                dquery = carried * product_exact(state, dout, 1, 1, flip=True) + product(dscore_h, key_h)
                weighted = beta * dsystem
                scaled = beta * carried
                dkey = product(turned(dscore), query_h) + last * product(update_h, grad, 1, 1)
                dkey = dkey - product(halves(weighted + weighted.T), key_h)
                dkey = dkey - scaled * product(dright_h, state, 1, 1)
                dvalue = beta * dright
                seen = carried * product(key_h, state)
                dbeta = jnp.sum(dright * (value - seen), axis=-1, keepdims=True) - jnp.sum(
                    dsystem * dots_ref[at], axis=-1, keepdims=True)
                dbetas.append(dbeta * beta * (1.0 - beta))
                sides = []
                for grads, unit, conv, gate in ((dquery, query, convs[0][0], gates[0]), (dkey, key, convs[1][0], gates[1])):
                    plain = conv * gate
                    inv_norm = lax.rsqrt(jnp.sum(plain * plain, axis=-1, keepdims=True) + unit_eps)
                    sides.append(inv_norm * (grads - unit * jnp.sum(unit * grads, axis=-1, keepdims=True)))
                sides.append(dvalue)
                for which in range(3):
                    conv, plain, moved = convs[which]
                    gate = gates[which]
                    dconv = sides[which] * gate * (1.0 + conv * (1.0 - gate))
                    column = which * span + head * width
                    dconv_ref[rows, pl.ds(column, width)] = dconv
                    sums = [jnp.sum(dconv * plain, axis=0, keepdims=True)]
                    for shifted in moved:
                        sums.append(jnp.sum(dconv * shifted, axis=0, keepdims=True))
                    new_sums.append(jnp.concatenate(sums[::-1], axis=0))
            lane = lax.broadcasted_iota(jnp.int32, (CHUNK, draw_ref.shape[1] - 4 * span), 1)
            packed = jnp.zeros(lane.shape, WIDE)
            for head in range(heads):
                packed = jnp.where(lane == head, dbetas[head], packed)
            draw_ref[rows, pl.ds(4 * span, lane.shape[1])] = packed.astype(draw_ref.dtype)
            tap_sums = tuple(old + new for old, new in zip(tap_sums, new_sums))
        return tap_sums

    zero = tuple(jnp.zeros((taps_ref.shape[1], width), WIDE) for _ in range(3 * heads))
    sums = lax.fori_loop(0, count // BACK_STEP, third, zero)
    for head in range(heads):
        for which in range(3):
            dtaps_ref[which, :, head * width:(head + 1) * width] = sums[head * 3 + which]
    taps_count = taps_ref.shape[1]

    def fourth(index, _):
        start = pl.multiple_of(index * CHUNK, CHUNK)
        pos_window = poscol_ref[pl.ds(start, CHUNK + HALO), :]
        for which in range(3):
            columns = pl.ds(which * span, span)
            window = dconv_ref[pl.ds(start, CHUNK + HALO), columns]
            result = taps_ref[which, taps_count - 1:taps_count, :] * window[0:CHUNK]
            for offset in range(1, taps_count):
                part = jnp.where(pos_window >= offset, window, 0.0)[offset:offset + CHUNK]
                result = result + taps_ref[which, taps_count - 1 - offset:taps_count - offset, :] * part
            draw_ref[pl.ds(start, CHUNK), columns] = result.astype(draw_ref.dtype)
        return 0

    lax.fori_loop(0, count, fourth, 0)

    def weigh(index, _):
        rows = pl.ds(pl.multiple_of(index * ENTER, ENTER), ENTER)
        sum_ref[...] += plain_dot(hidden_ref[rows, :], draw_ref[rows, :], 0, 0)
        return 0

    sum_ref[...] = jnp.zeros(sum_ref.shape, WIDE)
    lax.fori_loop(0, total // ENTER, weigh, 0)
    features = small_ref.shape[1]
    small_ref[...] = jnp.zeros(small_ref.shape, WIDE)
    small_ref[heads + 1:heads + 2, :] = dgffn_ref[...]
    own = pl.ds(pl.multiple_of(z_ref[0] * span, span), span)
    for which in range(3):
        first_row = heads + 2 + which * taps_count
        small_ref[first_row:first_row + taps_count, own] = dtaps_ref[which]
    last_row = heads + 2 + 3 * taps_count
    small_ref[last_row:last_row + 1, :] = product_exact(
        halves(jnp.broadcast_to(dgain, (8, width))), shard_places(width, features, shard_rows, False))[0:1]
    gain = win_ref[:, 4 * span + heads:4 * span + heads + 1].astype(WIDE)
    across = jnp.sum(sum_ref[...] * win_ref[...].astype(WIDE), axis=-1, keepdims=True) / gain
    beside = small_ref[...].T
    lane = lax.broadcasted_iota(jnp.int32, beside.shape, 1)
    gradin_ref[:, 0:4 * span] = sum_ref[:, 0:4 * span].astype(NARROW)
    beside = sum_ref[:, 4 * span:] + beside + jnp.where(lane == heads, across, 0.0)
    gradin_ref[:, 4 * span:] = beside.astype(NARROW)

    def leave(index, _):
        rows = pl.ds(pl.multiple_of(index * ENTER, ENTER), ENTER)
        dhid_ref[rows, :] = plain_dot(draw_ref[rows, :], win_ref[...], 1, 1).astype(NARROW)
        return 0

    lax.fori_loop(0, total // ENTER, leave, 0)
    for k, block in enumerate(blocks):
        block[...] = unpack_rows(far_ref[...], dhid_ref[...], k, total // n_fs)


def product_exact(left, exact, left_dim=1, right_dim=0, flip=False):
    def one(a):
        if flip:
            return lax.dot_general(exact, a, (((right_dim,), (left_dim,)), ((), ())), preferred_element_type=WIDE)
        return lax.dot_general(a, exact, (((left_dim,), (right_dim,)), ((), ())), preferred_element_type=WIDE)

    if PASSES == 1:
        return one(left[0])
    return one(left[0]) + one(left[1])


def cost(flops, size):
    return pl.CostEstimate(flops=flops, bytes_accessed=size, transcendentals=0)


def specs(count):
    return [pl.BlockSpec(memory_space=pltpu.VMEM)] * count


def anywhere():
    return pl.BlockSpec(memory_space=pl.ANY)


def in_scalars():
    return pl.BlockSpec(memory_space=pltpu.SMEM)


def delta_forward(pieces, w_in, near, far, segcol, poscol, segrow, edges, z, heads, width, n_taps, shard_rows):
    n_fs = len(pieces)
    total = near.shape[0]
    features, lanes = w_in.shape
    count = total // CHUNK
    span = heads * width
    thin = jax.ShapeDtypeStruct((total, span), NARROW)
    rows = jax.ShapeDtypeStruct((total, span), WIDE)
    full = jax.ShapeDtypeStruct((total, features), NARROW)
    square = jax.ShapeDtypeStruct((count * heads, CHUNK, CHUNK), WIDE)
    state = jax.ShapeDtypeStruct((count * heads, width, width), WIDE)
    block = jax.ShapeDtypeStruct((total // n_fs, span), NARROW)
    raw = jax.ShapeDtypeStruct((total, lanes), WIDE)
    side = jax.ShapeDtypeStruct((lanes - 4 * span, features), WIDE)
    taps = jax.ShapeDtypeStruct((3, n_taps, span), WIDE)
    gain = jax.ShapeDtypeStruct((1, width), WIDE)
    result = pl.pallas_call(
        functools.partial(forward_kernel, heads, width, n_fs, shard_rows),
        out_shape=(block,) * n_fs
        + (side, taps, gain, full, raw, thin, rows, rows, square, square, square, rows, state, state),
        in_specs=specs(n_fs + 6) + [in_scalars()] * 2,
        out_specs=tuple(specs(n_fs + 14)),
        scratch_shapes=[
            pltpu.VMEM((total + HALO, 3 * span), WIDE),
            pltpu.VMEM((total, span), WIDE),
            pltpu.VMEM((total, span), WIDE),
            pltpu.VMEM((total, span), NARROW),
        ],
        compiler_params=pltpu.CompilerParams(vmem_limit_bytes=52 << 20),
        cost_estimate=cost(30_000_000_000, 16 << 20),
        name="delta_forward",
    )(*pieces, w_in, near, far, segcol, poscol, segrow, edges, z)
    return result[:n_fs], result[n_fs], result[n_fs + 1 :]


def delta_backward(pieces, w_in, near, far, segcol, poscol, segrow, edges, z, dgffn, kept, heads, width, shard_rows):
    n_fs = len(pieces)
    total = near.shape[0]
    features, lanes = w_in.shape
    count = total // CHUNK
    span = heads * width
    block = jax.ShapeDtypeStruct((total // n_fs, features), NARROW)
    result = pl.pallas_call(
        functools.partial(backward_kernel, heads, width, n_fs, shard_rows),
        out_shape=(jax.ShapeDtypeStruct((features, lanes), NARROW),) + (block,) * n_fs,
        in_specs=specs(n_fs + 6) + [in_scalars()] * 2 + specs(14),
        out_specs=tuple(specs(n_fs + 1)),
        scratch_shapes=[
            pltpu.VMEM((total, lanes), NARROW),
            pltpu.VMEM((total, features), NARROW),
            pltpu.VMEM(kept[0].shape, WIDE),
            pltpu.VMEM((features, lanes), WIDE),
            pltpu.VMEM((lanes - 4 * span, features), WIDE),
            pltpu.VMEM((total + HALO, 3 * span), WIDE),
            pltpu.VMEM((count * heads, width, width), WIDE),
            pltpu.VMEM((total, span), WIDE),
            pltpu.VMEM((total + HALO, 3 * span), WIDE),
            pltpu.VMEM((total, span), NARROW),
            pltpu.VMEM((total, span), NARROW),
        ],
        compiler_params=pltpu.CompilerParams(vmem_limit_bytes=52 << 20),
        cost_estimate=cost(40_000_000_000, 16 << 20),
        name="delta_backward",
    )(*pieces, w_in, near, far, segcol, poscol, segrow, edges, z, dgffn, *kept)
    return result[0], list(result[1:])


def finish_kernel(heads, span, n_taps, z_ref, *refs):
    n_fs = len(refs) - 10
    pieces, refs = refs[:n_fs], refs[n_fs:]
    (*grads, wout_ref, beta_ref, taps_ref, gmix_ref, gffn_ref, ghead_ref) = refs
    side = pl.ds(4 * span, 128)
    lane = lax.broadcasted_iota(jnp.int32, (128, beta_ref.shape[1]), 0)
    column = lax.broadcasted_iota(jnp.int32, (128, beta_ref.shape[1]), 1)
    wout = jnp.zeros(wout_ref.shape, WIDE)
    small = jnp.zeros((wout_ref.shape[0], 128), WIDE)
    beta = jnp.zeros(beta_ref.shape, WIDE)
    for k, piece in enumerate(pieces):
        line = lax.rem(z_ref[0] + n_fs - k, n_fs)
        place = pl.ds(pl.multiple_of(line * span, span), span)
        for which, grad in enumerate(grads):
            grad[:, place] = piece[:, which * span:(which + 1) * span].astype(WIDE)
        wout = wout + piece[:, 4 * span + 128:].astype(WIDE)
        beside = piece[:, side]
        small = small + beside.astype(WIDE)
        chosen = jnp.where((lane < heads) & (column == line * heads + lane), 1.0, 0.0)
        beta = beta + plain_dot(beside, chosen.astype(NARROW))
    wout_ref[...] = wout
    beta_ref[...] = beta
    small = small.T
    gmix_ref[...] = small[heads:heads + 1]
    gffn_ref[...] = small[heads + 1:heads + 2]
    last_row = heads + 2 + 3 * n_taps
    taps_ref[...] = small[heads + 2:last_row]
    ghead_ref[...] = small[last_row:last_row + 1]


def finish(z, pieces, heads, span, n_taps):
    rows = pieces[0].shape[0]
    n_fs = len(pieces)
    full = jax.ShapeDtypeStruct((rows, n_fs * span), WIDE)
    line = jax.ShapeDtypeStruct((1, rows), WIDE)
    return pl.pallas_call(
        functools.partial(finish_kernel, heads, span, n_taps),
        out_shape=(full,) * 5
        + (
            jax.ShapeDtypeStruct((rows, n_fs * heads), WIDE),
            jax.ShapeDtypeStruct((3 * n_taps, rows), WIDE),
            line,
            line,
            line,
        ),
        in_specs=[in_scalars()] + specs(n_fs),
        out_specs=tuple(specs(10)),
        cost_estimate=cost(1_000_000, 1 << 20),
        name="finish_inputs",
    )(z, *pieces)


def mix_out_kernel(n_fs, row, z_ref, *refs):
    pieces, refs = refs[:n_fs], refs[n_fs:]
    wout_ref, tokens_ref, gain_ref, middle_ref, ffn_ref, normed_ref = refs
    span = pieces[0].shape[1]
    middle = tokens_ref[...].astype(WIDE)
    for k, piece in enumerate(pieces):
        place = pl.ds(pl.multiple_of(lax.rem(z_ref[0] + n_fs - k, n_fs) * span, span), span)
        normed_ref[:, place] = piece[...]
        middle = middle + plain_dot(piece[...], wout_ref[place, :])
    middle_ref[...] = middle
    scale = lax.rsqrt(jnp.mean(middle * middle, axis=-1, keepdims=True) + norm_eps)
    ffn_ref[...] = (middle * scale * gain_ref[row:row + 1, :]).astype(NARROW)


def mix_out(z, pieces, w_out, tokens, side, row):
    n_fs = len(pieces)
    shape = tokens.shape
    return pl.pallas_call(
        functools.partial(mix_out_kernel, n_fs, row),
        out_shape=(
            jax.ShapeDtypeStruct(shape, WIDE),
            jax.ShapeDtypeStruct(shape, NARROW),
            jax.ShapeDtypeStruct(shape, NARROW),
        ),
        in_specs=[in_scalars()] + specs(n_fs + 3),
        out_specs=tuple(specs(3)),
        compiler_params=pltpu.CompilerParams(vmem_limit_bytes=40 << 20),
        cost_estimate=cost(2_000_000_000, 6 << 20),
        name="mix_out",
    )(z, *pieces, w_out, tokens, side)


def ffn_kernel(keys, unit, block_ref, *refs):
    count = TP
    rows_in, refs = refs[:count], refs[count:]
    cots, refs = refs[:count], refs[count:]
    weights, refs = refs[:len(keys)], refs[len(keys):]
    (wdown_ref, active_ref, dboth_ref, sent_ref, later_ref, own_ref, part_ref, *ordered) = refs
    own_rows = rows_in[0].shape[0]
    if ordered:
        for near, far in zip(weights, ordered):
            n_fs, size = near.shape[:2]
            for by in range(n_fs):
                line = lax.rem(block_ref[1] + n_fs - by, n_fs)
                for at in range(size // unit):
                    place = pl.ds(pl.multiple_of((at * n_fs + line) * unit, unit), unit)
                    far[place, :] = near[by, at * unit:(at + 1) * unit, :]
        weights = ordered
    depth = weights[0].shape[0]
    units = wdown_ref.shape[0]
    spots = [pl.ds(pl.multiple_of((block_ref[0] ^ key) * depth, depth), depth) for key in keys]
    half = count // 2 * own_rows
    for at in range(count - 1, -1, -1):
        rows = slice(at * own_rows, (at + 1) * own_rows)
        both = plain_dot(rows_in[at][:, spots[0]], weights[0][...])
        for spot, weight in zip(spots[1:], weights[1:]):
            both = both + plain_dot(rows_in[at][:, spot], weight[...])
        gate, up = both[:, :units], both[:, units:]
        sig = jax.nn.sigmoid(gate)
        silu = gate * sig
        active_ref[rows, :] = (silu * up).astype(NARROW)
        dactive = plain_dot(cots[at][...], wdown_ref[...], 1, 1)
        dboth_ref[rows, :units] = (dactive * up * (sig * (1.0 + gate * (1.0 - sig)))).astype(NARROW)
        dboth_ref[rows, units:] = (dactive * silu).astype(NARROW)
        dboth = dboth_ref[rows, :]
        for spot, weight in zip(spots, weights):
            part_ref[:, spot] = plain_dot(dboth, weight[...], 1, 1)
        if at >= count // 2:
            place = at * own_rows - half
            sent_ref[place:place + own_rows, :] = part_ref[...].astype(NARROW)
        elif at:
            later_ref[(at - 1) * own_rows:at * own_rows, :] = part_ref[...]
        else:
            own_ref[...] = part_ref[...]


def ffn_units(block, rows_in, cots, weights, keys, w_down, unit):
    own_rows, features = rows_in[0].shape
    units = w_down.shape[0]
    total = TP * own_rows
    return pl.pallas_call(
        functools.partial(ffn_kernel, keys, unit),
        out_shape=(
            jax.ShapeDtypeStruct((total, units), NARROW),
            jax.ShapeDtypeStruct((total, 2 * units), NARROW),
            jax.ShapeDtypeStruct((total // 2, features), NARROW),
            jax.ShapeDtypeStruct((total // 2 - own_rows, features), WIDE),
            jax.ShapeDtypeStruct((own_rows, features), WIDE),
        ),
        in_specs=[in_scalars()] + specs(2 * TP + len(weights) + 1),
        out_specs=tuple(specs(5)),
        scratch_shapes=[pltpu.VMEM((own_rows, features), WIDE)]
        + [pltpu.VMEM((features // len(keys), 2 * units), NARROW) for w in weights if w.ndim == 3],
        compiler_params=pltpu.CompilerParams(vmem_limit_bytes=52 << 20),
        cost_estimate=cost(8_000_000_000, 16 << 20),
        name="ffn_units",
    )(block, *rows_in, *cots, *weights, w_down)


def mix_back_kernel(n_fs, row, z_ref, *refs):
    sources, refs = refs[:6], refs[6:]
    gain_ref, refs = refs[0], refs[1:]
    blocks, refs = refs[:n_fs], refs[n_fs:]
    (dmiddle_ref, dbranch_ref, dgain_ref, *places, sems) = refs
    fetches = [pltpu.make_async_copy(source, place, sems.at[k]) for k, (source, place) in enumerate(zip(sources, places))]
    quarter = places[5].shape[0] // 4
    parts = [pl.ds(k * quarter, quarter) for k in range(4)]
    fetches[5:] = [
        pltpu.make_async_copy(sources[5].at[part], places[5].at[part], sems.at[5 + k]) for k, part in enumerate(parts)
    ]
    for fetch in fetches:
        fetch.start()
    own_ref, core_ref, side_ref, middle_ref, cot_ref, wout_ref = places
    for fetch in fetches[:5]:
        fetch.wait()
    middle = middle_ref[...]
    given = own_ref[...] + core_ref[0:own_ref.shape[0], :].astype(WIDE) + side_ref[...].astype(WIDE)
    scale = lax.rsqrt(jnp.mean(middle * middle, axis=-1, keepdims=True) + norm_eps)
    unit = middle * scale
    dgain_ref[...] = jnp.sum(given * unit, axis=0, keepdims=True)
    given = given * gain_ref[row:row + 1, :]
    dmiddle = cot_ref[...].astype(WIDE) + scale * (given - unit * jnp.mean(unit * given, axis=-1, keepdims=True))
    dmiddle_ref[...] = dmiddle
    dbranch = dmiddle.astype(NARROW)
    dbranch_ref[...] = dbranch
    span = blocks[0].shape[1]
    for fetch in fetches[5:]:
        fetch.wait()
    for k, block in enumerate(blocks):
        place = pl.ds(pl.multiple_of(lax.rem(z_ref[0] + k, n_fs) * span, span), span)
        block[...] = plain_dot(dbranch, wout_ref[place, :], 1, 1).astype(NARROW)


def mix_back(z, parts, middle, side, row, cotangent, w_out, n_fs):
    count, features = middle.shape
    block = jax.ShapeDtypeStruct((count, features // n_fs), NARROW)
    sources = (*parts, middle, cotangent, w_out)
    result = pl.pallas_call(
        functools.partial(mix_back_kernel, n_fs, row),
        out_shape=(block,) * n_fs
        + (
            jax.ShapeDtypeStruct(middle.shape, WIDE),
            jax.ShapeDtypeStruct(middle.shape, NARROW),
            jax.ShapeDtypeStruct((1, features), WIDE),
        ),
        in_specs=[in_scalars()] + [anywhere()] * 6 + specs(1),
        out_specs=tuple(specs(n_fs + 3)),
        scratch_shapes=[pltpu.VMEM(part.shape, part.dtype) for part in sources] + [pltpu.SemaphoreType.DMA((9,))],
        compiler_params=pltpu.CompilerParams(vmem_limit_bytes=60 << 20),
        cost_estimate=cost(2_000_000_000, 6 << 20),
        name="mix_back",
    )(z, *sources, side)
    return (result[:n_fs],) + tuple(result[n_fs:])


def rms_scale(values, gain):
    return values * lax.rsqrt(jnp.mean(values * values, axis=-1, keepdims=True) + norm_eps) * gain


def swiglu(gate_proj, up_proj):
    return jax.nn.silu(gate_proj) * up_proj


def sequence_layout(lengths_row, total):
    ends = jnp.cumsum(lengths_row)
    index = jnp.arange(total, dtype=jnp.int32)
    before = index[:, None] >= ends[None, :]
    segment = jnp.sum(before.astype(jnp.int32), axis=1)
    start = jnp.sum(jnp.where(before, lengths_row[None, :], 0), axis=1)
    return (segment, index - start)


def project(left, right):
    return jnp.dot(left, right, preferred_element_type=WIDE)


def project_back(left, right):
    return lax.dot_general(left, right, (((1,), (1,)), ((), ())), preferred_element_type=WIDE)


def weight_grad(left, right):
    return lax.dot_general(left, right, (((0,), (0,)), ((), ())), preferred_element_type=WIDE)


def flip(value, bit, n_dp):
    return lax.ppermute(value, "dp", [(i, i ^ bit) for i in range(n_dp)])


def shift(value, by, n_fs):
    return lax.ppermute(value, "fsdp", [(i, (i + by) % n_fs) for i in range(n_fs)])


def line_pieces(shard, n_fs):
    return [shard] + [shift(shard, by, n_fs) for by in range(1, n_fs)]


def line_order(pieces, z):
    n_fs = len(pieces)
    shape = pieces[0].shape
    whole = jnp.zeros((shape[0], n_fs) + shape[1:], pieces[0].dtype)
    for by, piece in enumerate(pieces):
        whole = lax.dynamic_update_slice_in_dim(whole, piece[:, None], lax.rem(z + n_fs - by, n_fs), 1)
    return whole


def gather_cube(piece, order, n_dp):
    pieces = {0: piece}
    for bit in order:
        for key in list(pieces):
            pieces[key ^ bit] = flip(pieces[key], bit, n_dp)
    return pieces


def in_order(pieces, me):
    rows = pieces[0].shape[0]
    whole = jnp.zeros((len(pieces) * rows,) + pieces[0].shape[1:], pieces[0].dtype)
    unit = max(pieces).bit_length()
    step = (1 << unit) // len(pieces)
    for key, piece in pieces.items():
        whole = lax.dynamic_update_slice_in_dim(whole, piece, lax.bitwise_xor(me, key // step) * rows, 0)
    return whole


def per_device(
    n_dp,
    n_fs,
    tokens,
    lengths,
    packing,
    w_query,
    w_key,
    w_value,
    w_gate,
    w_beta,
    conv_taps,
    w_out,
    gain_mix,
    gain_head,
    gain_ffn,
    w_ffn_gate,
    w_ffn_up,
    w_ffn_down,
    cotangent,
):
    me = lax.axis_index("dp")
    z = lax.axis_index("fsdp")
    bits = [1 << k for k in range(n_dp.bit_length() - 1)]
    first_order = bits[:1] + bits[1:]
    second_order = bits[:1] + bits[1:][::-1]
    packing_row = packing[0]
    lengths_row = lengths[0]
    own_rows, features = tokens.shape
    total = own_rows * n_fs
    rows = w_query.shape[0]
    heads_all = w_beta.shape[1]
    heads = heads_all // n_fs
    span = features // n_fs
    width = span // heads
    hidden_ffn = w_ffn_gate.shape[1]
    head_rows = gain_head.shape[0]
    n_taps = conv_taps.shape[1]

    def by_owner(matrix):
        return jnp.swapaxes(matrix.reshape(rows, n_fs, -1), 0, 1)

    small = jnp.concatenate(
        [
            gain_mix[:, None],
            gain_ffn[:, None],
            conv_taps.reshape(3 * n_taps, rows).T,
            jnp.pad(gain_head, (0, rows - head_rows))[:, None],
        ],
        axis=1,
    )
    n_small = small.shape[1]
    side = jnp.concatenate(
        [by_owner(w_beta), jnp.broadcast_to(small[None], (n_fs, rows, n_small))], axis=2
    )
    side = jnp.pad(side, ((0, 0), (0, 0), (0, 128 - heads - n_small)))
    packet = jnp.concatenate(
        [by_owner(w_query), by_owner(w_key), by_owner(w_value), by_owner(w_gate), side], axis=2
    )
    member = lax.rem(me, TP)
    block = me // TP
    n_rest = n_dp // TP
    ff_block = hidden_ffn // n_dp
    ff_line = ff_block // n_fs
    ff_unit = -(-ff_line // 8) * 8
    while n_rest * n_fs * ff_unit % 128:
        ff_unit += 8
    ff_pad = n_rest * n_fs * ff_unit
    tp_bits = [bit for bit in bits if bit < TP]
    rest_bits = [bit for bit in bits if bit >= TP]

    def by_member(matrix):
        split = matrix.reshape(rows, n_rest, TP, n_fs, ff_line)
        split = jnp.pad(split, ((0, 0),) * 4 + ((0, ff_unit - ff_line),))
        return jnp.transpose(split, (2, 0, 1, 3, 4)).reshape(TP, rows, ff_pad)

    def hand_out(blocks):
        pieces = [lax.dynamic_index_in_dim(blocks, z, 0)]
        for by in range(1, n_fs):
            pieces.append(shift(lax.dynamic_index_in_dim(blocks, lax.rem(z + by, n_fs), 0), by, n_fs))
        return pieces

    lanes = 4 * span + 128
    packet = jnp.concatenate([packet, jnp.broadcast_to(w_out[None], (n_fs,) + w_out.shape)], axis=2)
    packet = hand_out(packet)
    token_pieces = [tokens] + [shift(tokens, by, n_fs) for by in range(1, n_fs)]
    packet, token_pieces[1] = lax.optimization_barrier((packet, token_pieces[1]))
    packet_in = line_order([piece[:, :, :lanes] for piece in packet], z).reshape(n_fs * rows, lanes)
    packet_out = line_order([piece[:, :, lanes:] for piece in packet], z).reshape(n_fs * rows, features)
    w_in = lax.all_gather(packet_in, "dp", axis=0, tiled=True)
    full_out = lax.all_gather(packet_out, "dp", axis=0, tiled=True)

    owner, place = packing_row // own_rows, lax.rem(packing_row, own_rows)
    near = (lax.rem(z + n_fs - owner, n_fs) * own_rows + place)[:, None]
    far = (lax.rem(owner + n_fs - z, n_fs) * own_rows + place)[None]
    segment, position = sequence_layout(lengths_row, total)
    seg_rows = segment.reshape(-1, CHUNK)
    ends = seg_rows[:, -1]
    edges = jnp.stack([jnp.concatenate([jnp.full((1,), -1, jnp.int32), ends[:-1]]), ends], axis=1)
    z_ref = z.reshape(1)
    layout = (segment[:, None], jnp.pad(position, (0, HALO))[:, None], seg_rows, edges, z_ref)
    shard_rows = (rows, head_rows)
    own_gate, own_up, _ = lax.optimization_barrier((w_ffn_gate, w_ffn_up, token_pieces[1]))
    both_sends = jnp.concatenate([by_member(own_gate), by_member(own_up)], axis=2)
    blocks, side, kept = delta_forward(
        token_pieces, w_in, near, far, *layout, heads, width, n_taps, shard_rows
    )
    gain_row = heads + 1

    both_pieces = {
        key: flip(lax.dynamic_index_in_dim(both_sends, member ^ key, 0, keepdims=False), key, n_dp)
        if key
        else lax.dynamic_index_in_dim(both_sends, member, 0, keepdims=False)
        for key in range(TP)
    }
    own_down, _ = lax.optimization_barrier((w_ffn_down, token_pieces[1]))
    own_down = jnp.pad(own_down, ((0, ff_unit - ff_line), (0, 0)))
    down_rows = in_order(gather_cube(own_down, rest_bits, n_dp), block).reshape(n_rest, -1, features)
    both_rows = in_order(both_pieces, member).reshape(TP, rows, 2 * ff_pad)
    own_cotangent, both_rows, down_rows = lax.optimization_barrier((cotangent, both_rows, down_rows))
    both_rows, down_rows, _ = lax.optimization_barrier((both_rows, down_rows, token_pieces))
    both_line = line_pieces(both_rows, n_fs)
    both_line, blocks, down_rows = lax.optimization_barrier((both_line, blocks, down_rows))
    if rows % 16 == 0:
        both_rows = jnp.stack([piece.reshape(TP * rows, 2 * ff_pad) for piece in both_line])
    else:
        both_rows = line_order(both_line, z).reshape(-1, 2 * ff_pad)
    both_pieces = gather_cube(both_rows, rest_bits, n_dp)
    unit = 1 << (TP.bit_length() - 1)
    rest_keys = [key // unit for key in both_pieces]
    tp_order = sorted(range(TP), key=lambda key: tuple((key & bit) != 0 for bit in tp_bits))

    cot_pieces = gather_cube(own_cotangent, tp_bits[::-1], n_dp)
    cot_pieces, blocks = lax.optimization_barrier((cot_pieces, blocks))

    def collect(left, right, dims):
        arrived = []
        keep = TP

        def term(lo, hi):
            value = lax.dot_general(
                left[lo * own_rows : hi * own_rows], right, (dims, ((), ())), preferred_element_type=WIDE
            )
            for earlier in arrived:
                value = value + earlier[lo * own_rows : hi * own_rows].astype(WIDE)
            return value

        for bit in tp_bits:
            keep //= 2
            sent = yield term(keep, 2 * keep).astype(NARROW)
            arrived.append(flip(sent, bit, n_dp))
        yield term(0, 1)

    def halve(value, index, some_bits):
        unit = some_bits[0] if some_bits else 1
        for bit in some_bits[::-1]:
            half = value.shape[0] // 2
            mine = (index // (bit // unit)) % 2
            sent = lax.dynamic_slice_in_dim(value, (1 - mine) * half, half, 0)
            value = lax.dynamic_slice_in_dim(value, mine * half, half, 0)
            value = value.astype(WIDE) + flip(sent.astype(NARROW), bit, n_dp).astype(WIDE)
        return value

    def sum_up(pieces, whole):
        total = lax.dynamic_index_in_dim(whole, z, 0, keepdims=False).astype(WIDE)
        for piece in pieces[1:]:
            total = total + piece[0].astype(WIDE)
        return total

    def pass_on(parts):
        return [parts[0]] + [shift(part, by, n_fs) for by, part in enumerate(parts) if by]

    mixed_pieces = pass_on(blocks)
    down_line = line_pieces(down_rows, n_fs)
    middle, ffn_in, normed_b = mix_out(z_ref, mixed_pieces, full_out, tokens, side, gain_row)
    w_down = line_order(down_line, z).reshape(ff_pad, features)
    ffn_pieces = gather_cube(ffn_in, tp_bits[::-1], n_dp)
    active_b, d_both, first, second, d_own = ffn_units(
        jnp.stack([block, z]),
        [ffn_pieces[key] for key in tp_order],
        [cot_pieces[key] for key in tp_order],
        list(both_pieces.values()),
        rest_keys,
        w_down,
        rows,
    )
    ffn_near = jnp.concatenate([ffn_pieces[key] for key in tp_order], axis=0)

    def both_part(lo, size):
        part = weight_grad(lax.dynamic_slice_in_dim(ffn_near, lo, size, 1), d_both)
        return part.reshape(-1, n_fs * rows, 2 * ff_pad)

    split = features // 2 if rest_bits else features
    top = block // max(n_rest // 2, 1)
    if rest_bits:
        both_sent = both_part((1 - top) * split, split).astype(NARROW)
    else:
        both_sent = None
    from_core = flip(first, tp_bits[0], n_dp)
    second = second + from_core[own_rows:].astype(WIDE)
    second, both_sent, active_late = lax.optimization_barrier((second.astype(NARROW), both_sent, active_b))
    from_side = flip(second, tp_bits[1], n_dp)
    cotangent_near = jnp.concatenate([cot_pieces[key] for key in tp_order], axis=0)
    down_terms = weight_grad(active_late, cotangent_near).astype(NARROW)
    down_sum = lax.psum_scatter(
        down_terms.reshape(n_rest, -1, features), "fsdp", scatter_dimension=1, tiled=True
    )
    from_side, down_terms, ffn_near, active_late = lax.optimization_barrier(
        (from_side, down_terms, ffn_near, active_late)
    )
    both_sum = both_part(top * split if rest_bits else 0, split)
    if rest_bits:
        both_sum = both_sum + flip(both_sent, rest_bits[-1], n_dp).astype(WIDE)
        both_sum = halve(both_sum, block, rest_bits[:-1])

    d_blocks, d_middle, d_branch, d_gffn = mix_back(
        z_ref, (d_own, from_core, from_side), middle, side, gain_row, cotangent, full_out, n_fs
    )
    d_pieces = pass_on(d_blocks)
    out_grad = weight_grad(normed_b, d_branch).astype(NARROW)
    sum_out = lax.psum_scatter(out_grad, "dp", scatter_dimension=0, tiled=True)
    both_sum = jnp.swapaxes(both_sum.reshape(TP, n_fs, rows, 2 * ff_pad), 0, 1)
    both_sum, d_pieces, out_grad = lax.optimization_barrier((both_sum, d_pieces, out_grad))
    both_line = hand_out(both_sum.astype(NARROW))

    grad_in, d_blocks = delta_backward(
        d_pieces, w_in, near, far, *layout, d_gffn, kept, heads, width, shard_rows
    )
    grad_in, both_line, down_sum, sum_out = lax.optimization_barrier((grad_in, both_line, down_sum, sum_out))
    part = lax.psum_scatter(grad_in, "dp", scatter_dimension=0, tiled=True)
    d_blocks, both_line, active_late = lax.optimization_barrier((d_blocks, both_line, active_late))
    d_blocks = pass_on(d_blocks)
    out_terms = collect(active_late, w_down, ((1,), (0,)))
    layer_out = (middle + out_terms.send(out_terms.send(next(out_terms)))).astype(NARROW)
    both_sum = sum_up(both_line, both_sum)
    grad_fdown = halve(down_sum, block, rest_bits)[0, :ff_line].astype(WIDE)
    both_pieces = {
        key: flip(lax.dynamic_index_in_dim(both_sum, member ^ key, 0, keepdims=False), key, n_dp)
        if key
        else lax.dynamic_index_in_dim(both_sum, member, 0, keepdims=False)
        for key in range(TP)
    }
    both_mine = in_order({key: piece[None] for key, piece in both_pieces.items()}, member)
    def units_of(which):
        part = both_mine[:, :, which * ff_pad : (which + 1) * ff_pad]
        part = part.reshape(TP, rows, n_rest, n_fs, ff_unit)[..., :ff_line]
        return jnp.transpose(part, (1, 2, 0, 3, 4)).reshape(rows, hidden_ffn)

    lanes = part.shape[1]
    joint = jnp.concatenate([part, sum_out], axis=1).reshape(n_fs, rows, -1)
    arrived = [piece[0] for piece in hand_out(joint)]
    d_blocks, arrived[0], layer_out = lax.optimization_barrier((d_blocks, arrived[0], layer_out))
    d_hidden = d_blocks[0].astype(WIDE)
    for block_of in d_blocks[1:]:
        d_hidden = d_hidden + block_of.astype(WIDE)

    d_hidden = d_blocks[0].astype(WIDE)
    for block_of in d_blocks[1:]:
        d_hidden = d_hidden + block_of.astype(WIDE)
    _, norm_mix_back = jax.vjp(rms_scale, tokens.astype(WIDE), side[heads])
    d_inputs_norm, _ = norm_mix_back(d_hidden)
    grad_tokens = d_middle + d_inputs_norm

    grads, (grad_wout, grad_beta, grad_taps, grad_gmix, grad_gffn, grad_ghead) = (
        lambda outs: (outs[:4], outs[4:])
    )(finish(z_ref, arrived, heads, span, n_taps))
    return (
        layer_out,
        grad_tokens,
        grads[0],
        grads[1],
        grads[2],
        grads[3],
        grad_beta,
        grad_taps.reshape(3, n_taps, rows),
        grad_wout,
        grad_gmix[0],
        grad_ghead[0, :head_rows],
        grad_gffn[0],
        units_of(0),
        units_of(1),
        grad_fdown,
    )


def solution(mesh):
    both = ("dp", "fsdp")
    rows = P(both, None)
    group = P("dp", None)
    taps = P(None, None, both)
    line = P(both)
    in_specs = (rows, group, group) + (rows,) * 5 + (taps, rows, line, line, line) + (rows,) * 4
    out_specs = (rows,) * 7 + (taps, rows, line, line, line) + (rows,) * 3
    return jax.shard_map(
        functools.partial(per_device, mesh.shape["dp"], mesh.shape["fsdp"]),
        mesh=mesh,
        in_specs=in_specs,
        out_specs=out_specs,
        check_vma=False,
    )
```

```python
import functools

import jax
import jax.numpy as jnp
from jax import lax
from jax.experimental import pallas as pl
from jax.experimental.pallas import tpu as pltpu
from jax.sharding import PartitionSpec as P

CHUNK = 128
TP = 4
PER_STEP = 4
BACK_STEP = 2
ENTER = 256
HALO = 8
norm_eps = 1e-05
unit_eps = 1e-06
NARROW = jnp.bfloat16
WIDE = jnp.float32


def halves(value):
    top = value.astype(NARROW)
    return top, (value - top.astype(WIDE)).astype(NARROW)


def product(left, right, left_dim=1, right_dim=0):
    dims = (((left_dim,), (right_dim,)), ((), ()))

    def one(a, b):
        return lax.dot_general(a, b, dims, preferred_element_type=WIDE)

    if PASSES == 1:
        return one(left[0], right[0])
    return one(left[0], right[0]) + (one(left[0], right[1]) + one(left[1], right[0]))


PASSES = 3


def turned(value):
    return halves(value.T)


def chunk_masks(seg_col, seg_row, before, after):
    size = seg_col.shape[0]
    down = lax.broadcasted_iota(jnp.int32, (size, size), 0)
    across = lax.broadcasted_iota(jnp.int32, (size, size), 1)
    same = seg_col == seg_row
    strict = same & (down > across)
    inclusive = same & (down >= across)
    carried = jnp.where(seg_col == before, 1.0, 0.0).astype(WIDE)
    last = jnp.where(seg_col == after, 1.0, 0.0).astype(WIDE)
    return strict, inclusive, carried, last


def unit_lower_inverses(systems):
    size = systems[0].shape[0]
    down = lax.broadcasted_iota(jnp.int32, (size, size), 0)
    across = lax.broadcasted_iota(jnp.int32, (size, size), 1)
    gap = jnp.where(down > across, down ^ across, 0)
    eye = jnp.where(down == across, 1.0, 0.0)
    results = [eye - jnp.where(gap == 1, system, 0.0) for system in systems]
    step = 2
    while step < size:
        picked = (gap >= step) & (gap < 2 * step)
        parts = [jnp.where(picked, system, 0.0).astype(NARROW) for system in systems]
        done = [result.astype(NARROW) for result in results]
        inner = [plain_dot(part, own).astype(NARROW) for part, own in zip(parts, done)]
        results = [result - plain_dot(own, side) for result, own, side in zip(results, done, inner)]
        step *= 2
    left = [eye - result - product(halves(system), halves(result)) for system, result in zip(systems, results)]
    results = [
        result + plain_dot(result.astype(NARROW), rest.astype(NARROW)) for result, rest in zip(results, left)
    ]
    return results


def conv_rows(pad_ref, taps, pos, start, column, width):
    window = pad_ref[pl.ds(start, CHUNK + HALO), pl.ds(column, width)]
    count = taps.shape[0]
    result = taps[count - 1 : count] * window[HALO : HALO + CHUNK]
    moved = []
    for offset in range(1, count):
        rows = jnp.where(pos >= offset, window[HALO - offset : HALO - offset + CHUNK], 0.0)
        moved.append(rows)
        result = result + taps[count - 1 - offset : count - offset] * rows
    return result, window[HALO : HALO + CHUNK], moved


def fill_padded(raw_ref, pad_ref, width):
    pad_ref[0:HALO, :] = jnp.zeros((HALO, width), WIDE)
    total = raw_ref.shape[0]

    def copy(index, _):
        start = pl.multiple_of(index * CHUNK, CHUNK)
        pad_ref[pl.ds(start + HALO, CHUNK), :] = raw_ref[pl.ds(start, CHUNK), 0:width].astype(NARROW).astype(WIDE)
        return 0

    lax.fori_loop(0, total // CHUNK, copy, 0)


def one_hot(first, second, offset):
    return jnp.where(first - offset == second, 1.0, 0.0).astype(NARROW)


def plain_dot(left, right, left_dim=1, right_dim=0):
    return lax.dot_general(left, right, (((left_dim,), (right_dim,)), ((), ())), preferred_element_type=WIDE)


def pack_rows(near_col, pieces):
    size = pieces[0].shape[0]
    lane = lax.broadcasted_iota(jnp.int32, (near_col.shape[0], size), 1)
    total = plain_dot(one_hot(near_col, lane, 0), pieces[0][...])
    for k in range(1, len(pieces)):
        total = total + plain_dot(one_hot(near_col, lane, k * size), pieces[k][...])
    return total


def unpack_rows(far_row, packed, k, size):
    down = lax.broadcasted_iota(jnp.int32, (size, far_row.shape[1]), 0)
    return plain_dot(one_hot(far_row, down, k * size), packed).astype(NARROW)


def beta_of(raw_ref, rows, lane):
    return jax.nn.sigmoid(raw_ref[rows, lane:lane + 1].astype(NARROW).astype(WIDE))


def shard_places(size, features, shard_rows, turned_round):
    unit, each = shard_rows
    shape = (features, size) if turned_round else (size, features)
    value = lax.broadcasted_iota(jnp.int32, shape, 1 if turned_round else 0)
    lane = lax.broadcasted_iota(jnp.int32, shape, 0 if turned_round else 1)
    chosen = (lane // unit == value // each) & (lane % unit == value % each)
    return jnp.where(chosen, 1.0, 0.0).astype(NARROW)


def spread_side(heads, width, shard_rows, z_ref, side_ref, taps_ref, gain_ref):
    span = heads * width
    taps_count = taps_ref.shape[1]
    own = pl.ds(pl.multiple_of(z_ref[0] * span, span), span)
    for which in range(3):
        first_row = heads + 2 + which * taps_count
        taps_ref[which] = side_ref[first_row:first_row + taps_count, own]
    last_row = heads + 2 + 3 * taps_count
    entries = jnp.broadcast_to(side_ref[last_row:last_row + 1, :], (8, side_ref.shape[1])).astype(NARROW)
    gain_ref[...] = plain_dot(entries, shard_places(width, side_ref.shape[1], shard_rows, True))[0:1]


def forward_kernel(heads, width, n_fs, shard_rows, *refs):
    pieces, refs = refs[:n_fs], refs[n_fs:]
    (win_ref, near_ref, far_ref, segcol_ref, poscol_ref, segrow_ref, edges_ref, z_ref, *refs) = refs
    blocks, refs = refs[:n_fs], refs[n_fs:]
    (side_ref, hidden_ref, raw_ref, out_ref, q_ref, k_ref, inv_ref, score_ref, dots_ref, upd_ref, state_ref,
     move_ref, taps_ref, gain_ref, pad_ref, base_ref, w_ref, normed_ref) = refs
    total = raw_ref.shape[0]
    count = total // CHUNK
    span = heads * width
    side_ref[...] = win_ref[:, 4 * span:].astype(WIDE).T
    spread_side(heads, width, shard_rows, z_ref, side_ref, taps_ref, gain_ref)

    pad_ref[0:HALO, :] = jnp.zeros((HALO, 3 * span), WIDE)

    def enter(index, _):
        rows = pl.ds(pl.multiple_of(index * ENTER, ENTER), ENTER)
        packed = pack_rows(near_ref[rows, :], pieces)
        scale = lax.rsqrt(jnp.mean(packed * packed, axis=-1, keepdims=True) + norm_eps)
        hidden = (packed * scale * side_ref[heads:heads + 1, :]).astype(NARROW)
        hidden_ref[rows, :] = hidden
        raw = plain_dot(hidden, win_ref[...])
        raw_ref[rows, :] = raw
        pad_ref[pl.ds(pl.multiple_of(index * ENTER + HALO, HALO), ENTER), :] = (
            raw[:, 0:3 * span].astype(NARROW).astype(WIDE))
        return 0

    lax.fori_loop(0, total // ENTER, enter, 0)

    def first(group, _):
        work = []
        for sub in range(PER_STEP):
            index = group * PER_STEP + sub
            start = pl.multiple_of(index * CHUNK, CHUNK)
            rows = pl.ds(start, CHUNK)
            pos = poscol_ref[rows, :]
            before, after = edges_ref[index, 0], edges_ref[index, 1]
            strict, inclusive, carried, last = chunk_masks(
                segcol_ref[rows, :], segrow_ref[pl.ds(index, 1), :], before, after)
            keep = jnp.where(before == after, 1.0, 0.0).astype(WIDE)
            for head in range(heads):
                cols = pl.ds(head * width, width)
                parts = []
                for which in range(3):
                    column = which * span + head * width
                    value = conv_rows(pad_ref, taps_ref[which, :, head * width:(head + 1) * width], pos,
                                      start, column, width)[0]
                    parts.append(value * jax.nn.sigmoid(value))
                query, key, value = parts
                query = query * lax.rsqrt(jnp.sum(query * query, axis=-1, keepdims=True) + unit_eps)
                key = key * lax.rsqrt(jnp.sum(key * key, axis=-1, keepdims=True) + unit_eps)
                q_ref[rows, cols] = query
                k_ref[rows, cols] = key
                beta = beta_of(raw_ref, rows, 4 * span + head)
                key_h, query_h = halves(key), halves(query)
                dots = product(key_h, key_h, 1, 1)
                score = jnp.where(inclusive, product(query_h, key_h, 1, 1), 0.0)
                at = index * heads + head
                dots_ref[at] = dots
                score_ref[at] = score
                work.append((at, rows, cols, keep, jnp.where(strict, beta * dots, 0.0),
                             beta * value, (beta * carried) * key, last * key))
        inverses = unit_lower_inverses([item[4] for item in work])
        for inverse, (at, rows, cols, keep, _, right, carry_in, tail_in) in zip(inverses, work):
            inv_h = halves(inverse)
            base = product(inv_h, halves(right))
            carry = product(inv_h, halves(carry_in))
            tail = turned(tail_in)
            eye = jnp.where(lax.broadcasted_iota(jnp.int32, (width, width), 0)
                            == lax.broadcasted_iota(jnp.int32, (width, width), 1), keep, 0.0)
            inv_ref[at] = inverse
            base_ref[rows, cols] = base
            w_ref[rows, cols] = carry
            move_ref[at] = eye - product(tail, halves(carry))
            state_ref[at] = product(tail, halves(base))
        return 0

    lax.fori_loop(0, count // PER_STEP, first, 0)

    def second(index, states):
        result = []
        for head in range(heads):
            at = index * heads + head
            added = state_ref[at]
            state_ref[at] = states[head]
            result.append(product(halves(move_ref[at]), halves(states[head])) + added)
        return tuple(result)

    lax.fori_loop(0, count, second, tuple(jnp.zeros((width, width), WIDE) for _ in range(heads)))

    def third(index, _):
        rows = pl.ds(pl.multiple_of(index * CHUNK, CHUNK), CHUNK)
        carried = jnp.where(segcol_ref[rows, :] == edges_ref[index, 0], 1.0, 0.0).astype(WIDE)
        for head in range(heads):
            cols = pl.ds(head * width, width)
            at = index * heads + head
            state = halves(state_ref[at])
            update = base_ref[rows, cols] - product(halves(w_ref[rows, cols]), state)
            upd_ref[rows, cols] = update
            out = carried * product(halves(q_ref[rows, cols]), state)
            out = out + product(halves(score_ref[at]), halves(update))
            mixed = out.astype(NARROW)
            out_ref[rows, cols] = mixed
            mixed = mixed.astype(WIDE)
            scale = lax.rsqrt(jnp.mean(mixed * mixed, axis=-1, keepdims=True) + norm_eps)
            gate = raw_ref[rows, pl.ds(3 * span + head * width, width)]
            normed = mixed * scale * gain_ref[...] * (gate * jax.nn.sigmoid(gate))
            normed_ref[rows, cols] = normed.astype(NARROW)
        return 0

    lax.fori_loop(0, count, third, 0)
    for k, block in enumerate(blocks):
        block[...] = unpack_rows(far_ref[...], normed_ref[...], k, total // n_fs)


def backward_kernel(heads, width, n_fs, shard_rows, *refs):
    pieces, refs = refs[:n_fs], refs[n_fs:]
    (win_ref, near_ref, far_ref, segcol_ref, poscol_ref, segrow_ref, edges_ref, z_ref, dgffn_ref,
     side_ref, hidden_ref, raw_ref, mixed_ref, q_ref, k_ref, inv_ref, score_ref, dots_ref, upd_ref, state_ref,
     move_ref, gradin_ref, *refs) = refs
    blocks, refs = refs[:n_fs], refs[n_fs:]
    (taps_ref, gain_ref, draw_ref, dhid_ref, dtaps_ref, sum_ref, small_ref, pad_ref, grad_ref, pdo_ref, dconv_ref, dout_ref, dnormed_ref) = refs
    total = raw_ref.shape[0]

    spread_side(heads, width, shard_rows, z_ref, side_ref, taps_ref, gain_ref)

    def enter(index, _):
        rows = pl.ds(pl.multiple_of(index * ENTER, ENTER), ENTER)
        dnormed_ref[rows, :] = pack_rows(near_ref[rows, :], pieces).astype(NARROW)
        return 0

    lax.fori_loop(0, total // ENTER, enter, 0)
    count = total // CHUNK
    span = heads * width
    fill_padded(raw_ref, pad_ref, 3 * span)

    def first(group, dgain):
        for sub in range(BACK_STEP):
            index = group * BACK_STEP + sub
            rows = pl.ds(pl.multiple_of(index * CHUNK, CHUNK), CHUNK)
            carried = jnp.where(segcol_ref[rows, :] == edges_ref[index, 0], 1.0, 0.0).astype(WIDE)
            for head in range(heads):
                cols = pl.ds(head * width, width)
                at = index * heads + head
                mixed = mixed_ref[rows, cols].astype(WIDE)
                scale = lax.rsqrt(jnp.mean(mixed * mixed, axis=-1, keepdims=True) + norm_eps)
                gate_cols = pl.ds(3 * span + head * width, width)
                gate = raw_ref[rows, gate_cols]
                sig = jax.nn.sigmoid(gate)
                given = dnormed_ref[rows, cols].astype(WIDE)
                unit = mixed * scale
                dgate = given * unit * gain_ref[...] * (sig * (1.0 + gate * (1.0 - sig)))
                draw_ref[rows, gate_cols] = dgate.astype(NARROW)
                given = given * (gate * sig)
                dgain = dgain + jnp.sum(given * unit, axis=0, keepdims=True)
                given = given * gain_ref[...]
                dout = scale * (given - unit * jnp.mean(unit * given, axis=-1, keepdims=True))
                dout = dout.astype(NARROW)
                dout_ref[rows, cols] = dout
                score_t = turned(score_ref[at])
                back = product_exact(score_t, dout)
                pdo_ref[rows, cols] = back
                inv_t = turned(inv_ref[at])
                back = product(inv_t, halves(back))
                query_t = turned(carried * q_ref[rows, cols])
                key_t = turned((beta_of(raw_ref, rows, 4 * span + head) * carried) * k_ref[rows, cols])
                grad_ref[at] = product_exact(query_t, dout) - product(key_t, halves(back))
        return dgain

    dgain = lax.fori_loop(0, count // BACK_STEP, first, jnp.zeros((1, width), WIDE))

    def second(step, grads):
        index = count - 1 - step
        result = []
        for head in range(heads):
            at = index * heads + head
            added = grad_ref[at]
            grad_ref[at] = grads[head]
            result.append(product(turned(move_ref[at]), halves(grads[head])) + added)
        return tuple(result)

    lax.fori_loop(0, count, second, tuple(jnp.zeros((width, width), WIDE) for _ in range(heads)))
    dconv_ref[total:total + HALO, :] = jnp.zeros((HALO, 3 * span), WIDE)

    def third(group, tap_sums):
        for sub in range(BACK_STEP):
            index = group * BACK_STEP + sub
            start = pl.multiple_of(index * CHUNK, CHUNK)
            rows = pl.ds(start, CHUNK)
            pos = poscol_ref[rows, :]
            strict, inclusive, carried, last = chunk_masks(
                segcol_ref[rows, :], segrow_ref[pl.ds(index, 1), :], edges_ref[index, 0], edges_ref[index, 1])
            new_sums = []
            dbetas = []
            for head in range(heads):
                cols = pl.ds(head * width, width)
                at = index * heads + head
                beta = beta_of(raw_ref, rows, 4 * span + head)
                query, key, update = q_ref[rows, cols], k_ref[rows, cols], upd_ref[rows, cols]
                query_h, key_h, update_h = halves(query), halves(key), halves(update)
                dout = dout_ref[rows, cols]
                state, grad = halves(state_ref[at]), halves(grad_ref[at])
                convs = []
                for which in range(3):
                    column = which * span + head * width
                    convs.append(conv_rows(pad_ref, taps_ref[which, :, head * width:(head + 1) * width], pos,
                                           start, column, width))
                gates = [jax.nn.sigmoid(c[0]) for c in convs]
                value = convs[2][0] * gates[2]
                dupdate = pdo_ref[rows, cols] + last * product(key_h, grad)
                dright = product(turned(inv_ref[at]), halves(dupdate))
                dright_h = halves(dright)
                dscore = jnp.where(inclusive, product_exact(update_h, dout, 1, 1, flip=True), 0.0)
                dsystem = jnp.where(strict, product(dright_h, update_h, 1, 1), 0.0)
                dscore_h = halves(dscore)
                dquery = carried * product_exact(state, dout, 1, 1, flip=True) + product(dscore_h, key_h)
                weighted = beta * dsystem
                scaled = beta * carried
                dkey = product(turned(dscore), query_h) + last * product(update_h, grad, 1, 1)
                dkey = dkey - product(halves(weighted + weighted.T), key_h)
                dkey = dkey - scaled * product(dright_h, state, 1, 1)
                dvalue = beta * dright
                seen = carried * product(key_h, state)
                dbeta = jnp.sum(dright * (value - seen), axis=-1, keepdims=True) - jnp.sum(
                    dsystem * dots_ref[at], axis=-1, keepdims=True)
                dbetas.append(dbeta * beta * (1.0 - beta))
                sides = []
                for grads, unit, conv, gate in ((dquery, query, convs[0][0], gates[0]), (dkey, key, convs[1][0], gates[1])):
                    plain = conv * gate
                    inv_norm = lax.rsqrt(jnp.sum(plain * plain, axis=-1, keepdims=True) + unit_eps)
                    sides.append(inv_norm * (grads - unit * jnp.sum(unit * grads, axis=-1, keepdims=True)))
                sides.append(dvalue)
                for which in range(3):
                    conv, plain, moved = convs[which]
                    gate = gates[which]
                    dconv = sides[which] * gate * (1.0 + conv * (1.0 - gate))
                    column = which * span + head * width
                    dconv_ref[rows, pl.ds(column, width)] = dconv
                    sums = [jnp.sum(dconv * plain, axis=0, keepdims=True)]
                    for shifted in moved:
                        sums.append(jnp.sum(dconv * shifted, axis=0, keepdims=True))
                    new_sums.append(jnp.concatenate(sums[::-1], axis=0))
            lane = lax.broadcasted_iota(jnp.int32, (CHUNK, draw_ref.shape[1] - 4 * span), 1)
            packed = jnp.zeros(lane.shape, WIDE)
            for head in range(heads):
                packed = jnp.where(lane == head, dbetas[head], packed)
            draw_ref[rows, pl.ds(4 * span, lane.shape[1])] = packed.astype(draw_ref.dtype)
            tap_sums = tuple(old + new for old, new in zip(tap_sums, new_sums))
        return tap_sums

    zero = tuple(jnp.zeros((taps_ref.shape[1], width), WIDE) for _ in range(3 * heads))
    sums = lax.fori_loop(0, count // BACK_STEP, third, zero)
    for head in range(heads):
        for which in range(3):
            dtaps_ref[which, :, head * width:(head + 1) * width] = sums[head * 3 + which]
    taps_count = taps_ref.shape[1]

    def fourth(index, _):
        start = pl.multiple_of(index * CHUNK, CHUNK)
        pos_window = poscol_ref[pl.ds(start, CHUNK + HALO), :]
        for which in range(3):
            columns = pl.ds(which * span, span)
            window = dconv_ref[pl.ds(start, CHUNK + HALO), columns]
            result = taps_ref[which, taps_count - 1:taps_count, :] * window[0:CHUNK]
            for offset in range(1, taps_count):
                part = jnp.where(pos_window >= offset, window, 0.0)[offset:offset + CHUNK]
                result = result + taps_ref[which, taps_count - 1 - offset:taps_count - offset, :] * part
            draw_ref[pl.ds(start, CHUNK), columns] = result.astype(draw_ref.dtype)
        return 0

    lax.fori_loop(0, count, fourth, 0)

    def weigh(index, _):
        rows = pl.ds(pl.multiple_of(index * ENTER, ENTER), ENTER)
        sum_ref[...] += plain_dot(hidden_ref[rows, :], draw_ref[rows, :], 0, 0)
        return 0

    sum_ref[...] = jnp.zeros(sum_ref.shape, WIDE)
    lax.fori_loop(0, total // ENTER, weigh, 0)
    features = small_ref.shape[1]
    small_ref[...] = jnp.zeros(small_ref.shape, WIDE)
    small_ref[heads + 1:heads + 2, :] = dgffn_ref[...]
    own = pl.ds(pl.multiple_of(z_ref[0] * span, span), span)
    for which in range(3):
        first_row = heads + 2 + which * taps_count
        small_ref[first_row:first_row + taps_count, own] = dtaps_ref[which]
    last_row = heads + 2 + 3 * taps_count
    small_ref[last_row:last_row + 1, :] = product_exact(
        halves(jnp.broadcast_to(dgain, (8, width))), shard_places(width, features, shard_rows, False))[0:1]
    gain = win_ref[:, 4 * span + heads:4 * span + heads + 1].astype(WIDE)
    across = jnp.sum(sum_ref[...] * win_ref[...].astype(WIDE), axis=-1, keepdims=True) / gain
    beside = small_ref[...].T
    lane = lax.broadcasted_iota(jnp.int32, beside.shape, 1)
    gradin_ref[:, 0:4 * span] = sum_ref[:, 0:4 * span].astype(NARROW)
    beside = sum_ref[:, 4 * span:] + beside + jnp.where(lane == heads, across, 0.0)
    gradin_ref[:, 4 * span:] = beside.astype(NARROW)

    def leave(index, _):
        rows = pl.ds(pl.multiple_of(index * ENTER, ENTER), ENTER)
        dhid_ref[rows, :] = plain_dot(draw_ref[rows, :], win_ref[...], 1, 1).astype(NARROW)
        return 0

    lax.fori_loop(0, total // ENTER, leave, 0)
    for k, block in enumerate(blocks):
        block[...] = unpack_rows(far_ref[...], dhid_ref[...], k, total // n_fs)


def product_exact(left, exact, left_dim=1, right_dim=0, flip=False):
    def one(a):
        if flip:
            return lax.dot_general(exact, a, (((right_dim,), (left_dim,)), ((), ())), preferred_element_type=WIDE)
        return lax.dot_general(a, exact, (((left_dim,), (right_dim,)), ((), ())), preferred_element_type=WIDE)

    if PASSES == 1:
        return one(left[0])
    return one(left[0]) + one(left[1])


def cost(flops, size):
    return pl.CostEstimate(flops=flops, bytes_accessed=size, transcendentals=0)


def specs(count):
    return [pl.BlockSpec(memory_space=pltpu.VMEM)] * count


def anywhere():
    return pl.BlockSpec(memory_space=pl.ANY)


def in_scalars():
    return pl.BlockSpec(memory_space=pltpu.SMEM)


def delta_forward(pieces, w_in, near, far, segcol, poscol, segrow, edges, z, heads, width, n_taps, shard_rows):
    n_fs = len(pieces)
    total = near.shape[0]
    features, lanes = w_in.shape
    count = total // CHUNK
    span = heads * width
    thin = jax.ShapeDtypeStruct((total, span), NARROW)
    rows = jax.ShapeDtypeStruct((total, span), WIDE)
    full = jax.ShapeDtypeStruct((total, features), NARROW)
    square = jax.ShapeDtypeStruct((count * heads, CHUNK, CHUNK), WIDE)
    state = jax.ShapeDtypeStruct((count * heads, width, width), WIDE)
    block = jax.ShapeDtypeStruct((total // n_fs, span), NARROW)
    raw = jax.ShapeDtypeStruct((total, lanes), WIDE)
    side = jax.ShapeDtypeStruct((lanes - 4 * span, features), WIDE)
    result = pl.pallas_call(
        functools.partial(forward_kernel, heads, width, n_fs, shard_rows),
        out_shape=(block,) * n_fs
        + (side, full, raw, thin, rows, rows, square, square, square, rows, state, state),
        in_specs=specs(n_fs + 6) + [in_scalars()] * 2,
        out_specs=tuple(specs(n_fs + 12)),
        scratch_shapes=[
            pltpu.VMEM((3, n_taps, span), WIDE),
            pltpu.VMEM((1, width), WIDE),
            pltpu.VMEM((total + HALO, 3 * span), WIDE),
            pltpu.VMEM((total, span), WIDE),
            pltpu.VMEM((total, span), WIDE),
            pltpu.VMEM((total, span), NARROW),
        ],
        compiler_params=pltpu.CompilerParams(vmem_limit_bytes=60 << 20),
        cost_estimate=cost(30_000_000_000, 16 << 20),
        name="delta_forward",
    )(*pieces, w_in, near, far, segcol, poscol, segrow, edges, z)
    return result[:n_fs], result[n_fs], result[n_fs + 1 :]


def delta_backward(pieces, w_in, near, far, segcol, poscol, segrow, edges, z, dgffn, side, kept, heads, width, n_taps, shard_rows):
    n_fs = len(pieces)
    total = near.shape[0]
    features, lanes = w_in.shape
    count = total // CHUNK
    span = heads * width
    block = jax.ShapeDtypeStruct((total // n_fs, features), NARROW)
    result = pl.pallas_call(
        functools.partial(backward_kernel, heads, width, n_fs, shard_rows),
        out_shape=(jax.ShapeDtypeStruct((features, lanes), NARROW),) + (block,) * n_fs,
        in_specs=specs(n_fs + 6) + [in_scalars()] * 2 + specs(13),
        out_specs=tuple(specs(n_fs + 1)),
        scratch_shapes=[
            pltpu.VMEM((3, n_taps, span), WIDE),
            pltpu.VMEM((1, width), WIDE),
            pltpu.VMEM((total, lanes), NARROW),
            pltpu.VMEM((total, features), NARROW),
            pltpu.VMEM((3, n_taps, span), WIDE),
            pltpu.VMEM((features, lanes), WIDE),
            pltpu.VMEM((lanes - 4 * span, features), WIDE),
            pltpu.VMEM((total + HALO, 3 * span), WIDE),
            pltpu.VMEM((count * heads, width, width), WIDE),
            pltpu.VMEM((total, span), WIDE),
            pltpu.VMEM((total + HALO, 3 * span), WIDE),
            pltpu.VMEM((total, span), NARROW),
            pltpu.VMEM((total, span), NARROW),
        ],
        compiler_params=pltpu.CompilerParams(vmem_limit_bytes=52 << 20),
        cost_estimate=cost(40_000_000_000, 16 << 20),
        name="delta_backward",
    )(*pieces, w_in, near, far, segcol, poscol, segrow, edges, z, dgffn, side, *kept)
    return result[0], list(result[1:])


def finish_kernel(heads, span, n_taps, z_ref, *refs):
    n_fs = len(refs) - 10
    pieces, refs = refs[:n_fs], refs[n_fs:]
    (*grads, wout_ref, beta_ref, taps_ref, gmix_ref, gffn_ref, ghead_ref) = refs
    side = pl.ds(4 * span, 128)
    lane = lax.broadcasted_iota(jnp.int32, (128, beta_ref.shape[0]), 0)
    column = lax.broadcasted_iota(jnp.int32, (128, beta_ref.shape[0]), 1)
    wout = jnp.zeros(wout_ref.shape, WIDE)
    small = jnp.zeros((wout_ref.shape[0], 128), WIDE)
    beta = jnp.zeros(beta_ref.shape, WIDE)
    for k, piece in enumerate(pieces):
        line = lax.rem(z_ref[0] + n_fs - k, n_fs)
        place = pl.ds(pl.multiple_of(line * span, span), span)
        for which, grad in enumerate(grads):
            grad[:, place] = piece[:, which * span:(which + 1) * span].astype(WIDE)
        wout = wout + piece[:, 4 * span + 128:].astype(WIDE)
        beside = piece[:, side]
        small = small + beside.astype(WIDE)
        chosen = jnp.where((lane < heads) & (column == line * heads + lane), 1.0, 0.0)
        beta = beta + plain_dot(chosen.astype(NARROW), beside, 0, 1)
    wout_ref[...] = wout
    beta_ref[...] = beta
    small = small.T
    gmix_ref[...] = small[heads:heads + 1]
    gffn_ref[...] = small[heads + 1:heads + 2]
    last_row = heads + 2 + 3 * n_taps
    for which in range(3):
        first_row = heads + 2 + which * n_taps
        taps_ref[which] = small[first_row:first_row + n_taps]
    ghead_ref[...] = small[last_row:last_row + 1, :ghead_ref.shape[1]]


def finish(z, pieces, heads, span, n_taps, head_rows):
    rows = pieces[0].shape[0]
    n_fs = len(pieces)
    full = jax.ShapeDtypeStruct((rows, n_fs * span), WIDE)
    line = jax.ShapeDtypeStruct((1, rows), WIDE)
    return pl.pallas_call(
        functools.partial(finish_kernel, heads, span, n_taps),
        out_shape=(full,) * 5
        + (
            jax.ShapeDtypeStruct((n_fs * heads, rows), WIDE),
            jax.ShapeDtypeStruct((3, n_taps, rows), WIDE),
            line,
            line,
            jax.ShapeDtypeStruct((1, head_rows), WIDE),
        ),
        in_specs=[in_scalars()] + specs(n_fs),
        out_specs=tuple(specs(10)),
        cost_estimate=cost(1_000_000, 1 << 20),
        name="finish_inputs",
    )(z, *pieces)


def mix_out_kernel(n_fs, row, z_ref, *refs):
    pieces, refs = refs[:n_fs], refs[n_fs:]
    wout_ref, tokens_ref, gain_ref, middle_ref, ffn_ref, normed_ref = refs
    span = pieces[0].shape[1]
    middle = tokens_ref[...].astype(WIDE)
    for k, piece in enumerate(pieces):
        place = pl.ds(pl.multiple_of(lax.rem(z_ref[0] + n_fs - k, n_fs) * span, span), span)
        normed_ref[:, place] = piece[...]
        middle = middle + plain_dot(piece[...], wout_ref[place, :])
    middle_ref[...] = middle
    scale = lax.rsqrt(jnp.mean(middle * middle, axis=-1, keepdims=True) + norm_eps)
    ffn_ref[...] = (middle * scale * gain_ref[row:row + 1, :]).astype(NARROW)


def mix_out(z, pieces, w_out, tokens, side, row):
    n_fs = len(pieces)
    shape = tokens.shape
    return pl.pallas_call(
        functools.partial(mix_out_kernel, n_fs, row),
        out_shape=(
            jax.ShapeDtypeStruct(shape, WIDE),
            jax.ShapeDtypeStruct(shape, NARROW),
            jax.ShapeDtypeStruct(shape, NARROW),
        ),
        in_specs=[in_scalars()] + specs(n_fs + 3),
        out_specs=tuple(specs(3)),
        compiler_params=pltpu.CompilerParams(vmem_limit_bytes=40 << 20),
        cost_estimate=cost(2_000_000_000, 6 << 20),
        name="mix_out",
    )(z, *pieces, w_out, tokens, side)


def ffn_kernel(keys, unit, block_ref, *refs):
    count = TP
    rows_in, refs = refs[:count], refs[count:]
    cots, refs = refs[:count], refs[count:]
    weights, refs = refs[:len(keys)], refs[len(keys):]
    (wdown_ref, active_ref, dboth_ref, sent_ref, later_ref, own_ref, part_ref, *ordered) = refs
    own_rows = rows_in[0].shape[0]
    if ordered:
        for near, far in zip(weights, ordered):
            n_fs, size = near.shape[:2]
            for by in range(n_fs):
                line = lax.rem(block_ref[1] + n_fs - by, n_fs)
                for at in range(size // unit):
                    place = pl.ds(pl.multiple_of((at * n_fs + line) * unit, unit), unit)
                    far[place, :] = near[by, at * unit:(at + 1) * unit, :]
        weights = ordered
    depth = weights[0].shape[0]
    units = wdown_ref.shape[0]
    spots = [pl.ds(pl.multiple_of((block_ref[0] ^ key) * depth, depth), depth) for key in keys]
    half = count // 2 * own_rows
    for at in range(count - 1, -1, -1):
        rows = slice(at * own_rows, (at + 1) * own_rows)
        both = plain_dot(rows_in[at][:, spots[0]], weights[0][...])
        for spot, weight in zip(spots[1:], weights[1:]):
            both = both + plain_dot(rows_in[at][:, spot], weight[...])
        gate, up = both[:, :units], both[:, units:]
        sig = jax.nn.sigmoid(gate)
        silu = gate * sig
        active_ref[rows, :] = (silu * up).astype(NARROW)
        dactive = plain_dot(cots[at][...], wdown_ref[...], 1, 1)
        dboth_ref[rows, :units] = (dactive * up * (sig * (1.0 + gate * (1.0 - sig)))).astype(NARROW)
        dboth_ref[rows, units:] = (dactive * silu).astype(NARROW)
        dboth = dboth_ref[rows, :]
        for spot, weight in zip(spots, weights):
            part_ref[:, spot] = plain_dot(dboth, weight[...], 1, 1)
        if at >= count // 2:
            place = at * own_rows - half
            sent_ref[place:place + own_rows, :] = part_ref[...].astype(NARROW)
        elif at:
            later_ref[(at - 1) * own_rows:at * own_rows, :] = part_ref[...]
        else:
            own_ref[...] = part_ref[...]


def ffn_units(block, rows_in, cots, weights, keys, w_down, unit):
    own_rows, features = rows_in[0].shape
    units = w_down.shape[0]
    total = TP * own_rows
    return pl.pallas_call(
        functools.partial(ffn_kernel, keys, unit),
        out_shape=(
            jax.ShapeDtypeStruct((total, units), NARROW),
            jax.ShapeDtypeStruct((total, 2 * units), NARROW),
            jax.ShapeDtypeStruct((total // 2, features), NARROW),
            jax.ShapeDtypeStruct((total // 2 - own_rows, features), WIDE),
            jax.ShapeDtypeStruct((own_rows, features), WIDE),
        ),
        in_specs=[in_scalars()] + specs(2 * TP + len(weights) + 1),
        out_specs=tuple(specs(5)),
        scratch_shapes=[pltpu.VMEM((own_rows, features), WIDE)]
        + [pltpu.VMEM((features // len(keys), 2 * units), NARROW) for w in weights if w.ndim == 3],
        compiler_params=pltpu.CompilerParams(vmem_limit_bytes=52 << 20),
        cost_estimate=cost(8_000_000_000, 16 << 20),
        name="ffn_units",
    )(block, *rows_in, *cots, *weights, w_down)


def mix_back_kernel(n_fs, row, z_ref, *refs):
    sources, refs = refs[:6], refs[6:]
    gain_ref, refs = refs[0], refs[1:]
    blocks, refs = refs[:n_fs], refs[n_fs:]
    (dmiddle_ref, dbranch_ref, dgain_ref, *places, sems) = refs
    fetches = [pltpu.make_async_copy(source, place, sems.at[k]) for k, (source, place) in enumerate(
        zip((sources[0], sources[1].at[pl.ds(0, places[1].shape[0])], *sources[2:5]), places))]
    quarter = places[5].shape[0] // 4
    parts = [pl.ds(k * quarter, quarter) for k in range(4)]
    fetches += [
        pltpu.make_async_copy(sources[5].at[part], places[5].at[part], sems.at[5 + k]) for k, part in enumerate(parts)
    ]
    for fetch in fetches:
        fetch.start()
    own_ref, core_ref, side_ref, middle_ref, cot_ref, wout_ref = places
    for fetch in fetches[:5]:
        fetch.wait()
    middle = middle_ref[...]
    given = own_ref[...] + core_ref[...].astype(WIDE) + side_ref[...].astype(WIDE)
    scale = lax.rsqrt(jnp.mean(middle * middle, axis=-1, keepdims=True) + norm_eps)
    unit = middle * scale
    dgain_ref[...] = jnp.sum(given * unit, axis=0, keepdims=True)
    given = given * gain_ref[row:row + 1, :]
    dmiddle = cot_ref[...].astype(WIDE) + scale * (given - unit * jnp.mean(unit * given, axis=-1, keepdims=True))
    dmiddle_ref[...] = dmiddle
    dbranch = dmiddle.astype(NARROW)
    dbranch_ref[...] = dbranch
    span = blocks[0].shape[1]
    for fetch in fetches[5:]:
        fetch.wait()
    for k, block in enumerate(blocks):
        place = pl.ds(pl.multiple_of(lax.rem(z_ref[0] + k, n_fs) * span, span), span)
        block[...] = plain_dot(dbranch, wout_ref[place, :], 1, 1).astype(NARROW)


def mix_back(z, parts, middle, side, row, cotangent, w_out, n_fs):
    count, features = middle.shape
    block = jax.ShapeDtypeStruct((count, features // n_fs), NARROW)
    sources = (*parts, middle, cotangent, w_out)
    result = pl.pallas_call(
        functools.partial(mix_back_kernel, n_fs, row),
        out_shape=(block,) * n_fs
        + (
            jax.ShapeDtypeStruct(middle.shape, WIDE),
            jax.ShapeDtypeStruct(middle.shape, NARROW),
            jax.ShapeDtypeStruct((1, features), WIDE),
        ),
        in_specs=[in_scalars()] + [anywhere()] * 6 + specs(1),
        out_specs=tuple(specs(n_fs + 3)),
        scratch_shapes=[pltpu.VMEM((min(part.shape[0], count) if k < 5 else part.shape[0], features), part.dtype) for k, part in enumerate(sources)] + [pltpu.SemaphoreType.DMA((9,))],
        compiler_params=pltpu.CompilerParams(vmem_limit_bytes=60 << 20),
        cost_estimate=cost(2_000_000_000, 6 << 20),
        name="mix_back",
    )(z, *sources, side)
    return (result[:n_fs],) + tuple(result[n_fs:])


def rms_scale(values, gain):
    return values * lax.rsqrt(jnp.mean(values * values, axis=-1, keepdims=True) + norm_eps) * gain


def swiglu(gate_proj, up_proj):
    return jax.nn.silu(gate_proj) * up_proj


def sequence_layout(lengths_row, total):
    ends = jnp.cumsum(lengths_row)
    index = jnp.arange(total, dtype=jnp.int32)
    before = index[:, None] >= ends[None, :]
    segment = jnp.sum(before.astype(jnp.int32), axis=1)
    start = jnp.sum(jnp.where(before, lengths_row[None, :], 0), axis=1)
    return (segment, index - start)


def project(left, right):
    return jnp.dot(left, right, preferred_element_type=WIDE)


def project_back(left, right):
    return lax.dot_general(left, right, (((1,), (1,)), ((), ())), preferred_element_type=WIDE)


def weight_grad(left, right):
    return lax.dot_general(left, right, (((0,), (0,)), ((), ())), preferred_element_type=WIDE)


def flip(value, bit, n_dp):
    return lax.ppermute(value, "dp", [(i, i ^ bit) for i in range(n_dp)])


def shift(value, by, n_fs):
    return lax.ppermute(value, "fsdp", [(i, (i + by) % n_fs) for i in range(n_fs)])


def line_pieces(shard, n_fs):
    return [shard] + [shift(shard, by, n_fs) for by in range(1, n_fs)]


def line_order(pieces, z):
    n_fs = len(pieces)
    shape = pieces[0].shape
    whole = jnp.zeros((shape[0], n_fs) + shape[1:], pieces[0].dtype)
    for by, piece in enumerate(pieces):
        whole = lax.dynamic_update_slice_in_dim(whole, piece[:, None], lax.rem(z + n_fs - by, n_fs), 1)
    return whole


def gather_cube(piece, order, n_dp):
    pieces = {0: piece}
    for bit in order:
        for key in list(pieces):
            pieces[key ^ bit] = flip(pieces[key], bit, n_dp)
    return pieces


def in_order(pieces, me):
    rows = pieces[0].shape[0]
    whole = jnp.zeros((len(pieces) * rows,) + pieces[0].shape[1:], pieces[0].dtype)
    unit = max(pieces).bit_length()
    step = (1 << unit) // len(pieces)
    for key, piece in pieces.items():
        whole = lax.dynamic_update_slice_in_dim(whole, piece, lax.bitwise_xor(me, key // step) * rows, 0)
    return whole


def per_device(
    n_dp,
    n_fs,
    tokens,
    lengths,
    packing,
    w_query,
    w_key,
    w_value,
    w_gate,
    w_beta,
    conv_taps,
    w_out,
    gain_mix,
    gain_head,
    gain_ffn,
    w_ffn_gate,
    w_ffn_up,
    w_ffn_down,
    cotangent,
):
    me = lax.axis_index("dp")
    z = lax.axis_index("fsdp")
    bits = [1 << k for k in range(n_dp.bit_length() - 1)]
    first_order = bits[:1] + bits[1:]
    second_order = bits[:1] + bits[1:][::-1]
    packing_row = packing[0]
    lengths_row = lengths[0]
    own_rows, features = tokens.shape
    total = own_rows * n_fs
    rows = w_query.shape[0]
    heads_all = w_beta.shape[1]
    heads = heads_all // n_fs
    span = features // n_fs
    width = span // heads
    hidden_ffn = w_ffn_gate.shape[1]
    head_rows = gain_head.shape[0]
    n_taps = conv_taps.shape[1]

    def by_owner(matrix):
        return jnp.swapaxes(matrix.reshape(rows, n_fs, -1), 0, 1)

    small = jnp.concatenate(
        [
            gain_mix[:, None],
            gain_ffn[:, None],
            conv_taps.reshape(3 * n_taps, rows).T,
            jnp.pad(gain_head, (0, rows - head_rows))[:, None],
        ],
        axis=1,
    )
    n_small = small.shape[1]
    side = jnp.concatenate(
        [by_owner(w_beta), jnp.broadcast_to(small[None], (n_fs, rows, n_small))], axis=2
    )
    side = jnp.pad(side, ((0, 0), (0, 0), (0, 128 - heads - n_small)))
    packet = jnp.concatenate(
        [by_owner(w_query), by_owner(w_key), by_owner(w_value), by_owner(w_gate), side], axis=2
    )
    member = lax.rem(me, TP)
    block = me // TP
    n_rest = n_dp // TP
    ff_block = hidden_ffn // n_dp
    ff_line = ff_block // n_fs
    ff_unit = -(-ff_line // 8) * 8
    while n_rest * n_fs * ff_unit % 128:
        ff_unit += 8
    ff_pad = n_rest * n_fs * ff_unit
    tp_bits = [bit for bit in bits if bit < TP]
    rest_bits = [bit for bit in bits if bit >= TP]

    def by_member(matrix):
        split = matrix.reshape(rows, n_rest, TP, n_fs, ff_line)
        split = jnp.pad(split, ((0, 0),) * 4 + ((0, ff_unit - ff_line),))
        return jnp.transpose(split, (2, 0, 1, 3, 4)).reshape(TP, rows, ff_pad)

    def hand_out(blocks):
        pieces = [lax.dynamic_index_in_dim(blocks, z, 0)]
        for by in range(1, n_fs):
            pieces.append(shift(lax.dynamic_index_in_dim(blocks, lax.rem(z + by, n_fs), 0), by, n_fs))
        return pieces

    lanes = 4 * span + 128
    packet = jnp.concatenate([packet, jnp.broadcast_to(w_out[None], (n_fs,) + w_out.shape)], axis=2)
    packet = hand_out(packet)
    token_pieces = [tokens] + [shift(tokens, by, n_fs) for by in range(1, n_fs)]
    packet, token_pieces[1] = lax.optimization_barrier((packet, token_pieces[1]))
    packet_in = line_order([piece[:, :, :lanes] for piece in packet], z).reshape(n_fs * rows, lanes)
    packet_out = line_order([piece[:, :, lanes:] for piece in packet], z).reshape(n_fs * rows, features)
    w_in = lax.all_gather(packet_in, "dp", axis=0, tiled=True)
    full_out = lax.all_gather(packet_out, "dp", axis=0, tiled=True)

    owner, place = packing_row // own_rows, lax.rem(packing_row, own_rows)
    near = (lax.rem(z + n_fs - owner, n_fs) * own_rows + place)[:, None]
    far = (lax.rem(owner + n_fs - z, n_fs) * own_rows + place)[None]
    segment, position = sequence_layout(lengths_row, total)
    seg_rows = segment.reshape(-1, CHUNK)
    ends = seg_rows[:, -1]
    edges = jnp.stack([jnp.concatenate([jnp.full((1,), -1, jnp.int32), ends[:-1]]), ends], axis=1)
    z_ref = z.reshape(1)
    layout = (segment[:, None], jnp.pad(position, (0, HALO))[:, None], seg_rows, edges, z_ref)
    shard_rows = (rows, head_rows)
    own_gate, own_up, _ = lax.optimization_barrier((w_ffn_gate, w_ffn_up, token_pieces[1]))
    both_sends = jnp.concatenate([by_member(own_gate), by_member(own_up)], axis=2)
    blocks, side, kept = delta_forward(
        token_pieces, w_in, near, far, *layout, heads, width, n_taps, shard_rows
    )
    gain_row = heads + 1

    both_pieces = {
        key: flip(lax.dynamic_index_in_dim(both_sends, member ^ key, 0, keepdims=False), key, n_dp)
        if key
        else lax.dynamic_index_in_dim(both_sends, member, 0, keepdims=False)
        for key in range(TP)
    }
    own_down, _ = lax.optimization_barrier((w_ffn_down, token_pieces[1]))
    own_down = jnp.pad(own_down, ((0, ff_unit - ff_line), (0, 0)))
    down_rows = in_order(gather_cube(own_down, rest_bits, n_dp), block).reshape(n_rest, -1, features)
    both_rows = in_order(both_pieces, member).reshape(TP, rows, 2 * ff_pad)
    own_cotangent, both_rows, down_rows = lax.optimization_barrier((cotangent, both_rows, down_rows))
    both_rows, down_rows, _ = lax.optimization_barrier((both_rows, down_rows, token_pieces))
    both_line = line_pieces(both_rows, n_fs)
    both_line, blocks, down_rows = lax.optimization_barrier((both_line, blocks, down_rows))
    if rows % 16 == 0:
        both_rows = jnp.stack([piece.reshape(TP * rows, 2 * ff_pad) for piece in both_line])
    else:
        both_rows = line_order(both_line, z).reshape(-1, 2 * ff_pad)
    both_pieces = gather_cube(both_rows, rest_bits, n_dp)
    unit = 1 << (TP.bit_length() - 1)
    rest_keys = [key // unit for key in both_pieces]
    tp_order = sorted(range(TP), key=lambda key: tuple((key & bit) != 0 for bit in tp_bits))

    cot_pieces = gather_cube(own_cotangent, tp_bits[::-1], n_dp)
    cot_pieces, blocks = lax.optimization_barrier((cot_pieces, blocks))

    def collect(left, right, dims):
        arrived = []
        keep = TP

        def term(lo, hi):
            value = lax.dot_general(
                left[lo * own_rows : hi * own_rows], right, (dims, ((), ())), preferred_element_type=WIDE
            )
            for earlier in arrived:
                value = value + earlier[lo * own_rows : hi * own_rows].astype(WIDE)
            return value

        for bit in tp_bits:
            keep //= 2
            sent = yield term(keep, 2 * keep).astype(NARROW)
            arrived.append(flip(sent, bit, n_dp))
        yield term(0, 1)

    def halve(value, index, some_bits):
        unit = some_bits[0] if some_bits else 1
        for bit in some_bits[::-1]:
            half = value.shape[0] // 2
            mine = (index // (bit // unit)) % 2
            sent = lax.dynamic_slice_in_dim(value, (1 - mine) * half, half, 0)
            value = lax.dynamic_slice_in_dim(value, mine * half, half, 0)
            value = value.astype(WIDE) + flip(sent.astype(NARROW), bit, n_dp).astype(WIDE)
        return value

    def sum_up(pieces, whole):
        total = lax.dynamic_index_in_dim(whole, z, 0, keepdims=False).astype(WIDE)
        for piece in pieces[1:]:
            total = total + piece[0].astype(WIDE)
        return total

    def pass_on(parts):
        return [parts[0]] + [shift(part, by, n_fs) for by, part in enumerate(parts) if by]

    mixed_pieces = pass_on(blocks)
    down_line = line_pieces(down_rows, n_fs)
    middle, ffn_in, normed_b = mix_out(z_ref, mixed_pieces, full_out, tokens, side, gain_row)
    w_down = line_order(down_line, z).reshape(ff_pad, features)
    ffn_pieces = gather_cube(ffn_in, tp_bits[::-1], n_dp)
    active_b, d_both, first, second, d_own = ffn_units(
        jnp.stack([block, z]),
        [ffn_pieces[key] for key in tp_order],
        [cot_pieces[key] for key in tp_order],
        list(both_pieces.values()),
        rest_keys,
        w_down,
        rows,
    )
    ffn_near = jnp.concatenate([ffn_pieces[key] for key in tp_order], axis=0)

    def both_part(lo, size):
        part = weight_grad(lax.dynamic_slice_in_dim(ffn_near, lo, size, 1), d_both)
        return part.reshape(-1, n_fs * rows, 2 * ff_pad)

    cotangent_near = jnp.concatenate([cot_pieces[key] for key in tp_order], axis=0)
    down_terms = weight_grad(active_b, cotangent_near).astype(NARROW)
    down_sum = lax.psum_scatter(
        down_terms.reshape(n_rest, -1, features), "fsdp", scatter_dimension=1, tiled=True
    )
    d_both, down_terms = lax.optimization_barrier((d_both, down_terms))
    split = features // 2 if rest_bits else features
    top = block // max(n_rest // 2, 1)
    if rest_bits:
        both_sent = both_part((1 - top) * split, split).astype(NARROW)
    else:
        both_sent = None
    from_core = flip(first, tp_bits[0], n_dp)
    second = second + from_core[own_rows:].astype(WIDE)
    second, both_sent, active_late = lax.optimization_barrier((second.astype(NARROW), both_sent, active_b))
    from_side = flip(second, tp_bits[1], n_dp)
    from_side, ffn_near, active_late = lax.optimization_barrier((from_side, ffn_near, active_late))
    both_sum = both_part(top * split if rest_bits else 0, split)
    if rest_bits:
        both_sum = both_sum + flip(both_sent, rest_bits[-1], n_dp).astype(WIDE)
        both_sum = halve(both_sum, block, rest_bits[:-1])

    d_blocks, d_middle, d_branch, d_gffn = mix_back(
        z_ref, (d_own, from_core, from_side), middle, side, gain_row, cotangent, full_out, n_fs
    )
    d_pieces = pass_on(d_blocks)
    out_grad = weight_grad(normed_b, d_branch).astype(NARROW)
    sum_out = lax.psum_scatter(out_grad, "dp", scatter_dimension=0, tiled=True)
    both_sum = jnp.swapaxes(both_sum.reshape(TP, n_fs, rows, 2 * ff_pad), 0, 1)
    both_sum, d_pieces, out_grad = lax.optimization_barrier((both_sum, d_pieces, out_grad))
    both_line = hand_out(both_sum.astype(NARROW))

    grad_in, d_blocks = delta_backward(
        d_pieces, w_in, near, far, *layout, d_gffn, side, kept, heads, width, n_taps, shard_rows
    )
    grad_in, both_line, down_sum, sum_out = lax.optimization_barrier((grad_in, both_line, down_sum, sum_out))
    part = lax.psum_scatter(grad_in, "dp", scatter_dimension=0, tiled=True)
    d_blocks, both_line, active_late = lax.optimization_barrier((d_blocks, both_line, active_late))
    d_blocks = pass_on(d_blocks)
    out_terms = collect(active_late, w_down, ((1,), (0,)))
    layer_out = (middle + out_terms.send(out_terms.send(next(out_terms)))).astype(NARROW)
    both_sum = sum_up(both_line, both_sum)
    grad_fdown = halve(down_sum, block, rest_bits)[0, :ff_line].astype(WIDE)
    both_pieces = {
        key: flip(
            lax.dynamic_index_in_dim(both_sum, member ^ key, 0, keepdims=False).astype(NARROW), key, n_dp
        ).astype(WIDE)
        if key
        else lax.dynamic_index_in_dim(both_sum, member, 0, keepdims=False)
        for key in range(TP)
    }
    both_mine = in_order({key: piece[None] for key, piece in both_pieces.items()}, member)
    def units_of(which):
        part = both_mine[:, :, which * ff_pad : (which + 1) * ff_pad]
        part = part.reshape(TP, rows, n_rest, n_fs, ff_unit)[..., :ff_line]
        return jnp.transpose(part, (1, 2, 0, 3, 4)).reshape(rows, hidden_ffn)

    lanes = part.shape[1]
    joint = jnp.concatenate([part, sum_out], axis=1).reshape(n_fs, rows, -1)
    arrived = [piece[0] for piece in hand_out(joint)]
    d_blocks, arrived[0], layer_out = lax.optimization_barrier((d_blocks, arrived[0], layer_out))
    d_hidden = d_blocks[0].astype(WIDE)
    for block_of in d_blocks[1:]:
        d_hidden = d_hidden + block_of.astype(WIDE)
    _, norm_mix_back = jax.vjp(rms_scale, tokens.astype(WIDE), side[heads])
    d_inputs_norm, _ = norm_mix_back(d_hidden)
    grad_tokens = d_middle + d_inputs_norm

    grads, (grad_wout, grad_beta, grad_taps, grad_gmix, grad_gffn, grad_ghead) = (
        lambda outs: (outs[:4], outs[4:])
    )(finish(z_ref, arrived, heads, span, n_taps, head_rows))
    return (
        layer_out,
        grad_tokens,
        grads[0],
        grads[1],
        grads[2],
        grads[3],
        grad_beta.T,
        grad_taps,
        grad_wout,
        grad_gmix[0],
        grad_ghead[0],
        grad_gffn[0],
        units_of(0),
        units_of(1),
        grad_fdown,
    )


def solution(mesh):
    both = ("dp", "fsdp")
    rows = P(both, None)
    group = P("dp", None)
    taps = P(None, None, both)
    line = P(both)
    in_specs = (rows, group, group) + (rows,) * 5 + (taps, rows, line, line, line) + (rows,) * 4
    out_specs = (rows,) * 7 + (taps, rows, line, line, line) + (rows,) * 3
    return jax.shard_map(
        functools.partial(per_device, mesh.shape["dp"], mesh.shape["fsdp"]),
        mesh=mesh,
        in_specs=in_specs,
        out_specs=out_specs,
        check_vma=False,
    )
```

```python
import functools

import jax
import jax.numpy as jnp
from jax import lax
from jax.experimental import pallas as pl
from jax.experimental.pallas import tpu as pltpu
from jax.sharding import PartitionSpec as P

CHUNK = 128
TP = 4
PER_STEP = 4
BACK_STEP = 2
ENTER = 256
HALO = 8
norm_eps = 1e-05
unit_eps = 1e-06
NARROW = jnp.bfloat16
WIDE = jnp.float32


def halves(value):
    top = value.astype(NARROW)
    return top, (value - top.astype(WIDE)).astype(NARROW)


def product(left, right, left_dim=1, right_dim=0):
    dims = (((left_dim,), (right_dim,)), ((), ()))

    def one(a, b):
        return lax.dot_general(a, b, dims, preferred_element_type=WIDE)

    if PASSES == 1:
        return one(left[0], right[0])
    return one(left[0], right[0]) + (one(left[0], right[1]) + one(left[1], right[0]))


PASSES = 3


def turned(value):
    return halves(value.T)


def chunk_masks(seg_col, seg_row, before, after):
    size = seg_col.shape[0]
    down = lax.broadcasted_iota(jnp.int32, (size, size), 0)
    across = lax.broadcasted_iota(jnp.int32, (size, size), 1)
    same = seg_col == seg_row
    strict = same & (down > across)
    inclusive = same & (down >= across)
    carried = jnp.where(seg_col == before, 1.0, 0.0).astype(WIDE)
    last = jnp.where(seg_col == after, 1.0, 0.0).astype(WIDE)
    return strict, inclusive, carried, last


def unit_lower_inverses(systems):
    size = systems[0].shape[0]
    down = lax.broadcasted_iota(jnp.int32, (size, size), 0)
    across = lax.broadcasted_iota(jnp.int32, (size, size), 1)
    gap = jnp.where(down > across, down ^ across, 0)
    eye = jnp.where(down == across, 1.0, 0.0)
    results = [eye - jnp.where(gap == 1, system, 0.0) for system in systems]
    step = 2
    while step < size:
        picked = (gap >= step) & (gap < 2 * step)
        parts = [jnp.where(picked, system, 0.0).astype(NARROW) for system in systems]
        done = [result.astype(NARROW) for result in results]
        inner = [plain_dot(part, own).astype(NARROW) for part, own in zip(parts, done)]
        results = [result - plain_dot(own, side) for result, own, side in zip(results, done, inner)]
        step *= 2
    left = [eye - result - product(halves(system), halves(result)) for system, result in zip(systems, results)]
    results = [
        result + plain_dot(result.astype(NARROW), rest.astype(NARROW)) for result, rest in zip(results, left)
    ]
    return results


def conv_rows(pad_ref, taps, pos, start, column, width):
    window = pad_ref[pl.ds(start, CHUNK + HALO), pl.ds(column, width)]
    count = taps.shape[0]
    result = taps[count - 1 : count] * window[HALO : HALO + CHUNK]
    moved = []
    for offset in range(1, count):
        rows = jnp.where(pos >= offset, window[HALO - offset : HALO - offset + CHUNK], 0.0)
        moved.append(rows)
        result = result + taps[count - 1 - offset : count - offset] * rows
    return result, window[HALO : HALO + CHUNK], moved


def fill_padded(raw_ref, pad_ref, width):
    pad_ref[0:HALO, :] = jnp.zeros((HALO, width), WIDE)
    total = raw_ref.shape[0]

    def copy(index, _):
        start = pl.multiple_of(index * CHUNK, CHUNK)
        pad_ref[pl.ds(start + HALO, CHUNK), :] = raw_ref[pl.ds(start, CHUNK), 0:width].astype(NARROW).astype(WIDE)
        return 0

    lax.fori_loop(0, total // CHUNK, copy, 0)


def one_hot(first, second, offset):
    return jnp.where(first - offset == second, 1.0, 0.0).astype(NARROW)


def plain_dot(left, right, left_dim=1, right_dim=0):
    return lax.dot_general(left, right, (((left_dim,), (right_dim,)), ((), ())), preferred_element_type=WIDE)


def pack_rows(near_col, pieces):
    size = pieces[0].shape[0]
    lane = lax.broadcasted_iota(jnp.int32, (near_col.shape[0], size), 1)
    total = plain_dot(one_hot(near_col, lane, 0), pieces[0][...])
    for k in range(1, len(pieces)):
        total = total + plain_dot(one_hot(near_col, lane, k * size), pieces[k][...])
    return total


def unpack_rows(far_row, packed, k, size):
    down = lax.broadcasted_iota(jnp.int32, (size, far_row.shape[1]), 0)
    return plain_dot(one_hot(far_row, down, k * size), packed).astype(NARROW)


def beta_of(raw_ref, rows, lane):
    return jax.nn.sigmoid(raw_ref[rows, lane:lane + 1].astype(NARROW).astype(WIDE))


def shard_places(size, features, shard_rows, turned_round):
    unit, each = shard_rows
    shape = (features, size) if turned_round else (size, features)
    value = lax.broadcasted_iota(jnp.int32, shape, 1 if turned_round else 0)
    lane = lax.broadcasted_iota(jnp.int32, shape, 0 if turned_round else 1)
    chosen = (lane // unit == value // each) & (lane % unit == value % each)
    return jnp.where(chosen, 1.0, 0.0).astype(NARROW)


def spread_side(heads, width, shard_rows, z_ref, side_ref, taps_ref, gain_ref):
    span = heads * width
    taps_count = taps_ref.shape[1]
    own = pl.ds(pl.multiple_of(z_ref[0] * span, span), span)
    for which in range(3):
        first_row = heads + 2 + which * taps_count
        taps_ref[which] = side_ref[first_row:first_row + taps_count, own]
    last_row = heads + 2 + 3 * taps_count
    entries = jnp.broadcast_to(side_ref[last_row:last_row + 1, :], (8, side_ref.shape[1])).astype(NARROW)
    gain_ref[...] = plain_dot(entries, shard_places(width, side_ref.shape[1], shard_rows, True))[0:1]


def forward_kernel(heads, width, n_fs, shard_rows, *refs):
    pieces, refs = refs[:n_fs], refs[n_fs:]
    (win_ref, near_ref, far_ref, segcol_ref, poscol_ref, segrow_ref, edges_ref, z_ref, *refs) = refs
    blocks, refs = refs[:n_fs], refs[n_fs:]
    (side_ref, hidden_ref, raw_ref, out_ref, q_ref, k_ref, inv_ref, score_ref, dots_ref, upd_ref, state_ref,
     move_ref, taps_ref, gain_ref, pad_ref, base_ref, w_ref, normed_ref) = refs
    total = raw_ref.shape[0]
    count = total // CHUNK
    span = heads * width
    side_ref[...] = win_ref[:, 4 * span:].astype(WIDE).T
    spread_side(heads, width, shard_rows, z_ref, side_ref, taps_ref, gain_ref)

    pad_ref[0:HALO, :] = jnp.zeros((HALO, 3 * span), WIDE)

    def enter(index, _):
        rows = pl.ds(pl.multiple_of(index * ENTER, ENTER), ENTER)
        packed = pack_rows(near_ref[rows, :], pieces)
        scale = lax.rsqrt(jnp.mean(packed * packed, axis=-1, keepdims=True) + norm_eps)
        hidden = (packed * scale * side_ref[heads:heads + 1, :]).astype(NARROW)
        hidden_ref[rows, :] = hidden
        raw = plain_dot(hidden, win_ref[...])
        raw_ref[rows, :] = raw
        pad_ref[pl.ds(pl.multiple_of(index * ENTER + HALO, HALO), ENTER), :] = (
            raw[:, 0:3 * span].astype(NARROW).astype(WIDE))
        return 0

    lax.fori_loop(0, total // ENTER, enter, 0)

    def first(group, _):
        work = []
        for sub in range(PER_STEP):
            index = group * PER_STEP + sub
            start = pl.multiple_of(index * CHUNK, CHUNK)
            rows = pl.ds(start, CHUNK)
            pos = poscol_ref[rows, :]
            before, after = edges_ref[index, 0], edges_ref[index, 1]
            strict, inclusive, carried, last = chunk_masks(
                segcol_ref[rows, :], segrow_ref[pl.ds(index, 1), :], before, after)
            keep = jnp.where(before == after, 1.0, 0.0).astype(WIDE)
            for head in range(heads):
                cols = pl.ds(head * width, width)
                parts = []
                for which in range(3):
                    column = which * span + head * width
                    value = conv_rows(pad_ref, taps_ref[which, :, head * width:(head + 1) * width], pos,
                                      start, column, width)[0]
                    parts.append(value * jax.nn.sigmoid(value))
                query, key, value = parts
                query = query * lax.rsqrt(jnp.sum(query * query, axis=-1, keepdims=True) + unit_eps)
                key = key * lax.rsqrt(jnp.sum(key * key, axis=-1, keepdims=True) + unit_eps)
                q_ref[rows, cols] = query
                k_ref[rows, cols] = key
                beta = beta_of(raw_ref, rows, 4 * span + head)
                key_h, query_h = halves(key), halves(query)
                dots = product(key_h, key_h, 1, 1)
                score = jnp.where(inclusive, product(query_h, key_h, 1, 1), 0.0)
                at = index * heads + head
                dots_ref[at] = dots
                score_ref[at] = score
                work.append((at, rows, cols, keep, jnp.where(strict, beta * dots, 0.0),
                             beta * value, (beta * carried) * key, last * key))
        inverses = unit_lower_inverses([item[4] for item in work])
        for inverse, (at, rows, cols, keep, _, right, carry_in, tail_in) in zip(inverses, work):
            inv_h = halves(inverse)
            base = product(inv_h, halves(right))
            carry = product(inv_h, halves(carry_in))
            tail = turned(tail_in)
            eye = jnp.where(lax.broadcasted_iota(jnp.int32, (width, width), 0)
                            == lax.broadcasted_iota(jnp.int32, (width, width), 1), keep, 0.0)
            inv_ref[at] = inverse
            base_ref[rows, cols] = base
            w_ref[rows, cols] = carry
            move_ref[at] = eye - product(tail, halves(carry))
            state_ref[at] = product(tail, halves(base))
        return 0

    lax.fori_loop(0, count // PER_STEP, first, 0)

    def second(index, states):
        result = []
        for head in range(heads):
            at = index * heads + head
            added = state_ref[at]
            state_ref[at] = states[head]
            result.append(product(halves(move_ref[at]), halves(states[head])) + added)
        return tuple(result)

    lax.fori_loop(0, count, second, tuple(jnp.zeros((width, width), WIDE) for _ in range(heads)))

    def third(index, _):
        rows = pl.ds(pl.multiple_of(index * CHUNK, CHUNK), CHUNK)
        carried = jnp.where(segcol_ref[rows, :] == edges_ref[index, 0], 1.0, 0.0).astype(WIDE)
        for head in range(heads):
            cols = pl.ds(head * width, width)
            at = index * heads + head
            state = halves(state_ref[at])
            update = base_ref[rows, cols] - product(halves(w_ref[rows, cols]), state)
            upd_ref[rows, cols] = update
            out = carried * product(halves(q_ref[rows, cols]), state)
            out = out + product(halves(score_ref[at]), halves(update))
            mixed = out.astype(NARROW)
            out_ref[rows, cols] = mixed
            mixed = mixed.astype(WIDE)
            scale = lax.rsqrt(jnp.mean(mixed * mixed, axis=-1, keepdims=True) + norm_eps)
            gate = raw_ref[rows, pl.ds(3 * span + head * width, width)]
            normed = mixed * scale * gain_ref[...] * (gate * jax.nn.sigmoid(gate))
            normed_ref[rows, cols] = normed.astype(NARROW)
        return 0

    lax.fori_loop(0, count, third, 0)
    for k, block in enumerate(blocks):
        block[...] = unpack_rows(far_ref[...], normed_ref[...], k, total // n_fs)


def backward_kernel(heads, width, n_fs, shard_rows, *refs):
    pieces, refs = refs[:n_fs], refs[n_fs:]
    (win_ref, near_ref, far_ref, segcol_ref, poscol_ref, segrow_ref, edges_ref, z_ref, dgffn_ref,
     side_ref, hidden_ref, raw_ref, mixed_ref, q_ref, k_ref, inv_ref, score_ref, dots_ref, upd_ref, state_ref,
     move_ref, gradin_ref, *refs) = refs
    blocks, refs = refs[:n_fs], refs[n_fs:]
    (taps_ref, gain_ref, draw_ref, dhid_ref, dtaps_ref, sum_ref, small_ref, pad_ref, grad_ref, pdo_ref, dconv_ref, dout_ref, dnormed_ref) = refs
    total = raw_ref.shape[0]

    spread_side(heads, width, shard_rows, z_ref, side_ref, taps_ref, gain_ref)

    def enter(index, _):
        rows = pl.ds(pl.multiple_of(index * ENTER, ENTER), ENTER)
        dnormed_ref[rows, :] = pack_rows(near_ref[rows, :], pieces).astype(NARROW)
        return 0

    lax.fori_loop(0, total // ENTER, enter, 0)
    count = total // CHUNK
    span = heads * width
    fill_padded(raw_ref, pad_ref, 3 * span)

    def first(group, dgain):
        for sub in range(BACK_STEP):
            index = group * BACK_STEP + sub
            rows = pl.ds(pl.multiple_of(index * CHUNK, CHUNK), CHUNK)
            carried = jnp.where(segcol_ref[rows, :] == edges_ref[index, 0], 1.0, 0.0).astype(WIDE)
            for head in range(heads):
                cols = pl.ds(head * width, width)
                at = index * heads + head
                mixed = mixed_ref[rows, cols].astype(WIDE)
                scale = lax.rsqrt(jnp.mean(mixed * mixed, axis=-1, keepdims=True) + norm_eps)
                gate_cols = pl.ds(3 * span + head * width, width)
                gate = raw_ref[rows, gate_cols]
                sig = jax.nn.sigmoid(gate)
                given = dnormed_ref[rows, cols].astype(WIDE)
                unit = mixed * scale
                dgate = given * unit * gain_ref[...] * (sig * (1.0 + gate * (1.0 - sig)))
                draw_ref[rows, gate_cols] = dgate.astype(NARROW)
                given = given * (gate * sig)
                dgain = dgain + jnp.sum(given * unit, axis=0, keepdims=True)
                given = given * gain_ref[...]
                dout = scale * (given - unit * jnp.mean(unit * given, axis=-1, keepdims=True))
                dout = dout.astype(NARROW)
                dout_ref[rows, cols] = dout
                score_t = turned(score_ref[at])
                back = product_exact(score_t, dout)
                pdo_ref[rows, cols] = back
                inv_t = turned(inv_ref[at])
                back = product(inv_t, halves(back))
                query_t = turned(carried * q_ref[rows, cols])
                key_t = turned((beta_of(raw_ref, rows, 4 * span + head) * carried) * k_ref[rows, cols])
                grad_ref[at] = product_exact(query_t, dout) - product(key_t, halves(back))
        return dgain

    dgain = lax.fori_loop(0, count // BACK_STEP, first, jnp.zeros((1, width), WIDE))

    def second(step, grads):
        index = count - 1 - step
        result = []
        for head in range(heads):
            at = index * heads + head
            added = grad_ref[at]
            grad_ref[at] = grads[head]
            result.append(product(turned(move_ref[at]), halves(grads[head])) + added)
        return tuple(result)

    lax.fori_loop(0, count, second, tuple(jnp.zeros((width, width), WIDE) for _ in range(heads)))
    dconv_ref[total:total + HALO, :] = jnp.zeros((HALO, 3 * span), WIDE)

    def third(group, tap_sums):
        for sub in range(BACK_STEP):
            index = group * BACK_STEP + sub
            start = pl.multiple_of(index * CHUNK, CHUNK)
            rows = pl.ds(start, CHUNK)
            pos = poscol_ref[rows, :]
            strict, inclusive, carried, last = chunk_masks(
                segcol_ref[rows, :], segrow_ref[pl.ds(index, 1), :], edges_ref[index, 0], edges_ref[index, 1])
            new_sums = []
            dbetas = []
            for head in range(heads):
                cols = pl.ds(head * width, width)
                at = index * heads + head
                beta = beta_of(raw_ref, rows, 4 * span + head)
                query, key, update = q_ref[rows, cols], k_ref[rows, cols], upd_ref[rows, cols]
                query_h, key_h, update_h = halves(query), halves(key), halves(update)
                dout = dout_ref[rows, cols]
                state, grad = halves(state_ref[at]), halves(grad_ref[at])
                convs = []
                for which in range(3):
                    column = which * span + head * width
                    convs.append(conv_rows(pad_ref, taps_ref[which, :, head * width:(head + 1) * width], pos,
                                           start, column, width))
                gates = [jax.nn.sigmoid(c[0]) for c in convs]
                value = convs[2][0] * gates[2]
                dupdate = pdo_ref[rows, cols] + last * product(key_h, grad)
                dright = product(turned(inv_ref[at]), halves(dupdate))
                dright_h = halves(dright)
                dscore = jnp.where(inclusive, product_exact(update_h, dout, 1, 1, flip=True), 0.0)
                dsystem = jnp.where(strict, product(dright_h, update_h, 1, 1), 0.0)
                dscore_h = halves(dscore)
                dquery = carried * product_exact(state, dout, 1, 1, flip=True) + product(dscore_h, key_h)
                weighted = beta * dsystem
                scaled = beta * carried
                dkey = product(turned(dscore), query_h) + last * product(update_h, grad, 1, 1)
                dkey = dkey - product(halves(weighted + weighted.T), key_h)
                dkey = dkey - scaled * product(dright_h, state, 1, 1)
                dvalue = beta * dright
                seen = carried * product(key_h, state)
                dbeta = jnp.sum(dright * (value - seen), axis=-1, keepdims=True) - jnp.sum(
                    dsystem * dots_ref[at], axis=-1, keepdims=True)
                dbetas.append(dbeta * beta * (1.0 - beta))
                sides = []
                for grads, unit, conv, gate in ((dquery, query, convs[0][0], gates[0]), (dkey, key, convs[1][0], gates[1])):
                    plain = conv * gate
                    inv_norm = lax.rsqrt(jnp.sum(plain * plain, axis=-1, keepdims=True) + unit_eps)
                    sides.append(inv_norm * (grads - unit * jnp.sum(unit * grads, axis=-1, keepdims=True)))
                sides.append(dvalue)
                for which in range(3):
                    conv, plain, moved = convs[which]
                    gate = gates[which]
                    dconv = sides[which] * gate * (1.0 + conv * (1.0 - gate))
                    column = which * span + head * width
                    dconv_ref[rows, pl.ds(column, width)] = dconv
                    sums = [jnp.sum(dconv * plain, axis=0, keepdims=True)]
                    for shifted in moved:
                        sums.append(jnp.sum(dconv * shifted, axis=0, keepdims=True))
                    new_sums.append(jnp.concatenate(sums[::-1], axis=0))
            lane = lax.broadcasted_iota(jnp.int32, (CHUNK, draw_ref.shape[1] - 4 * span), 1)
            packed = jnp.zeros(lane.shape, WIDE)
            for head in range(heads):
                packed = jnp.where(lane == head, dbetas[head], packed)
            draw_ref[rows, pl.ds(4 * span, lane.shape[1])] = packed.astype(draw_ref.dtype)
            tap_sums = tuple(old + new for old, new in zip(tap_sums, new_sums))
        return tap_sums

    zero = tuple(jnp.zeros((taps_ref.shape[1], width), WIDE) for _ in range(3 * heads))
    sums = lax.fori_loop(0, count // BACK_STEP, third, zero)
    for head in range(heads):
        for which in range(3):
            dtaps_ref[which, :, head * width:(head + 1) * width] = sums[head * 3 + which]
    taps_count = taps_ref.shape[1]

    def fourth(index, _):
        start = pl.multiple_of(index * CHUNK, CHUNK)
        pos_window = poscol_ref[pl.ds(start, CHUNK + HALO), :]
        for which in range(3):
            columns = pl.ds(which * span, span)
            window = dconv_ref[pl.ds(start, CHUNK + HALO), columns]
            result = taps_ref[which, taps_count - 1:taps_count, :] * window[0:CHUNK]
            for offset in range(1, taps_count):
                part = jnp.where(pos_window >= offset, window, 0.0)[offset:offset + CHUNK]
                result = result + taps_ref[which, taps_count - 1 - offset:taps_count - offset, :] * part
            draw_ref[pl.ds(start, CHUNK), columns] = result.astype(draw_ref.dtype)
        return 0

    lax.fori_loop(0, count, fourth, 0)

    def weigh(index, _):
        rows = pl.ds(pl.multiple_of(index * ENTER, ENTER), ENTER)
        sum_ref[...] += plain_dot(hidden_ref[rows, :], draw_ref[rows, :], 0, 0)
        return 0

    sum_ref[...] = jnp.zeros(sum_ref.shape, WIDE)
    lax.fori_loop(0, total // ENTER, weigh, 0)
    features = small_ref.shape[1]
    small_ref[...] = jnp.zeros(small_ref.shape, WIDE)
    small_ref[heads + 1:heads + 2, :] = dgffn_ref[...]
    own = pl.ds(pl.multiple_of(z_ref[0] * span, span), span)
    for which in range(3):
        first_row = heads + 2 + which * taps_count
        small_ref[first_row:first_row + taps_count, own] = dtaps_ref[which]
    last_row = heads + 2 + 3 * taps_count
    small_ref[last_row:last_row + 1, :] = product_exact(
        halves(jnp.broadcast_to(dgain, (8, width))), shard_places(width, features, shard_rows, False))[0:1]
    gain = win_ref[:, 4 * span + heads:4 * span + heads + 1].astype(WIDE)
    across = jnp.sum(sum_ref[...] * win_ref[...].astype(WIDE), axis=-1, keepdims=True) / gain
    beside = small_ref[...].T
    lane = lax.broadcasted_iota(jnp.int32, beside.shape, 1)
    gradin_ref[:, 0:4 * span] = sum_ref[:, 0:4 * span].astype(NARROW)
    beside = sum_ref[:, 4 * span:] + beside + jnp.where(lane == heads, across, 0.0)
    gradin_ref[:, 4 * span:] = beside.astype(NARROW)

    def leave(index, _):
        rows = pl.ds(pl.multiple_of(index * ENTER, ENTER), ENTER)
        dhid_ref[rows, :] = plain_dot(draw_ref[rows, :], win_ref[...], 1, 1).astype(NARROW)
        return 0

    lax.fori_loop(0, total // ENTER, leave, 0)
    for k, block in enumerate(blocks):
        block[...] = unpack_rows(far_ref[...], dhid_ref[...], k, total // n_fs)


def product_exact(left, exact, left_dim=1, right_dim=0, flip=False):
    def one(a):
        if flip:
            return lax.dot_general(exact, a, (((right_dim,), (left_dim,)), ((), ())), preferred_element_type=WIDE)
        return lax.dot_general(a, exact, (((left_dim,), (right_dim,)), ((), ())), preferred_element_type=WIDE)

    if PASSES == 1:
        return one(left[0])
    return one(left[0]) + one(left[1])


def cost(flops, size):
    return pl.CostEstimate(flops=flops, bytes_accessed=size, transcendentals=0)


def specs(count):
    return [pl.BlockSpec(memory_space=pltpu.VMEM)] * count


def anywhere():
    return pl.BlockSpec(memory_space=pl.ANY)


def in_scalars():
    return pl.BlockSpec(memory_space=pltpu.SMEM)


def delta_forward(pieces, w_in, near, far, segcol, poscol, segrow, edges, z, heads, width, n_taps, shard_rows):
    n_fs = len(pieces)
    total = near.shape[0]
    features, lanes = w_in.shape
    count = total // CHUNK
    span = heads * width
    thin = jax.ShapeDtypeStruct((total, span), NARROW)
    rows = jax.ShapeDtypeStruct((total, span), WIDE)
    full = jax.ShapeDtypeStruct((total, features), NARROW)
    square = jax.ShapeDtypeStruct((count * heads, CHUNK, CHUNK), WIDE)
    state = jax.ShapeDtypeStruct((count * heads, width, width), WIDE)
    block = jax.ShapeDtypeStruct((total // n_fs, span), NARROW)
    raw = jax.ShapeDtypeStruct((total, lanes), WIDE)
    side = jax.ShapeDtypeStruct((lanes - 4 * span, features), WIDE)
    result = pl.pallas_call(
        functools.partial(forward_kernel, heads, width, n_fs, shard_rows),
        out_shape=(block,) * n_fs
        + (side, full, raw, thin, rows, rows, square, square, square, rows, state, state),
        in_specs=specs(n_fs + 6) + [in_scalars()] * 2,
        out_specs=tuple(specs(n_fs + 12)),
        scratch_shapes=[
            pltpu.VMEM((3, n_taps, span), WIDE),
            pltpu.VMEM((1, width), WIDE),
            pltpu.VMEM((total + HALO, 3 * span), WIDE),
            pltpu.VMEM((total, span), WIDE),
            pltpu.VMEM((total, span), WIDE),
            pltpu.VMEM((total, span), NARROW),
        ],
        compiler_params=pltpu.CompilerParams(vmem_limit_bytes=60 << 20),
        cost_estimate=cost(30_000_000_000, 16 << 20),
        name="delta_forward",
    )(*pieces, w_in, near, far, segcol, poscol, segrow, edges, z)
    return result[:n_fs], result[n_fs], result[n_fs + 1 :]


def delta_backward(pieces, w_in, near, far, segcol, poscol, segrow, edges, z, dgffn, side, kept, heads, width, n_taps, shard_rows):
    n_fs = len(pieces)
    total = near.shape[0]
    features, lanes = w_in.shape
    count = total // CHUNK
    span = heads * width
    block = jax.ShapeDtypeStruct((total // n_fs, features), NARROW)
    result = pl.pallas_call(
        functools.partial(backward_kernel, heads, width, n_fs, shard_rows),
        out_shape=(jax.ShapeDtypeStruct((features, lanes), NARROW),) + (block,) * n_fs,
        in_specs=specs(n_fs + 6) + [in_scalars()] * 2 + specs(13),
        out_specs=tuple(specs(n_fs + 1)),
        scratch_shapes=[
            pltpu.VMEM((3, n_taps, span), WIDE),
            pltpu.VMEM((1, width), WIDE),
            pltpu.VMEM((total, lanes), NARROW),
            pltpu.VMEM((total, features), NARROW),
            pltpu.VMEM((3, n_taps, span), WIDE),
            pltpu.VMEM((features, lanes), WIDE),
            pltpu.VMEM((lanes - 4 * span, features), WIDE),
            pltpu.VMEM((total + HALO, 3 * span), WIDE),
            pltpu.VMEM((count * heads, width, width), WIDE),
            pltpu.VMEM((total, span), WIDE),
            pltpu.VMEM((total + HALO, 3 * span), WIDE),
            pltpu.VMEM((total, span), NARROW),
            pltpu.VMEM((total, span), NARROW),
        ],
        compiler_params=pltpu.CompilerParams(vmem_limit_bytes=52 << 20),
        cost_estimate=cost(40_000_000_000, 16 << 20),
        name="delta_backward",
    )(*pieces, w_in, near, far, segcol, poscol, segrow, edges, z, dgffn, side, *kept)
    return result[0], list(result[1:])


def finish_kernel(heads, span, n_taps, z_ref, *refs):
    n_fs = len(refs) - 10
    pieces, refs = refs[:n_fs], refs[n_fs:]
    (*grads, wout_ref, beta_ref, taps_ref, gmix_ref, gffn_ref, ghead_ref) = refs
    side = pl.ds(4 * span, 128)
    lane = lax.broadcasted_iota(jnp.int32, (128, beta_ref.shape[0]), 0)
    column = lax.broadcasted_iota(jnp.int32, (128, beta_ref.shape[0]), 1)
    wout = jnp.zeros(wout_ref.shape, WIDE)
    small = jnp.zeros((wout_ref.shape[0], 128), WIDE)
    beta = jnp.zeros(beta_ref.shape, WIDE)
    for k, piece in enumerate(pieces):
        line = lax.rem(z_ref[0] + n_fs - k, n_fs)
        place = pl.ds(pl.multiple_of(line * span, span), span)
        for which, grad in enumerate(grads):
            grad[:, place] = piece[:, which * span:(which + 1) * span].astype(WIDE)
        wout = wout + piece[:, 4 * span + 128:].astype(WIDE)
        beside = piece[:, side]
        small = small + beside.astype(WIDE)
        chosen = jnp.where((lane < heads) & (column == line * heads + lane), 1.0, 0.0)
        beta = beta + plain_dot(chosen.astype(NARROW), beside, 0, 1)
    wout_ref[...] = wout
    beta_ref[...] = beta
    small = small.T
    gmix_ref[...] = small[heads:heads + 1]
    gffn_ref[...] = small[heads + 1:heads + 2]
    last_row = heads + 2 + 3 * n_taps
    for which in range(3):
        first_row = heads + 2 + which * n_taps
        taps_ref[which] = small[first_row:first_row + n_taps]
    ghead_ref[...] = small[last_row:last_row + 1, :ghead_ref.shape[1]]


def finish(z, pieces, heads, span, n_taps, head_rows):
    rows = pieces[0].shape[0]
    n_fs = len(pieces)
    full = jax.ShapeDtypeStruct((rows, n_fs * span), WIDE)
    line = jax.ShapeDtypeStruct((1, rows), WIDE)
    return pl.pallas_call(
        functools.partial(finish_kernel, heads, span, n_taps),
        out_shape=(full,) * 5
        + (
            jax.ShapeDtypeStruct((n_fs * heads, rows), WIDE),
            jax.ShapeDtypeStruct((3, n_taps, rows), WIDE),
            line,
            line,
            jax.ShapeDtypeStruct((1, head_rows), WIDE),
        ),
        in_specs=[in_scalars()] + specs(n_fs),
        out_specs=tuple(specs(10)),
        cost_estimate=cost(1_000_000, 1 << 20),
        name="finish_inputs",
    )(z, *pieces)


def mix_out_kernel(n_fs, row, z_ref, *refs):
    pieces, refs = refs[:n_fs], refs[n_fs:]
    wout_ref, tokens_ref, gain_ref, middle_ref, ffn_ref, normed_ref = refs
    span = pieces[0].shape[1]
    middle = tokens_ref[...].astype(WIDE)
    for k, piece in enumerate(pieces):
        place = pl.ds(pl.multiple_of(lax.rem(z_ref[0] + n_fs - k, n_fs) * span, span), span)
        normed_ref[:, place] = piece[...]
        middle = middle + plain_dot(piece[...], wout_ref[place, :])
    middle_ref[...] = middle
    scale = lax.rsqrt(jnp.mean(middle * middle, axis=-1, keepdims=True) + norm_eps)
    ffn_ref[...] = (middle * scale * gain_ref[row:row + 1, :]).astype(NARROW)


def mix_out(z, pieces, w_out, tokens, side, row):
    n_fs = len(pieces)
    shape = tokens.shape
    return pl.pallas_call(
        functools.partial(mix_out_kernel, n_fs, row),
        out_shape=(
            jax.ShapeDtypeStruct(shape, WIDE),
            jax.ShapeDtypeStruct(shape, NARROW),
            jax.ShapeDtypeStruct(shape, NARROW),
        ),
        in_specs=[in_scalars()] + specs(n_fs + 3),
        out_specs=tuple(specs(3)),
        compiler_params=pltpu.CompilerParams(vmem_limit_bytes=40 << 20),
        cost_estimate=cost(2_000_000_000, 6 << 20),
        name="mix_out",
    )(z, *pieces, w_out, tokens, side)


def ffn_kernel(keys, unit, block_ref, *refs):
    count = TP
    rows_in, refs = refs[:count], refs[count:]
    cots, refs = refs[:count], refs[count:]
    weights, refs = refs[:len(keys)], refs[len(keys):]
    (wdown_ref, active_ref, dboth_ref, sent_ref, later_ref, own_ref, part_ref, *ordered) = refs
    own_rows = rows_in[0].shape[0]
    if ordered:
        for near, far in zip(weights, ordered):
            n_fs, size = near.shape[:2]
            for by in range(n_fs):
                line = lax.rem(block_ref[1] + n_fs - by, n_fs)
                for at in range(size // unit):
                    place = pl.ds(pl.multiple_of((at * n_fs + line) * unit, unit), unit)
                    far[place, :] = near[by, at * unit:(at + 1) * unit, :]
        weights = ordered
    depth = weights[0].shape[0]
    units = wdown_ref.shape[0]
    spots = [pl.ds(pl.multiple_of((block_ref[0] ^ key) * depth, depth), depth) for key in keys]
    half = count // 2 * own_rows
    for at in range(count - 1, -1, -1):
        rows = slice(at * own_rows, (at + 1) * own_rows)
        both = plain_dot(rows_in[at][:, spots[0]], weights[0][...])
        for spot, weight in zip(spots[1:], weights[1:]):
            both = both + plain_dot(rows_in[at][:, spot], weight[...])
        gate, up = both[:, :units], both[:, units:]
        sig = jax.nn.sigmoid(gate)
        silu = gate * sig
        active_ref[rows, :] = (silu * up).astype(NARROW)
        dactive = plain_dot(cots[at][...], wdown_ref[...], 1, 1)
        dboth_ref[rows, :units] = (dactive * up * (sig * (1.0 + gate * (1.0 - sig)))).astype(NARROW)
        dboth_ref[rows, units:] = (dactive * silu).astype(NARROW)
        dboth = dboth_ref[rows, :]
        for spot, weight in zip(spots, weights):
            part_ref[:, spot] = plain_dot(dboth, weight[...], 1, 1)
        if at >= count // 2:
            place = at * own_rows - half
            sent_ref[place:place + own_rows, :] = part_ref[...].astype(NARROW)
        elif at:
            later_ref[(at - 1) * own_rows:at * own_rows, :] = part_ref[...]
        else:
            own_ref[...] = part_ref[...]


def ffn_units(block, rows_in, cots, weights, keys, w_down, unit):
    own_rows, features = rows_in[0].shape
    units = w_down.shape[0]
    total = TP * own_rows
    return pl.pallas_call(
        functools.partial(ffn_kernel, keys, unit),
        out_shape=(
            jax.ShapeDtypeStruct((total, units), NARROW),
            jax.ShapeDtypeStruct((total, 2 * units), NARROW),
            jax.ShapeDtypeStruct((total // 2, features), NARROW),
            jax.ShapeDtypeStruct((total // 2 - own_rows, features), WIDE),
            jax.ShapeDtypeStruct((own_rows, features), WIDE),
        ),
        in_specs=[in_scalars()] + specs(2 * TP + len(weights) + 1),
        out_specs=tuple(specs(5)),
        scratch_shapes=[pltpu.VMEM((own_rows, features), WIDE)]
        + [pltpu.VMEM((features // len(keys), 2 * units), NARROW) for w in weights if w.ndim == 3],
        compiler_params=pltpu.CompilerParams(vmem_limit_bytes=52 << 20),
        cost_estimate=cost(8_000_000_000, 16 << 20),
        name="ffn_units",
    )(block, *rows_in, *cots, *weights, w_down)


def mix_back_kernel(n_fs, row, z_ref, *refs):
    sources, refs = refs[:6], refs[6:]
    gain_ref, refs = refs[0], refs[1:]
    blocks, refs = refs[:n_fs], refs[n_fs:]
    (dmiddle_ref, dbranch_ref, dgain_ref, *places, sems) = refs
    fetches = [pltpu.make_async_copy(source, place, sems.at[k]) for k, (source, place) in enumerate(
        zip((sources[0], sources[1].at[pl.ds(0, places[1].shape[0])], *sources[2:5]), places))]
    quarter = places[5].shape[0] // 4
    parts = [pl.ds(k * quarter, quarter) for k in range(4)]
    fetches += [
        pltpu.make_async_copy(sources[5].at[part], places[5].at[part], sems.at[5 + k]) for k, part in enumerate(parts)
    ]
    for fetch in fetches:
        fetch.start()
    own_ref, core_ref, side_ref, middle_ref, cot_ref, wout_ref = places
    for fetch in fetches[:5]:
        fetch.wait()
    middle = middle_ref[...]
    given = own_ref[...] + core_ref[...].astype(WIDE) + side_ref[...].astype(WIDE)
    scale = lax.rsqrt(jnp.mean(middle * middle, axis=-1, keepdims=True) + norm_eps)
    unit = middle * scale
    dgain_ref[...] = jnp.sum(given * unit, axis=0, keepdims=True)
    given = given * gain_ref[row:row + 1, :]
    dmiddle = cot_ref[...].astype(WIDE) + scale * (given - unit * jnp.mean(unit * given, axis=-1, keepdims=True))
    dmiddle_ref[...] = dmiddle
    dbranch = dmiddle.astype(NARROW)
    dbranch_ref[...] = dbranch
    span = blocks[0].shape[1]
    for fetch in fetches[5:]:
        fetch.wait()
    for k, block in enumerate(blocks):
        place = pl.ds(pl.multiple_of(lax.rem(z_ref[0] + k, n_fs) * span, span), span)
        block[...] = plain_dot(dbranch, wout_ref[place, :], 1, 1).astype(NARROW)


def mix_back(z, parts, middle, side, row, cotangent, w_out, n_fs):
    count, features = middle.shape
    block = jax.ShapeDtypeStruct((count, features // n_fs), NARROW)
    sources = (*parts, middle, cotangent, w_out)
    result = pl.pallas_call(
        functools.partial(mix_back_kernel, n_fs, row),
        out_shape=(block,) * n_fs
        + (
            jax.ShapeDtypeStruct(middle.shape, WIDE),
            jax.ShapeDtypeStruct(middle.shape, NARROW),
            jax.ShapeDtypeStruct((1, features), WIDE),
        ),
        in_specs=[in_scalars()] + [anywhere()] * 6 + specs(1),
        out_specs=tuple(specs(n_fs + 3)),
        scratch_shapes=[pltpu.VMEM((min(part.shape[0], count) if k < 5 else part.shape[0], features), part.dtype) for k, part in enumerate(sources)] + [pltpu.SemaphoreType.DMA((9,))],
        compiler_params=pltpu.CompilerParams(vmem_limit_bytes=60 << 20),
        cost_estimate=cost(2_000_000_000, 6 << 20),
        name="mix_back",
    )(z, *sources, side)
    return (result[:n_fs],) + tuple(result[n_fs:])


def rms_scale(values, gain):
    return values * lax.rsqrt(jnp.mean(values * values, axis=-1, keepdims=True) + norm_eps) * gain


def swiglu(gate_proj, up_proj):
    return jax.nn.silu(gate_proj) * up_proj


def sequence_layout(lengths_row, total):
    ends = jnp.cumsum(lengths_row)
    index = jnp.arange(total, dtype=jnp.int32)
    before = index[:, None] >= ends[None, :]
    segment = jnp.sum(before.astype(jnp.int32), axis=1)
    start = jnp.sum(jnp.where(before, lengths_row[None, :], 0), axis=1)
    return (segment, index - start)


def project(left, right):
    return jnp.dot(left, right, preferred_element_type=WIDE)


def project_back(left, right):
    return lax.dot_general(left, right, (((1,), (1,)), ((), ())), preferred_element_type=WIDE)


def weight_grad(left, right):
    return lax.dot_general(left, right, (((0,), (0,)), ((), ())), preferred_element_type=WIDE)


def flip(value, bit, n_dp):
    return lax.ppermute(value, "dp", [(i, i ^ bit) for i in range(n_dp)])


def shift(value, by, n_fs):
    return lax.ppermute(value, "fsdp", [(i, (i + by) % n_fs) for i in range(n_fs)])


def line_pieces(shard, n_fs):
    return [shard] + [shift(shard, by, n_fs) for by in range(1, n_fs)]


def line_order(pieces, z):
    n_fs = len(pieces)
    shape = pieces[0].shape
    whole = jnp.zeros((shape[0], n_fs) + shape[1:], pieces[0].dtype)
    for by, piece in enumerate(pieces):
        whole = lax.dynamic_update_slice_in_dim(whole, piece[:, None], lax.rem(z + n_fs - by, n_fs), 1)
    return whole


def gather_cube(piece, order, n_dp):
    pieces = {0: piece}
    for bit in order:
        for key in list(pieces):
            pieces[key ^ bit] = flip(pieces[key], bit, n_dp)
    return pieces


def in_order(pieces, me):
    rows = pieces[0].shape[0]
    whole = jnp.zeros((len(pieces) * rows,) + pieces[0].shape[1:], pieces[0].dtype)
    unit = max(pieces).bit_length()
    step = (1 << unit) // len(pieces)
    for key, piece in pieces.items():
        whole = lax.dynamic_update_slice_in_dim(whole, piece, lax.bitwise_xor(me, key // step) * rows, 0)
    return whole


def per_device(
    n_dp,
    n_fs,
    tokens,
    lengths,
    packing,
    w_query,
    w_key,
    w_value,
    w_gate,
    w_beta,
    conv_taps,
    w_out,
    gain_mix,
    gain_head,
    gain_ffn,
    w_ffn_gate,
    w_ffn_up,
    w_ffn_down,
    cotangent,
):
    me = lax.axis_index("dp")
    z = lax.axis_index("fsdp")
    bits = [1 << k for k in range(n_dp.bit_length() - 1)]
    first_order = bits[:1] + bits[1:]
    second_order = bits[:1] + bits[1:][::-1]
    packing_row = packing[0]
    lengths_row = lengths[0]
    own_rows, features = tokens.shape
    total = own_rows * n_fs
    rows = w_query.shape[0]
    heads_all = w_beta.shape[1]
    heads = heads_all // n_fs
    span = features // n_fs
    width = span // heads
    hidden_ffn = w_ffn_gate.shape[1]
    head_rows = gain_head.shape[0]
    n_taps = conv_taps.shape[1]

    def by_owner(matrix):
        return jnp.swapaxes(matrix.reshape(rows, n_fs, -1), 0, 1)

    small = jnp.concatenate(
        [
            gain_mix[:, None],
            gain_ffn[:, None],
            conv_taps.reshape(3 * n_taps, rows).T,
            jnp.pad(gain_head, (0, rows - head_rows))[:, None],
        ],
        axis=1,
    )
    n_small = small.shape[1]
    side = jnp.concatenate(
        [by_owner(w_beta), jnp.broadcast_to(small[None], (n_fs, rows, n_small))], axis=2
    )
    side = jnp.pad(side, ((0, 0), (0, 0), (0, 128 - heads - n_small)))
    packet = jnp.concatenate(
        [by_owner(w_query), by_owner(w_key), by_owner(w_value), by_owner(w_gate), side], axis=2
    )
    member = lax.rem(me, TP)
    block = me // TP
    n_rest = n_dp // TP
    ff_block = hidden_ffn // n_dp
    ff_line = ff_block // n_fs
    ff_unit = -(-ff_line // 8) * 8
    while n_rest * n_fs * ff_unit % 128:
        ff_unit += 8
    ff_pad = n_rest * n_fs * ff_unit
    tp_bits = [bit for bit in bits if bit < TP]
    rest_bits = [bit for bit in bits if bit >= TP]

    def by_member(matrix):
        split = matrix.reshape(rows, n_rest, TP, n_fs, ff_line)
        split = jnp.pad(split, ((0, 0),) * 4 + ((0, ff_unit - ff_line),))
        return jnp.transpose(split, (2, 0, 1, 3, 4)).reshape(TP, rows, ff_pad)

    def hand_out(blocks):
        pieces = [lax.dynamic_index_in_dim(blocks, z, 0)]
        for by in range(1, n_fs):
            pieces.append(shift(lax.dynamic_index_in_dim(blocks, lax.rem(z + by, n_fs), 0), by, n_fs))
        return pieces

    lanes = 4 * span + 128
    packet = jnp.concatenate([packet, jnp.broadcast_to(w_out[None], (n_fs,) + w_out.shape)], axis=2)
    packet = hand_out(packet)
    token_pieces = [tokens] + [shift(tokens, by, n_fs) for by in range(1, n_fs)]
    packet, token_pieces[1] = lax.optimization_barrier((packet, token_pieces[1]))
    packet_in = line_order([piece[:, :, :lanes] for piece in packet], z).reshape(n_fs * rows, lanes)
    packet_out = line_order([piece[:, :, lanes:] for piece in packet], z).reshape(n_fs * rows, features)
    w_in = lax.all_gather(packet_in, "dp", axis=0, tiled=True)
    full_out = lax.all_gather(packet_out, "dp", axis=0, tiled=True)

    owner, place = packing_row // own_rows, lax.rem(packing_row, own_rows)
    near = (lax.rem(z + n_fs - owner, n_fs) * own_rows + place)[:, None]
    far = (lax.rem(owner + n_fs - z, n_fs) * own_rows + place)[None]
    segment, position = sequence_layout(lengths_row, total)
    seg_rows = segment.reshape(-1, CHUNK)
    ends = seg_rows[:, -1]
    edges = jnp.stack([jnp.concatenate([jnp.full((1,), -1, jnp.int32), ends[:-1]]), ends], axis=1)
    z_ref = z.reshape(1)
    layout = (segment[:, None], jnp.pad(position, (0, HALO))[:, None], seg_rows, edges, z_ref)
    shard_rows = (rows, head_rows)
    own_gate, own_up, _ = lax.optimization_barrier((w_ffn_gate, w_ffn_up, token_pieces[1]))
    both_sends = jnp.concatenate([by_member(own_gate), by_member(own_up)], axis=2)
    blocks, side, kept = delta_forward(
        token_pieces, w_in, near, far, *layout, heads, width, n_taps, shard_rows
    )
    gain_row = heads + 1

    both_pieces = {
        key: flip(lax.dynamic_index_in_dim(both_sends, member ^ key, 0, keepdims=False), key, n_dp)
        if key
        else lax.dynamic_index_in_dim(both_sends, member, 0, keepdims=False)
        for key in range(TP)
    }
    own_down, _ = lax.optimization_barrier((w_ffn_down, token_pieces[1]))
    own_down = jnp.pad(own_down, ((0, ff_unit - ff_line), (0, 0)))
    down_rows = in_order(gather_cube(own_down, rest_bits, n_dp), block).reshape(n_rest, -1, features)
    both_rows = in_order(both_pieces, member).reshape(TP, rows, 2 * ff_pad)
    own_cotangent, both_rows, down_rows = lax.optimization_barrier((cotangent, both_rows, down_rows))
    both_rows, down_rows, _ = lax.optimization_barrier((both_rows, down_rows, token_pieces))
    both_line = line_pieces(both_rows, n_fs)
    both_line, blocks, down_rows = lax.optimization_barrier((both_line, blocks, down_rows))
    if rows % 16 == 0:
        both_rows = jnp.stack([piece.reshape(TP * rows, 2 * ff_pad) for piece in both_line])
    else:
        both_rows = line_order(both_line, z).reshape(-1, 2 * ff_pad)
    both_pieces = gather_cube(both_rows, rest_bits, n_dp)
    unit = 1 << (TP.bit_length() - 1)
    rest_keys = [key // unit for key in both_pieces]
    tp_order = sorted(range(TP), key=lambda key: tuple((key & bit) != 0 for bit in tp_bits))

    cot_pieces = gather_cube(own_cotangent, tp_bits[::-1], n_dp)
    cot_pieces, blocks = lax.optimization_barrier((cot_pieces, blocks))

    def halve(value, index, some_bits):
        unit = some_bits[0] if some_bits else 1
        for bit in some_bits[::-1]:
            half = value.shape[0] // 2
            mine = (index // (bit // unit)) % 2
            sent = lax.dynamic_slice_in_dim(value, (1 - mine) * half, half, 0)
            value = lax.dynamic_slice_in_dim(value, mine * half, half, 0)
            value = value.astype(WIDE) + flip(sent.astype(NARROW), bit, n_dp).astype(WIDE)
        return value

    def sum_up(pieces, whole):
        total = lax.dynamic_index_in_dim(whole, z, 0, keepdims=False).astype(WIDE)
        for piece in pieces[1:]:
            total = total + piece[0].astype(WIDE)
        return total

    def pass_on(parts):
        return [parts[0]] + [shift(part, by, n_fs) for by, part in enumerate(parts) if by]

    mixed_pieces = pass_on(blocks)
    down_line = line_pieces(down_rows, n_fs)
    middle, ffn_in, normed_b = mix_out(z_ref, mixed_pieces, full_out, tokens, side, gain_row)
    w_down = line_order(down_line, z).reshape(ff_pad, features)
    ffn_pieces = gather_cube(ffn_in, tp_bits[::-1], n_dp)
    active_b, d_both, first, second, d_own = ffn_units(
        jnp.stack([block, z]),
        [ffn_pieces[key] for key in tp_order],
        [cot_pieces[key] for key in tp_order],
        list(both_pieces.values()),
        rest_keys,
        w_down,
        rows,
    )
    ffn_near = jnp.concatenate([ffn_pieces[key] for key in tp_order], axis=0)

    def both_part(lo, size):
        part = weight_grad(lax.dynamic_slice_in_dim(ffn_near, lo, size, 1), d_both)
        return part.reshape(-1, n_fs * rows, 2 * ff_pad)

    cotangent_near = jnp.concatenate([cot_pieces[key] for key in tp_order], axis=0)
    down_terms = weight_grad(active_b, cotangent_near).astype(NARROW)
    down_sum = lax.psum_scatter(
        down_terms.reshape(n_rest, -1, features), "fsdp", scatter_dimension=1, tiled=True
    )
    d_both, down_terms = lax.optimization_barrier((d_both, down_terms))
    split = features // 2 if rest_bits else features
    top = block // max(n_rest // 2, 1)
    if rest_bits:
        both_sent = both_part((1 - top) * split, split).astype(NARROW)
    else:
        both_sent = None
    from_core = flip(first, tp_bits[0], n_dp)
    second = second + from_core[own_rows:].astype(WIDE)
    second, both_sent, active_late = lax.optimization_barrier((second.astype(NARROW), both_sent, active_b))
    from_side = flip(second, tp_bits[1], n_dp)
    from_side, ffn_near, active_late = lax.optimization_barrier((from_side, ffn_near, active_late))
    both_sum = both_part(top * split if rest_bits else 0, split)

    d_blocks, d_middle, d_branch, d_gffn = mix_back(
        z_ref, (d_own, from_core, from_side), middle, side, gain_row, cotangent, full_out, n_fs
    )
    d_pieces = pass_on(d_blocks)
    d_branch, active_late = lax.optimization_barrier((d_branch, active_late))

    def out_term(units, lo):
        return project(units[lo * own_rows : (lo + 1) * own_rows], w_down)

    out_core = flip(project(active_late[2 * own_rows :], w_down).astype(NARROW), tp_bits[0], n_dp)
    out_sent = (out_term(active_late, 1) + out_core[own_rows:].astype(WIDE)).astype(NARROW)
    if rest_bits:
        both_came, out_sent = lax.optimization_barrier((flip(both_sent, rest_bits[-1], n_dp), out_sent))
        both_sum = both_sum + both_came.astype(WIDE)
        both_sum = halve(both_sum, block, rest_bits[:-1])
    out_side = flip(out_sent, tp_bits[1], n_dp)
    out_grad = weight_grad(normed_b, d_branch).astype(NARROW)
    sum_out = lax.psum_scatter(out_grad, "dp", scatter_dimension=0, tiled=True)
    both_sum = jnp.swapaxes(both_sum.reshape(TP, n_fs, rows, 2 * ff_pad), 0, 1)
    both_sum, d_pieces, out_grad = lax.optimization_barrier((both_sum, d_pieces, out_grad))
    both_line = hand_out(both_sum.astype(NARROW))

    grad_in, d_blocks = delta_backward(
        d_pieces, w_in, near, far, *layout, d_gffn, side, kept, heads, width, n_taps, shard_rows
    )
    grad_in, both_line, down_sum, sum_out = lax.optimization_barrier((grad_in, both_line, down_sum, sum_out))
    part = lax.psum_scatter(grad_in, "dp", scatter_dimension=0, tiled=True)
    d_blocks, both_line, active_late = lax.optimization_barrier((d_blocks, both_line, active_late))
    d_blocks = pass_on(d_blocks)
    layer_out = middle + out_term(active_late, 0) + out_core[:own_rows].astype(WIDE) + out_side.astype(WIDE)
    layer_out = layer_out.astype(NARROW)
    both_sum = sum_up(both_line, both_sum)
    grad_fdown = halve(down_sum, block, rest_bits)[0, :ff_line].astype(WIDE)
    both_pieces = {
        key: flip(
            lax.dynamic_index_in_dim(both_sum, member ^ key, 0, keepdims=False).astype(NARROW), key, n_dp
        ).astype(WIDE)
        if key
        else lax.dynamic_index_in_dim(both_sum, member, 0, keepdims=False)
        for key in range(TP)
    }
    both_mine = in_order({key: piece[None] for key, piece in both_pieces.items()}, member)
    def units_of(which):
        part = both_mine[:, :, which * ff_pad : (which + 1) * ff_pad]
        part = part.reshape(TP, rows, n_rest, n_fs, ff_unit)[..., :ff_line]
        return jnp.transpose(part, (1, 2, 0, 3, 4)).reshape(rows, hidden_ffn)

    lanes = part.shape[1]
    joint = jnp.concatenate([part, sum_out], axis=1).reshape(n_fs, rows, -1)
    arrived = [piece[0] for piece in hand_out(joint)]
    d_blocks, arrived[0], layer_out = lax.optimization_barrier((d_blocks, arrived[0], layer_out))
    d_hidden = d_blocks[0].astype(WIDE)
    for block_of in d_blocks[1:]:
        d_hidden = d_hidden + block_of.astype(WIDE)
    _, norm_mix_back = jax.vjp(rms_scale, tokens.astype(WIDE), side[heads])
    d_inputs_norm, _ = norm_mix_back(d_hidden)
    grad_tokens = d_middle + d_inputs_norm

    grads, (grad_wout, grad_beta, grad_taps, grad_gmix, grad_gffn, grad_ghead) = (
        lambda outs: (outs[:4], outs[4:])
    )(finish(z_ref, arrived, heads, span, n_taps, head_rows))
    return (
        layer_out,
        grad_tokens,
        grads[0],
        grads[1],
        grads[2],
        grads[3],
        grad_beta.T,
        grad_taps,
        grad_wout,
        grad_gmix[0],
        grad_ghead[0],
        grad_gffn[0],
        units_of(0),
        units_of(1),
        grad_fdown,
    )


def solution(mesh):
    both = ("dp", "fsdp")
    rows = P(both, None)
    group = P("dp", None)
    taps = P(None, None, both)
    line = P(both)
    in_specs = (rows, group, group) + (rows,) * 5 + (taps, rows, line, line, line) + (rows,) * 4
    out_specs = (rows,) * 7 + (taps, rows, line, line, line) + (rows,) * 3
    return jax.shard_map(
        functools.partial(per_device, mesh.shape["dp"], mesh.shape["fsdp"]),
        mesh=mesh,
        in_specs=in_specs,
        out_specs=out_specs,
        check_vma=False,
    )
```

```python
import functools

import jax
import jax.numpy as jnp
from jax import lax
from jax.experimental import pallas as pl
from jax.experimental.pallas import tpu as pltpu
from jax.sharding import PartitionSpec as P

CHUNK = 128
TP = 4
PER_STEP = 4
BACK_STEP = 4
ENTER = 512
HALO = 8
norm_eps = 1e-05
unit_eps = 1e-06
NARROW = jnp.bfloat16
WIDE = jnp.float32


def halves(value):
    top = value.astype(NARROW)
    return top, (value - top.astype(WIDE)).astype(NARROW)


def product(left, right, left_dim=1, right_dim=0):
    dims = (((left_dim,), (right_dim,)), ((), ()))

    def one(a, b):
        return lax.dot_general(a, b, dims, preferred_element_type=WIDE)

    if PASSES == 1:
        return one(left[0], right[0])
    return one(left[0], right[0]) + (one(left[0], right[1]) + one(left[1], right[0]))


PASSES = 3


def turned(value):
    return halves(value.T)


def chunk_masks(seg_col, seg_row, before, after):
    size = seg_col.shape[0]
    down = lax.broadcasted_iota(jnp.int32, (size, size), 0)
    across = lax.broadcasted_iota(jnp.int32, (size, size), 1)
    same = seg_col == seg_row
    strict = same & (down > across)
    inclusive = same & (down >= across)
    carried = jnp.where(seg_col == before, 1.0, 0.0).astype(WIDE)
    last = jnp.where(seg_col == after, 1.0, 0.0).astype(WIDE)
    return strict, inclusive, carried, last


def unit_lower_inverses(systems):
    size = systems[0].shape[0]
    down = lax.broadcasted_iota(jnp.int32, (size, size), 0)
    across = lax.broadcasted_iota(jnp.int32, (size, size), 1)
    gap = jnp.where(down > across, down ^ across, 0)
    eye = jnp.where(down == across, 1.0, 0.0)
    results = [eye - jnp.where(gap == 1, system, 0.0) for system in systems]
    step = 2
    while step < size:
        picked = (gap >= step) & (gap < 2 * step)
        parts = [jnp.where(picked, system, 0.0).astype(NARROW) for system in systems]
        done = [result.astype(NARROW) for result in results]
        inner = [plain_dot(part, own).astype(NARROW) for part, own in zip(parts, done)]
        results = [result - plain_dot(own, side) for result, own, side in zip(results, done, inner)]
        step *= 2
    left = [eye - result - product(halves(system), halves(result)) for system, result in zip(systems, results)]
    results = [
        result + plain_dot(result.astype(NARROW), rest.astype(NARROW)) for result, rest in zip(results, left)
    ]
    return results


def conv_rows(pad_ref, taps, pos, start, column, width):
    window = pad_ref[pl.ds(start, CHUNK + HALO), pl.ds(column, width)]
    count = taps.shape[0]
    result = taps[count - 1 : count] * window[HALO : HALO + CHUNK]
    moved = []
    for offset in range(1, count):
        rows = jnp.where(pos >= offset, window[HALO - offset : HALO - offset + CHUNK], 0.0)
        moved.append(rows)
        result = result + taps[count - 1 - offset : count - offset] * rows
    return result, window[HALO : HALO + CHUNK], moved


def fill_padded(raw_ref, pad_ref, width):
    pad_ref[0:HALO, :] = jnp.zeros((HALO, width), WIDE)
    total = raw_ref.shape[0]

    def copy(index, _):
        start = pl.multiple_of(index * CHUNK, CHUNK)
        pad_ref[pl.ds(start + HALO, CHUNK), :] = raw_ref[pl.ds(start, CHUNK), 0:width].astype(NARROW).astype(WIDE)
        return 0

    lax.fori_loop(0, total // CHUNK, copy, 0)


def one_hot(first, second, offset):
    return jnp.where(first - offset == second, 1.0, 0.0).astype(NARROW)


def plain_dot(left, right, left_dim=1, right_dim=0):
    return lax.dot_general(left, right, (((left_dim,), (right_dim,)), ((), ())), preferred_element_type=WIDE)


def pack_rows(near_col, pieces):
    size = pieces[0].shape[0]
    lane = lax.broadcasted_iota(jnp.int32, (near_col.shape[0], size), 1)
    total = plain_dot(one_hot(near_col, lane, 0), pieces[0][...])
    for k in range(1, len(pieces)):
        total = total + plain_dot(one_hot(near_col, lane, k * size), pieces[k][...])
    return total


def unpack_rows(far_row, packed, k, size):
    down = lax.broadcasted_iota(jnp.int32, (size, far_row.shape[1]), 0)
    return plain_dot(one_hot(far_row, down, k * size), packed).astype(NARROW)


def beta_of(raw_ref, rows, lane):
    return jax.nn.sigmoid(raw_ref[rows, lane:lane + 1].astype(NARROW).astype(WIDE))


def shard_places(size, features, shard_rows, turned_round):
    unit, each = shard_rows
    shape = (features, size) if turned_round else (size, features)
    value = lax.broadcasted_iota(jnp.int32, shape, 1 if turned_round else 0)
    lane = lax.broadcasted_iota(jnp.int32, shape, 0 if turned_round else 1)
    chosen = (lane // unit == value // each) & (lane % unit == value % each)
    return jnp.where(chosen, 1.0, 0.0).astype(NARROW)


def spread_side(heads, width, shard_rows, z_ref, side_ref, taps_ref, gain_ref):
    span = heads * width
    taps_count = taps_ref.shape[1]
    own = pl.ds(pl.multiple_of(z_ref[0] * span, span), span)
    for which in range(3):
        first_row = heads + 2 + which * taps_count
        taps_ref[which] = side_ref[first_row:first_row + taps_count, own]
    last_row = heads + 2 + 3 * taps_count
    entries = jnp.broadcast_to(side_ref[last_row:last_row + 1, :], (8, side_ref.shape[1])).astype(NARROW)
    gain_ref[...] = plain_dot(entries, shard_places(width, side_ref.shape[1], shard_rows, True))[0:1]


def forward_kernel(heads, width, n_fs, shard_rows, *refs):
    pieces, refs = refs[:n_fs], refs[n_fs:]
    (win_ref, near_ref, far_ref, segcol_ref, poscol_ref, segrow_ref, edges_ref, z_ref, *refs) = refs
    blocks, refs = refs[:n_fs], refs[n_fs:]
    (side_ref, hidden_ref, raw_ref, out_ref, q_ref, k_ref, inv_ref, score_ref, dots_ref, upd_ref, state_ref,
     move_ref, taps_ref, gain_ref, pad_ref, base_ref, w_ref, normed_ref) = refs
    total = raw_ref.shape[0]
    count = total // CHUNK
    span = heads * width
    side_ref[...] = win_ref[:, 4 * span:].astype(WIDE).T
    spread_side(heads, width, shard_rows, z_ref, side_ref, taps_ref, gain_ref)

    pad_ref[0:HALO, :] = jnp.zeros((HALO, 3 * span), WIDE)

    def enter(index, _):
        rows = pl.ds(pl.multiple_of(index * ENTER, ENTER), ENTER)
        packed = pack_rows(near_ref[rows, :], pieces)
        scale = lax.rsqrt(jnp.mean(packed * packed, axis=-1, keepdims=True) + norm_eps)
        hidden = (packed * scale * side_ref[heads:heads + 1, :]).astype(NARROW)
        hidden_ref[rows, :] = hidden
        raw = plain_dot(hidden, win_ref[...])
        raw_ref[rows, :] = raw
        pad_ref[pl.ds(pl.multiple_of(index * ENTER + HALO, HALO), ENTER), :] = (
            raw[:, 0:3 * span].astype(NARROW).astype(WIDE))
        return 0

    lax.fori_loop(0, total // ENTER, enter, 0)

    def first(group, _):
        work = []
        for sub in range(PER_STEP):
            index = group * PER_STEP + sub
            start = pl.multiple_of(index * CHUNK, CHUNK)
            rows = pl.ds(start, CHUNK)
            pos = poscol_ref[rows, :]
            before, after = edges_ref[index, 0], edges_ref[index, 1]
            strict, inclusive, carried, last = chunk_masks(
                segcol_ref[rows, :], segrow_ref[pl.ds(index, 1), :], before, after)
            keep = jnp.where(before == after, 1.0, 0.0).astype(WIDE)
            for head in range(heads):
                cols = pl.ds(head * width, width)
                parts = []
                for which in range(3):
                    column = which * span + head * width
                    value = conv_rows(pad_ref, taps_ref[which, :, head * width:(head + 1) * width], pos,
                                      start, column, width)[0]
                    parts.append(value * jax.nn.sigmoid(value))
                query, key, value = parts
                query = query * lax.rsqrt(jnp.sum(query * query, axis=-1, keepdims=True) + unit_eps)
                key = key * lax.rsqrt(jnp.sum(key * key, axis=-1, keepdims=True) + unit_eps)
                q_ref[rows, cols] = query
                k_ref[rows, cols] = key
                beta = beta_of(raw_ref, rows, 4 * span + head)
                key_h, query_h = halves(key), halves(query)
                dots = product(key_h, key_h, 1, 1)
                score = jnp.where(inclusive, product(query_h, key_h, 1, 1), 0.0)
                at = index * heads + head
                dots_ref[at] = dots
                score_ref[at] = score
                work.append((at, rows, cols, keep, jnp.where(strict, beta * dots, 0.0),
                             beta * value, (beta * carried) * key, last * key))
        inverses = unit_lower_inverses([item[4] for item in work])
        for inverse, (at, rows, cols, keep, _, right, carry_in, tail_in) in zip(inverses, work):
            inv_h = halves(inverse)
            base = product(inv_h, halves(right))
            carry = product(inv_h, halves(carry_in))
            tail = turned(tail_in)
            eye = jnp.where(lax.broadcasted_iota(jnp.int32, (width, width), 0)
                            == lax.broadcasted_iota(jnp.int32, (width, width), 1), keep, 0.0)
            inv_ref[at] = inverse
            base_ref[rows, cols] = base
            w_ref[rows, cols] = carry
            move_ref[at] = eye - product(tail, halves(carry))
            state_ref[at] = product(tail, halves(base))
        return 0

    lax.fori_loop(0, count // PER_STEP, first, 0)

    def second(index, states):
        result = []
        for head in range(heads):
            at = index * heads + head
            added = state_ref[at]
            state_ref[at] = states[head]
            result.append(product(halves(move_ref[at]), halves(states[head])) + added)
        return tuple(result)

    lax.fori_loop(0, count, second, tuple(jnp.zeros((width, width), WIDE) for _ in range(heads)))

    def third(index, _):
        rows = pl.ds(pl.multiple_of(index * CHUNK, CHUNK), CHUNK)
        carried = jnp.where(segcol_ref[rows, :] == edges_ref[index, 0], 1.0, 0.0).astype(WIDE)
        for head in range(heads):
            cols = pl.ds(head * width, width)
            at = index * heads + head
            state = halves(state_ref[at])
            update = base_ref[rows, cols] - product(halves(w_ref[rows, cols]), state)
            upd_ref[rows, cols] = update
            out = carried * product(halves(q_ref[rows, cols]), state)
            out = out + product(halves(score_ref[at]), halves(update))
            mixed = out.astype(NARROW)
            out_ref[rows, cols] = mixed
            mixed = mixed.astype(WIDE)
            scale = lax.rsqrt(jnp.mean(mixed * mixed, axis=-1, keepdims=True) + norm_eps)
            gate = raw_ref[rows, pl.ds(3 * span + head * width, width)]
            normed = mixed * scale * gain_ref[...] * (gate * jax.nn.sigmoid(gate))
            normed_ref[rows, cols] = normed.astype(NARROW)
        return 0

    lax.fori_loop(0, count, third, 0)
    for k, block in enumerate(blocks):
        block[...] = unpack_rows(far_ref[...], normed_ref[...], k, total // n_fs)


def backward_kernel(heads, width, n_fs, shard_rows, *refs):
    pieces, refs = refs[:n_fs], refs[n_fs:]
    (win_ref, near_ref, far_ref, segcol_ref, poscol_ref, segrow_ref, edges_ref, z_ref, dgffn_ref,
     side_ref, hidden_ref, raw_ref, mixed_ref, q_ref, k_ref, inv_ref, score_ref, dots_ref, upd_ref, state_ref,
     move_ref, gradin_ref, *refs) = refs
    blocks, refs = refs[:n_fs], refs[n_fs:]
    (taps_ref, gain_ref, draw_ref, dhid_ref, dtaps_ref, sum_ref, small_ref, pad_ref, grad_ref, pdo_ref, dconv_ref, dout_ref, dnormed_ref) = refs
    total = raw_ref.shape[0]

    spread_side(heads, width, shard_rows, z_ref, side_ref, taps_ref, gain_ref)

    def enter(index, _):
        rows = pl.ds(pl.multiple_of(index * ENTER, ENTER), ENTER)
        dnormed_ref[rows, :] = pack_rows(near_ref[rows, :], pieces).astype(NARROW)
        return 0

    lax.fori_loop(0, total // ENTER, enter, 0)
    count = total // CHUNK
    span = heads * width
    fill_padded(raw_ref, pad_ref, 3 * span)

    def first(group, dgain):
        for sub in range(BACK_STEP):
            index = group * BACK_STEP + sub
            rows = pl.ds(pl.multiple_of(index * CHUNK, CHUNK), CHUNK)
            carried = jnp.where(segcol_ref[rows, :] == edges_ref[index, 0], 1.0, 0.0).astype(WIDE)
            for head in range(heads):
                cols = pl.ds(head * width, width)
                at = index * heads + head
                mixed = mixed_ref[rows, cols].astype(WIDE)
                scale = lax.rsqrt(jnp.mean(mixed * mixed, axis=-1, keepdims=True) + norm_eps)
                gate_cols = pl.ds(3 * span + head * width, width)
                gate = raw_ref[rows, gate_cols]
                sig = jax.nn.sigmoid(gate)
                given = dnormed_ref[rows, cols].astype(WIDE)
                unit = mixed * scale
                dgate = given * unit * gain_ref[...] * (sig * (1.0 + gate * (1.0 - sig)))
                draw_ref[rows, gate_cols] = dgate.astype(NARROW)
                given = given * (gate * sig)
                dgain = dgain + jnp.sum(given * unit, axis=0, keepdims=True)
                given = given * gain_ref[...]
                dout = scale * (given - unit * jnp.mean(unit * given, axis=-1, keepdims=True))
                dout = dout.astype(NARROW)
                dout_ref[rows, cols] = dout
                score_t = turned(score_ref[at])
                back = product_exact(score_t, dout)
                pdo_ref[rows, cols] = back
                inv_t = turned(inv_ref[at])
                back = product(inv_t, halves(back))
                query_t = turned(carried * q_ref[rows, cols])
                key_t = turned((beta_of(raw_ref, rows, 4 * span + head) * carried) * k_ref[rows, cols])
                grad_ref[at] = product_exact(query_t, dout) - product(key_t, halves(back))
        return dgain

    dgain = lax.fori_loop(0, count // BACK_STEP, first, jnp.zeros((1, width), WIDE))

    def second(step, grads):
        index = count - 1 - step
        result = []
        for head in range(heads):
            at = index * heads + head
            added = grad_ref[at]
            grad_ref[at] = grads[head]
            result.append(product(turned(move_ref[at]), halves(grads[head])) + added)
        return tuple(result)

    lax.fori_loop(0, count, second, tuple(jnp.zeros((width, width), WIDE) for _ in range(heads)))
    dconv_ref[total:total + HALO, :] = jnp.zeros((HALO, 3 * span), WIDE)

    def third(group, tap_sums):
        for sub in range(BACK_STEP):
            index = group * BACK_STEP + sub
            start = pl.multiple_of(index * CHUNK, CHUNK)
            rows = pl.ds(start, CHUNK)
            pos = poscol_ref[rows, :]
            strict, inclusive, carried, last = chunk_masks(
                segcol_ref[rows, :], segrow_ref[pl.ds(index, 1), :], edges_ref[index, 0], edges_ref[index, 1])
            new_sums = []
            dbetas = []
            for head in range(heads):
                cols = pl.ds(head * width, width)
                at = index * heads + head
                beta = beta_of(raw_ref, rows, 4 * span + head)
                query, key, update = q_ref[rows, cols], k_ref[rows, cols], upd_ref[rows, cols]
                query_h, key_h, update_h = halves(query), halves(key), halves(update)
                dout = dout_ref[rows, cols]
                state, grad = halves(state_ref[at]), halves(grad_ref[at])
                convs = []
                for which in range(3):
                    column = which * span + head * width
                    convs.append(conv_rows(pad_ref, taps_ref[which, :, head * width:(head + 1) * width], pos,
                                           start, column, width))
                gates = [jax.nn.sigmoid(c[0]) for c in convs]
                value = convs[2][0] * gates[2]
                dupdate = pdo_ref[rows, cols] + last * product(key_h, grad)
                dright = product(turned(inv_ref[at]), halves(dupdate))
                dright_h = halves(dright)
                dscore = jnp.where(inclusive, product_exact(update_h, dout, 1, 1, flip=True), 0.0)
                dsystem = jnp.where(strict, product(dright_h, update_h, 1, 1), 0.0)
                dscore_h = halves(dscore)
                dquery = carried * product_exact(state, dout, 1, 1, flip=True) + product(dscore_h, key_h)
                weighted = beta * dsystem
                scaled = beta * carried
                dkey = product(turned(dscore), query_h) + last * product(update_h, grad, 1, 1)
                dkey = dkey - product(halves(weighted + weighted.T), key_h)
                dkey = dkey - scaled * product(dright_h, state, 1, 1)
                dvalue = beta * dright
                seen = carried * product(key_h, state)
                dbeta = jnp.sum(dright * (value - seen), axis=-1, keepdims=True) - jnp.sum(
                    dsystem * dots_ref[at], axis=-1, keepdims=True)
                dbetas.append(dbeta * beta * (1.0 - beta))
                sides = []
                for grads, unit, conv, gate in ((dquery, query, convs[0][0], gates[0]), (dkey, key, convs[1][0], gates[1])):
                    plain = conv * gate
                    inv_norm = lax.rsqrt(jnp.sum(plain * plain, axis=-1, keepdims=True) + unit_eps)
                    sides.append(inv_norm * (grads - unit * jnp.sum(unit * grads, axis=-1, keepdims=True)))
                sides.append(dvalue)
                for which in range(3):
                    conv, plain, moved = convs[which]
                    gate = gates[which]
                    dconv = sides[which] * gate * (1.0 + conv * (1.0 - gate))
                    column = which * span + head * width
                    dconv_ref[rows, pl.ds(column, width)] = dconv
                    sums = [jnp.sum(dconv * plain, axis=0, keepdims=True)]
                    for shifted in moved:
                        sums.append(jnp.sum(dconv * shifted, axis=0, keepdims=True))
                    new_sums.append(jnp.concatenate(sums[::-1], axis=0))
            lane = lax.broadcasted_iota(jnp.int32, (CHUNK, draw_ref.shape[1] - 4 * span), 1)
            packed = jnp.zeros(lane.shape, WIDE)
            for head in range(heads):
                packed = jnp.where(lane == head, dbetas[head], packed)
            draw_ref[rows, pl.ds(4 * span, lane.shape[1])] = packed.astype(draw_ref.dtype)
            tap_sums = tuple(old + new for old, new in zip(tap_sums, new_sums))
        return tap_sums

    zero = tuple(jnp.zeros((taps_ref.shape[1], width), WIDE) for _ in range(3 * heads))
    sums = lax.fori_loop(0, count // BACK_STEP, third, zero)
    for head in range(heads):
        for which in range(3):
            dtaps_ref[which, :, head * width:(head + 1) * width] = sums[head * 3 + which]
    taps_count = taps_ref.shape[1]

    def fourth(index, _):
        start = pl.multiple_of(index * CHUNK, CHUNK)
        pos_window = poscol_ref[pl.ds(start, CHUNK + HALO), :]
        for which in range(3):
            columns = pl.ds(which * span, span)
            window = dconv_ref[pl.ds(start, CHUNK + HALO), columns]
            result = taps_ref[which, taps_count - 1:taps_count, :] * window[0:CHUNK]
            for offset in range(1, taps_count):
                part = jnp.where(pos_window >= offset, window, 0.0)[offset:offset + CHUNK]
                result = result + taps_ref[which, taps_count - 1 - offset:taps_count - offset, :] * part
            draw_ref[pl.ds(start, CHUNK), columns] = result.astype(draw_ref.dtype)
        return 0

    lax.fori_loop(0, count, fourth, 0)

    def weigh(index, _):
        rows = pl.ds(pl.multiple_of(index * ENTER, ENTER), ENTER)
        sum_ref[...] += plain_dot(hidden_ref[rows, :], draw_ref[rows, :], 0, 0)
        return 0

    sum_ref[...] = jnp.zeros(sum_ref.shape, WIDE)
    lax.fori_loop(0, total // ENTER, weigh, 0)
    features = small_ref.shape[1]
    small_ref[...] = jnp.zeros(small_ref.shape, WIDE)
    small_ref[heads + 1:heads + 2, :] = dgffn_ref[...]
    own = pl.ds(pl.multiple_of(z_ref[0] * span, span), span)
    for which in range(3):
        first_row = heads + 2 + which * taps_count
        small_ref[first_row:first_row + taps_count, own] = dtaps_ref[which]
    last_row = heads + 2 + 3 * taps_count
    small_ref[last_row:last_row + 1, :] = product_exact(
        halves(jnp.broadcast_to(dgain, (8, width))), shard_places(width, features, shard_rows, False))[0:1]
    gain = win_ref[:, 4 * span + heads:4 * span + heads + 1].astype(WIDE)
    across = jnp.sum(sum_ref[...] * win_ref[...].astype(WIDE), axis=-1, keepdims=True) / gain
    beside = small_ref[...].T
    lane = lax.broadcasted_iota(jnp.int32, beside.shape, 1)
    gradin_ref[:, 0:4 * span] = sum_ref[:, 0:4 * span].astype(NARROW)
    beside = sum_ref[:, 4 * span:] + beside + jnp.where(lane == heads, across, 0.0)
    gradin_ref[:, 4 * span:] = beside.astype(NARROW)

    def leave(index, _):
        rows = pl.ds(pl.multiple_of(index * ENTER, ENTER), ENTER)
        dhid_ref[rows, :] = plain_dot(draw_ref[rows, :], win_ref[...], 1, 1).astype(NARROW)
        return 0

    lax.fori_loop(0, total // ENTER, leave, 0)
    for k, block in enumerate(blocks):
        block[...] = unpack_rows(far_ref[...], dhid_ref[...], k, total // n_fs)


def product_exact(left, exact, left_dim=1, right_dim=0, flip=False):
    def one(a):
        if flip:
            return lax.dot_general(exact, a, (((right_dim,), (left_dim,)), ((), ())), preferred_element_type=WIDE)
        return lax.dot_general(a, exact, (((left_dim,), (right_dim,)), ((), ())), preferred_element_type=WIDE)

    if PASSES == 1:
        return one(left[0])
    return one(left[0]) + one(left[1])


def cost(flops, size):
    return pl.CostEstimate(flops=flops, bytes_accessed=size, transcendentals=0)


def specs(count):
    return [pl.BlockSpec(memory_space=pltpu.VMEM)] * count


def anywhere():
    return pl.BlockSpec(memory_space=pl.ANY)


def in_scalars():
    return pl.BlockSpec(memory_space=pltpu.SMEM)


def delta_forward(pieces, w_in, near, far, segcol, poscol, segrow, edges, z, heads, width, n_taps, shard_rows):
    n_fs = len(pieces)
    total = near.shape[0]
    features, lanes = w_in.shape
    count = total // CHUNK
    span = heads * width
    thin = jax.ShapeDtypeStruct((total, span), NARROW)
    rows = jax.ShapeDtypeStruct((total, span), WIDE)
    full = jax.ShapeDtypeStruct((total, features), NARROW)
    square = jax.ShapeDtypeStruct((count * heads, CHUNK, CHUNK), WIDE)
    state = jax.ShapeDtypeStruct((count * heads, width, width), WIDE)
    block = jax.ShapeDtypeStruct((total // n_fs, span), NARROW)
    raw = jax.ShapeDtypeStruct((total, lanes), WIDE)
    side = jax.ShapeDtypeStruct((lanes - 4 * span, features), WIDE)
    result = pl.pallas_call(
        functools.partial(forward_kernel, heads, width, n_fs, shard_rows),
        out_shape=(block,) * n_fs
        + (side, full, raw, thin, rows, rows, square, square, square, rows, state, state),
        in_specs=specs(n_fs + 6) + [in_scalars()] * 2,
        out_specs=tuple(specs(n_fs + 12)),
        scratch_shapes=[
            pltpu.VMEM((3, n_taps, span), WIDE),
            pltpu.VMEM((1, width), WIDE),
            pltpu.VMEM((total + HALO, 3 * span), WIDE),
            pltpu.VMEM((total, span), WIDE),
            pltpu.VMEM((total, span), WIDE),
            pltpu.VMEM((total, span), NARROW),
        ],
        compiler_params=pltpu.CompilerParams(vmem_limit_bytes=60 << 20),
        cost_estimate=cost(30_000_000_000, 16 << 20),
        name="delta_forward",
    )(*pieces, w_in, near, far, segcol, poscol, segrow, edges, z)
    return result[:n_fs], result[n_fs], result[n_fs + 1 :]


def delta_backward(pieces, w_in, near, far, segcol, poscol, segrow, edges, z, dgffn, side, kept, heads, width, n_taps, shard_rows):
    n_fs = len(pieces)
    total = near.shape[0]
    features, lanes = w_in.shape
    count = total // CHUNK
    span = heads * width
    block = jax.ShapeDtypeStruct((total // n_fs, features), NARROW)
    result = pl.pallas_call(
        functools.partial(backward_kernel, heads, width, n_fs, shard_rows),
        out_shape=(jax.ShapeDtypeStruct((features, lanes), NARROW),) + (block,) * n_fs,
        in_specs=specs(n_fs + 6) + [in_scalars()] * 2 + specs(13),
        out_specs=tuple(specs(n_fs + 1)),
        scratch_shapes=[
            pltpu.VMEM((3, n_taps, span), WIDE),
            pltpu.VMEM((1, width), WIDE),
            pltpu.VMEM((total, lanes), NARROW),
            pltpu.VMEM((total, features), NARROW),
            pltpu.VMEM((3, n_taps, span), WIDE),
            pltpu.VMEM((features, lanes), WIDE),
            pltpu.VMEM((lanes - 4 * span, features), WIDE),
            pltpu.VMEM((total + HALO, 3 * span), WIDE),
            pltpu.VMEM((count * heads, width, width), WIDE),
            pltpu.VMEM((total, span), WIDE),
            pltpu.VMEM((total + HALO, 3 * span), WIDE),
            pltpu.VMEM((total, span), NARROW),
            pltpu.VMEM((total, span), NARROW),
        ],
        compiler_params=pltpu.CompilerParams(vmem_limit_bytes=52 << 20),
        cost_estimate=cost(40_000_000_000, 16 << 20),
        name="delta_backward",
    )(*pieces, w_in, near, far, segcol, poscol, segrow, edges, z, dgffn, side, *kept)
    return result[0], list(result[1:])


def finish_kernel(heads, span, n_taps, z_ref, *refs):
    n_fs = len(refs) - 10
    pieces, refs = refs[:n_fs], refs[n_fs:]
    (*grads, wout_ref, beta_ref, taps_ref, gmix_ref, gffn_ref, ghead_ref) = refs
    side = pl.ds(4 * span, 128)
    lane = lax.broadcasted_iota(jnp.int32, (128, beta_ref.shape[0]), 0)
    column = lax.broadcasted_iota(jnp.int32, (128, beta_ref.shape[0]), 1)
    wout = jnp.zeros(wout_ref.shape, WIDE)
    small = jnp.zeros((wout_ref.shape[0], 128), WIDE)
    beta = jnp.zeros(beta_ref.shape, WIDE)
    for k, piece in enumerate(pieces):
        line = lax.rem(z_ref[0] + n_fs - k, n_fs)
        place = pl.ds(pl.multiple_of(line * span, span), span)
        for which, grad in enumerate(grads):
            grad[:, place] = piece[:, which * span:(which + 1) * span].astype(WIDE)
        wout = wout + piece[:, 4 * span + 128:].astype(WIDE)
        beside = piece[:, side]
        small = small + beside.astype(WIDE)
        chosen = jnp.where((lane < heads) & (column == line * heads + lane), 1.0, 0.0)
        beta = beta + plain_dot(chosen.astype(NARROW), beside, 0, 1)
    wout_ref[...] = wout
    beta_ref[...] = beta
    small = small.T
    gmix_ref[...] = small[heads:heads + 1]
    gffn_ref[...] = small[heads + 1:heads + 2]
    last_row = heads + 2 + 3 * n_taps
    for which in range(3):
        first_row = heads + 2 + which * n_taps
        taps_ref[which] = small[first_row:first_row + n_taps]
    ghead_ref[...] = small[last_row:last_row + 1, :ghead_ref.shape[1]]


def finish(z, pieces, heads, span, n_taps, head_rows):
    rows = pieces[0].shape[0]
    n_fs = len(pieces)
    full = jax.ShapeDtypeStruct((rows, n_fs * span), WIDE)
    line = jax.ShapeDtypeStruct((1, rows), WIDE)
    return pl.pallas_call(
        functools.partial(finish_kernel, heads, span, n_taps),
        out_shape=(full,) * 5
        + (
            jax.ShapeDtypeStruct((n_fs * heads, rows), WIDE),
            jax.ShapeDtypeStruct((3, n_taps, rows), WIDE),
            line,
            line,
            jax.ShapeDtypeStruct((1, head_rows), WIDE),
        ),
        in_specs=[in_scalars()] + specs(n_fs),
        out_specs=tuple(specs(10)),
        cost_estimate=cost(1_000_000, 1 << 20),
        name="finish_inputs",
    )(z, *pieces)


def mix_out_kernel(n_fs, row, z_ref, *refs):
    pieces, refs = refs[:n_fs], refs[n_fs:]
    wout_ref, tokens_ref, gain_ref, middle_ref, ffn_ref, normed_ref = refs
    span = pieces[0].shape[1]
    middle = tokens_ref[...].astype(WIDE)
    for k, piece in enumerate(pieces):
        place = pl.ds(pl.multiple_of(lax.rem(z_ref[0] + n_fs - k, n_fs) * span, span), span)
        normed_ref[:, place] = piece[...]
        middle = middle + plain_dot(piece[...], wout_ref[place, :])
    middle_ref[...] = middle
    scale = lax.rsqrt(jnp.mean(middle * middle, axis=-1, keepdims=True) + norm_eps)
    ffn_ref[...] = (middle * scale * gain_ref[row:row + 1, :]).astype(NARROW)


def mix_out(z, pieces, w_out, tokens, side, row):
    n_fs = len(pieces)
    shape = tokens.shape
    return pl.pallas_call(
        functools.partial(mix_out_kernel, n_fs, row),
        out_shape=(
            jax.ShapeDtypeStruct(shape, WIDE),
            jax.ShapeDtypeStruct(shape, NARROW),
            jax.ShapeDtypeStruct(shape, NARROW),
        ),
        in_specs=[in_scalars()] + specs(n_fs + 3),
        out_specs=tuple(specs(3)),
        compiler_params=pltpu.CompilerParams(vmem_limit_bytes=40 << 20),
        cost_estimate=cost(2_000_000_000, 6 << 20),
        name="mix_out",
    )(z, *pieces, w_out, tokens, side)


def ffn_kernel(keys, unit, block_ref, *refs):
    count = TP
    rows_in, refs = refs[:count], refs[count:]
    cots, refs = refs[:count], refs[count:]
    weights, refs = refs[:len(keys)], refs[len(keys):]
    (wdown_ref, active_ref, dboth_ref, sent_ref, later_ref, own_ref, part_ref, *ordered) = refs
    own_rows = rows_in[0].shape[0]
    if ordered:
        for near, far in zip(weights, ordered):
            n_fs, size = near.shape[:2]
            for by in range(n_fs):
                line = lax.rem(block_ref[1] + n_fs - by, n_fs)
                for at in range(size // unit):
                    place = pl.ds(pl.multiple_of((at * n_fs + line) * unit, unit), unit)
                    far[place, :] = near[by, at * unit:(at + 1) * unit, :]
        weights = ordered
    depth = weights[0].shape[0]
    units = wdown_ref.shape[0]
    spots = [pl.ds(pl.multiple_of((block_ref[0] ^ key) * depth, depth), depth) for key in keys]
    half = count // 2 * own_rows
    for at in range(count - 1, -1, -1):
        rows = slice(at * own_rows, (at + 1) * own_rows)
        both = plain_dot(rows_in[at][:, spots[0]], weights[0][...])
        for spot, weight in zip(spots[1:], weights[1:]):
            both = both + plain_dot(rows_in[at][:, spot], weight[...])
        gate, up = both[:, :units], both[:, units:]
        sig = jax.nn.sigmoid(gate)
        silu = gate * sig
        active_ref[rows, :] = (silu * up).astype(NARROW)
        dactive = plain_dot(cots[at][...], wdown_ref[...], 1, 1)
        dboth_ref[rows, :units] = (dactive * up * (sig * (1.0 + gate * (1.0 - sig)))).astype(NARROW)
        dboth_ref[rows, units:] = (dactive * silu).astype(NARROW)
        dboth = dboth_ref[rows, :]
        for spot, weight in zip(spots, weights):
            part_ref[:, spot] = plain_dot(dboth, weight[...], 1, 1)
        if at >= count // 2:
            place = at * own_rows - half
            sent_ref[place:place + own_rows, :] = part_ref[...].astype(NARROW)
        elif at:
            later_ref[(at - 1) * own_rows:at * own_rows, :] = part_ref[...]
        else:
            own_ref[...] = part_ref[...]


def ffn_units(block, rows_in, cots, weights, keys, w_down, unit):
    own_rows, features = rows_in[0].shape
    units = w_down.shape[0]
    total = TP * own_rows
    return pl.pallas_call(
        functools.partial(ffn_kernel, keys, unit),
        out_shape=(
            jax.ShapeDtypeStruct((total, units), NARROW),
            jax.ShapeDtypeStruct((total, 2 * units), NARROW),
            jax.ShapeDtypeStruct((total // 2, features), NARROW),
            jax.ShapeDtypeStruct((total // 2 - own_rows, features), WIDE),
            jax.ShapeDtypeStruct((own_rows, features), WIDE),
        ),
        in_specs=[in_scalars()] + specs(2 * TP + len(weights) + 1),
        out_specs=tuple(specs(5)),
        scratch_shapes=[pltpu.VMEM((own_rows, features), WIDE)]
        + [pltpu.VMEM((features // len(keys), 2 * units), NARROW) for w in weights if w.ndim == 3],
        compiler_params=pltpu.CompilerParams(vmem_limit_bytes=52 << 20),
        cost_estimate=cost(8_000_000_000, 16 << 20),
        name="ffn_units",
    )(block, *rows_in, *cots, *weights, w_down)


def mix_back_kernel(n_fs, row, z_ref, *refs):
    sources, refs = refs[:6], refs[6:]
    gain_ref, refs = refs[0], refs[1:]
    blocks, refs = refs[:n_fs], refs[n_fs:]
    (dmiddle_ref, dbranch_ref, dgain_ref, *places, sems) = refs
    fetches = [pltpu.make_async_copy(source, place, sems.at[k]) for k, (source, place) in enumerate(
        zip((sources[0], sources[1].at[pl.ds(0, places[1].shape[0])], *sources[2:5]), places))]
    quarter = places[5].shape[0] // 4
    parts = [pl.ds(k * quarter, quarter) for k in range(4)]
    fetches += [
        pltpu.make_async_copy(sources[5].at[part], places[5].at[part], sems.at[5 + k]) for k, part in enumerate(parts)
    ]
    for fetch in fetches:
        fetch.start()
    own_ref, core_ref, side_ref, middle_ref, cot_ref, wout_ref = places
    for fetch in fetches[:5]:
        fetch.wait()
    middle = middle_ref[...]
    given = own_ref[...] + core_ref[...].astype(WIDE) + side_ref[...].astype(WIDE)
    scale = lax.rsqrt(jnp.mean(middle * middle, axis=-1, keepdims=True) + norm_eps)
    unit = middle * scale
    dgain_ref[...] = jnp.sum(given * unit, axis=0, keepdims=True)
    given = given * gain_ref[row:row + 1, :]
    dmiddle = cot_ref[...].astype(WIDE) + scale * (given - unit * jnp.mean(unit * given, axis=-1, keepdims=True))
    dmiddle_ref[...] = dmiddle
    dbranch = dmiddle.astype(NARROW)
    dbranch_ref[...] = dbranch
    span = blocks[0].shape[1]
    for fetch in fetches[5:]:
        fetch.wait()
    for k, block in enumerate(blocks):
        place = pl.ds(pl.multiple_of(lax.rem(z_ref[0] + k, n_fs) * span, span), span)
        block[...] = plain_dot(dbranch, wout_ref[place, :], 1, 1).astype(NARROW)


def mix_back(z, parts, middle, side, row, cotangent, w_out, n_fs):
    count, features = middle.shape
    block = jax.ShapeDtypeStruct((count, features // n_fs), NARROW)
    sources = (*parts, middle, cotangent, w_out)
    result = pl.pallas_call(
        functools.partial(mix_back_kernel, n_fs, row),
        out_shape=(block,) * n_fs
        + (
            jax.ShapeDtypeStruct(middle.shape, WIDE),
            jax.ShapeDtypeStruct(middle.shape, NARROW),
            jax.ShapeDtypeStruct((1, features), WIDE),
        ),
        in_specs=[in_scalars()] + [anywhere()] * 6 + specs(1),
        out_specs=tuple(specs(n_fs + 3)),
        scratch_shapes=[pltpu.VMEM((min(part.shape[0], count) if k < 5 else part.shape[0], features), part.dtype) for k, part in enumerate(sources)] + [pltpu.SemaphoreType.DMA((9,))],
        compiler_params=pltpu.CompilerParams(vmem_limit_bytes=60 << 20),
        cost_estimate=cost(2_000_000_000, 6 << 20),
        name="mix_back",
    )(z, *sources, side)
    return (result[:n_fs],) + tuple(result[n_fs:])


def rms_scale(values, gain):
    return values * lax.rsqrt(jnp.mean(values * values, axis=-1, keepdims=True) + norm_eps) * gain


def swiglu(gate_proj, up_proj):
    return jax.nn.silu(gate_proj) * up_proj


def sequence_layout(lengths_row, total):
    ends = jnp.cumsum(lengths_row)
    index = jnp.arange(total, dtype=jnp.int32)
    before = index[:, None] >= ends[None, :]
    segment = jnp.sum(before.astype(jnp.int32), axis=1)
    start = jnp.sum(jnp.where(before, lengths_row[None, :], 0), axis=1)
    return (segment, index - start)


def project(left, right):
    return jnp.dot(left, right, preferred_element_type=WIDE)


def project_back(left, right):
    return lax.dot_general(left, right, (((1,), (1,)), ((), ())), preferred_element_type=WIDE)


def weight_grad(left, right):
    return lax.dot_general(left, right, (((0,), (0,)), ((), ())), preferred_element_type=WIDE)


def flip(value, bit, n_dp):
    return lax.ppermute(value, "dp", [(i, i ^ bit) for i in range(n_dp)])


def shift(value, by, n_fs):
    return lax.ppermute(value, "fsdp", [(i, (i + by) % n_fs) for i in range(n_fs)])


def line_pieces(shard, n_fs):
    return [shard] + [shift(shard, by, n_fs) for by in range(1, n_fs)]


def line_order(pieces, z):
    n_fs = len(pieces)
    shape = pieces[0].shape
    whole = jnp.zeros((shape[0], n_fs) + shape[1:], pieces[0].dtype)
    for by, piece in enumerate(pieces):
        whole = lax.dynamic_update_slice_in_dim(whole, piece[:, None], lax.rem(z + n_fs - by, n_fs), 1)
    return whole


def gather_cube(piece, order, n_dp):
    pieces = {0: piece}
    for bit in order:
        for key in list(pieces):
            pieces[key ^ bit] = flip(pieces[key], bit, n_dp)
    return pieces


def in_order(pieces, me):
    rows = pieces[0].shape[0]
    whole = jnp.zeros((len(pieces) * rows,) + pieces[0].shape[1:], pieces[0].dtype)
    unit = max(pieces).bit_length()
    step = (1 << unit) // len(pieces)
    for key, piece in pieces.items():
        whole = lax.dynamic_update_slice_in_dim(whole, piece, lax.bitwise_xor(me, key // step) * rows, 0)
    return whole


def per_device(
    n_dp,
    n_fs,
    tokens,
    lengths,
    packing,
    w_query,
    w_key,
    w_value,
    w_gate,
    w_beta,
    conv_taps,
    w_out,
    gain_mix,
    gain_head,
    gain_ffn,
    w_ffn_gate,
    w_ffn_up,
    w_ffn_down,
    cotangent,
):
    me = lax.axis_index("dp")
    z = lax.axis_index("fsdp")
    bits = [1 << k for k in range(n_dp.bit_length() - 1)]
    first_order = bits[:1] + bits[1:]
    second_order = bits[:1] + bits[1:][::-1]
    packing_row = packing[0]
    lengths_row = lengths[0]
    own_rows, features = tokens.shape
    total = own_rows * n_fs
    rows = w_query.shape[0]
    heads_all = w_beta.shape[1]
    heads = heads_all // n_fs
    span = features // n_fs
    width = span // heads
    hidden_ffn = w_ffn_gate.shape[1]
    head_rows = gain_head.shape[0]
    n_taps = conv_taps.shape[1]

    def by_owner(matrix):
        return jnp.swapaxes(matrix.reshape(rows, n_fs, -1), 0, 1)

    small = jnp.concatenate(
        [
            gain_mix[:, None],
            gain_ffn[:, None],
            conv_taps.reshape(3 * n_taps, rows).T,
            jnp.pad(gain_head, (0, rows - head_rows))[:, None],
        ],
        axis=1,
    )
    n_small = small.shape[1]
    side = jnp.concatenate(
        [by_owner(w_beta), jnp.broadcast_to(small[None], (n_fs, rows, n_small))], axis=2
    )
    side = jnp.pad(side, ((0, 0), (0, 0), (0, 128 - heads - n_small)))
    packet = jnp.concatenate(
        [by_owner(w_query), by_owner(w_key), by_owner(w_value), by_owner(w_gate), side], axis=2
    )
    member = lax.rem(me, TP)
    block = me // TP
    n_rest = n_dp // TP
    ff_block = hidden_ffn // n_dp
    ff_line = ff_block // n_fs
    ff_unit = -(-ff_line // 8) * 8
    while n_rest * n_fs * ff_unit % 128:
        ff_unit += 8
    ff_pad = n_rest * n_fs * ff_unit
    tp_bits = [bit for bit in bits if bit < TP]
    rest_bits = [bit for bit in bits if bit >= TP]

    def by_member(matrix):
        split = matrix.reshape(rows, n_rest, TP, n_fs, ff_line)
        split = jnp.pad(split, ((0, 0),) * 4 + ((0, ff_unit - ff_line),))
        return jnp.transpose(split, (2, 0, 1, 3, 4)).reshape(TP, rows, ff_pad)

    def hand_out(blocks):
        pieces = [lax.dynamic_index_in_dim(blocks, z, 0)]
        for by in range(1, n_fs):
            pieces.append(shift(lax.dynamic_index_in_dim(blocks, lax.rem(z + by, n_fs), 0), by, n_fs))
        return pieces

    lanes = 4 * span + 128
    packet = jnp.concatenate([packet, jnp.broadcast_to(w_out[None], (n_fs,) + w_out.shape)], axis=2)
    packet = hand_out(packet)
    token_pieces = [tokens] + [shift(tokens, by, n_fs) for by in range(1, n_fs)]
    packet, token_pieces[1] = lax.optimization_barrier((packet, token_pieces[1]))
    packet_in = line_order([piece[:, :, :lanes] for piece in packet], z).reshape(n_fs * rows, lanes)
    packet_out = line_order([piece[:, :, lanes:] for piece in packet], z).reshape(n_fs * rows, features)
    w_in = lax.all_gather(packet_in, "dp", axis=0, tiled=True)
    full_out = lax.all_gather(packet_out, "dp", axis=0, tiled=True)

    owner, place = packing_row // own_rows, lax.rem(packing_row, own_rows)
    near = (lax.rem(z + n_fs - owner, n_fs) * own_rows + place)[:, None]
    far = (lax.rem(owner + n_fs - z, n_fs) * own_rows + place)[None]
    segment, position = sequence_layout(lengths_row, total)
    seg_rows = segment.reshape(-1, CHUNK)
    ends = seg_rows[:, -1]
    edges = jnp.stack([jnp.concatenate([jnp.full((1,), -1, jnp.int32), ends[:-1]]), ends], axis=1)
    z_ref = z.reshape(1)
    layout = (segment[:, None], jnp.pad(position, (0, HALO))[:, None], seg_rows, edges, z_ref)
    shard_rows = (rows, head_rows)
    own_gate, own_up, _ = lax.optimization_barrier((w_ffn_gate, w_ffn_up, token_pieces[1]))
    both_sends = jnp.concatenate([by_member(own_gate), by_member(own_up)], axis=2)
    blocks, side, kept = delta_forward(
        token_pieces, w_in, near, far, *layout, heads, width, n_taps, shard_rows
    )
    gain_row = heads + 1

    both_pieces = {
        key: flip(lax.dynamic_index_in_dim(both_sends, member ^ key, 0, keepdims=False), key, n_dp)
        if key
        else lax.dynamic_index_in_dim(both_sends, member, 0, keepdims=False)
        for key in range(TP)
    }
    own_down, _ = lax.optimization_barrier((w_ffn_down, token_pieces[1]))
    own_down = jnp.pad(own_down, ((0, ff_unit - ff_line), (0, 0)))
    down_rows = in_order(gather_cube(own_down, rest_bits, n_dp), block).reshape(n_rest, -1, features)
    both_rows = in_order(both_pieces, member).reshape(TP, rows, 2 * ff_pad)
    own_cotangent, both_rows, down_rows = lax.optimization_barrier((cotangent, both_rows, down_rows))
    both_rows, down_rows, _ = lax.optimization_barrier((both_rows, down_rows, token_pieces))
    both_line = line_pieces(both_rows, n_fs)
    both_line, blocks, down_rows = lax.optimization_barrier((both_line, blocks, down_rows))
    if rows % 16 == 0:
        both_rows = jnp.stack([piece.reshape(TP * rows, 2 * ff_pad) for piece in both_line])
    else:
        both_rows = line_order(both_line, z).reshape(-1, 2 * ff_pad)
    both_pieces = gather_cube(both_rows, rest_bits, n_dp)
    unit = 1 << (TP.bit_length() - 1)
    rest_keys = [key // unit for key in both_pieces]
    tp_order = sorted(range(TP), key=lambda key: tuple((key & bit) != 0 for bit in tp_bits))

    cot_pieces = gather_cube(own_cotangent, tp_bits[::-1], n_dp)
    cot_pieces, blocks = lax.optimization_barrier((cot_pieces, blocks))

    def halve(value, index, some_bits):
        unit = some_bits[0] if some_bits else 1
        for bit in some_bits[::-1]:
            half = value.shape[0] // 2
            mine = (index // (bit // unit)) % 2
            sent = lax.dynamic_slice_in_dim(value, (1 - mine) * half, half, 0)
            value = lax.dynamic_slice_in_dim(value, mine * half, half, 0)
            value = value.astype(WIDE) + flip(sent.astype(NARROW), bit, n_dp).astype(WIDE)
        return value

    def sum_up(pieces, whole):
        total = lax.dynamic_index_in_dim(whole, z, 0, keepdims=False).astype(WIDE)
        for piece in pieces[1:]:
            total = total + piece[0].astype(WIDE)
        return total

    def pass_on(parts):
        return [parts[0]] + [shift(part, by, n_fs) for by, part in enumerate(parts) if by]

    mixed_pieces = pass_on(blocks)
    down_line = line_pieces(down_rows, n_fs)
    middle, ffn_in, normed_b = mix_out(z_ref, mixed_pieces, full_out, tokens, side, gain_row)
    w_down = line_order(down_line, z).reshape(ff_pad, features)
    ffn_pieces = gather_cube(ffn_in, tp_bits[::-1], n_dp)
    active_b, d_both, first, second, d_own = ffn_units(
        jnp.stack([block, z]),
        [ffn_pieces[key] for key in tp_order],
        [cot_pieces[key] for key in tp_order],
        list(both_pieces.values()),
        rest_keys,
        w_down,
        rows,
    )
    ffn_near = jnp.concatenate([ffn_pieces[key] for key in tp_order], axis=0)

    def both_part(lo, size):
        part = weight_grad(lax.dynamic_slice_in_dim(ffn_near, lo, size, 1), d_both)
        return part.reshape(-1, n_fs * rows, 2 * ff_pad)

    cotangent_near = jnp.concatenate([cot_pieces[key] for key in tp_order], axis=0)
    down_terms = weight_grad(active_b, cotangent_near).astype(NARROW)
    down_sum = lax.psum_scatter(
        down_terms.reshape(n_rest, -1, features), "fsdp", scatter_dimension=1, tiled=True
    )
    d_both, down_terms = lax.optimization_barrier((d_both, down_terms))
    split = features // 2 if rest_bits else features
    top = block // max(n_rest // 2, 1)
    if rest_bits:
        both_sent = both_part((1 - top) * split, split).astype(NARROW)
    else:
        both_sent = None
    from_core = flip(first, tp_bits[0], n_dp)
    second = second + from_core[own_rows:].astype(WIDE)
    second, both_sent, active_late = lax.optimization_barrier((second.astype(NARROW), both_sent, active_b))
    from_side = flip(second, tp_bits[1], n_dp)
    from_side, ffn_near, active_late = lax.optimization_barrier((from_side, ffn_near, active_late))
    both_sum = both_part(top * split if rest_bits else 0, split)

    d_blocks, d_middle, d_branch, d_gffn = mix_back(
        z_ref, (d_own, from_core, from_side), middle, side, gain_row, cotangent, full_out, n_fs
    )
    d_pieces = pass_on(d_blocks)
    d_branch, active_late = lax.optimization_barrier((d_branch, active_late))

    def out_term(units, lo):
        return project(units[lo * own_rows : (lo + 1) * own_rows], w_down)

    out_core = flip(project(active_late[2 * own_rows :], w_down).astype(NARROW), tp_bits[0], n_dp)
    out_sent = (out_term(active_late, 1) + out_core[own_rows:].astype(WIDE)).astype(NARROW)
    if rest_bits:
        both_came, out_sent = lax.optimization_barrier((flip(both_sent, rest_bits[-1], n_dp), out_sent))
        both_sum = both_sum + both_came.astype(WIDE)
        both_sum = halve(both_sum, block, rest_bits[:-1])
    out_side = flip(out_sent, tp_bits[1], n_dp)
    out_grad = weight_grad(normed_b, d_branch).astype(NARROW)
    sum_out = lax.psum_scatter(out_grad, "dp", scatter_dimension=0, tiled=True)
    both_sum = jnp.swapaxes(both_sum.reshape(TP, n_fs, rows, 2 * ff_pad), 0, 1)
    both_sum, d_pieces, out_grad = lax.optimization_barrier((both_sum, d_pieces, out_grad))
    both_line = hand_out(both_sum.astype(NARROW))

    grad_in, d_blocks = delta_backward(
        d_pieces, w_in, near, far, *layout, d_gffn, side, kept, heads, width, n_taps, shard_rows
    )
    grad_in, both_line, down_sum, sum_out = lax.optimization_barrier((grad_in, both_line, down_sum, sum_out))
    part = lax.psum_scatter(grad_in, "dp", scatter_dimension=0, tiled=True)
    d_blocks, both_line, active_late = lax.optimization_barrier((d_blocks, both_line, active_late))
    d_blocks = pass_on(d_blocks)
    layer_out = middle + out_term(active_late, 0) + out_core[:own_rows].astype(WIDE) + out_side.astype(WIDE)
    layer_out = layer_out.astype(NARROW)
    both_sum = sum_up(both_line, both_sum)
    grad_fdown = halve(down_sum, block, rest_bits)[0, :ff_line].astype(WIDE)
    both_pieces = {
        key: flip(
            lax.dynamic_index_in_dim(both_sum, member ^ key, 0, keepdims=False).astype(NARROW), key, n_dp
        ).astype(WIDE)
        if key
        else lax.dynamic_index_in_dim(both_sum, member, 0, keepdims=False)
        for key in range(TP)
    }
    both_mine = in_order({key: piece[None] for key, piece in both_pieces.items()}, member)
    def units_of(which):
        part = both_mine[:, :, which * ff_pad : (which + 1) * ff_pad]
        part = part.reshape(TP, rows, n_rest, n_fs, ff_unit)[..., :ff_line]
        return jnp.transpose(part, (1, 2, 0, 3, 4)).reshape(rows, hidden_ffn)

    lanes = part.shape[1]
    joint = jnp.concatenate([part, sum_out], axis=1).reshape(n_fs, rows, -1)
    arrived = [piece[0] for piece in hand_out(joint)]
    d_blocks, arrived[0], layer_out = lax.optimization_barrier((d_blocks, arrived[0], layer_out))
    d_hidden = d_blocks[0].astype(WIDE)
    for block_of in d_blocks[1:]:
        d_hidden = d_hidden + block_of.astype(WIDE)
    _, norm_mix_back = jax.vjp(rms_scale, tokens.astype(WIDE), side[heads])
    d_inputs_norm, _ = norm_mix_back(d_hidden)
    grad_tokens = d_middle + d_inputs_norm

    grads, (grad_wout, grad_beta, grad_taps, grad_gmix, grad_gffn, grad_ghead) = (
        lambda outs: (outs[:4], outs[4:])
    )(finish(z_ref, arrived, heads, span, n_taps, head_rows))
    return (
        layer_out,
        grad_tokens,
        grads[0],
        grads[1],
        grads[2],
        grads[3],
        grad_beta.T,
        grad_taps,
        grad_wout,
        grad_gmix[0],
        grad_ghead[0],
        grad_gffn[0],
        units_of(0),
        units_of(1),
        grad_fdown,
    )


def solution(mesh):
    both = ("dp", "fsdp")
    rows = P(both, None)
    group = P("dp", None)
    taps = P(None, None, both)
    line = P(both)
    in_specs = (rows, group, group) + (rows,) * 5 + (taps, rows, line, line, line) + (rows,) * 4
    out_specs = (rows,) * 7 + (taps, rows, line, line, line) + (rows,) * 3
    return jax.shard_map(
        functools.partial(per_device, mesh.shape["dp"], mesh.shape["fsdp"]),
        mesh=mesh,
        in_specs=in_specs,
        out_specs=out_specs,
        check_vma=False,
    )
```

```python
import functools

import jax
import jax.numpy as jnp
from jax import lax
from jax.experimental import pallas as pl
from jax.experimental.pallas import tpu as pltpu
from jax.sharding import PartitionSpec as P

CHUNK = 128
TP = 4
PER_STEP = 4
BACK_STEP = 4
ENTER = 512
HALO = 8
norm_eps = 1e-05
unit_eps = 1e-06
NARROW = jnp.bfloat16
WIDE = jnp.float32


def halves(value):
    top = value.astype(NARROW)
    return top, (value - top.astype(WIDE)).astype(NARROW)


def product(left, right, left_dim=1, right_dim=0):
    dims = (((left_dim,), (right_dim,)), ((), ()))

    def one(a, b):
        return lax.dot_general(a, b, dims, preferred_element_type=WIDE)

    if PASSES == 1:
        return one(left[0], right[0])
    return one(left[0], right[0]) + (one(left[0], right[1]) + one(left[1], right[0]))


PASSES = 3


def turned(value):
    return halves(value.T)


def chunk_masks(seg_col, seg_row, before, after):
    size = seg_col.shape[0]
    down = lax.broadcasted_iota(jnp.int32, (size, size), 0)
    across = lax.broadcasted_iota(jnp.int32, (size, size), 1)
    same = seg_col == seg_row
    strict = same & (down > across)
    inclusive = same & (down >= across)
    carried = jnp.where(seg_col == before, 1.0, 0.0).astype(WIDE)
    last = jnp.where(seg_col == after, 1.0, 0.0).astype(WIDE)
    return strict, inclusive, carried, last


def unit_lower_inverses(systems):
    size = systems[0].shape[0]
    down = lax.broadcasted_iota(jnp.int32, (size, size), 0)
    across = lax.broadcasted_iota(jnp.int32, (size, size), 1)
    gap = jnp.where(down > across, down ^ across, 0)
    eye = jnp.where(down == across, 1.0, 0.0)
    results = [eye - jnp.where(gap == 1, system, 0.0) for system in systems]
    step = 2
    while step < size:
        picked = (gap >= step) & (gap < 2 * step)
        parts = [jnp.where(picked, system, 0.0).astype(NARROW) for system in systems]
        done = [result.astype(NARROW) for result in results]
        inner = [plain_dot(part, own).astype(NARROW) for part, own in zip(parts, done)]
        results = [result - plain_dot(own, side) for result, own, side in zip(results, done, inner)]
        step *= 2
    left = [eye - result - product(halves(system), halves(result)) for system, result in zip(systems, results)]
    results = [
        result + plain_dot(result.astype(NARROW), rest.astype(NARROW)) for result, rest in zip(results, left)
    ]
    return results


def conv_rows(pad_ref, taps, pos, start, column, width):
    window = pad_ref[pl.ds(start, CHUNK + HALO), pl.ds(column, width)]
    count = taps.shape[0]
    result = taps[count - 1 : count] * window[HALO : HALO + CHUNK]
    moved = []
    for offset in range(1, count):
        rows = jnp.where(pos >= offset, window[HALO - offset : HALO - offset + CHUNK], 0.0)
        moved.append(rows)
        result = result + taps[count - 1 - offset : count - offset] * rows
    return result, window[HALO : HALO + CHUNK], moved


def fill_padded(raw_ref, pad_ref, width):
    pad_ref[0:HALO, :] = jnp.zeros((HALO, width), WIDE)
    total = raw_ref.shape[0]

    def copy(index, _):
        start = pl.multiple_of(index * CHUNK, CHUNK)
        pad_ref[pl.ds(start + HALO, CHUNK), :] = raw_ref[pl.ds(start, CHUNK), 0:width].astype(NARROW).astype(WIDE)
        return 0

    lax.fori_loop(0, total // CHUNK, copy, 0)


def one_hot(first, second, offset):
    return jnp.where(first - offset == second, 1.0, 0.0).astype(NARROW)


def plain_dot(left, right, left_dim=1, right_dim=0):
    return lax.dot_general(left, right, (((left_dim,), (right_dim,)), ((), ())), preferred_element_type=WIDE)


def pack_rows(near_col, pieces):
    size = pieces[0].shape[0]
    lane = lax.broadcasted_iota(jnp.int32, (near_col.shape[0], size), 1)
    total = plain_dot(one_hot(near_col, lane, 0), pieces[0][...])
    for k in range(1, len(pieces)):
        total = total + plain_dot(one_hot(near_col, lane, k * size), pieces[k][...])
    return total


def unpack_rows(far_row, packed, k, size):
    down = lax.broadcasted_iota(jnp.int32, (size, far_row.shape[1]), 0)
    return plain_dot(one_hot(far_row, down, k * size), packed).astype(NARROW)


def beta_of(raw_ref, rows, lane):
    return jax.nn.sigmoid(raw_ref[rows, lane:lane + 1].astype(NARROW).astype(WIDE))


def shard_places(size, features, shard_rows, turned_round):
    unit, each = shard_rows
    shape = (features, size) if turned_round else (size, features)
    value = lax.broadcasted_iota(jnp.int32, shape, 1 if turned_round else 0)
    lane = lax.broadcasted_iota(jnp.int32, shape, 0 if turned_round else 1)
    chosen = (lane // unit == value // each) & (lane % unit == value % each)
    return jnp.where(chosen, 1.0, 0.0).astype(NARROW)


def spread_side(heads, width, shard_rows, z_ref, side_ref, taps_ref, gain_ref):
    span = heads * width
    taps_count = taps_ref.shape[1]
    own = pl.ds(pl.multiple_of(z_ref[0] * span, span), span)
    for which in range(3):
        first_row = heads + 2 + which * taps_count
        taps_ref[which] = side_ref[first_row:first_row + taps_count, own]
    last_row = heads + 2 + 3 * taps_count
    entries = jnp.broadcast_to(side_ref[last_row:last_row + 1, :], (8, side_ref.shape[1])).astype(NARROW)
    gain_ref[...] = plain_dot(entries, shard_places(width, side_ref.shape[1], shard_rows, True))[0:1]


def forward_kernel(heads, width, n_fs, shard_rows, *refs):
    pieces, refs = refs[:n_fs], refs[n_fs:]
    (win_ref, near_ref, far_ref, segcol_ref, poscol_ref, segrow_ref, edges_ref, z_ref, *refs) = refs
    blocks, refs = refs[:n_fs], refs[n_fs:]
    (side_ref, hidden_ref, raw_ref, out_ref, q_ref, k_ref, inv_ref, score_ref, dots_ref, upd_ref, state_ref,
     move_ref, taps_ref, gain_ref, pad_ref, base_ref, w_ref, normed_ref) = refs
    total = raw_ref.shape[0]
    count = total // CHUNK
    span = heads * width
    side_ref[...] = win_ref[:, 4 * span:].astype(WIDE).T
    spread_side(heads, width, shard_rows, z_ref, side_ref, taps_ref, gain_ref)

    pad_ref[0:HALO, :] = jnp.zeros((HALO, 3 * span), WIDE)

    def enter(index, _):
        rows = pl.ds(pl.multiple_of(index * ENTER, ENTER), ENTER)
        packed = pack_rows(near_ref[rows, :], pieces)
        scale = lax.rsqrt(jnp.mean(packed * packed, axis=-1, keepdims=True) + norm_eps)
        hidden = (packed * scale * side_ref[heads:heads + 1, :]).astype(NARROW)
        hidden_ref[rows, :] = hidden
        raw = plain_dot(hidden, win_ref[...])
        raw_ref[rows, :] = raw
        pad_ref[pl.ds(pl.multiple_of(index * ENTER + HALO, HALO), ENTER), :] = (
            raw[:, 0:3 * span].astype(NARROW).astype(WIDE))
        return 0

    lax.fori_loop(0, total // ENTER, enter, 0)

    def first(group, _):
        work = []
        for sub in range(PER_STEP):
            index = group * PER_STEP + sub
            start = pl.multiple_of(index * CHUNK, CHUNK)
            rows = pl.ds(start, CHUNK)
            pos = poscol_ref[rows, :]
            before, after = edges_ref[index, 0], edges_ref[index, 1]
            strict, inclusive, carried, last = chunk_masks(
                segcol_ref[rows, :], segrow_ref[pl.ds(index, 1), :], before, after)
            keep = jnp.where(before == after, 1.0, 0.0).astype(WIDE)
            for head in range(heads):
                cols = pl.ds(head * width, width)
                parts = []
                for which in range(3):
                    column = which * span + head * width
                    value = conv_rows(pad_ref, taps_ref[which, :, head * width:(head + 1) * width], pos,
                                      start, column, width)[0]
                    parts.append(value * jax.nn.sigmoid(value))
                query, key, value = parts
                query = query * lax.rsqrt(jnp.sum(query * query, axis=-1, keepdims=True) + unit_eps)
                key = key * lax.rsqrt(jnp.sum(key * key, axis=-1, keepdims=True) + unit_eps)
                q_ref[rows, cols] = query
                k_ref[rows, cols] = key
                beta = beta_of(raw_ref, rows, 4 * span + head)
                key_h, query_h = halves(key), halves(query)
                dots = product(key_h, key_h, 1, 1)
                score = jnp.where(inclusive, product(query_h, key_h, 1, 1), 0.0)
                at = index * heads + head
                dots_ref[at] = dots
                score_ref[at] = score
                work.append((at, rows, cols, keep, jnp.where(strict, beta * dots, 0.0),
                             beta * value, (beta * carried) * key, last * key))
        inverses = unit_lower_inverses([item[4] for item in work])
        for inverse, (at, rows, cols, keep, _, right, carry_in, tail_in) in zip(inverses, work):
            inv_h = halves(inverse)
            base = product(inv_h, halves(right))
            carry = product(inv_h, halves(carry_in))
            tail = turned(tail_in)
            eye = jnp.where(lax.broadcasted_iota(jnp.int32, (width, width), 0)
                            == lax.broadcasted_iota(jnp.int32, (width, width), 1), keep, 0.0)
            inv_ref[at] = inverse
            base_ref[rows, cols] = base
            w_ref[rows, cols] = carry
            move_ref[at] = eye - product(tail, halves(carry))
            state_ref[at] = product(tail, halves(base))
        return 0

    lax.fori_loop(0, count // PER_STEP, first, 0)

    def second(index, states):
        result = []
        for head in range(heads):
            at = index * heads + head
            added = state_ref[at]
            state_ref[at] = states[head]
            result.append(product(halves(move_ref[at]), halves(states[head])) + added)
        return tuple(result)

    lax.fori_loop(
        0, count, second, tuple(jnp.zeros((width, width), WIDE) for _ in range(heads)), unroll=True
    )

    def third(index, _):
        rows = pl.ds(pl.multiple_of(index * CHUNK, CHUNK), CHUNK)
        carried = jnp.where(segcol_ref[rows, :] == edges_ref[index, 0], 1.0, 0.0).astype(WIDE)
        for head in range(heads):
            cols = pl.ds(head * width, width)
            at = index * heads + head
            state = halves(state_ref[at])
            update = base_ref[rows, cols] - product(halves(w_ref[rows, cols]), state)
            upd_ref[rows, cols] = update
            out = carried * product(halves(q_ref[rows, cols]), state)
            out = out + product(halves(score_ref[at]), halves(update))
            mixed = out.astype(NARROW)
            out_ref[rows, cols] = mixed
            mixed = mixed.astype(WIDE)
            scale = lax.rsqrt(jnp.mean(mixed * mixed, axis=-1, keepdims=True) + norm_eps)
            gate = raw_ref[rows, pl.ds(3 * span + head * width, width)]
            normed = mixed * scale * gain_ref[...] * (gate * jax.nn.sigmoid(gate))
            normed_ref[rows, cols] = normed.astype(NARROW)
        return 0

    lax.fori_loop(0, count, third, 0)
    for k, block in enumerate(blocks):
        block[...] = unpack_rows(far_ref[...], normed_ref[...], k, total // n_fs)


def backward_kernel(heads, width, n_fs, shard_rows, *refs):
    pieces, refs = refs[:n_fs], refs[n_fs:]
    (win_ref, near_ref, far_ref, segcol_ref, poscol_ref, segrow_ref, edges_ref, z_ref, dgffn_ref,
     side_ref, hidden_ref, raw_ref, mixed_ref, q_ref, k_ref, inv_ref, score_ref, dots_ref, upd_ref, state_ref,
     move_ref, gradin_ref, *refs) = refs
    blocks, refs = refs[:n_fs], refs[n_fs:]
    (taps_ref, gain_ref, draw_ref, dhid_ref, dtaps_ref, sum_ref, small_ref, pad_ref, grad_ref, pdo_ref, dconv_ref, dout_ref, dnormed_ref) = refs
    total = raw_ref.shape[0]

    spread_side(heads, width, shard_rows, z_ref, side_ref, taps_ref, gain_ref)

    def enter(index, _):
        rows = pl.ds(pl.multiple_of(index * ENTER, ENTER), ENTER)
        dnormed_ref[rows, :] = pack_rows(near_ref[rows, :], pieces).astype(NARROW)
        return 0

    lax.fori_loop(0, total // ENTER, enter, 0)
    count = total // CHUNK
    span = heads * width
    fill_padded(raw_ref, pad_ref, 3 * span)

    def first(group, dgain):
        for sub in range(BACK_STEP):
            index = group * BACK_STEP + sub
            rows = pl.ds(pl.multiple_of(index * CHUNK, CHUNK), CHUNK)
            carried = jnp.where(segcol_ref[rows, :] == edges_ref[index, 0], 1.0, 0.0).astype(WIDE)
            for head in range(heads):
                cols = pl.ds(head * width, width)
                at = index * heads + head
                mixed = mixed_ref[rows, cols].astype(WIDE)
                scale = lax.rsqrt(jnp.mean(mixed * mixed, axis=-1, keepdims=True) + norm_eps)
                gate_cols = pl.ds(3 * span + head * width, width)
                gate = raw_ref[rows, gate_cols]
                sig = jax.nn.sigmoid(gate)
                given = dnormed_ref[rows, cols].astype(WIDE)
                unit = mixed * scale
                dgate = given * unit * gain_ref[...] * (sig * (1.0 + gate * (1.0 - sig)))
                draw_ref[rows, gate_cols] = dgate.astype(NARROW)
                given = given * (gate * sig)
                dgain = dgain + jnp.sum(given * unit, axis=0, keepdims=True)
                given = given * gain_ref[...]
                dout = scale * (given - unit * jnp.mean(unit * given, axis=-1, keepdims=True))
                dout = dout.astype(NARROW)
                dout_ref[rows, cols] = dout
                score_t = turned(score_ref[at])
                back = product_exact(score_t, dout)
                pdo_ref[rows, cols] = back
                inv_t = turned(inv_ref[at])
                back = product(inv_t, halves(back))
                query_t = turned(carried * q_ref[rows, cols])
                key_t = turned((beta_of(raw_ref, rows, 4 * span + head) * carried) * k_ref[rows, cols])
                grad_ref[at] = product_exact(query_t, dout) - product(key_t, halves(back))
        return dgain

    dgain = lax.fori_loop(0, count // BACK_STEP, first, jnp.zeros((1, width), WIDE))

    def second(step, grads):
        index = count - 1 - step
        result = []
        for head in range(heads):
            at = index * heads + head
            added = grad_ref[at]
            grad_ref[at] = grads[head]
            result.append(product(turned(move_ref[at]), halves(grads[head])) + added)
        return tuple(result)

    lax.fori_loop(
        0, count, second, tuple(jnp.zeros((width, width), WIDE) for _ in range(heads)), unroll=True
    )
    dconv_ref[total:total + HALO, :] = jnp.zeros((HALO, 3 * span), WIDE)

    def third(group, tap_sums):
        for sub in range(BACK_STEP):
            index = group * BACK_STEP + sub
            start = pl.multiple_of(index * CHUNK, CHUNK)
            rows = pl.ds(start, CHUNK)
            pos = poscol_ref[rows, :]
            strict, inclusive, carried, last = chunk_masks(
                segcol_ref[rows, :], segrow_ref[pl.ds(index, 1), :], edges_ref[index, 0], edges_ref[index, 1])
            new_sums = []
            dbetas = []
            for head in range(heads):
                cols = pl.ds(head * width, width)
                at = index * heads + head
                beta = beta_of(raw_ref, rows, 4 * span + head)
                query, key, update = q_ref[rows, cols], k_ref[rows, cols], upd_ref[rows, cols]
                query_h, key_h, update_h = halves(query), halves(key), halves(update)
                dout = dout_ref[rows, cols]
                state, grad = halves(state_ref[at]), halves(grad_ref[at])
                convs = []
                for which in range(3):
                    column = which * span + head * width
                    convs.append(conv_rows(pad_ref, taps_ref[which, :, head * width:(head + 1) * width], pos,
                                           start, column, width))
                gates = [jax.nn.sigmoid(c[0]) for c in convs]
                value = convs[2][0] * gates[2]
                dupdate = pdo_ref[rows, cols] + last * product(key_h, grad)
                dright = product(turned(inv_ref[at]), halves(dupdate))
                dright_h = halves(dright)
                dscore = jnp.where(inclusive, product_exact(update_h, dout, 1, 1, flip=True), 0.0)
                dsystem = jnp.where(strict, product(dright_h, update_h, 1, 1), 0.0)
                dscore_h = halves(dscore)
                dquery = carried * product_exact(state, dout, 1, 1, flip=True) + product(dscore_h, key_h)
                weighted = beta * dsystem
                scaled = beta * carried
                dkey = product(turned(dscore), query_h) + last * product(update_h, grad, 1, 1)
                dkey = dkey - product(halves(weighted + weighted.T), key_h)
                dkey = dkey - scaled * product(dright_h, state, 1, 1)
                dvalue = beta * dright
                seen = carried * product(key_h, state)
                dbeta = jnp.sum(dright * (value - seen), axis=-1, keepdims=True) - jnp.sum(
                    dsystem * dots_ref[at], axis=-1, keepdims=True)
                dbetas.append(dbeta * beta * (1.0 - beta))
                sides = []
                for grads, unit, conv, gate in ((dquery, query, convs[0][0], gates[0]), (dkey, key, convs[1][0], gates[1])):
                    plain = conv * gate
                    inv_norm = lax.rsqrt(jnp.sum(plain * plain, axis=-1, keepdims=True) + unit_eps)
                    sides.append(inv_norm * (grads - unit * jnp.sum(unit * grads, axis=-1, keepdims=True)))
                sides.append(dvalue)
                for which in range(3):
                    conv, plain, moved = convs[which]
                    gate = gates[which]
                    dconv = sides[which] * gate * (1.0 + conv * (1.0 - gate))
                    column = which * span + head * width
                    dconv_ref[rows, pl.ds(column, width)] = dconv
                    sums = [jnp.sum(dconv * plain, axis=0, keepdims=True)]
                    for shifted in moved:
                        sums.append(jnp.sum(dconv * shifted, axis=0, keepdims=True))
                    new_sums.append(jnp.concatenate(sums[::-1], axis=0))
            lane = lax.broadcasted_iota(jnp.int32, (CHUNK, draw_ref.shape[1] - 4 * span), 1)
            packed = jnp.zeros(lane.shape, WIDE)
            for head in range(heads):
                packed = jnp.where(lane == head, dbetas[head], packed)
            draw_ref[rows, pl.ds(4 * span, lane.shape[1])] = packed.astype(draw_ref.dtype)
            tap_sums = tuple(old + new for old, new in zip(tap_sums, new_sums))
        return tap_sums

    zero = tuple(jnp.zeros((taps_ref.shape[1], width), WIDE) for _ in range(3 * heads))
    sums = lax.fori_loop(0, count // BACK_STEP, third, zero)
    for head in range(heads):
        for which in range(3):
            dtaps_ref[which, :, head * width:(head + 1) * width] = sums[head * 3 + which]
    taps_count = taps_ref.shape[1]

    def fourth(index, _):
        start = pl.multiple_of(index * CHUNK, CHUNK)
        pos_window = poscol_ref[pl.ds(start, CHUNK + HALO), :]
        for which in range(3):
            columns = pl.ds(which * span, span)
            window = dconv_ref[pl.ds(start, CHUNK + HALO), columns]
            result = taps_ref[which, taps_count - 1:taps_count, :] * window[0:CHUNK]
            for offset in range(1, taps_count):
                part = jnp.where(pos_window >= offset, window, 0.0)[offset:offset + CHUNK]
                result = result + taps_ref[which, taps_count - 1 - offset:taps_count - offset, :] * part
            draw_ref[pl.ds(start, CHUNK), columns] = result.astype(draw_ref.dtype)
        return 0

    lax.fori_loop(0, count, fourth, 0)

    def weigh(index, _):
        rows = pl.ds(pl.multiple_of(index * ENTER, ENTER), ENTER)
        sum_ref[...] += plain_dot(hidden_ref[rows, :], draw_ref[rows, :], 0, 0)
        return 0

    sum_ref[...] = jnp.zeros(sum_ref.shape, WIDE)
    lax.fori_loop(0, total // ENTER, weigh, 0)
    features = small_ref.shape[1]
    small_ref[...] = jnp.zeros(small_ref.shape, WIDE)
    small_ref[heads + 1:heads + 2, :] = dgffn_ref[...]
    own = pl.ds(pl.multiple_of(z_ref[0] * span, span), span)
    for which in range(3):
        first_row = heads + 2 + which * taps_count
        small_ref[first_row:first_row + taps_count, own] = dtaps_ref[which]
    last_row = heads + 2 + 3 * taps_count
    small_ref[last_row:last_row + 1, :] = product_exact(
        halves(jnp.broadcast_to(dgain, (8, width))), shard_places(width, features, shard_rows, False))[0:1]
    gain = win_ref[:, 4 * span + heads:4 * span + heads + 1].astype(WIDE)
    across = jnp.sum(sum_ref[...] * win_ref[...].astype(WIDE), axis=-1, keepdims=True) / gain
    beside = small_ref[...].T
    lane = lax.broadcasted_iota(jnp.int32, beside.shape, 1)
    gradin_ref[:, 0:4 * span] = sum_ref[:, 0:4 * span].astype(NARROW)
    beside = sum_ref[:, 4 * span:] + beside + jnp.where(lane == heads, across, 0.0)
    gradin_ref[:, 4 * span:] = beside.astype(NARROW)

    def leave(index, _):
        rows = pl.ds(pl.multiple_of(index * ENTER, ENTER), ENTER)
        dhid_ref[rows, :] = plain_dot(draw_ref[rows, :], win_ref[...], 1, 1).astype(NARROW)
        return 0

    lax.fori_loop(0, total // ENTER, leave, 0)
    for k, block in enumerate(blocks):
        block[...] = unpack_rows(far_ref[...], dhid_ref[...], k, total // n_fs)


def product_exact(left, exact, left_dim=1, right_dim=0, flip=False):
    def one(a):
        if flip:
            return lax.dot_general(exact, a, (((right_dim,), (left_dim,)), ((), ())), preferred_element_type=WIDE)
        return lax.dot_general(a, exact, (((left_dim,), (right_dim,)), ((), ())), preferred_element_type=WIDE)

    if PASSES == 1:
        return one(left[0])
    return one(left[0]) + one(left[1])


def cost(flops, size):
    return pl.CostEstimate(flops=flops, bytes_accessed=size, transcendentals=0)


def specs(count):
    return [pl.BlockSpec(memory_space=pltpu.VMEM)] * count


def anywhere():
    return pl.BlockSpec(memory_space=pl.ANY)


def in_scalars():
    return pl.BlockSpec(memory_space=pltpu.SMEM)


def delta_forward(pieces, w_in, near, far, segcol, poscol, segrow, edges, z, heads, width, n_taps, shard_rows):
    n_fs = len(pieces)
    total = near.shape[0]
    features, lanes = w_in.shape
    count = total // CHUNK
    span = heads * width
    thin = jax.ShapeDtypeStruct((total, span), NARROW)
    rows = jax.ShapeDtypeStruct((total, span), WIDE)
    full = jax.ShapeDtypeStruct((total, features), NARROW)
    square = jax.ShapeDtypeStruct((count * heads, CHUNK, CHUNK), WIDE)
    state = jax.ShapeDtypeStruct((count * heads, width, width), WIDE)
    block = jax.ShapeDtypeStruct((total // n_fs, span), NARROW)
    raw = jax.ShapeDtypeStruct((total, lanes), WIDE)
    side = jax.ShapeDtypeStruct((lanes - 4 * span, features), WIDE)
    result = pl.pallas_call(
        functools.partial(forward_kernel, heads, width, n_fs, shard_rows),
        out_shape=(block,) * n_fs
        + (side, full, raw, thin, rows, rows, square, square, square, rows, state, state),
        in_specs=specs(n_fs + 6) + [in_scalars()] * 2,
        out_specs=tuple(specs(n_fs + 12)),
        scratch_shapes=[
            pltpu.VMEM((3, n_taps, span), WIDE),
            pltpu.VMEM((1, width), WIDE),
            pltpu.VMEM((total + HALO, 3 * span), WIDE),
            pltpu.VMEM((total, span), WIDE),
            pltpu.VMEM((total, span), WIDE),
            pltpu.VMEM((total, span), NARROW),
        ],
        compiler_params=pltpu.CompilerParams(vmem_limit_bytes=60 << 20),
        cost_estimate=cost(30_000_000_000, 16 << 20),
        name="delta_forward",
    )(*pieces, w_in, near, far, segcol, poscol, segrow, edges, z)
    return result[:n_fs], result[n_fs], result[n_fs + 1 :]


def delta_backward(pieces, w_in, near, far, segcol, poscol, segrow, edges, z, dgffn, side, kept, heads, width, n_taps, shard_rows):
    n_fs = len(pieces)
    total = near.shape[0]
    features, lanes = w_in.shape
    count = total // CHUNK
    span = heads * width
    block = jax.ShapeDtypeStruct((total // n_fs, features), NARROW)
    result = pl.pallas_call(
        functools.partial(backward_kernel, heads, width, n_fs, shard_rows),
        out_shape=(jax.ShapeDtypeStruct((features, lanes), NARROW),) + (block,) * n_fs,
        in_specs=specs(n_fs + 6) + [in_scalars()] * 2 + specs(13),
        out_specs=tuple(specs(n_fs + 1)),
        scratch_shapes=[
            pltpu.VMEM((3, n_taps, span), WIDE),
            pltpu.VMEM((1, width), WIDE),
            pltpu.VMEM((total, lanes), NARROW),
            pltpu.VMEM((total, features), NARROW),
            pltpu.VMEM((3, n_taps, span), WIDE),
            pltpu.VMEM((features, lanes), WIDE),
            pltpu.VMEM((lanes - 4 * span, features), WIDE),
            pltpu.VMEM((total + HALO, 3 * span), WIDE),
            pltpu.VMEM((count * heads, width, width), WIDE),
            pltpu.VMEM((total, span), WIDE),
            pltpu.VMEM((total + HALO, 3 * span), WIDE),
            pltpu.VMEM((total, span), NARROW),
            pltpu.VMEM((total, span), NARROW),
        ],
        compiler_params=pltpu.CompilerParams(vmem_limit_bytes=52 << 20),
        cost_estimate=cost(40_000_000_000, 16 << 20),
        name="delta_backward",
    )(*pieces, w_in, near, far, segcol, poscol, segrow, edges, z, dgffn, side, *kept)
    return result[0], list(result[1:])


def finish_kernel(heads, span, n_taps, z_ref, *refs):
    n_fs = len(refs) - 10
    pieces, refs = refs[:n_fs], refs[n_fs:]
    (*grads, wout_ref, beta_ref, taps_ref, gmix_ref, gffn_ref, ghead_ref) = refs
    side = pl.ds(4 * span, 128)
    lane = lax.broadcasted_iota(jnp.int32, (128, beta_ref.shape[0]), 0)
    column = lax.broadcasted_iota(jnp.int32, (128, beta_ref.shape[0]), 1)
    wout = jnp.zeros(wout_ref.shape, WIDE)
    small = jnp.zeros((wout_ref.shape[0], 128), WIDE)
    beta = jnp.zeros(beta_ref.shape, WIDE)
    for k, piece in enumerate(pieces):
        line = lax.rem(z_ref[0] + n_fs - k, n_fs)
        place = pl.ds(pl.multiple_of(line * span, span), span)
        for which, grad in enumerate(grads):
            grad[:, place] = piece[:, which * span:(which + 1) * span].astype(WIDE)
        wout = wout + piece[:, 4 * span + 128:].astype(WIDE)
        beside = piece[:, side]
        small = small + beside.astype(WIDE)
        chosen = jnp.where((lane < heads) & (column == line * heads + lane), 1.0, 0.0)
        beta = beta + plain_dot(chosen.astype(NARROW), beside, 0, 1)
    wout_ref[...] = wout
    beta_ref[...] = beta
    small = small.T
    gmix_ref[...] = small[heads:heads + 1]
    gffn_ref[...] = small[heads + 1:heads + 2]
    last_row = heads + 2 + 3 * n_taps
    for which in range(3):
        first_row = heads + 2 + which * n_taps
        taps_ref[which] = small[first_row:first_row + n_taps]
    ghead_ref[...] = small[last_row:last_row + 1, :ghead_ref.shape[1]]


def finish(z, pieces, heads, span, n_taps, head_rows):
    rows = pieces[0].shape[0]
    n_fs = len(pieces)
    full = jax.ShapeDtypeStruct((rows, n_fs * span), WIDE)
    line = jax.ShapeDtypeStruct((1, rows), WIDE)
    return pl.pallas_call(
        functools.partial(finish_kernel, heads, span, n_taps),
        out_shape=(full,) * 5
        + (
            jax.ShapeDtypeStruct((n_fs * heads, rows), WIDE),
            jax.ShapeDtypeStruct((3, n_taps, rows), WIDE),
            line,
            line,
            jax.ShapeDtypeStruct((1, head_rows), WIDE),
        ),
        in_specs=[in_scalars()] + specs(n_fs),
        out_specs=tuple(specs(10)),
        cost_estimate=cost(1_000_000, 1 << 20),
        name="finish_inputs",
    )(z, *pieces)


def mix_out_kernel(n_fs, row, z_ref, *refs):
    pieces, refs = refs[:n_fs], refs[n_fs:]
    wout_ref, tokens_ref, gain_ref, middle_ref, ffn_ref, normed_ref = refs
    span = pieces[0].shape[1]
    middle = tokens_ref[...].astype(WIDE)
    for k, piece in enumerate(pieces):
        place = pl.ds(pl.multiple_of(lax.rem(z_ref[0] + n_fs - k, n_fs) * span, span), span)
        normed_ref[:, place] = piece[...]
        middle = middle + plain_dot(piece[...], wout_ref[place, :])
    middle_ref[...] = middle
    scale = lax.rsqrt(jnp.mean(middle * middle, axis=-1, keepdims=True) + norm_eps)
    ffn_ref[...] = (middle * scale * gain_ref[row:row + 1, :]).astype(NARROW)


def mix_out(z, pieces, w_out, tokens, side, row):
    n_fs = len(pieces)
    shape = tokens.shape
    return pl.pallas_call(
        functools.partial(mix_out_kernel, n_fs, row),
        out_shape=(
            jax.ShapeDtypeStruct(shape, WIDE),
            jax.ShapeDtypeStruct(shape, NARROW),
            jax.ShapeDtypeStruct(shape, NARROW),
        ),
        in_specs=[in_scalars()] + specs(n_fs + 3),
        out_specs=tuple(specs(3)),
        compiler_params=pltpu.CompilerParams(vmem_limit_bytes=40 << 20),
        cost_estimate=cost(2_000_000_000, 6 << 20),
        name="mix_out",
    )(z, *pieces, w_out, tokens, side)


def ffn_kernel(keys, unit, block_ref, *refs):
    count = TP
    rows_in, refs = refs[:count], refs[count:]
    cots, refs = refs[:count], refs[count:]
    weights, refs = refs[:len(keys)], refs[len(keys):]
    (wdown_ref, active_ref, dboth_ref, sent_ref, later_ref, own_ref, part_ref, *ordered) = refs
    own_rows = rows_in[0].shape[0]
    if ordered:
        for near, far in zip(weights, ordered):
            n_fs, size = near.shape[:2]
            for by in range(n_fs):
                line = lax.rem(block_ref[1] + n_fs - by, n_fs)
                for at in range(size // unit):
                    place = pl.ds(pl.multiple_of((at * n_fs + line) * unit, unit), unit)
                    far[place, :] = near[by, at * unit:(at + 1) * unit, :]
        weights = ordered
    depth = weights[0].shape[0]
    units = wdown_ref.shape[0]
    spots = [pl.ds(pl.multiple_of((block_ref[0] ^ key) * depth, depth), depth) for key in keys]
    half = count // 2 * own_rows
    for at in range(count - 1, -1, -1):
        rows = slice(at * own_rows, (at + 1) * own_rows)
        both = plain_dot(rows_in[at][:, spots[0]], weights[0][...])
        for spot, weight in zip(spots[1:], weights[1:]):
            both = both + plain_dot(rows_in[at][:, spot], weight[...])
        gate, up = both[:, :units], both[:, units:]
        sig = jax.nn.sigmoid(gate)
        silu = gate * sig
        active_ref[rows, :] = (silu * up).astype(NARROW)
        dactive = plain_dot(cots[at][...], wdown_ref[...], 1, 1)
        dboth_ref[rows, :units] = (dactive * up * (sig * (1.0 + gate * (1.0 - sig)))).astype(NARROW)
        dboth_ref[rows, units:] = (dactive * silu).astype(NARROW)
        dboth = dboth_ref[rows, :]
        for spot, weight in zip(spots, weights):
            part_ref[:, spot] = plain_dot(dboth, weight[...], 1, 1)
        if at >= count // 2:
            place = at * own_rows - half
            sent_ref[place:place + own_rows, :] = part_ref[...].astype(NARROW)
        elif at:
            later_ref[(at - 1) * own_rows:at * own_rows, :] = part_ref[...]
        else:
            own_ref[...] = part_ref[...]


def ffn_units(block, rows_in, cots, weights, keys, w_down, unit):
    own_rows, features = rows_in[0].shape
    units = w_down.shape[0]
    total = TP * own_rows
    return pl.pallas_call(
        functools.partial(ffn_kernel, keys, unit),
        out_shape=(
            jax.ShapeDtypeStruct((total, units), NARROW),
            jax.ShapeDtypeStruct((total, 2 * units), NARROW),
            jax.ShapeDtypeStruct((total // 2, features), NARROW),
            jax.ShapeDtypeStruct((total // 2 - own_rows, features), WIDE),
            jax.ShapeDtypeStruct((own_rows, features), WIDE),
        ),
        in_specs=[in_scalars()] + specs(2 * TP + len(weights) + 1),
        out_specs=tuple(specs(5)),
        scratch_shapes=[pltpu.VMEM((own_rows, features), WIDE)]
        + [pltpu.VMEM((features // len(keys), 2 * units), NARROW) for w in weights if w.ndim == 3],
        compiler_params=pltpu.CompilerParams(vmem_limit_bytes=52 << 20),
        cost_estimate=cost(8_000_000_000, 16 << 20),
        name="ffn_units",
    )(block, *rows_in, *cots, *weights, w_down)


def mix_back_kernel(n_fs, row, z_ref, *refs):
    sources, refs = refs[:6], refs[6:]
    gain_ref, refs = refs[0], refs[1:]
    blocks, refs = refs[:n_fs], refs[n_fs:]
    (dmiddle_ref, dbranch_ref, dgain_ref, *places, sems) = refs
    fetches = [pltpu.make_async_copy(source, place, sems.at[k]) for k, (source, place) in enumerate(
        zip((sources[0], sources[1].at[pl.ds(0, places[1].shape[0])], *sources[2:5]), places))]
    quarter = places[5].shape[0] // 4
    parts = [pl.ds(k * quarter, quarter) for k in range(4)]
    fetches += [
        pltpu.make_async_copy(sources[5].at[part], places[5].at[part], sems.at[5 + k]) for k, part in enumerate(parts)
    ]
    for fetch in fetches:
        fetch.start()
    own_ref, core_ref, side_ref, middle_ref, cot_ref, wout_ref = places
    for fetch in fetches[:5]:
        fetch.wait()
    middle = middle_ref[...]
    given = own_ref[...] + core_ref[...].astype(WIDE) + side_ref[...].astype(WIDE)
    scale = lax.rsqrt(jnp.mean(middle * middle, axis=-1, keepdims=True) + norm_eps)
    unit = middle * scale
    dgain_ref[...] = jnp.sum(given * unit, axis=0, keepdims=True)
    given = given * gain_ref[row:row + 1, :]
    dmiddle = cot_ref[...].astype(WIDE) + scale * (given - unit * jnp.mean(unit * given, axis=-1, keepdims=True))
    dmiddle_ref[...] = dmiddle
    dbranch = dmiddle.astype(NARROW)
    dbranch_ref[...] = dbranch
    span = blocks[0].shape[1]
    for fetch in fetches[5:]:
        fetch.wait()
    for k, block in enumerate(blocks):
        place = pl.ds(pl.multiple_of(lax.rem(z_ref[0] + k, n_fs) * span, span), span)
        block[...] = plain_dot(dbranch, wout_ref[place, :], 1, 1).astype(NARROW)


def mix_back(z, parts, middle, side, row, cotangent, w_out, n_fs):
    count, features = middle.shape
    block = jax.ShapeDtypeStruct((count, features // n_fs), NARROW)
    sources = (*parts, middle, cotangent, w_out)
    result = pl.pallas_call(
        functools.partial(mix_back_kernel, n_fs, row),
        out_shape=(block,) * n_fs
        + (
            jax.ShapeDtypeStruct(middle.shape, WIDE),
            jax.ShapeDtypeStruct(middle.shape, NARROW),
            jax.ShapeDtypeStruct((1, features), WIDE),
        ),
        in_specs=[in_scalars()] + [anywhere()] * 6 + specs(1),
        out_specs=tuple(specs(n_fs + 3)),
        scratch_shapes=[pltpu.VMEM((min(part.shape[0], count) if k < 5 else part.shape[0], features), part.dtype) for k, part in enumerate(sources)] + [pltpu.SemaphoreType.DMA((9,))],
        compiler_params=pltpu.CompilerParams(vmem_limit_bytes=60 << 20),
        cost_estimate=cost(2_000_000_000, 6 << 20),
        name="mix_back",
    )(z, *sources, side)
    return (result[:n_fs],) + tuple(result[n_fs:])


def rms_scale(values, gain):
    return values * lax.rsqrt(jnp.mean(values * values, axis=-1, keepdims=True) + norm_eps) * gain


def swiglu(gate_proj, up_proj):
    return jax.nn.silu(gate_proj) * up_proj


def sequence_layout(lengths_row, total):
    ends = jnp.cumsum(lengths_row)
    index = jnp.arange(total, dtype=jnp.int32)
    before = index[:, None] >= ends[None, :]
    segment = jnp.sum(before.astype(jnp.int32), axis=1)
    start = jnp.sum(jnp.where(before, lengths_row[None, :], 0), axis=1)
    return (segment, index - start)


def project(left, right):
    return jnp.dot(left, right, preferred_element_type=WIDE)


def project_back(left, right):
    return lax.dot_general(left, right, (((1,), (1,)), ((), ())), preferred_element_type=WIDE)


def weight_grad(left, right):
    return lax.dot_general(left, right, (((0,), (0,)), ((), ())), preferred_element_type=WIDE)


def flip(value, bit, n_dp):
    return lax.ppermute(value, "dp", [(i, i ^ bit) for i in range(n_dp)])


def shift(value, by, n_fs):
    return lax.ppermute(value, "fsdp", [(i, (i + by) % n_fs) for i in range(n_fs)])


def line_pieces(shard, n_fs):
    return [shard] + [shift(shard, by, n_fs) for by in range(1, n_fs)]


def line_order(pieces, z):
    n_fs = len(pieces)
    shape = pieces[0].shape
    whole = jnp.zeros((shape[0], n_fs) + shape[1:], pieces[0].dtype)
    for by, piece in enumerate(pieces):
        whole = lax.dynamic_update_slice_in_dim(whole, piece[:, None], lax.rem(z + n_fs - by, n_fs), 1)
    return whole


def gather_cube(piece, order, n_dp):
    pieces = {0: piece}
    for bit in order:
        for key in list(pieces):
            pieces[key ^ bit] = flip(pieces[key], bit, n_dp)
    return pieces


def in_order(pieces, me):
    rows = pieces[0].shape[0]
    whole = jnp.zeros((len(pieces) * rows,) + pieces[0].shape[1:], pieces[0].dtype)
    unit = max(pieces).bit_length()
    step = (1 << unit) // len(pieces)
    for key, piece in pieces.items():
        whole = lax.dynamic_update_slice_in_dim(whole, piece, lax.bitwise_xor(me, key // step) * rows, 0)
    return whole


def per_device(
    n_dp,
    n_fs,
    tokens,
    lengths,
    packing,
    w_query,
    w_key,
    w_value,
    w_gate,
    w_beta,
    conv_taps,
    w_out,
    gain_mix,
    gain_head,
    gain_ffn,
    w_ffn_gate,
    w_ffn_up,
    w_ffn_down,
    cotangent,
):
    me = lax.axis_index("dp")
    z = lax.axis_index("fsdp")
    bits = [1 << k for k in range(n_dp.bit_length() - 1)]
    first_order = bits[:1] + bits[1:]
    second_order = bits[:1] + bits[1:][::-1]
    packing_row = packing[0]
    lengths_row = lengths[0]
    own_rows, features = tokens.shape
    total = own_rows * n_fs
    rows = w_query.shape[0]
    heads_all = w_beta.shape[1]
    heads = heads_all // n_fs
    span = features // n_fs
    width = span // heads
    hidden_ffn = w_ffn_gate.shape[1]
    head_rows = gain_head.shape[0]
    n_taps = conv_taps.shape[1]

    def by_owner(matrix):
        return jnp.swapaxes(matrix.reshape(rows, n_fs, -1), 0, 1)

    small = jnp.concatenate(
        [
            gain_mix[:, None],
            gain_ffn[:, None],
            conv_taps.reshape(3 * n_taps, rows).T,
            jnp.pad(gain_head, (0, rows - head_rows))[:, None],
        ],
        axis=1,
    )
    n_small = small.shape[1]
    side = jnp.concatenate(
        [by_owner(w_beta), jnp.broadcast_to(small[None], (n_fs, rows, n_small))], axis=2
    )
    side = jnp.pad(side, ((0, 0), (0, 0), (0, 128 - heads - n_small)))
    packet = jnp.concatenate(
        [by_owner(w_query), by_owner(w_key), by_owner(w_value), by_owner(w_gate), side], axis=2
    )
    member = lax.rem(me, TP)
    block = me // TP
    n_rest = n_dp // TP
    ff_block = hidden_ffn // n_dp
    ff_line = ff_block // n_fs
    ff_unit = -(-ff_line // 8) * 8
    while n_rest * n_fs * ff_unit % 128:
        ff_unit += 8
    ff_pad = n_rest * n_fs * ff_unit
    tp_bits = [bit for bit in bits if bit < TP]
    rest_bits = [bit for bit in bits if bit >= TP]

    def by_member(matrix):
        split = matrix.reshape(rows, n_rest, TP, n_fs, ff_line)
        split = jnp.pad(split, ((0, 0),) * 4 + ((0, ff_unit - ff_line),))
        return jnp.transpose(split, (2, 0, 1, 3, 4)).reshape(TP, rows, ff_pad)

    def hand_out(blocks):
        pieces = [lax.dynamic_index_in_dim(blocks, z, 0)]
        for by in range(1, n_fs):
            pieces.append(shift(lax.dynamic_index_in_dim(blocks, lax.rem(z + by, n_fs), 0), by, n_fs))
        return pieces

    lanes = 4 * span + 128
    packet = jnp.concatenate([packet, jnp.broadcast_to(w_out[None], (n_fs,) + w_out.shape)], axis=2)
    packet = hand_out(packet)
    token_pieces = [tokens] + [shift(tokens, by, n_fs) for by in range(1, n_fs)]
    packet, token_pieces[1] = lax.optimization_barrier((packet, token_pieces[1]))
    packet_in = line_order([piece[:, :, :lanes] for piece in packet], z).reshape(n_fs * rows, lanes)
    packet_out = line_order([piece[:, :, lanes:] for piece in packet], z).reshape(n_fs * rows, features)
    w_in = lax.all_gather(packet_in, "dp", axis=0, tiled=True)
    full_out = lax.all_gather(packet_out, "dp", axis=0, tiled=True)

    owner, place = packing_row // own_rows, lax.rem(packing_row, own_rows)
    near = (lax.rem(z + n_fs - owner, n_fs) * own_rows + place)[:, None]
    far = (lax.rem(owner + n_fs - z, n_fs) * own_rows + place)[None]
    segment, position = sequence_layout(lengths_row, total)
    seg_rows = segment.reshape(-1, CHUNK)
    ends = seg_rows[:, -1]
    edges = jnp.stack([jnp.concatenate([jnp.full((1,), -1, jnp.int32), ends[:-1]]), ends], axis=1)
    z_ref = z.reshape(1)
    layout = (segment[:, None], jnp.pad(position, (0, HALO))[:, None], seg_rows, edges, z_ref)
    shard_rows = (rows, head_rows)
    own_gate, own_up, _ = lax.optimization_barrier((w_ffn_gate, w_ffn_up, token_pieces[1]))
    both_sends = jnp.concatenate([by_member(own_gate), by_member(own_up)], axis=2)
    blocks, side, kept = delta_forward(
        token_pieces, w_in, near, far, *layout, heads, width, n_taps, shard_rows
    )
    gain_row = heads + 1

    both_pieces = {
        key: flip(lax.dynamic_index_in_dim(both_sends, member ^ key, 0, keepdims=False), key, n_dp)
        if key
        else lax.dynamic_index_in_dim(both_sends, member, 0, keepdims=False)
        for key in range(TP)
    }
    own_down, _ = lax.optimization_barrier((w_ffn_down, token_pieces[1]))
    own_down = jnp.pad(own_down, ((0, ff_unit - ff_line), (0, 0)))
    down_rows = in_order(gather_cube(own_down, rest_bits, n_dp), block).reshape(n_rest, -1, features)
    both_rows = in_order(both_pieces, member).reshape(TP, rows, 2 * ff_pad)
    own_cotangent, both_rows, down_rows = lax.optimization_barrier((cotangent, both_rows, down_rows))
    both_rows, down_rows, _ = lax.optimization_barrier((both_rows, down_rows, token_pieces))
    both_line = line_pieces(both_rows, n_fs)
    both_line, blocks, down_rows = lax.optimization_barrier((both_line, blocks, down_rows))
    if rows % 16 == 0:
        both_rows = jnp.stack([piece.reshape(TP * rows, 2 * ff_pad) for piece in both_line])
    else:
        both_rows = line_order(both_line, z).reshape(-1, 2 * ff_pad)
    both_pieces = gather_cube(both_rows, rest_bits, n_dp)
    unit = 1 << (TP.bit_length() - 1)
    rest_keys = [key // unit for key in both_pieces]
    tp_order = sorted(range(TP), key=lambda key: tuple((key & bit) != 0 for bit in tp_bits))

    cot_pieces = gather_cube(own_cotangent, tp_bits[::-1], n_dp)
    cot_pieces, blocks = lax.optimization_barrier((cot_pieces, blocks))

    def halve(value, index, some_bits):
        unit = some_bits[0] if some_bits else 1
        for bit in some_bits[::-1]:
            half = value.shape[0] // 2
            mine = (index // (bit // unit)) % 2
            sent = lax.dynamic_slice_in_dim(value, (1 - mine) * half, half, 0)
            value = lax.dynamic_slice_in_dim(value, mine * half, half, 0)
            value = value.astype(WIDE) + flip(sent.astype(NARROW), bit, n_dp).astype(WIDE)
        return value

    def sum_up(pieces, whole):
        total = lax.dynamic_index_in_dim(whole, z, 0, keepdims=False).astype(WIDE)
        for piece in pieces[1:]:
            total = total + piece[0].astype(WIDE)
        return total

    def pass_on(parts):
        return [parts[0]] + [shift(part, by, n_fs) for by, part in enumerate(parts) if by]

    mixed_pieces = pass_on(blocks)
    down_line = line_pieces(down_rows, n_fs)
    middle, ffn_in, normed_b = mix_out(z_ref, mixed_pieces, full_out, tokens, side, gain_row)
    w_down = line_order(down_line, z).reshape(ff_pad, features)
    ffn_pieces = gather_cube(ffn_in, tp_bits[::-1], n_dp)
    active_b, d_both, first, second, d_own = ffn_units(
        jnp.stack([block, z]),
        [ffn_pieces[key] for key in tp_order],
        [cot_pieces[key] for key in tp_order],
        list(both_pieces.values()),
        rest_keys,
        w_down,
        rows,
    )
    ffn_near = jnp.concatenate([ffn_pieces[key] for key in tp_order], axis=0)

    def both_part(lo, size):
        part = weight_grad(lax.dynamic_slice_in_dim(ffn_near, lo, size, 1), d_both)
        return part.reshape(-1, n_fs * rows, 2 * ff_pad)

    cotangent_near = jnp.concatenate([cot_pieces[key] for key in tp_order], axis=0)
    down_terms = weight_grad(active_b, cotangent_near).astype(NARROW)
    down_sum = lax.psum_scatter(
        down_terms.reshape(n_rest, -1, features), "fsdp", scatter_dimension=1, tiled=True
    )
    d_both, down_terms = lax.optimization_barrier((d_both, down_terms))
    split = features // 2 if rest_bits else features
    top = block // max(n_rest // 2, 1)
    if rest_bits:
        both_sent = both_part((1 - top) * split, split).astype(NARROW)
    else:
        both_sent = None
    from_core = flip(first, tp_bits[0], n_dp)
    second = second + from_core[own_rows:].astype(WIDE)
    second, both_sent, active_late = lax.optimization_barrier((second.astype(NARROW), both_sent, active_b))
    from_side = flip(second, tp_bits[1], n_dp)
    from_side, ffn_near, active_late = lax.optimization_barrier((from_side, ffn_near, active_late))
    both_sum = both_part(top * split if rest_bits else 0, split)

    d_blocks, d_middle, d_branch, d_gffn = mix_back(
        z_ref, (d_own, from_core, from_side), middle, side, gain_row, cotangent, full_out, n_fs
    )
    d_pieces = pass_on(d_blocks)
    d_branch, active_late = lax.optimization_barrier((d_branch, active_late))

    def out_term(units, lo):
        return project(units[lo * own_rows : (lo + 1) * own_rows], w_down)

    out_core = flip(project(active_late[2 * own_rows :], w_down).astype(NARROW), tp_bits[0], n_dp)
    out_sent = (out_term(active_late, 1) + out_core[own_rows:].astype(WIDE)).astype(NARROW)
    if rest_bits:
        both_came, out_sent = lax.optimization_barrier((flip(both_sent, rest_bits[-1], n_dp), out_sent))
        both_sum = both_sum + both_came.astype(WIDE)
        both_sum = halve(both_sum, block, rest_bits[:-1])
    out_side = flip(out_sent, tp_bits[1], n_dp)
    out_grad = weight_grad(normed_b, d_branch).astype(NARROW)
    sum_out = lax.psum_scatter(out_grad, "dp", scatter_dimension=0, tiled=True)
    both_sum = jnp.swapaxes(both_sum.reshape(TP, n_fs, rows, 2 * ff_pad), 0, 1)
    both_sum, d_pieces, out_grad = lax.optimization_barrier((both_sum, d_pieces, out_grad))
    both_line = hand_out(both_sum.astype(NARROW))

    grad_in, d_blocks = delta_backward(
        d_pieces, w_in, near, far, *layout, d_gffn, side, kept, heads, width, n_taps, shard_rows
    )
    grad_in, both_line, down_sum, sum_out = lax.optimization_barrier((grad_in, both_line, down_sum, sum_out))
    part = lax.psum_scatter(grad_in, "dp", scatter_dimension=0, tiled=True)
    d_blocks, both_line, active_late = lax.optimization_barrier((d_blocks, both_line, active_late))
    d_blocks = pass_on(d_blocks)
    layer_out = middle + out_term(active_late, 0) + out_core[:own_rows].astype(WIDE) + out_side.astype(WIDE)
    layer_out = layer_out.astype(NARROW)
    both_sum = sum_up(both_line, both_sum)
    grad_fdown = halve(down_sum, block, rest_bits)[0, :ff_line].astype(WIDE)
    both_pieces = {
        key: flip(
            lax.dynamic_index_in_dim(both_sum, member ^ key, 0, keepdims=False).astype(NARROW), key, n_dp
        ).astype(WIDE)
        if key
        else lax.dynamic_index_in_dim(both_sum, member, 0, keepdims=False)
        for key in range(TP)
    }
    both_mine = in_order({key: piece[None] for key, piece in both_pieces.items()}, member)
    def units_of(which):
        part = both_mine[:, :, which * ff_pad : (which + 1) * ff_pad]
        part = part.reshape(TP, rows, n_rest, n_fs, ff_unit)[..., :ff_line]
        return jnp.transpose(part, (1, 2, 0, 3, 4)).reshape(rows, hidden_ffn)

    lanes = part.shape[1]
    joint = jnp.concatenate([part, sum_out], axis=1).reshape(n_fs, rows, -1)
    arrived = [piece[0] for piece in hand_out(joint)]
    d_blocks, arrived[0], layer_out = lax.optimization_barrier((d_blocks, arrived[0], layer_out))
    d_hidden = d_blocks[0].astype(WIDE)
    for block_of in d_blocks[1:]:
        d_hidden = d_hidden + block_of.astype(WIDE)
    _, norm_mix_back = jax.vjp(rms_scale, tokens.astype(WIDE), side[heads])
    d_inputs_norm, _ = norm_mix_back(d_hidden)
    grad_tokens = d_middle + d_inputs_norm

    grads, (grad_wout, grad_beta, grad_taps, grad_gmix, grad_gffn, grad_ghead) = (
        lambda outs: (outs[:4], outs[4:])
    )(finish(z_ref, arrived, heads, span, n_taps, head_rows))
    return (
        layer_out,
        grad_tokens,
        grads[0],
        grads[1],
        grads[2],
        grads[3],
        grad_beta.T,
        grad_taps,
        grad_wout,
        grad_gmix[0],
        grad_ghead[0],
        grad_gffn[0],
        units_of(0),
        units_of(1),
        grad_fdown,
    )


def solution(mesh):
    both = ("dp", "fsdp")
    rows = P(both, None)
    group = P("dp", None)
    taps = P(None, None, both)
    line = P(both)
    in_specs = (rows, group, group) + (rows,) * 5 + (taps, rows, line, line, line) + (rows,) * 4
    out_specs = (rows,) * 7 + (taps, rows, line, line, line) + (rows,) * 3
    return jax.shard_map(
        functools.partial(per_device, mesh.shape["dp"], mesh.shape["fsdp"]),
        mesh=mesh,
        in_specs=in_specs,
        out_specs=out_specs,
        check_vma=False,
    )
```
